256 devices in a mesh: dp: 32 (over x_lo, z, core), expert: 8 (over x_hi, y).
Axes of the slice: x: 4 (x_hi: 2, x_lo: 2; x = x_hi * 2 + x_lo), y: 4, z: 8, core: 2. Of those that a mesh axis runs over, the one named last changes fastest.
Arguments:
- tokens: bfloat16 [49152, 4096], P(('dp', 'expert')), may hold values from -24 to 24
- routes: int32 [49152, 2], P(('dp', 'expert')), may hold values from 0 to 7, all different within a row; in each aligned block of 192 rows (0 to 191, 192 to 383, ...) at most 64 rows name the same one
- positives: int32 [512], P(('dp', 'expert')), may hold values from 0 to 511, each once
- expert_out: bfloat16 [32, 8, 8, 64, 4096], P('dp', 'expert'), may hold values from -6 to 6
- router: bfloat16 [4096, 8], replicated, may hold values from -0.09375 to 0.09375
- norm_gain: float32 [4096], replicated, may hold values from 0.25 to 1.75
- loss_scale: float32 [], replicated, may hold values from 8192 to 65536
Outputs:
- token_grad: bfloat16 [49152, 4096], P(('dp', 'expert'))
- expert_grad: bfloat16 [32, 8, 8, 64, 4096], P('dp', 'expert')
- router_grad: float32 [4096, 8], replicated
- loss: float32 [], replicated
The draws below stay inside these ranges and needn't reach their ends.
Inputs may be any that keep to these rules, and one draw needn't show every extreme that they name: `routes`: each row names 2 different experts; among the rows of one device no expert is named by more than 64 rows, a bound that some block reaches. `positives`: A permutation of the records.
All inputs are finite; a program needn't handle non-finite values.
Results may differ from the reference program's by a relative error of at most 0.0061.
Values may be sent and summed in bfloat16 or wider, within the bound.
No kernel may reach another device: no remote copies, remote signals or barrier semaphores. Data moves between devices by JAX's collectives and lax.ppermute only.
A program may use at most 128 MiB of HBM per device.

```python
import math
import jax
import jax.numpy as jnp
import numpy as np
from jax import lax

D = 4096
TOPK = 2
PAIR_DEV = 2
SEQ = 48
EXPERTS = 8
TOK_DEV = 192
CAP = 64
PAIRS = 512
TOKENS = 49152
N_DP = 32
N_EXPERT = 8


def draw_tokens(key, part):
    base_key = jax.random.fold_in(key, 7)
    key_common, key_noise = jax.random.split(base_key, 2)
    seq_count = TOKENS // SEQ
    common = jax.random.normal(key_common, (seq_count, 1, D), jnp.float32)
    noise_rows = jax.random.normal(key_noise, (seq_count, SEQ, D), jnp.float32)
    values = jnp.clip(common + noise_rows, -24.0, 24.0)
    return values.reshape(TOKENS, D).astype(jnp.bfloat16)


def level_of(stream_key, extent, cuts, low, high):
    def one(position, shards_of):
        draws = jax.random.uniform(jax.random.fold_in(jax.random.fold_in(stream_key, 6), position), (shards_of,), jnp.float32, low / len(cuts), high / len(cuts))
        return jnp.repeat(jnp.exp(draws), extent[position] // shards_of).reshape((-1,) + (1,) * (len(extent) - position - 1))

    factor_of = one(*cuts[0])
    for cut in cuts[1:]:
        factor_of = factor_of * one(*cut)
    return factor_of


def deal_out(stream_key, own, number, rows, amount, top, reach, slope):
    ranking = jax.random.permutation(stream_key, amount)
    crowded, usual = load_shares(amount, rows * top, reach, slope, True), load_shares(amount, rows * top, reach, slope, False)
    places = jnp.arange(amount)

    def named(tallies, rotation):
        used = int((tallies > 0).sum())
        fixed = max(1, used // 4)
        passed = fixed + (places - fixed + rotation * (used - fixed)) % max(1, amount - fixed)
        return jnp.zeros((amount,), jnp.int32).at[ranking[jnp.where(places < fixed, places, passed)]].set(jnp.asarray(tallies, jnp.int32))

    tallies = jnp.where(number % 4 == 0, named(crowded, number // 4), named(usual, number - number // 4 - 1))
    mixed = jax.random.permutation(jax.random.fold_in(own, 3), amount)
    source_of, sink = mixed[0:amount // 2 * 2:2], mixed[1:amount // 2 * 2:2]
    slack = jnp.minimum(tallies[source_of] - 1, reach - tallies[sink]) // 2
    slack = jnp.where((source_of == ranking[0]) | (sink == ranking[0]) | (tallies[sink] == 0), 0, jnp.maximum(slack, 0))
    passed = jax.random.randint(jax.random.fold_in(own, 4), (amount // 2,), 0, 1 << 20) % (slack + 1)
    tallies = tallies.at[source_of].add(-passed).at[sink].add(passed)
    labels = jnp.searchsorted(jnp.cumsum(tallies), jnp.arange(rows * top), side="right").astype(jnp.int32)
    listing = labels.reshape(top, rows).T
    listing = listing[jax.random.permutation(jax.random.fold_in(own, 1), rows)]
    rotation = jax.random.randint(jax.random.fold_in(own, 2), (rows, 1), 0, top)
    return jnp.take_along_axis(listing, (jnp.arange(top)[None, :] + rotation) % top, axis=1)


def load_shares(count, total, most, skew, full):
    portions = [(1 << 20) // math.isqrt(standing ** skew) + 1 for standing in range(1, count + 1)]
    largest = most if full else min(most, max(-(-total // count), total * portions[0] // sum(portions)))
    least = 1 if total - largest >= count - 1 else 0
    counts, spare = [largest] + [least] * (count - 1), total - largest - least * (count - 1)
    while spare > 0:
        candidates = [i for i in range(1, count) if counts[i] < largest] or [i for i in range(1, count) if counts[i] < most]
        whole, budget = sum([portions[i] for i in candidates]), spare
        for i in candidates:
            more = min(most - counts[i], max(1, budget * portions[i] // whole), spare)
            counts[i] = counts[i] + more
            spare = spare - more
    return np.array(counts)


def normal_values(rng, dims, deviation, most, shards=(), kind=jnp.bfloat16):
    array = deviation * jax.random.normal(rng, dims, jnp.float32)
    if shards:
        array = array * level_of(rng, dims, shards, -0.22, 0.18)
    return jnp.clip(array, -most, most).astype(kind)


def setup_inputs(seed: int = 0) -> dict:
    keys = jax.random.split(jax.random.key(seed), 8)
    tokens = draw_tokens(jax.random.fold_in(keys[7], 71), 0)
    routes_keys = jax.random.split(jax.random.fold_in(keys[1], 1), TOKENS // TOK_DEV)
    routes_turns = jax.random.permutation(jax.random.fold_in(keys[1], 3), TOKENS // TOK_DEV)
    routes = jax.vmap(lambda own, number: deal_out(jax.random.fold_in(keys[1], 2), own, number, TOK_DEV, EXPERTS, TOPK, CAP, 1))(routes_keys, routes_turns).reshape((TOKENS, TOPK))
    positives = jax.random.permutation(keys[2], PAIRS).astype(jnp.int32)
    expert_out = normal_values(keys[3], (N_DP, EXPERTS, EXPERTS, CAP, D), 1.0, 6.0, ((0, 32), (1, 8)))
    router = normal_values(keys[4], (D, EXPERTS), D ** -0.5, 0.09375)
    norm_gain = jnp.clip(1.0 + 0.15 * jax.random.normal(keys[5], (D,), jnp.float32), 0.25, 1.75)
    loss_scale = jnp.clip(jnp.exp(jax.random.uniform(keys[6], (), jnp.float32, math.log(8192.0), math.log(65536.0))), 8192.0, 65536.0)
    return {"tokens": tokens, "routes": routes, "positives": positives, "expert_out": expert_out, "router": router, "norm_gain": norm_gain, "loss_scale": loss_scale}


norm_eps = 1e-05

def slot_where(routes, experts, capacity):
    hit_table = (routes[:, :, None] == jnp.arange(experts, dtype=jnp.int32)[None, None, :]).astype(jnp.int32)
    flat_hits = hit_table.reshape(-1, experts)
    before = jnp.cumsum(flat_hits, axis=0) - flat_hits
    slot_rank = lax.optimization_barrier(jnp.sum(before * flat_hits, axis=1)).reshape(routes.shape)
    return (routes * capacity + slot_rank).astype(jnp.int32)

def forward_rows(tokens, routes, received, router, norm_gain):
    experts = received.shape[0]
    capacity = received.shape[1]
    hidden_width = received.shape[2]
    logits = jnp.dot(tokens, router, preferred_element_type=jnp.float32)
    one_hot = (routes[:, :, None] == jnp.arange(experts, dtype=jnp.int32)[None, None, :]).astype(jnp.float32)
    chosen = lax.optimization_barrier(jnp.sum(one_hot * logits[:, None, :], axis=2))
    gate_mix = jax.nn.softmax(chosen, axis=1)
    slot_rows = slot_where(routes, experts, capacity)
    fetched = received.reshape(experts * capacity, hidden_width)[slot_rows]
    summed_rows = tokens.astype(jnp.float32) + gate_mix[:, 0:1] * fetched[:, 0].astype(jnp.float32) + gate_mix[:, 1:2] * fetched[:, 1].astype(jnp.float32)
    inverse = lax.rsqrt(lax.optimization_barrier(jnp.mean(summed_rows * summed_rows, axis=1, keepdims=True)) + norm_eps)
    normed = summed_rows * inverse * norm_gain
    pooled = lax.optimization_barrier(jnp.mean(normed.reshape(-1, SEQ, hidden_width), axis=1)).astype(jnp.bfloat16)
    return (pooled, (gate_mix, one_hot, slot_rows, fetched, summed_rows, inverse))

def backward_rows(tokens, router, norm_gain, saved, grad_pool, experts, capacity):
    gate_mix, one_hot, slot_rows, fetched, summed_rows, inverse = saved
    hidden_width = tokens.shape[1]
    grad_rows = jnp.broadcast_to(grad_pool[:, None, :] / SEQ, (grad_pool.shape[0], SEQ, hidden_width)).reshape(-1, hidden_width)
    weighted = grad_rows * norm_gain
    grad_summed = inverse * weighted - summed_rows * inverse ** 3 * lax.optimization_barrier(jnp.mean(weighted * summed_rows, axis=1, keepdims=True))
    grad_gate = lax.optimization_barrier(jnp.sum(grad_summed[:, None, :] * fetched.astype(jnp.float32), axis=2))
    grad_chosen = gate_mix * (grad_gate - lax.optimization_barrier(jnp.sum(gate_mix * grad_gate, axis=1, keepdims=True)))
    grad_logits = lax.optimization_barrier(jnp.sum(one_hot * grad_chosen[:, :, None], axis=1)).astype(jnp.bfloat16)
    router_part = lax.dot_general(tokens, grad_logits, (((0,), (0,)), ((), ())), preferred_element_type=jnp.float32)
    through_router = lax.dot_general(grad_logits, router, (((1,), (1,)), ((), ())), preferred_element_type=jnp.float32)
    token_grad = (grad_summed + through_router).astype(jnp.bfloat16)
    outgoing = (gate_mix[:, :, None] * grad_summed[:, None, :]).astype(jnp.bfloat16).reshape(-1, hidden_width)
    sendback = jnp.zeros((experts * capacity, hidden_width), jnp.bfloat16).at[slot_rows.reshape(-1)].set(outgoing)
    return (token_grad, sendback.reshape(experts, capacity, hidden_width), router_part)

def reference(tokens, routes, positives, expert_out, router, norm_gain, loss_scale):
    device_count = N_DP * N_EXPERT
    experts = expert_out.shape[1]
    capacity = expert_out.shape[3]
    hidden_width = tokens.shape[1]
    row_blocks = tokens.reshape(device_count, -1, hidden_width)
    route_blocks = routes.reshape(device_count, -1, TOPK)
    received = jnp.transpose(expert_out, (0, 2, 1, 3, 4)).reshape(device_count, experts, capacity, hidden_width)

    def embed_block(bundle):
        return forward_rows(bundle[0], bundle[1], bundle[2], router, norm_gain)[0]
    pooled = lax.map(embed_block, (row_blocks, route_blocks, received))
    queries = pooled[:, :PAIR_DEV].reshape(PAIRS, hidden_width)
    records = pooled[:, PAIR_DEV:].reshape(PAIRS, hidden_width)
    score_scale = 4.0 / math.sqrt(D)
    scores = lax.dot_general(queries, records, (((1,), (1,)), ((), ())), preferred_element_type=jnp.float32) * score_scale
    highest = lax.optimization_barrier(jnp.max(scores, axis=1, keepdims=True))
    log_total = highest[:, 0] + jnp.log(lax.optimization_barrier(jnp.sum(jnp.exp(scores - highest), axis=1)))
    is_positive = jnp.arange(PAIRS, dtype=jnp.int32)[None, :] == positives[:, None]
    positive_score = lax.optimization_barrier(jnp.sum(jnp.where(is_positive, scores, jnp.zeros_like(scores)), axis=1))
    loss = jnp.mean(log_total - positive_score)
    softmax_rows = jnp.exp(scores - log_total[:, None])
    score_grad = ((softmax_rows - is_positive.astype(jnp.float32)) * (loss_scale / PAIRS)).astype(jnp.bfloat16)
    grad_queries = jnp.dot(score_grad, records, preferred_element_type=jnp.float32) * score_scale
    grad_records = lax.dot_general(score_grad, queries, (((0,), (0,)), ((), ())), preferred_element_type=jnp.float32) * score_scale
    grad_pool = jnp.concatenate([grad_queries.reshape(device_count, PAIR_DEV, hidden_width), grad_records.reshape(device_count, PAIR_DEV, hidden_width)], axis=1)

    def back_block(bundle):
        pooled_rows, saved = forward_rows(bundle[0], bundle[1], bundle[2], router, norm_gain)
        return backward_rows(bundle[0], router, norm_gain, saved, bundle[3], experts, capacity)
    token_parts, sendback, router_parts = lax.map(back_block, (row_blocks, route_blocks, received, grad_pool))
    token_grad = token_parts.reshape(-1, hidden_width)
    expert_grad = jnp.transpose(sendback.reshape(N_DP, N_EXPERT, experts, capacity, hidden_width), (0, 2, 1, 3, 4))
    router_grad = lax.optimization_barrier(jnp.sum(router_parts, axis=0))
    return (token_grad, expert_grad, router_grad, loss)
```

```python
import math

import jax
import jax.numpy as jnp
from jax import lax
from jax.sharding import Mesh, PartitionSpec as P

PAIR_DEV = 2
SEQ = 48
EPS = 1e-05
CORES = 2
F32 = jnp.float32
BF16 = jnp.bfloat16


def swap_core(x):
    return lax.ppermute(x, "c", [(0, 1), (1, 0)])


def spread(x, axes, size):
    return lax.all_to_all(
        jnp.broadcast_to(x[None], (size,) + x.shape), axes, split_axis=0, concat_axis=0, tiled=True
    )


def routing(tokens, routes, router, experts, capacity):
    logits = jnp.dot(tokens, router, preferred_element_type=F32)
    lanes = jnp.arange(experts, dtype=jnp.int32)[None, None, :]
    one_hot = (routes[:, :, None] == lanes).astype(F32)
    chosen = jnp.sum(one_hot * logits[:, None, :], axis=2)
    gates = jax.nn.softmax(chosen, axis=1)
    rows = routes.shape[0]
    hits = jnp.sum(one_hot, axis=1)
    order = jnp.arange(rows, dtype=jnp.int32)
    earlier = (order[None, :] < order[:, None]).astype(BF16)
    before = jnp.dot(earlier, hits.astype(BF16), preferred_element_type=F32)
    rank = jnp.sum(one_hot * before[:, None, :], axis=2).astype(jnp.int32)
    return gates, one_hot, routes * capacity + rank


def split_bf16(x):
    high = x.astype(BF16)
    rest = x - high.astype(F32)
    mid = rest.astype(BF16)
    low = (rest - mid.astype(F32)).astype(BF16)
    return jnp.concatenate([high, mid, low], axis=0)


def shards(tokens, routes, positives, expert_out, router, norm_gain, loss_scale):
    experts, capacity, width = expert_out.shape[2:]
    rows = tokens.shape[0]
    slots = experts * capacity
    outer = lax.axis_size("u")
    place = lax.axis_index("u")
    core = lax.axis_index("c")
    mine = lax.axis_index("expert")
    wide = outer * experts
    part = width // experts
    group = PAIR_DEV * experts
    pairs = group * outer * CORES
    scale = 4.0 / math.sqrt(width)

    received = lax.all_to_all(
        expert_out.reshape(experts, capacity, width), "expert", split_axis=0, concat_axis=0, tiled=True
    ).reshape(slots, width)
    gates, one_hot, slot = routing(tokens, routes, router, experts, capacity)

    slot_ids = jnp.arange(slots, dtype=jnp.int32)[None, :]
    picks = [(slot[:, k : k + 1] == slot_ids) for k in range(2)]
    fetched = [jnp.dot(p.astype(BF16), received, preferred_element_type=F32) for p in picks]
    summed = tokens.astype(F32) + gates[:, 0:1] * fetched[0] + gates[:, 1:2] * fetched[1]
    inverse = lax.rsqrt(jnp.mean(summed * summed, axis=1, keepdims=True) + EPS)
    overlap = jnp.concatenate([jnp.sum(summed * f, axis=1, keepdims=True) for f in fetched], axis=1)
    normed = summed * inverse * norm_gain
    pooled = jnp.mean(normed.reshape(-1, SEQ, width), axis=1).astype(BF16)
    taken = picks[0] | picks[1]
    sendback = lax.dot_general(
        taken.astype(BF16), summed.astype(BF16), (((0,), (0,)), ((), ())), preferred_element_type=F32
    ).astype(BF16)
    gate_slot = jnp.sum(
        jnp.where(picks[0], gates[:, 0:1], 0.0) + jnp.where(picks[1], gates[:, 1:2], 0.0), axis=0
    )
    inverse_slot = jnp.sum(jnp.where(taken, inverse, 0.0), axis=0)
    sequence = (jnp.arange(rows, dtype=jnp.int32) // SEQ).astype(F32)
    sequence_slot = jnp.sum(jnp.where(taken, sequence[:, None], 0.0), axis=0)

    sliced = jnp.transpose(pooled.reshape(2 * PAIR_DEV, experts, part), (1, 0, 2))
    offered = jnp.broadcast_to(sliced[None], (outer,) + sliced.shape).reshape(wide, 2 * PAIR_DEV, part)
    near = lax.all_to_all(offered, ("u", "expert"), split_axis=0, concat_axis=0, tiled=True)
    returned = lax.all_to_all(
        sendback.reshape(experts, capacity, width), "expert", split_axis=0, concat_axis=0, tiled=True
    )
    far = swap_core(near)
    queries = jnp.concatenate([x[:, :PAIR_DEV].reshape(-1, part) for x in (near, far)], axis=0)
    records = jnp.concatenate([x[:, PAIR_DEV:].reshape(-1, part) for x in (near, far)], axis=0)
    own = lax.dynamic_slice_in_dim(near, place * experts, experts, axis=0)
    own_queries = own[:, :PAIR_DEV].reshape(group, part)
    own_records = own[:, PAIR_DEV:].reshape(group, part)
    contract = (((1,), (1,)), ((), ()))
    by_query = lax.dot_general(own_queries, records, contract, preferred_element_type=F32)
    by_record = lax.dot_general(own_records, queries, contract, preferred_element_type=F32)
    notes = jnp.stack(
        [gate_slot, inverse_slot, sequence_slot, jnp.pad(positives.astype(F32), (0, slots - PAIR_DEV))]
        + [jnp.zeros_like(gate_slot)] * 4
    )
    gathered = spread(jnp.concatenate([by_query, by_record, notes], axis=0), "expert", experts)
    scores = jnp.sum(gathered[:, : 2 * group], axis=0) * scale
    by_query, by_record = scores[:group], scores[group:]
    own_positive = gathered[:, 2 * group + 3, :PAIR_DEV].reshape(group)

    column = jnp.arange(pairs // CORES, dtype=jnp.int32)
    column = (column // group) * (CORES * group) + column % group
    names = jnp.concatenate([column + core * group, column + (1 - core) * group]).astype(F32)
    hit = own_positive[:, None] == names[None, :]
    highest = jnp.max(by_query, axis=1, keepdims=True)
    log_total = highest + jnp.log(jnp.sum(jnp.exp(by_query - highest), axis=1, keepdims=True))
    row_loss = log_total[:, 0] - jnp.sum(jnp.where(hit, by_query, 0.0), axis=1)
    told = jnp.concatenate([log_total[:, 0], own_positive, jnp.sum(row_loss)[None]])
    told = jnp.pad(told, (0, 128 - told.shape[0]))
    heard = spread(told[None], ("u", "c"), outer * CORES).reshape(outer, CORES, 128)
    loss = jnp.sum(heard[:, :, 2 * group]) / pairs
    heard = jnp.concatenate(
        [lax.dynamic_index_in_dim(heard, i, axis=1, keepdims=False) for i in (core, 1 - core)], axis=0
    )
    all_total = heard[:, :group].reshape(1, pairs)
    all_positive = heard[:, group : 2 * group].reshape(1, pairs)
    own_names = ((place * CORES + core) * group + jnp.arange(group, dtype=jnp.int32)).astype(F32)
    factor = loss_scale / pairs
    grad_by_query = ((jnp.exp(by_query - log_total) - hit.astype(F32)) * factor).astype(BF16)
    hit_record = (all_positive == own_names[:, None]).astype(F32)
    grad_by_record = ((jnp.exp(by_record - all_total) - hit_record) * factor).astype(BF16)
    grad_sliced = scale * jnp.concatenate(
        [
            jnp.dot(grad_by_query, records, preferred_element_type=F32),
            jnp.dot(grad_by_record, queries, preferred_element_type=F32),
        ],
        axis=0,
    )
    grads = spread(grad_sliced, "expert", experts)
    grads = jnp.transpose(grads, (1, 0, 2)).reshape(2 * group, width)
    weighted_all = grads * (norm_gain / SEQ)[None, :]

    by_source = weighted_all.reshape(2, experts, PAIR_DEV, width)
    weighted = lax.dynamic_index_in_dim(by_source, mine, axis=1, keepdims=False).reshape(-1, width)
    count = weighted.shape[0]
    on_slots = jnp.dot(split_bf16(weighted), received.T, preferred_element_type=F32)
    on_slots = jnp.sum(on_slots.reshape(3, count, slots), axis=0)
    on_rows = jnp.repeat(on_slots, SEQ, axis=0)
    along = jnp.concatenate(
        [jnp.sum(jnp.where(p, on_rows, 0.0), axis=1, keepdims=True) for p in picks], axis=1
    )
    weighted_rows = jnp.repeat(weighted, SEQ, axis=0)
    shrink = inverse**3 * jnp.mean(weighted_rows * summed, axis=1, keepdims=True)
    grad_gate = inverse * along - shrink * overlap
    grad_chosen = gates * (grad_gate - jnp.sum(gates * grad_gate, axis=1, keepdims=True))
    grad_logits = jnp.sum(one_hot * grad_chosen[:, :, None], axis=1).astype(BF16)
    router_part = lax.dot_general(
        grad_logits, tokens, (((0,), (0,)), ((), ())), preferred_element_type=F32
    )
    router_part = router_part + swap_core(router_part)
    router_part = router_part.reshape(wide, 1, -1)
    router_part = lax.all_to_all(
        router_part, ("u", "expert"), split_axis=0, concat_axis=0, tiled=True
    )
    router_sum = jnp.sum(router_part, axis=0)
    router_grad = spread(router_sum, ("u", "expert"), wide).reshape(experts, width).T
    through = lax.dot_general(
        grad_logits, router, (((1,), (1,)), ((), ())), preferred_element_type=F32
    )
    token_grad = (inverse * weighted_rows - shrink * summed + through).astype(BF16)

    held = lax.dynamic_slice_in_dim(gathered[:, 2 * group : 2 * group + 3], mine * capacity, capacity, axis=2)
    gate_here, inverse_here, sequence_here = held[:, 0], held[:, 1], held[:, 2].astype(jnp.int32)
    by_slot = jnp.zeros((experts, capacity, width), F32)
    per_source = jnp.transpose(by_source, (1, 0, 2, 3)).reshape(experts, 2 * PAIR_DEV, width)
    for s in range(2 * PAIR_DEV):
        by_slot = jnp.where((sequence_here == s)[:, :, None], per_source[:, s : s + 1], by_slot)
    back = returned.astype(F32)
    shrink_here = inverse_here**3 * jnp.mean(by_slot * back, axis=2)
    expert_grad = gate_here[:, :, None] * (inverse_here[:, :, None] * by_slot - shrink_here[:, :, None] * back)
    expert_grad = expert_grad.astype(BF16).reshape(1, 1, experts, capacity, width)
    return token_grad, expert_grad, router_grad, loss


def solution(mesh):
    outer = mesh.shape["dp"] // CORES
    fine = Mesh(
        mesh.devices.reshape(outer, CORES, mesh.shape["expert"]), ("u", "c", "expert")
    )
    everywhere = ("u", "c", "expert")
    placed = (
        P(everywhere, None),
        P(everywhere, None),
        P(everywhere),
        P(("u", "c"), "expert", None, None, None),
        P(),
        P(),
        P(),
    )
    return jax.shard_map(
        shards,
        mesh=fine,
        in_specs=placed,
        out_specs=(P(everywhere, None), P(("u", "c"), "expert", None, None, None), P(), P()),
        check_vma=False,
    )
```

```python
import functools
import math

import jax
import jax.numpy as jnp
from jax import lax
from jax.experimental import pallas as pl
from jax.experimental.pallas import tpu as pltpu
from jax.sharding import Mesh, PartitionSpec as P

PAIR_DEV = 2
SEQ = 48
EPS = 1e-05
CORES = 2
ROWS_DEV = 2 * PAIR_DEV
F32 = jnp.float32
BF16 = jnp.bfloat16
I32 = jnp.int32
VMEM = pl.BlockSpec(memory_space=pltpu.VMEM)
SMEM = pl.BlockSpec(memory_space=pltpu.SMEM)
NT = (((1,), (1,)), ((), ()))


def iota(shape, dim):
    return lax.broadcasted_iota(I32, shape, dim)


def params(**more):
    return pltpu.CompilerParams(vmem_limit_bytes=40 << 20, **more)


def cost(flops, moved):
    return pl.CostEstimate(flops=flops, bytes_accessed=moved, transcendentals=0)


def fold(x):
    total = x[:, :128]
    for k in range(1, x.shape[1] // 128):
        total = total + x[:, 128 * k : 128 * (k + 1)]
    return total


def swap_core(x):
    return lax.ppermute(x, "c", [(0, 1), (1, 0)])


def exchange(x, axes):
    return lax.all_to_all(x, axes, split_axis=0, concat_axis=0, tiled=True)


def routing(tokens, routes, router, experts, capacity):
    logits = jnp.dot(tokens, router, preferred_element_type=F32)
    lanes = jnp.arange(experts, dtype=I32)[None, None, :]
    one_hot = (routes[:, :, None] == lanes).astype(F32)
    chosen = jnp.sum(one_hot * logits[:, None, :], axis=2)
    gates = jax.nn.softmax(chosen, axis=1)
    rows = routes.shape[0]
    hits = jnp.sum(one_hot, axis=1)
    order = jnp.arange(rows, dtype=I32)
    earlier = (order[None, :] < order[:, None]).astype(BF16)
    before = jnp.dot(earlier, hits.astype(BF16), preferred_element_type=F32)
    rank = jnp.sum(one_hot * before[:, None, :], axis=2).astype(I32)
    return gates, routes * capacity + rank


def forward_kernel(steps, outer, tok, rec, slot, gate, gain, summed, offered, inverse, held, square):
    step = pl.program_id(0)
    part = tok.shape[1]
    rows, slots = tok.shape[0], rec.shape[0]
    ids = iota((rows, slots), 1)
    first = (slot[:, 0:1] == ids).astype(BF16)
    second = (slot[:, 1:2] == ids).astype(BF16)

    @pl.when(step == 0)
    def _():
        square[...] = jnp.zeros_like(square)

    for k in range(part // 256):
        cols = slice(256 * k, 256 * (k + 1))
        block = rec[:, cols]
        x = (
            tok[:, cols].astype(F32)
            + gate[:, 0:1] * jnp.dot(first, block, preferred_element_type=F32)
            + gate[:, 1:2] * jnp.dot(second, block, preferred_element_type=F32)
        )
        summed[:, cols] = x
        held[step, :, cols] = x
        square[...] += fold(x * x)

    @pl.when(step == steps - 1)
    def _():
        mean = jnp.sum(square[...], axis=1, keepdims=True) / (steps * part)
        scale = lax.rsqrt(mean + EPS)
        inverse[...] = scale
        count = rows // SEQ
        for e in range(steps):
            x = held[e] * scale
            x = jnp.sum(x.reshape(count, SEQ, part), axis=1) / SEQ
            x = (x * gain[:, part * e : part * (e + 1)]).astype(BF16)
            for u in range(outer):
                offered[u * steps + e] = x


def forward(tokens, received, slot, gates, gain, experts, outer):
    rows, width = tokens.shape
    slots = received.shape[0]
    part = width // experts
    whole = lambda shape: pl.BlockSpec(shape, lambda i: (0,) * len(shape))
    return pl.pallas_call(
        functools.partial(forward_kernel, experts, outer),
        grid=(experts,),
        in_specs=[
            pl.BlockSpec((rows, part), lambda i: (0, i)),
            pl.BlockSpec((slots, part), lambda i: (0, i)),
            whole((rows, 2)),
            whole((rows, 2)),
            whole((1, width)),
        ],
        out_specs=[
            pl.BlockSpec((rows, part), lambda i: (0, i)),
            whole((outer * experts, rows // SEQ, part)),
            whole((rows, 1)),
        ],
        out_shape=[
            jax.ShapeDtypeStruct((rows, width), F32),
            jax.ShapeDtypeStruct((outer * experts, rows // SEQ, part), BF16),
            jax.ShapeDtypeStruct((rows, 1), F32),
        ],
        scratch_shapes=[pltpu.VMEM((experts, rows, part), F32), pltpu.VMEM((rows, 128), F32)],
        compiler_params=params(),
        cost_estimate=cost(4 * rows * slots * width, 10 << 20),
    )(tokens, received, slot, gates, gain)


def pack_kernel(steps, place, x, rec, slot, turned, overlap, *rest):
    outs, dots = rest[:-1], rest[-1]
    step = pl.program_id(0)
    rows, part = x.shape
    slots = rec.shape[0]
    capacity = slots // len(outs)
    ids = iota((rows, slots), 1)
    first = (slot[:, 0:1] == ids).astype(BF16)
    second = (slot[:, 1:2] == ids).astype(BF16)
    target = lax.rem(iota((slots, rows), 0) + place[0] * capacity, slots)
    spot = ((turned[0:1, :] == target) | (turned[1:2, :] == target)).astype(BF16)

    @pl.when(step == 0)
    def _():
        dots[...] = jnp.zeros_like(dots)

    for k in range(part // 256):
        cols = slice(256 * k, 256 * (k + 1))
        value = x[:, cols]
        block = rec[:, cols]
        dots[0] += fold(value * jnp.dot(first, block, preferred_element_type=F32))
        dots[1] += fold(value * jnp.dot(second, block, preferred_element_type=F32))
        moved = jnp.dot(spot, value.astype(BF16), preferred_element_type=F32).astype(BF16)
        for r, out in enumerate(outs):
            out[:, cols] = moved[capacity * r : capacity * (r + 1)]

    @pl.when(step == steps - 1)
    def _():
        overlap[...] = jnp.concatenate(
            [jnp.sum(dots[k], axis=1, keepdims=True) for k in range(2)], axis=1
        )


def pack(place, summed, received, slot, experts, capacity):
    rows, width = summed.shape
    slots = received.shape[0]
    part = width // experts
    whole = lambda shape: pl.BlockSpec(shape, lambda i: (0,) * len(shape))
    return pl.pallas_call(
        functools.partial(pack_kernel, experts),
        grid=(experts,),
        in_specs=[
            SMEM,
            pl.BlockSpec((rows, part), lambda i: (0, i)),
            pl.BlockSpec((slots, part), lambda i: (0, i)),
            whole((rows, 2)),
            whole((2, rows)),
        ],
        out_specs=[whole((rows, 2))] + [pl.BlockSpec((capacity, part), lambda i: (0, i))] * experts,
        out_shape=[jax.ShapeDtypeStruct((rows, 2), F32)]
        + [jax.ShapeDtypeStruct((capacity, width), BF16)] * experts,
        scratch_shapes=[pltpu.VMEM((2, rows, 128), F32)],
        compiler_params=params(),
        cost_estimate=cost(6 * rows * slots * width, 11 << 20),
    )(place, summed, received, slot, slot.T)


def lanes_of(shape, dim):
    lane = iota(shape, dim)
    kind = lax.rem(lane, ROWS_DEV)
    return lane, kind, kind >= PAIR_DEV


def picker(group, kind, turned=False):
    wide = 2 * group
    shape, pair, row = ((wide, group), 1, 0) if turned else ((group, wide), 0, 1)
    a = iota(shape, pair)
    b = iota(shape, row)
    source = (a // PAIR_DEV) * ROWS_DEV + lax.rem(a, PAIR_DEV) + PAIR_DEV * kind
    return (source == b).astype(BF16)


def scores_kernel(place, near, far, notes, offered):
    experts, total, columns = offered.shape
    group = experts * PAIR_DEV
    wide = 2 * group
    own = near[pl.ds(pl.multiple_of(place[0] * wide, wide), wide), :]
    queries, records = [
        jnp.dot(picker(group, kind), own, preferred_element_type=F32).astype(BF16) for kind in (0, 1)
    ]
    at_record = lanes_of((group, columns), 1)[2]
    blocks = []
    for side in (near, far):
        every = side[...]
        by_query = lax.dot_general(queries, every, NT, preferred_element_type=F32)
        by_record = lax.dot_general(records, every, NT, preferred_element_type=F32)
        blocks.append(jnp.where(at_record, by_query, by_record))
    blocks.append(notes[...])
    for e in range(experts):
        for k, block in enumerate(blocks):
            offered[e, group * k : group * k + block.shape[0], :] = block


def totals_kernel(scale, devices, place, gathered, offered, kept, own_total, own_positive, loss_row):
    experts, total, columns = gathered.shape
    group = experts * PAIR_DEV
    outer_size = columns // (2 * group)
    both = gathered[0]
    for e in range(1, experts):
        both = both + gathered[e]
    positive_lane = both[2 * group + 3 : 2 * group + 4, :]
    near, far = both[:group] * scale, both[group : 2 * group] * scale
    kept[0:group] = near
    kept[group : 2 * group] = far

    shape = (group, columns)
    lane, kind, at_record = lanes_of(shape, 1)
    pair = iota(shape, 0)
    within = lax.rem(lane, 2 * group)
    matching = (within // ROWS_DEV == pair // PAIR_DEV) & (kind == lax.rem(pair, PAIR_DEV))
    here = matching & (lane // (2 * group) == place[0])
    positive = jnp.sum(jnp.where(here, positive_lane, 0.0), axis=1, keepdims=True)

    low = jnp.float32(-jnp.inf)
    near_records = jnp.where(at_record, near, low)
    far_records = jnp.where(at_record, far, low)
    highest = jnp.maximum(
        jnp.max(near_records, axis=1, keepdims=True), jnp.max(far_records, axis=1, keepdims=True)
    )
    weight = jnp.sum(jnp.exp(near_records - highest), axis=1, keepdims=True) + jnp.sum(
        jnp.exp(far_records - highest), axis=1, keepdims=True
    )
    log_total = highest + jnp.log(weight)
    chosen = jnp.zeros((group, 1), F32)
    for side, core in ((near, place[1]), (far, 1 - place[1])):
        name = column_names(lane, kind, group, core)
        hit = at_record & (name.astype(F32) == positive)
        chosen = chosen + jnp.sum(jnp.where(hit, side, 0.0), axis=1, keepdims=True)
    own_total[...] = log_total
    own_positive[...] = positive
    row_loss = log_total - chosen

    total_lane = jnp.sum(jnp.where(here, log_total, 0.0), axis=0, keepdims=True)
    loss_lane = jnp.sum(
        jnp.where(matching & (lane // (2 * group) == place[0]), row_loss, 0.0), axis=0, keepdims=True
    )
    own_lane = jnp.where(lane[0:1] // (2 * group) == place[0], positive_lane, 0.0)
    loss_row[...] = loss_lane
    pieces = [x[:, 128 * k : 128 * (k + 1)] for x in (total_lane, own_lane) for k in range(columns // 128)]
    loss_pieces = [
        pltpu.roll(loss_lane, PAIR_DEV, 1)[:, 128 * k : 128 * (k + 1)] for k in range(columns // 128)
    ]
    pieces = [a + b for a, b in zip(pieces, loss_pieces)] + pieces[columns // 128 :]
    message = jnp.concatenate(pieces, axis=0)
    for d in range(devices):
        offered[d] = message


def column_names(lane, kind, group, core):
    wide = 2 * group
    block = (lane // wide) * CORES + core
    return block * group + (lax.rem(lane, wide) // ROWS_DEV) * PAIR_DEV + lax.rem(kind, PAIR_DEV)


def gradient_kernel(scale, place, factor, heard, kept, own_total, own_positive, near, far, offered, loss):
    experts, wide, columns = offered.shape
    group = wide // 2
    outer_size = heard.shape[0] // CORES
    pieces = columns // 128
    shape = (group, columns)
    lane, kind, at_record = lanes_of(shape, 1)
    pair = iota(shape, 0)
    own_name = (place[0] * CORES + place[1]) * group + iota((group, 1), 0)
    row_lane = lane[0:1]
    result = jnp.zeros((wide, columns), F32)
    losses = jnp.zeros((1, columns), F32)
    for k, (side, core) in enumerate(((near, place[1]), (far, 1 - place[1]))):
        told = heard[core]
        for u in range(1, outer_size):
            told = told + heard[u * CORES + core]
        total = jnp.concatenate([told[i : i + 1] for i in range(pieces)], axis=1)
        positive = jnp.concatenate([told[pieces + i : pieces + i + 1] for i in range(pieces)], axis=1)
        losses = losses + jnp.where(at_record[0:1], total, 0.0)
        value = kept[group * k : group * (k + 1), :]
        name = column_names(lane, kind, group, core).astype(F32)
        hit = jnp.where(name == own_positive[...], 1.0, 0.0)
        by_query = (jnp.exp(value - own_total[...]) - hit) * factor[0]
        by_query = jnp.where(at_record, by_query, 0.0).astype(BF16)
        hit = jnp.where(positive == own_name.astype(F32), 1.0, 0.0)
        by_record = (jnp.exp(jnp.where(at_record, 0.0, value - total)) - hit) * factor[0]
        by_record = jnp.where(at_record, 0.0, by_record).astype(BF16)
        rows = jnp.dot(picker(group, 0, True), by_query, preferred_element_type=F32) + jnp.dot(
            picker(group, 1, True), by_record, preferred_element_type=F32
        )
        result = result + jnp.dot(rows.astype(BF16), side[...], preferred_element_type=F32)
    result = result * scale
    for e in range(experts):
        offered[e] = result
    loss[...] = jnp.sum(losses, axis=1, keepdims=True)


def rows_of(grads, e, index):
    tile = grads[e, pl.ds(pl.multiple_of((index // 2) * 8, 8), 8), :]
    return jnp.where(lax.rem(index, 2) == 0, tile[:ROWS_DEV], tile[ROWS_DEV:])


def split_bf16(x):
    high = x.astype(BF16)
    rest = x - high.astype(F32)
    mid = rest.astype(BF16)
    low = (rest - mid.astype(F32)).astype(BF16)
    return high, mid, low


def router_kernel(place, grads, gain, summed, rec, tok, slot, routes, gate, inverse, overlap, part_out, shrink_out, choice_out, weighted_out):
    experts, _, part = grads.shape
    rows = summed.shape[0]
    slots = rec.shape[0]
    count = rows // SEQ
    acc = [jnp.zeros((SEQ, 128), F32) for _ in range(count)]
    on_slots = jnp.zeros((16, slots), F32)
    for e in range(experts):
        cols = slice(part * e, part * (e + 1))
        w = rows_of(grads, e, place[0]) * (gain[:, cols] / SEQ)
        weighted_out[:, cols] = w
        lhs = jnp.concatenate(list(split_bf16(w)) + [jnp.zeros((count, part), BF16)], axis=0)
        on_slots = on_slots + lax.dot_general(lhs, rec[:, cols], NT, preferred_element_type=F32)
        for q in range(count):
            acc[q] = acc[q] + fold(summed[SEQ * q : SEQ * (q + 1), cols] * w[q : q + 1, :])
    on_slots = on_slots[0:count] + on_slots[count : 2 * count] + on_slots[2 * count : 3 * count]
    ids = iota((SEQ, slots), 1)
    lanes = iota((SEQ, 128), 1)
    choices = []
    for q in range(count):
        at = slice(SEQ * q, SEQ * (q + 1))
        inv = inverse[at]
        shrink = inv * inv * inv * (jnp.sum(acc[q], axis=1, keepdims=True) / (experts * part))
        shrink_out[at] = shrink
        row = on_slots[q : q + 1, :]
        grad_gate = []
        for k in range(2):
            along = jnp.sum(jnp.where(slot[at, k : k + 1] == ids, row, 0.0), axis=1, keepdims=True)
            grad_gate.append(inv * along - shrink * overlap[at, k : k + 1])
        gates = [gate[at, k : k + 1] for k in range(2)]
        mean = gates[0] * grad_gate[0] + gates[1] * grad_gate[1]
        choice = jnp.zeros((SEQ, 128), F32)
        for k in range(2):
            chosen = gates[k] * (grad_gate[k] - mean)
            choice = choice + jnp.where(routes[at, k : k + 1] == lanes, chosen, 0.0)
        choices.append(choice)
    choice = jnp.concatenate(choices, axis=0)
    choice_out[...] = choice.astype(BF16)
    lhs = jnp.transpose(choice)[:experts].astype(BF16)
    block = part_out.shape[1]
    for k in range(tok.shape[1] // block):
        cols = slice(block * k, block * (k + 1))
        part_out[experts * k : experts * (k + 1), :] = jnp.dot(
            lhs, tok[:, cols], preferred_element_type=F32
        )


def token_kernel(summed, weighted, inverse, shrink, choice, router, out):
    rows = summed.shape[0]
    through = jnp.dot(choice[...], router[...], preferred_element_type=F32)
    for q in range(rows // SEQ):
        at = slice(SEQ * q, SEQ * (q + 1))
        x = inverse[at] * weighted[q : q + 1, :] - shrink[at] * summed[at]
        out[at] = (x + through[SEQ * q : SEQ * (q + 1)]).astype(BF16)


def token_rows(summed, weighted, inverse, shrink, choice, router, parts):
    rows, width = summed.shape
    part = width // parts
    whole = lambda shape: pl.BlockSpec(shape, lambda i: (0, 0))
    split = lambda count: pl.BlockSpec((count, part), lambda i: (0, i))
    return pl.pallas_call(
        token_kernel,
        grid=(parts,),
        in_specs=[split(rows), split(weighted.shape[0]), whole((rows, 1)), whole((rows, 1)), whole((rows, 128)), split(128)],
        out_specs=split(rows),
        out_shape=jax.ShapeDtypeStruct((rows, width), BF16),
        compiler_params=params(),
        cost_estimate=cost(2 * rows * 128 * width, 5 << 20),
    )(summed, weighted, inverse, shrink, choice, router)


def expert_kernel(place, grads, gain, notes, *rest):
    experts = len(rest) - 1
    backs, out = rest[:experts], rest[experts]
    _, _, part = grads.shape
    step = pl.program_id(0)
    source = lax.rem(place[0] + experts - step, experts)
    gate, inv, seq = notes[0, :, 0:1], notes[0, :, 1:2], notes[0, :, 2:3]
    capacity = gate.shape[0]
    for r in range(experts):

        @pl.when(step == r)
        def _():
            back = backs[r]
            acc = jnp.zeros((capacity, 128), F32)
            rows = []
            for e in range(experts):
                cols = slice(part * e, part * (e + 1))
                w = rows_of(grads, e, source) * (gain[:, cols] / SEQ)
                x = jnp.broadcast_to(w[0:1], (capacity, part))
                for s in range(1, ROWS_DEV):
                    x = jnp.where(seq == s, w[s : s + 1], x)
                rows.append(w)
                acc = acc + fold(x * back[:, cols].astype(F32))
            shrink = inv * inv * inv * (jnp.sum(acc, axis=1, keepdims=True) / (experts * part))
            for e in range(experts):
                cols = slice(part * e, part * (e + 1))
                w = rows[e]
                x = jnp.broadcast_to(w[0:1], (capacity, part))
                for s in range(1, ROWS_DEV):
                    x = jnp.where(seq == s, w[s : s + 1], x)
                x = gate * (inv * x - shrink * back[:, cols].astype(F32))
                out[0, :, cols] = x.astype(BF16)


def expert_rows(place, grads, gain, notes, backs):
    experts, capacity = notes.shape[:2]
    width = gain.shape[1]
    whole = lambda shape: pl.BlockSpec(shape, lambda i, p: (0,) * len(shape))
    source = lambda i, p: (lax.rem(p[0] + experts - i, experts), 0, 0)
    return pl.pallas_call(
        expert_kernel,
        grid_spec=pltpu.PrefetchScalarGridSpec(
            num_scalar_prefetch=1,
            grid=(experts,),
            in_specs=[
                whole(grads.shape),
                whole((1, width)),
                pl.BlockSpec((1, capacity, notes.shape[2]), source),
            ]
            + [whole((capacity, width))] * experts,
            out_specs=pl.BlockSpec((1, capacity, width), source),
        ),
        out_shape=jax.ShapeDtypeStruct((experts, capacity, width), BF16),
        compiler_params=params(),
        cost_estimate=cost(12 * experts * capacity * width, 9 << 20),
    )(place, grads, gain, notes, *backs)


def turn_kernel(x, out):
    experts = out.shape[1]
    block = x.shape[1]
    for k in range(x.shape[0] // experts):
        out[block * k : block * (k + 1), :] = jnp.transpose(x[experts * k : experts * (k + 1), :])


def shards(tokens, routes, positives, expert_out, router, norm_gain, loss_scale):
    experts, capacity, width = expert_out.shape[2:]
    rows = tokens.shape[0]
    slots = experts * capacity
    outer = lax.axis_size("u")
    mine = lax.axis_index("expert").astype(I32)
    where = jnp.stack([lax.axis_index("u").astype(I32), lax.axis_index("c").astype(I32)])
    mine_at = mine[None]
    wide = outer * experts
    part = width // experts
    group = PAIR_DEV * experts
    pairs = group * outer * CORES
    scale = 4.0 / math.sqrt(width)
    gain = norm_gain[None, :]
    columns = outer * experts * ROWS_DEV

    received = exchange(expert_out.reshape(experts, capacity, width), "expert").reshape(slots, width)
    gates, slot = routing(tokens, routes, router, experts, capacity)
    lane = jnp.arange(columns, dtype=I32)
    spread_positive = jnp.where(
        (lane % (2 * group)) // ROWS_DEV == mine,
        jnp.where(lane % ROWS_DEV == 0, positives[0], positives[1]) * (lane % ROWS_DEV < PAIR_DEV),
        0,
    ).astype(F32)

    summed, offered, inverse = forward(tokens, received, slot, gates, gain, experts, outer)
    near = exchange(offered, ("u", "expert"))
    overlap, *outgoing = pack(mine_at, summed, received, slot, experts, capacity)
    backs = [outgoing[0]] + [
        lax.ppermute(outgoing[r], "expert", [(i, (i + r) % experts) for i in range(experts)])
        for r in range(1, experts)
    ]
    slot_ids = jnp.arange(slots, dtype=I32)[None, :]
    picks = [slot[:, k : k + 1] == slot_ids for k in range(2)]
    gate_slot = jnp.sum(
        jnp.where(picks[0], gates[:, 0:1], 0.0) + jnp.where(picks[1], gates[:, 1:2], 0.0), axis=0
    )
    taken = picks[0] | picks[1]
    inverse_slot = jnp.sum(jnp.where(taken, inverse, 0.0), axis=0)
    sequence = (jnp.arange(rows, dtype=I32) // SEQ).astype(F32)
    sequence_slot = jnp.sum(jnp.where(taken, sequence[:, None], 0.0), axis=0)
    notes = jnp.stack([gate_slot, inverse_slot, sequence_slot, spread_positive])
    notes = jnp.pad(notes, ((0, 4), (0, 0)))

    far = swap_core(near)
    near, far = near.reshape(columns, part), far.reshape(columns, part)
    offered = pl.pallas_call(
        scores_kernel,
        in_specs=[SMEM, VMEM, VMEM, VMEM],
        out_specs=VMEM,
        out_shape=jax.ShapeDtypeStruct((experts, 2 * group + 8, columns), F32),
        compiler_params=params(),
    )(where, near, far, notes)
    gathered = exchange(offered, "expert")
    column = jax.ShapeDtypeStruct((group, 1), F32)
    offered, kept, own_total, own_positive, _ = pl.pallas_call(
        functools.partial(totals_kernel, scale, outer * CORES),
        in_specs=[SMEM, VMEM],
        out_specs=[VMEM] * 5,
        out_shape=[
            jax.ShapeDtypeStruct((outer * CORES, 8, 128), F32),
            jax.ShapeDtypeStruct((2 * group, columns), F32),
            column,
            column,
            jax.ShapeDtypeStruct((1, columns), F32),
        ],
        compiler_params=params(),
    )(where, gathered)
    heard = exchange(offered, ("u", "c"))
    offered, loss = pl.pallas_call(
        functools.partial(gradient_kernel, scale),
        in_specs=[SMEM, SMEM] + [VMEM] * 6,
        out_specs=[VMEM, VMEM],
        out_shape=[
            jax.ShapeDtypeStruct((experts, 2 * group, part), F32),
            jax.ShapeDtypeStruct((1, 1), F32),
        ],
        compiler_params=params(),
    )(where, (loss_scale / pairs)[None], heard, kept, own_total, own_positive, near, far)
    grads = exchange(offered, "expert")

    router_part, shrink, choice, weighted = pl.pallas_call(
        router_kernel,
        in_specs=[SMEM] + [VMEM] * 10,
        out_specs=[VMEM] * 4,
        out_shape=[
            jax.ShapeDtypeStruct((wide, width * experts // wide), F32),
            jax.ShapeDtypeStruct((rows, 1), F32),
            jax.ShapeDtypeStruct((rows, 128), BF16),
            jax.ShapeDtypeStruct((rows // SEQ, width), F32),
        ],
        compiler_params=params(),
    )(mine_at, grads, gain, summed, received, tokens, slot, routes, gates, inverse, overlap)
    router_part = router_part + swap_core(router_part)
    router_part = exchange(router_part[:, None, :], ("u", "expert"))
    router_sum = jnp.sum(router_part, axis=0)
    router_all = exchange(jnp.broadcast_to(router_sum[None], (wide,) + router_sum.shape), ("u", "expert"))
    router_grad = pl.pallas_call(
        turn_kernel,
        in_specs=[VMEM],
        out_specs=VMEM,
        out_shape=jax.ShapeDtypeStruct((width, experts), F32),
        compiler_params=params(),
    )(router_all.reshape(wide, -1))

    turned = jnp.pad(router.T, ((0, 128 - experts), (0, 0)))
    token_grad = token_rows(summed, weighted, inverse, shrink, choice, turned, experts)
    held = lax.dynamic_slice_in_dim(gathered[:, 2 * group : 2 * group + 3], mine * capacity, capacity, axis=2)
    held = jnp.pad(jnp.transpose(held, (0, 2, 1)), ((0, 0), (0, 0), (0, 5)))
    expert_grad = expert_rows(mine_at, grads, gain, held, backs)
    return token_grad, expert_grad.reshape(1, 1, experts, capacity, width), router_grad, loss[0, 0] / pairs


def solution(mesh):
    outer = mesh.shape["dp"] // CORES
    fine = Mesh(mesh.devices.reshape(outer, CORES, mesh.shape["expert"]), ("u", "c", "expert"))
    everywhere = ("u", "c", "expert")
    return jax.shard_map(
        shards,
        mesh=fine,
        in_specs=(
            P(everywhere, None),
            P(everywhere, None),
            P(everywhere),
            P(("u", "c"), "expert", None, None, None),
            P(),
            P(),
            P(),
        ),
        out_specs=(P(everywhere, None), P(("u", "c"), "expert", None, None, None), P(), P()),
        check_vma=False,
    )
```

```python
import functools
import math

import jax
import jax.numpy as jnp
from jax import lax
from jax.experimental import pallas as pl
from jax.experimental.pallas import tpu as pltpu
from jax.sharding import Mesh, PartitionSpec as P

PAIR_DEV = 2
SEQ = 48
EPS = 1e-05
CORES = 2
ROWS_DEV = 2 * PAIR_DEV
F32 = jnp.float32
BF16 = jnp.bfloat16
I32 = jnp.int32
VMEM = pl.BlockSpec(memory_space=pltpu.VMEM)
SMEM = pl.BlockSpec(memory_space=pltpu.SMEM)
HBM = pl.BlockSpec(memory_space=pltpu.HBM)
NT = (((1,), (1,)), ((), ()))


def iota(shape, dim):
    return lax.broadcasted_iota(I32, shape, dim)


def params(mib):
    return pltpu.CompilerParams(vmem_limit_bytes=mib << 20)


def cost(flops, moved):
    return pl.CostEstimate(flops=flops, bytes_accessed=moved, transcendentals=0)


def fold(x):
    total = x[:, :128]
    for k in range(1, x.shape[1] // 128):
        total = total + x[:, 128 * k : 128 * (k + 1)]
    return total


def swap_core(x):
    return lax.ppermute(x, "c", [(0, 1), (1, 0)])


def exchange(x, axes):
    return lax.all_to_all(x, axes, split_axis=0, concat_axis=0, tiled=True)


def routing(tokens, routes, router, experts, capacity):
    logits = jnp.dot(tokens, router, preferred_element_type=F32)
    lanes = jnp.arange(experts, dtype=I32)[None, None, :]
    one_hot = (routes[:, :, None] == lanes).astype(F32)
    chosen = jnp.sum(one_hot * logits[:, None, :], axis=2)
    gates = jax.nn.softmax(chosen, axis=1)
    rows = routes.shape[0]
    hits = jnp.sum(one_hot, axis=1)
    order = jnp.arange(rows, dtype=I32)
    earlier = (order[None, :] < order[:, None]).astype(BF16)
    before = jnp.dot(earlier, hits.astype(BF16), preferred_element_type=F32)
    rank = jnp.sum(one_hot * before[:, None, :], axis=2).astype(I32)
    return gates, routes * capacity + rank


def forward_kernel(
    steps, outer, tok, rec, slot, gate, gain, summed, offered, inverse, held, square, sliced, row_sem, slice_sem
):
    step = pl.program_id(0)
    part = tok.shape[1]

    def keep(e):
        start = pl.multiple_of(e * part, part)
        return pltpu.make_async_copy(held.at[e], summed.at[:, pl.ds(start, part)], row_sem.at[e])

    def offer(u):
        return pltpu.make_async_copy(sliced, offered.at[pl.ds(u * steps, steps)], slice_sem.at[u])

    rows, slots = tok.shape[0], rec.shape[0]
    ids = iota((rows, slots), 1)
    first = (slot[:, 0:1] == ids).astype(BF16)
    second = (slot[:, 1:2] == ids).astype(BF16)

    @pl.when(step == 0)
    def _():
        square[...] = jnp.zeros_like(square)

    for k in range(part // 256):
        cols = slice(256 * k, 256 * (k + 1))
        block = rec[:, cols]
        x = (
            tok[:, cols].astype(F32)
            + gate[:, 0:1] * jnp.dot(first, block, preferred_element_type=F32)
            + gate[:, 1:2] * jnp.dot(second, block, preferred_element_type=F32)
        )
        held[step, :, cols] = x
        square[...] += fold(x * x)
    keep(step).start()

    @pl.when(step == steps - 1)
    def _():
        mean = jnp.sum(square[...], axis=1, keepdims=True) / (steps * part)
        scale = lax.rsqrt(mean + EPS)
        inverse[...] = scale
        count = rows // SEQ
        for e in range(steps):
            x = held[e] * scale
            x = jnp.sum(x.reshape(count, SEQ, part), axis=1) / SEQ
            sliced[e] = (x * gain[:, part * e : part * (e + 1)]).astype(BF16)
        for u in range(outer):
            offer(u).start()
        for e in range(steps):
            keep(e).wait()
        for u in range(outer):
            offer(u).wait()


def forward(tokens, received, slot, gates, gain, experts, outer):
    rows, width = tokens.shape
    slots = received.shape[0]
    part = width // experts
    whole = lambda shape: pl.BlockSpec(shape, lambda i: (0,) * len(shape))
    return pl.pallas_call(
        functools.partial(forward_kernel, experts, outer),
        grid=(experts,),
        in_specs=[
            pl.BlockSpec((rows, part), lambda i: (0, i)),
            pl.BlockSpec((slots, part), lambda i: (0, i)),
            whole((rows, 2)),
            whole((rows, 2)),
            whole((1, width)),
        ],
        out_specs=[HBM, HBM, whole((rows, 1))],
        out_shape=[
            pltpu.HBM((rows, width), F32),
            pltpu.HBM((outer * experts, rows // SEQ, part), BF16),
            jax.ShapeDtypeStruct((rows, 1), F32),
        ],
        scratch_shapes=[
            pltpu.VMEM((experts, rows, part), F32),
            pltpu.VMEM((rows, 128), F32),
            pltpu.VMEM((experts, rows // SEQ, part), BF16),
            pltpu.SemaphoreType.DMA((experts,)),
            pltpu.SemaphoreType.DMA((outer,)),
        ],
        compiler_params=params(14),
        cost_estimate=cost(4 * rows * slots * width, 10 << 20),
    )(tokens, received, slot, gates, gain)


def pack_kernel(steps, place, x, rec, slot, turned, overlap, *rest):
    *outs, dots, packed, sems = rest
    step = pl.program_id(0)
    rows, part = x.shape

    def leave(e, r):
        start = pl.multiple_of(e * part, part)
        return pltpu.make_async_copy(
            packed.at[e, pl.ds(r * capacity, capacity)], outs[r].at[:, pl.ds(start, part)], sems.at[e, r]
        )

    slots = rec.shape[0]
    capacity = slots // len(outs)
    ids = iota((rows, slots), 1)
    first = (slot[:, 0:1] == ids).astype(BF16)
    second = (slot[:, 1:2] == ids).astype(BF16)
    target = lax.rem(iota((slots, rows), 0) + place[0] * capacity, slots)
    spot = ((turned[0:1, :] == target) | (turned[1:2, :] == target)).astype(BF16)

    @pl.when(step == 0)
    def _():
        dots[...] = jnp.zeros_like(dots)

    for k in range(part // 256):
        cols = slice(256 * k, 256 * (k + 1))
        value = x[:, cols]
        block = rec[:, cols]
        dots[0] += fold(value * jnp.dot(first, block, preferred_element_type=F32))
        dots[1] += fold(value * jnp.dot(second, block, preferred_element_type=F32))
        moved = jnp.dot(spot, value.astype(BF16), preferred_element_type=F32).astype(BF16)
        packed[step, :, cols] = moved
    for r in range(len(outs)):
        leave(step, r).start()

    @pl.when(step == steps - 1)
    def _():
        overlap[...] = jnp.concatenate(
            [jnp.sum(dots[k], axis=1, keepdims=True) for k in range(2)], axis=1
        )
        for e in range(steps):
            for r in range(len(outs)):
                leave(e, r).wait()


def pack(place, summed, received, slot, experts, capacity):
    rows, width = summed.shape
    slots = received.shape[0]
    part = width // experts
    whole = lambda shape: pl.BlockSpec(shape, lambda i: (0,) * len(shape))
    return pl.pallas_call(
        functools.partial(pack_kernel, experts),
        grid=(experts,),
        in_specs=[
            SMEM,
            pl.BlockSpec((rows, part), lambda i: (0, i)),
            pl.BlockSpec((slots, part), lambda i: (0, i)),
            whole((rows, 2)),
            whole((2, rows)),
        ],
        out_specs=[whole((rows, 2))] + [HBM] * experts,
        out_shape=[jax.ShapeDtypeStruct((rows, 2), F32)]
        + [pltpu.HBM((capacity, width), BF16)] * experts,
        scratch_shapes=[
            pltpu.VMEM((2, rows, 128), F32),
            pltpu.VMEM((experts, slots, part), BF16),
            pltpu.SemaphoreType.DMA((experts, experts)),
        ],
        compiler_params=params(12),
        cost_estimate=cost(6 * rows * slots * width, 11 << 20),
    )(place, summed, received, slot, slot.T)


def lanes_of(shape, dim):
    lane = iota(shape, dim)
    kind = lax.rem(lane, ROWS_DEV)
    return lane, kind, kind >= PAIR_DEV


def picker(group, kind, turned=False):
    wide = 2 * group
    shape, pair, row = ((wide, group), 1, 0) if turned else ((group, wide), 0, 1)
    a = iota(shape, pair)
    b = iota(shape, row)
    source = (a // PAIR_DEV) * ROWS_DEV + lax.rem(a, PAIR_DEV) + PAIR_DEV * kind
    return (source == b).astype(BF16)


def scores_kernel(near, far, notes, offered):
    experts, total, columns = offered.shape
    group = experts * PAIR_DEV
    wide = 2 * group
    own = near[pl.ds(pl.multiple_of(lax.axis_index("u") * wide, wide), wide), :]
    queries, records = [
        jnp.dot(picker(group, kind), own, preferred_element_type=F32).astype(BF16) for kind in (0, 1)
    ]
    at_record = lanes_of((group, columns), 1)[2]
    blocks = []
    for side in (near, far):
        every = side[...]
        by_query = lax.dot_general(queries, every, NT, preferred_element_type=F32)
        by_record = lax.dot_general(records, every, NT, preferred_element_type=F32)
        blocks.append(jnp.where(at_record, by_query, by_record))
    blocks.append(notes[...])
    for e in range(experts):
        for k, block in enumerate(blocks):
            offered[e, group * k : group * k + block.shape[0], :] = block


def totals_kernel(scale, devices, gathered, offered, kept):
    place, core = lax.axis_index("u"), lax.axis_index("c")
    experts, total, columns = gathered.shape
    group = experts * PAIR_DEV
    both = gathered[0]
    for e in range(1, experts):
        both = both + gathered[e]
    positive_lane = both[2 * group + 3 : 2 * group + 4, :]
    near, far = both[:group] * scale, both[group : 2 * group] * scale
    kept[0:group] = near
    kept[group : 2 * group] = far

    shape = (group, columns)
    lane, kind, at_record = lanes_of(shape, 1)
    pair = iota(shape, 0)
    within = lax.rem(lane, 2 * group)
    matching = (within // ROWS_DEV == pair // PAIR_DEV) & (kind == lax.rem(pair, PAIR_DEV))
    here = matching & (lane // (2 * group) == place)
    positive = jnp.sum(jnp.where(here, positive_lane, 0.0), axis=1, keepdims=True)

    low = jnp.float32(-jnp.inf)
    near_records = jnp.where(at_record, near, low)
    far_records = jnp.where(at_record, far, low)
    highest = jnp.maximum(
        jnp.max(near_records, axis=1, keepdims=True), jnp.max(far_records, axis=1, keepdims=True)
    )
    weight = jnp.sum(jnp.exp(near_records - highest), axis=1, keepdims=True) + jnp.sum(
        jnp.exp(far_records - highest), axis=1, keepdims=True
    )
    log_total = highest + jnp.log(weight)
    chosen = jnp.zeros((group, 1), F32)
    for side, where in ((near, core), (far, 1 - core)):
        name = column_names(lane, kind, group, where)
        hit = at_record & (name.astype(F32) == positive)
        chosen = chosen + jnp.sum(jnp.where(hit, side, 0.0), axis=1, keepdims=True)
    kept[2 * group : 3 * group, :128] = jnp.broadcast_to(log_total, (group, 128))
    kept[2 * group : 3 * group, 128:256] = jnp.broadcast_to(positive, (group, 128))
    row_loss = log_total - chosen

    total_lane = jnp.sum(jnp.where(here, log_total, 0.0), axis=0, keepdims=True)
    loss_lane = jnp.sum(jnp.where(here, row_loss, 0.0), axis=0, keepdims=True)
    own_lane = jnp.where(lane[0:1] // (2 * group) == place, positive_lane, 0.0)
    pieces = [x[:, 128 * k : 128 * (k + 1)] for x in (total_lane, own_lane) for k in range(columns // 128)]
    loss_pieces = [
        pltpu.roll(loss_lane, PAIR_DEV, 1)[:, 128 * k : 128 * (k + 1)] for k in range(columns // 128)
    ]
    pieces = [a + b for a, b in zip(pieces, loss_pieces)] + pieces[columns // 128 :]
    message = jnp.concatenate(pieces, axis=0)
    for d in range(devices):
        offered[d] = message


def column_names(lane, kind, group, core):
    wide = 2 * group
    block = (lane // wide) * CORES + core
    return block * group + (lax.rem(lane, wide) // ROWS_DEV) * PAIR_DEV + lax.rem(kind, PAIR_DEV)


def gradient_kernel(scale, factor, heard, kept, near, far, offered, loss):
    place, core = lax.axis_index("u"), lax.axis_index("c")
    experts, wide, columns = offered.shape
    group = wide // 2
    outer_size = heard.shape[0] // CORES
    pieces = columns // 128
    shape = (group, columns)
    lane, kind, at_record = lanes_of(shape, 1)
    pair = iota(shape, 0)
    own_name = (place * CORES + core) * group + iota((group, 1), 0)
    own_total = kept[2 * group : 3 * group, 0:1]
    own_positive = kept[2 * group : 3 * group, 128:129]
    result = jnp.zeros((wide, columns), F32)
    losses = jnp.zeros((1, columns), F32)
    for k, (side, where) in enumerate(((near, core), (far, 1 - core))):
        told = heard[where]
        for u in range(1, outer_size):
            told = told + heard[u * CORES + where]
        total = jnp.concatenate([told[i : i + 1] for i in range(pieces)], axis=1)
        positive = jnp.concatenate([told[pieces + i : pieces + i + 1] for i in range(pieces)], axis=1)
        losses = losses + jnp.where(at_record[0:1], total, 0.0)
        value = kept[group * k : group * (k + 1), :]
        name = column_names(lane, kind, group, where).astype(F32)
        hit = jnp.where(name == own_positive, 1.0, 0.0)
        by_query = (jnp.exp(value - own_total) - hit) * factor[0]
        by_query = jnp.where(at_record, by_query, 0.0).astype(BF16)
        hit = jnp.where(positive == own_name.astype(F32), 1.0, 0.0)
        by_record = (jnp.exp(jnp.where(at_record, 0.0, value - total)) - hit) * factor[0]
        by_record = jnp.where(at_record, 0.0, by_record).astype(BF16)
        rows = jnp.dot(picker(group, 0, True), by_query, preferred_element_type=F32) + jnp.dot(
            picker(group, 1, True), by_record, preferred_element_type=F32
        )
        result = result + jnp.dot(rows.astype(BF16), side[...], preferred_element_type=F32)
    result = result * scale
    for e in range(experts):
        offered[e] = result
    loss[...] = jnp.sum(losses, axis=1, keepdims=True)


def rows_of(grads, e, index):
    tile = grads[e, pl.ds(pl.multiple_of((index // 2) * 8, 8), 8), :]
    return jnp.where(lax.rem(index, 2) == 0, tile[:ROWS_DEV], tile[ROWS_DEV:])


def split_bf16(x):
    high = x.astype(BF16)
    rest = x - high.astype(F32)
    mid = rest.astype(BF16)
    low = (rest - mid.astype(F32)).astype(BF16)
    return high, mid, low


def router_kernel(grads, gain, summed, rec, tok, slot, routes, gate, inverse, overlap, part_out, shrink_out, choice_out, weighted_out):
    experts, _, part = grads.shape
    rows = summed.shape[0]
    slots = rec.shape[0]
    count = rows // SEQ
    acc = [jnp.zeros((SEQ, 128), F32) for _ in range(count)]
    on_slots = jnp.zeros((16, slots), F32)
    for e in range(experts):
        cols = slice(part * e, part * (e + 1))
        w = rows_of(grads, e, lax.axis_index("expert")) * (gain[:, cols] / SEQ)
        weighted_out[:, cols] = w
        lhs = jnp.concatenate(list(split_bf16(w)) + [jnp.zeros((count, part), BF16)], axis=0)
        on_slots = on_slots + lax.dot_general(lhs, rec[:, cols], NT, preferred_element_type=F32)
        for q in range(count):
            acc[q] = acc[q] + fold(summed[SEQ * q : SEQ * (q + 1), cols] * w[q : q + 1, :])
    on_slots = on_slots[0:count] + on_slots[count : 2 * count] + on_slots[2 * count : 3 * count]
    ids = iota((SEQ, slots), 1)
    lanes = iota((SEQ, 128), 1)
    choices = []
    for q in range(count):
        at = slice(SEQ * q, SEQ * (q + 1))
        inv = inverse[at]
        shrink = inv * inv * inv * (jnp.sum(acc[q], axis=1, keepdims=True) / (experts * part))
        shrink_out[at] = shrink
        row = on_slots[q : q + 1, :]
        grad_gate = []
        for k in range(2):
            along = jnp.sum(jnp.where(slot[at, k : k + 1] == ids, row, 0.0), axis=1, keepdims=True)
            grad_gate.append(inv * along - shrink * overlap[at, k : k + 1])
        gates = [gate[at, k : k + 1] for k in range(2)]
        mean = gates[0] * grad_gate[0] + gates[1] * grad_gate[1]
        choice = jnp.zeros((SEQ, 128), F32)
        for k in range(2):
            chosen = gates[k] * (grad_gate[k] - mean)
            choice = choice + jnp.where(routes[at, k : k + 1] == lanes, chosen, 0.0)
        choices.append(choice)
    choice = jnp.concatenate(choices, axis=0)
    choice_out[...] = choice.astype(BF16)
    lhs = jnp.transpose(choice)[:experts].astype(BF16)
    for k in range(experts):
        cols = slice(part * k, part * (k + 1))
        part_out[:, cols] = jnp.dot(lhs, tok[:, cols], preferred_element_type=F32)


def token_kernel(summed, weighted, inverse, shrink, choice, router, out):
    rows = summed.shape[0]
    through = jnp.dot(choice[...], router[...], preferred_element_type=F32)
    for q in range(rows // SEQ):
        at = slice(SEQ * q, SEQ * (q + 1))
        x = inverse[at] * weighted[q : q + 1, :] - shrink[at] * summed[at]
        out[at] = (x + through[SEQ * q : SEQ * (q + 1)]).astype(BF16)


def token_rows(summed, weighted, inverse, shrink, choice, router, parts):
    rows, width = summed.shape
    part = width // parts
    whole = lambda shape: pl.BlockSpec(shape, lambda i: (0, 0))
    split = lambda count: pl.BlockSpec((count, part), lambda i: (0, i))
    return pl.pallas_call(
        token_kernel,
        grid=(parts,),
        in_specs=[split(rows), split(weighted.shape[0]), whole((rows, 1)), whole((rows, 1)), whole((rows, 128)), split(128)],
        out_specs=split(rows),
        out_shape=jax.ShapeDtypeStruct((rows, width), BF16),
        compiler_params=params(10),
        cost_estimate=cost(2 * rows * 128 * width, 5 << 20),
    )(summed, weighted, inverse, shrink, choice, router)


def expert_kernel(place, grads, gain, notes, *rest):
    experts = len(rest) - 1
    backs, out = rest[:experts], rest[experts]
    _, _, part = grads.shape
    step = pl.program_id(0)
    source = lax.rem(place[0] + experts - step, experts)
    gate, inv, seq = notes[0, :, 0:1], notes[0, :, 1:2], notes[0, :, 2:3]
    capacity = gate.shape[0]
    for r in range(experts):

        @pl.when(step == r)
        def _():
            back = backs[r]
            acc = jnp.zeros((capacity, 128), F32)
            rows = []
            for e in range(experts):
                cols = slice(part * e, part * (e + 1))
                w = rows_of(grads, e, source) * (gain[:, cols] / SEQ)
                x = jnp.broadcast_to(w[0:1], (capacity, part))
                for s in range(1, ROWS_DEV):
                    x = jnp.where(seq == s, w[s : s + 1], x)
                rows.append(w)
                acc = acc + fold(x * back[:, cols].astype(F32))
            shrink = inv * inv * inv * (jnp.sum(acc, axis=1, keepdims=True) / (experts * part))
            for e in range(experts):
                cols = slice(part * e, part * (e + 1))
                w = rows[e]
                x = jnp.broadcast_to(w[0:1], (capacity, part))
                for s in range(1, ROWS_DEV):
                    x = jnp.where(seq == s, w[s : s + 1], x)
                x = gate * (inv * x - shrink * back[:, cols].astype(F32))
                out[0, :, cols] = x.astype(BF16)


def expert_rows(place, grads, gain, notes, backs):
    experts, capacity = notes.shape[:2]
    width = gain.shape[1]
    whole = lambda shape: pl.BlockSpec(shape, lambda i, p: (0,) * len(shape))
    source = lambda i, p: (lax.rem(p[0] + experts - i, experts), 0, 0)
    return pl.pallas_call(
        expert_kernel,
        grid_spec=pltpu.PrefetchScalarGridSpec(
            num_scalar_prefetch=1,
            grid=(experts,),
            in_specs=[
                whole(grads.shape),
                whole((1, width)),
                pl.BlockSpec((1, capacity, notes.shape[2]), source),
            ]
            + [whole((capacity, width))] * experts,
            out_specs=pl.BlockSpec((1, capacity, width), source),
        ),
        out_shape=jax.ShapeDtypeStruct((experts, capacity, width), BF16),
        compiler_params=params(24),
        cost_estimate=cost(12 * experts * capacity * width, 9 << 20),
    )(place, grads, gain, notes, *backs)


def shards(tokens, routes, positives, expert_out, router, norm_gain, loss_scale):
    experts, capacity, width = expert_out.shape[2:]
    rows = tokens.shape[0]
    slots = experts * capacity
    outer = lax.axis_size("u")
    mine = lax.axis_index("expert").astype(I32)
    mine_at = mine[None]
    wide = outer * experts
    part = width // experts
    group = PAIR_DEV * experts
    pairs = group * outer * CORES
    scale = 4.0 / math.sqrt(width)
    gain = norm_gain[None, :]
    columns = outer * experts * ROWS_DEV

    received = exchange(expert_out.reshape(experts, capacity, width), "expert").reshape(slots, width)
    gates, slot = routing(tokens, routes, router, experts, capacity)
    lane = jnp.arange(columns, dtype=I32)
    spread_positive = jnp.where(
        (lane % (2 * group)) // ROWS_DEV == mine,
        jnp.where(lane % ROWS_DEV == 0, positives[0], positives[1]) * (lane % ROWS_DEV < PAIR_DEV),
        0,
    ).astype(F32)

    summed, offered, inverse = forward(tokens, received, slot, gates, gain, experts, outer)
    near = exchange(offered, ("u", "expert"))
    overlap, *outgoing = pack(mine_at, summed, received, slot, experts, capacity)
    backs = [outgoing[0]] + [
        lax.ppermute(outgoing[r], "expert", [(i, (i + r) % experts) for i in range(experts)])
        for r in range(1, experts)
    ]
    slot_ids = jnp.arange(slots, dtype=I32)[None, :]
    picks = [slot[:, k : k + 1] == slot_ids for k in range(2)]
    gate_slot = jnp.sum(
        jnp.where(picks[0], gates[:, 0:1], 0.0) + jnp.where(picks[1], gates[:, 1:2], 0.0), axis=0
    )
    taken = picks[0] | picks[1]
    inverse_slot = jnp.sum(jnp.where(taken, inverse, 0.0), axis=0)
    sequence = (jnp.arange(rows, dtype=I32) // SEQ).astype(F32)
    sequence_slot = jnp.sum(jnp.where(taken, sequence[:, None], 0.0), axis=0)
    notes = jnp.stack([gate_slot, inverse_slot, sequence_slot, spread_positive])
    notes = jnp.pad(notes, ((0, 4), (0, 0)))

    near, overlap = lax.optimization_barrier((near, overlap))
    far = swap_core(near)
    near, far = near.reshape(columns, part), far.reshape(columns, part)
    offered = pl.pallas_call(
        scores_kernel,
        in_specs=[VMEM] * 3,
        out_specs=VMEM,
        out_shape=jax.ShapeDtypeStruct((experts, 2 * group + 8, columns), F32),
        compiler_params=params(2),
    )(near, far, notes)
    gathered = exchange(offered, "expert")
    gathered, *backs[1:4] = lax.optimization_barrier((gathered, *backs[1:4]))
    offered, kept = pl.pallas_call(
        functools.partial(totals_kernel, scale, outer * CORES),
        in_specs=[VMEM],
        out_specs=[VMEM] * 2,
        out_shape=[
            jax.ShapeDtypeStruct((outer * CORES, 8, 128), F32),
            jax.ShapeDtypeStruct((3 * group, columns), F32),
        ],
        compiler_params=params(2),
    )(gathered)
    heard = exchange(offered, ("u", "c"))
    heard, *backs[4:6] = lax.optimization_barrier((heard, *backs[4:6]))
    offered, loss = pl.pallas_call(
        functools.partial(gradient_kernel, scale),
        in_specs=[SMEM] + [VMEM] * 4,
        out_specs=[VMEM, VMEM],
        out_shape=[
            jax.ShapeDtypeStruct((experts, 2 * group, part), F32),
            jax.ShapeDtypeStruct((1, 1), F32),
        ],
        compiler_params=params(2),
    )((loss_scale / pairs)[None], heard, kept, near, far)
    grads = exchange(offered, "expert")
    grads, *backs[6:8] = lax.optimization_barrier((grads, *backs[6:8]))

    router_part, shrink, choice, weighted = pl.pallas_call(
        router_kernel,
        in_specs=[VMEM] * 10,
        out_specs=[VMEM] * 4,
        out_shape=[
            jax.ShapeDtypeStruct((experts, width), F32),
            jax.ShapeDtypeStruct((rows, 1), F32),
            jax.ShapeDtypeStruct((rows, 128), BF16),
            jax.ShapeDtypeStruct((rows // SEQ, width), F32),
        ],
        compiler_params=params(6),
    )(grads, gain, summed, received, tokens, slot, routes, gates, inverse, overlap)
    router_part = router_part + swap_core(router_part)
    router_part = exchange(router_part.reshape(wide, 1, -1), ("u", "expert"))
    router_sum = jnp.sum(router_part, axis=0)
    router_all = exchange(jnp.broadcast_to(router_sum[None], (wide,) + router_sum.shape), ("u", "expert"))
    router_grad = router_all.reshape(experts, width).T

    turned = jnp.pad(router.T, ((0, 128 - experts), (0, 0)))
    token_grad = token_rows(summed, weighted, inverse, shrink, choice, turned, experts)
    held = lax.dynamic_slice_in_dim(gathered[:, 2 * group : 2 * group + 3], mine * capacity, capacity, axis=2)
    held = jnp.pad(jnp.transpose(held, (0, 2, 1)), ((0, 0), (0, 0), (0, 5)))
    expert_grad = expert_rows(mine_at, grads, gain, held, backs)
    return token_grad, expert_grad.reshape(1, 1, experts, capacity, width), router_grad, loss[0, 0] / pairs


def solution(mesh):
    outer = mesh.shape["dp"] // CORES
    fine = Mesh(mesh.devices.reshape(outer, CORES, mesh.shape["expert"]), ("u", "c", "expert"))
    everywhere = ("u", "c", "expert")
    return jax.shard_map(
        shards,
        mesh=fine,
        in_specs=(
            P(everywhere, None),
            P(everywhere, None),
            P(everywhere),
            P(("u", "c"), "expert", None, None, None),
            P(),
            P(),
            P(),
        ),
        out_specs=(P(everywhere, None), P(("u", "c"), "expert", None, None, None), P(), P()),
        check_vma=False,
    )
```

```python
import functools
import math

import jax
import jax.numpy as jnp
from jax import lax
from jax.experimental import pallas as pl
from jax.experimental.pallas import tpu as pltpu
from jax.sharding import Mesh, PartitionSpec as P

PAIR_DEV = 2
SEQ = 48
EPS = 1e-05
CORES = 2
ROWS_DEV = 2 * PAIR_DEV
F32 = jnp.float32
BF16 = jnp.bfloat16
I32 = jnp.int32
VMEM = pl.BlockSpec(memory_space=pltpu.VMEM)
SMEM = pl.BlockSpec(memory_space=pltpu.SMEM)
HBM = pl.BlockSpec(memory_space=pltpu.HBM)
NT = (((1,), (1,)), ((), ()))
TURNS = ((4, 1, 7), (3, 5), (2, 6))


def iota(shape, dim):
    return lax.broadcasted_iota(I32, shape, dim)


def params(mib):
    return pltpu.CompilerParams(vmem_limit_bytes=mib << 20)


def cost(flops, moved):
    return pl.CostEstimate(flops=flops, bytes_accessed=moved, transcendentals=0)


def fold(x):
    total = x[:, :128]
    for k in range(1, x.shape[1] // 128):
        total = total + x[:, 128 * k : 128 * (k + 1)]
    return total


def in_hbm(*arrays):
    return [pltpu.with_memory_space_constraint(x, pltpu.HBM) for x in arrays]


def copy_all(copies):
    for copy in copies:
        copy.start()
    for copy in copies:
        copy.wait()


def to_each(source, target, sems):
    copy_all([pltpu.make_async_copy(source, target.at[i], sems.at[i]) for i in range(target.shape[0])])


def swap_core(x):
    return lax.ppermute(x, "c", [(0, 1), (1, 0)])


def exchange(x, axes):
    return lax.all_to_all(x, axes, split_axis=0, concat_axis=0, tiled=True)


def routing(tokens, routes, router, experts, capacity):
    logits = jnp.dot(tokens, router, preferred_element_type=F32)
    lanes = jnp.arange(experts, dtype=I32)[None, None, :]
    one_hot = (routes[:, :, None] == lanes).astype(F32)
    chosen = jnp.sum(one_hot * logits[:, None, :], axis=2)
    gates = jax.nn.softmax(chosen, axis=1)
    rows = routes.shape[0]
    hits = jnp.sum(one_hot, axis=1)
    order = jnp.arange(rows, dtype=I32)
    earlier = (order[None, :] < order[:, None]).astype(BF16)
    before = jnp.dot(earlier, hits.astype(BF16), preferred_element_type=F32)
    rank = jnp.sum(one_hot * before[:, None, :], axis=2).astype(I32)
    return gates, routes * capacity + rank


def forward_kernel(
    steps, outer, tok, rec, slot, gate, gain, summed, offered, inverse, held, square, sliced, row_sem, slice_sem
):
    step = pl.program_id(0)
    part = tok.shape[1]

    def keep(e):
        start = pl.multiple_of(e * part, part)
        return pltpu.make_async_copy(held.at[e], summed.at[:, pl.ds(start, part)], row_sem.at[e])

    def offer(u):
        return pltpu.make_async_copy(sliced, offered.at[pl.ds(u * steps, steps)], slice_sem.at[u])

    rows, slots = tok.shape[0], rec.shape[0]
    ids = iota((rows, slots), 1)
    first = (slot[:, 0:1] == ids).astype(BF16)
    second = (slot[:, 1:2] == ids).astype(BF16)

    @pl.when(step == 0)
    def _():
        square[...] = jnp.zeros_like(square)

    for k in range(part // 256):
        cols = slice(256 * k, 256 * (k + 1))
        block = rec[:, cols]
        x = (
            tok[:, cols].astype(F32)
            + gate[:, 0:1] * jnp.dot(first, block, preferred_element_type=F32)
            + gate[:, 1:2] * jnp.dot(second, block, preferred_element_type=F32)
        )
        held[step, :, cols] = x
        square[...] += fold(x * x)
    keep(step).start()

    @pl.when(step == steps - 1)
    def _():
        mean = jnp.sum(square[...], axis=1, keepdims=True) / (steps * part)
        scale = lax.rsqrt(mean + EPS)
        inverse[...] = scale
        count = rows // SEQ
        for e in range(steps):
            x = held[e] * scale
            x = jnp.sum(x.reshape(count, SEQ, part), axis=1) / SEQ
            sliced[e] = (x * gain[:, part * e : part * (e + 1)]).astype(BF16)
        for u in range(outer):
            offer(u).start()
        for e in range(steps):
            keep(e).wait()
        for u in range(outer):
            offer(u).wait()


def forward(tokens, received, slot, gates, gain, experts, outer):
    rows, width = tokens.shape
    slots = received.shape[0]
    part = width // experts
    whole = lambda shape: pl.BlockSpec(shape, lambda i: (0,) * len(shape))
    return pl.pallas_call(
        functools.partial(forward_kernel, experts, outer),
        grid=(experts,),
        in_specs=[
            pl.BlockSpec((rows, part), lambda i: (0, i)),
            pl.BlockSpec((slots, part), lambda i: (0, i)),
            whole((rows, 2)),
            whole((rows, 2)),
            whole((1, width)),
        ],
        out_specs=[HBM, HBM, whole((rows, 1))],
        out_shape=[
            pltpu.HBM((rows, width), F32),
            pltpu.HBM((outer * experts, rows // SEQ, part), BF16),
            jax.ShapeDtypeStruct((rows, 1), F32),
        ],
        scratch_shapes=[
            pltpu.VMEM((experts, rows, part), F32),
            pltpu.VMEM((rows, 128), F32),
            pltpu.VMEM((experts, rows // SEQ, part), BF16),
            pltpu.SemaphoreType.DMA((experts,)),
            pltpu.SemaphoreType.DMA((outer,)),
        ],
        compiler_params=params(14),
        cost_estimate=cost(4 * rows * slots * width, 10 << 20),
    )(tokens, received, slot, gates, gain)


def pack_kernel(steps, place, x, rec, slot, turned, facts, overlap, *rest):
    *outs, dots, packed, sems = rest
    step = pl.program_id(0)
    rows, part = x.shape

    def leave(e, r):
        start = pl.multiple_of(e * part, part)
        return pltpu.make_async_copy(
            packed.at[e, pl.ds(r * capacity, capacity)], outs[r].at[:, pl.ds(start, part)], sems.at[e, r]
        )

    slots = rec.shape[0]
    capacity = slots // len(outs)
    ids = iota((rows, slots), 1)
    first = (slot[:, 0:1] == ids).astype(BF16)
    second = (slot[:, 1:2] == ids).astype(BF16)
    target = lax.rem(iota((slots, rows), 0) + place[0] * capacity, slots)
    spot = ((turned[0:1, :] == target) | (turned[1:2, :] == target)).astype(BF16)

    @pl.when(step == 0)
    def _():
        dots[...] = jnp.zeros_like(dots)

    for k in range(part // 256):
        cols = slice(256 * k, 256 * (k + 1))
        value = x[:, cols]
        block = rec[:, cols]
        dots[0] += fold(value * jnp.dot(first, block, preferred_element_type=F32))
        dots[1] += fold(value * jnp.dot(second, block, preferred_element_type=F32))
        moved = jnp.dot(spot, value.astype(BF16), preferred_element_type=F32).astype(BF16)
        packed[step, :, cols] = moved
    for r in range(len(outs)):
        leave(step, r).start()

    @pl.when(step == steps - 1)
    def _():
        lane = iota((rows, 128), 1)
        known = facts[...]
        for k in range(2):
            known = jnp.where(lane == k, jnp.sum(dots[k], axis=1, keepdims=True), known)
        overlap[...] = known
        for e in range(steps):
            for r in range(len(outs)):
                leave(e, r).wait()


def pack(place, summed, received, slot, facts, experts, capacity):
    rows, width = summed.shape
    slots = received.shape[0]
    part = width // experts
    whole = lambda shape: pl.BlockSpec(shape, lambda i: (0,) * len(shape))
    return pl.pallas_call(
        functools.partial(pack_kernel, experts),
        grid=(experts,),
        in_specs=[
            SMEM,
            pl.BlockSpec((rows, part), lambda i: (0, i)),
            pl.BlockSpec((slots, part), lambda i: (0, i)),
            whole((rows, 2)),
            whole((2, rows)),
            whole((rows, 128)),
        ],
        out_specs=[whole((rows, 128))] + [HBM] * experts,
        out_shape=[jax.ShapeDtypeStruct((rows, 128), F32)]
        + [pltpu.HBM((capacity, width), BF16)] * experts,
        scratch_shapes=[
            pltpu.VMEM((2, rows, 128), F32),
            pltpu.VMEM((experts, slots, part), BF16),
            pltpu.SemaphoreType.DMA((experts, experts)),
        ],
        compiler_params=params(12),
        cost_estimate=cost(6 * rows * slots * width, 11 << 20),
    )(place, *in_hbm(summed, received), slot, slot.T, facts)


def lanes_of(shape, dim):
    lane = iota(shape, dim)
    kind = lax.rem(lane, ROWS_DEV)
    return lane, kind, kind >= PAIR_DEV


def picker(group, kind, turned=False):
    wide = 2 * group
    shape, pair, row = ((wide, group), 1, 0) if turned else ((group, wide), 0, 1)
    a = iota(shape, pair)
    b = iota(shape, row)
    source = (a // PAIR_DEV) * ROWS_DEV + lax.rem(a, PAIR_DEV) + PAIR_DEV * kind
    return (source == b).astype(BF16)


def scores_kernel(near, far, notes, offered, whole, sems):
    experts, total, columns = offered.shape
    group = experts * PAIR_DEV
    wide = 2 * group
    own = near[pl.ds(pl.multiple_of(lax.axis_index("u") * wide, wide), wide), :]
    queries, records = [
        jnp.dot(picker(group, kind), own, preferred_element_type=F32).astype(BF16) for kind in (0, 1)
    ]
    at_record = lanes_of((group, columns), 1)[2]
    for k, side in enumerate((near, far)):
        every = side[...]
        by_query = lax.dot_general(queries, every, NT, preferred_element_type=F32)
        by_record = lax.dot_general(records, every, NT, preferred_element_type=F32)
        whole[group * k : group * (k + 1)] = jnp.where(at_record, by_query, by_record)
    whole[2 * group :] = notes[...]
    to_each(whole, offered, sems)


def totals_kernel(scale, gathered, offered, kept_out, kept, spread, kept_sem, sem):
    place, core = lax.axis_index("u"), lax.axis_index("c")
    experts, total, columns = gathered.shape
    group = experts * PAIR_DEV
    both = gathered[0]
    for e in range(1, experts):
        both = both + gathered[e]
    positive_lane = both[2 * group + 3 : 2 * group + 4, :]
    near, far = both[:group] * scale, both[group : 2 * group] * scale
    kept[0:group] = near
    kept[group : 2 * group] = far

    shape = (group, columns)
    lane, kind, at_record = lanes_of(shape, 1)
    pair = iota(shape, 0)
    within = lax.rem(lane, 2 * group)
    matching = (within // ROWS_DEV == pair // PAIR_DEV) & (kind == lax.rem(pair, PAIR_DEV))
    here = matching & (lane // (2 * group) == place)
    positive = jnp.sum(jnp.where(here, positive_lane, 0.0), axis=1, keepdims=True)

    low = jnp.float32(-jnp.inf)
    near_records = jnp.where(at_record, near, low)
    far_records = jnp.where(at_record, far, low)
    highest = jnp.maximum(
        jnp.max(near_records, axis=1, keepdims=True), jnp.max(far_records, axis=1, keepdims=True)
    )
    weight = jnp.sum(jnp.exp(near_records - highest), axis=1, keepdims=True) + jnp.sum(
        jnp.exp(far_records - highest), axis=1, keepdims=True
    )
    log_total = highest + jnp.log(weight)
    chosen = jnp.zeros((group, 1), F32)
    for side, where in ((near, core), (far, 1 - core)):
        name = column_names(lane, kind, group, where)
        hit = at_record & (name.astype(F32) == positive)
        chosen = chosen + jnp.sum(jnp.where(hit, side, 0.0), axis=1, keepdims=True)
    kept[2 * group : 3 * group, :128] = jnp.broadcast_to(log_total, (group, 128))
    kept[2 * group : 3 * group, 128:256] = jnp.broadcast_to(positive, (group, 128))
    saved = pltpu.make_async_copy(kept, kept_out, kept_sem)
    saved.start()
    row_loss = log_total - chosen

    total_lane = jnp.sum(jnp.where(here, log_total, 0.0), axis=0, keepdims=True)
    loss_lane = jnp.sum(jnp.where(here, row_loss, 0.0), axis=0, keepdims=True)
    own_lane = jnp.where(lane[0:1] // (2 * group) == place, positive_lane, 0.0)
    pieces = [x[:, 128 * k : 128 * (k + 1)] for x in (total_lane, own_lane) for k in range(columns // 128)]
    loss_pieces = [
        pltpu.roll(loss_lane, PAIR_DEV, 1)[:, 128 * k : 128 * (k + 1)] for k in range(columns // 128)
    ]
    pieces = [a + b for a, b in zip(pieces, loss_pieces)] + pieces[columns // 128 :]
    message = jnp.concatenate(pieces, axis=0)
    for d in range(spread.shape[0]):
        spread[d] = message
    copy_all([pltpu.make_async_copy(spread, offered, sem)])
    saved.wait()


def column_names(lane, kind, group, core):
    wide = 2 * group
    block = (lane // wide) * CORES + core
    return block * group + (lax.rem(lane, wide) // ROWS_DEV) * PAIR_DEV + lax.rem(kind, PAIR_DEV)


def gradient_kernel(scale, factor, heard, kept, near, far, offered, loss, whole, sems):
    place, core = lax.axis_index("u"), lax.axis_index("c")
    experts, wide, columns = offered.shape
    group = wide // 2
    outer_size = heard.shape[0] // CORES
    pieces = columns // 128
    shape = (group, columns)
    lane, kind, at_record = lanes_of(shape, 1)
    pair = iota(shape, 0)
    own_name = (place * CORES + core) * group + iota((group, 1), 0)
    own_total = kept[2 * group : 3 * group, 0:1]
    own_positive = kept[2 * group : 3 * group, 128:129]
    result = jnp.zeros((wide, columns), F32)
    losses = jnp.zeros((1, columns), F32)
    for k, (side, where) in enumerate(((near, core), (far, 1 - core))):
        told = heard[where]
        for u in range(1, outer_size):
            told = told + heard[u * CORES + where]
        total = jnp.concatenate([told[i : i + 1] for i in range(pieces)], axis=1)
        positive = jnp.concatenate([told[pieces + i : pieces + i + 1] for i in range(pieces)], axis=1)
        losses = losses + jnp.where(at_record[0:1], total, 0.0)
        value = kept[group * k : group * (k + 1), :]
        name = column_names(lane, kind, group, where).astype(F32)
        hit = jnp.where(name == own_positive, 1.0, 0.0)
        by_query = (jnp.exp(value - own_total) - hit) * factor[0]
        by_query = jnp.where(at_record, by_query, 0.0).astype(BF16)
        hit = jnp.where(positive == own_name.astype(F32), 1.0, 0.0)
        by_record = (jnp.exp(jnp.where(at_record, 0.0, value - total)) - hit) * factor[0]
        by_record = jnp.where(at_record, 0.0, by_record).astype(BF16)
        rows = jnp.dot(picker(group, 0, True), by_query, preferred_element_type=F32) + jnp.dot(
            picker(group, 1, True), by_record, preferred_element_type=F32
        )
        result = result + jnp.dot(rows.astype(BF16), side[...], preferred_element_type=F32)
    whole[...] = result * scale
    to_each(whole, offered, sems)
    loss[...] = jnp.sum(losses, axis=1, keepdims=True)


def rows_of(grads, e, index):
    tile = grads[e, pl.ds(pl.multiple_of((index // 2) * 8, 8), 8), :]
    return jnp.where(lax.rem(index, 2) == 0, tile[:ROWS_DEV], tile[ROWS_DEV:])


def split_bf16(x):
    high = x.astype(BF16)
    rest = x - high.astype(F32)
    mid = rest.astype(BF16)
    low = (rest - mid.astype(F32)).astype(BF16)
    return high, mid, low


def router_kernel(
    grads, gain, summed_in, rec_in, tok_in, facts_in, part_out, state_out, weighted_out,
    summed, rec, tok, facts, state, weighted, sems, facts_sem, out_sems
):
    experts, _, part = grads.shape
    rows = summed.shape[1]
    slots = rec.shape[1]
    count = rows // SEQ

    def load(e):
        cols = pl.ds(e * part, part)
        pairs = ((summed_in, summed), (rec_in, rec), (tok_in, tok))
        return [
            pltpu.make_async_copy(a.at[:, cols], b.at[e], sems.at[k, e]) for k, (a, b) in enumerate(pairs)
        ]

    known = pltpu.make_async_copy(facts_in, facts, facts_sem)
    loads = [load(e) for e in range(experts)]
    for k in (1, 0):
        for e in range(experts):
            loads[e][k].start()
    known.start()
    for e in range(experts):
        loads[e][2].start()

    w = []
    for e in range(experts):
        cols = slice(part * e, part * (e + 1))
        w.append(rows_of(grads, e, lax.axis_index("expert")) * (gain[:, cols] / SEQ))
        weighted[:, cols] = w[e]
    on_slots = jnp.zeros((16, slots), F32)
    for e in range(experts):
        lhs = jnp.concatenate(list(split_bf16(w[e])) + [jnp.zeros((count, part), BF16)], axis=0)
        loads[e][1].wait()
        on_slots = on_slots + lax.dot_general(lhs, rec[e], NT, preferred_element_type=F32)
    acc = [jnp.zeros((SEQ, 128), F32) for _ in range(count)]
    for e in range(experts):
        loads[e][0].wait()
        for q in range(count):
            acc[q] = acc[q] + fold(summed[e, SEQ * q : SEQ * (q + 1), :] * w[e][q : q + 1, :])
    known.wait()
    on_slots = on_slots[0:count] + on_slots[count : 2 * count] + on_slots[2 * count : 3 * count]
    ids = iota((SEQ, slots), 1)
    lanes = iota((SEQ, 128), 1)
    choices = []
    for q in range(count):
        at = slice(SEQ * q, SEQ * (q + 1))
        fact = facts[at, :]
        inv = fact[:, 2:3]
        shrink = inv * inv * inv * (jnp.sum(acc[q], axis=1, keepdims=True) / (experts * part))
        row = on_slots[q : q + 1, :]
        grad_gate = []
        for k in range(2):
            spot = fact[:, 5 + k : 6 + k].astype(I32)
            along = jnp.sum(jnp.where(spot == ids, row, 0.0), axis=1, keepdims=True)
            grad_gate.append(inv * along - shrink * fact[:, k : k + 1])
        gates = [fact[:, 3 + k : 4 + k] for k in range(2)]
        mean = gates[0] * grad_gate[0] + gates[1] * grad_gate[1]
        choice = jnp.zeros((SEQ, 128), F32)
        for k in range(2):
            chosen = gates[k] * (grad_gate[k] - mean)
            route = fact[:, 7 + k : 8 + k].astype(I32)
            choice = choice + jnp.where(route == lanes, chosen, 0.0)
        choices.append(choice)
        choice = jnp.where(lanes == experts, inv, choice)
        state[at] = jnp.where(lanes == experts + 1, shrink, choice)
    saved = [
        pltpu.make_async_copy(state, state_out, out_sems.at[0]),
        pltpu.make_async_copy(weighted, weighted_out, out_sems.at[1]),
    ]
    for copy in saved:
        copy.start()
    lhs = jnp.transpose(jnp.concatenate(choices, axis=0))[:experts].astype(BF16)
    tiles = part // 128
    for e in range(experts):
        loads[e][2].wait()
        block = jnp.dot(lhs, tok[e], preferred_element_type=F32)
        for k in range(tiles):
            at = experts * (tiles * e + k)
            part_out[at : at + experts, :] = block[:, 128 * k : 128 * (k + 1)]
    for copy in saved:
        copy.wait()


def token_kernel(experts, summed, weighted, state, router, out):
    rows = summed.shape[0]
    known = state[...]
    choice = jnp.where(iota(known.shape, 1) < experts, known, 0.0).astype(BF16)
    through = jnp.dot(choice, router[...], preferred_element_type=F32)
    for q in range(rows // SEQ):
        at = slice(SEQ * q, SEQ * (q + 1))
        inverse, shrink = known[at, experts : experts + 1], known[at, experts + 1 : experts + 2]
        x = inverse * weighted[q : q + 1, :] - shrink * summed[at]
        out[at] = (x + through[SEQ * q : SEQ * (q + 1)]).astype(BF16)


def token_rows(summed, weighted, state, router, experts):
    rows, width = summed.shape
    part = width // experts
    split = lambda count: pl.BlockSpec((count, part), lambda i: (0, i))
    return pl.pallas_call(
        functools.partial(token_kernel, experts),
        grid=(experts,),
        in_specs=[
            split(rows),
            split(weighted.shape[0]),
            pl.BlockSpec((rows, 128), lambda i: (0, 0)),
            split(128),
        ],
        out_specs=split(rows),
        out_shape=jax.ShapeDtypeStruct((rows, width), BF16),
        compiler_params=params(10),
        cost_estimate=cost(2 * rows * 128 * width, 5 << 20),
    )(*in_hbm(summed, weighted, state), router)


def expert_kernel(place, grads, gain, notes, *rest):
    *sources, out, backs, sems = rest
    experts = len(sources)
    _, _, part = grads.shape
    step = pl.program_id(0)
    source = lax.rem(place[0] + experts - step, experts)
    gate, inv, seq = notes[0, :, 0:1], notes[0, :, 1:2], notes[0, :, 2:3]
    capacity = gate.shape[0]
    loads = [pltpu.make_async_copy(sources[r], backs.at[r], sems.at[r]) for r in range(experts)]

    @pl.when(step == 0)
    def _():
        for load in loads:
            load.start()

    for r in range(experts):

        @pl.when(step == r)
        def _():
            loads[r].wait()
            back = backs.at[r]
            acc = jnp.zeros((capacity, 128), F32)
            rows = []
            for e in range(experts):
                cols = slice(part * e, part * (e + 1))
                w = rows_of(grads, e, source) * (gain[:, cols] / SEQ)
                x = jnp.broadcast_to(w[0:1], (capacity, part))
                for s in range(1, ROWS_DEV):
                    x = jnp.where(seq == s, w[s : s + 1], x)
                rows.append(w)
                acc = acc + fold(x * back[:, cols].astype(F32))
            shrink = inv * inv * inv * (jnp.sum(acc, axis=1, keepdims=True) / (experts * part))
            for e in range(experts):
                cols = slice(part * e, part * (e + 1))
                w = rows[e]
                x = jnp.broadcast_to(w[0:1], (capacity, part))
                for s in range(1, ROWS_DEV):
                    x = jnp.where(seq == s, w[s : s + 1], x)
                x = gate * (inv * x - shrink * back[:, cols].astype(F32))
                out[0, :, cols] = x.astype(BF16)


def expert_rows(place, grads, gain, notes, backs):
    experts, capacity = notes.shape[:2]
    width = gain.shape[1]
    whole = lambda shape: pl.BlockSpec(shape, lambda i, p: (0,) * len(shape))
    source = lambda i, p: (lax.rem(p[0] + experts - i, experts), 0, 0)
    return pl.pallas_call(
        expert_kernel,
        grid_spec=pltpu.PrefetchScalarGridSpec(
            num_scalar_prefetch=1,
            grid=(experts,),
            in_specs=[
                whole(grads.shape),
                whole((1, width)),
                pl.BlockSpec((1, capacity, notes.shape[2]), source),
            ]
            + [HBM] * experts,
            out_specs=pl.BlockSpec((1, capacity, width), source),
            scratch_shapes=[
                pltpu.VMEM((experts, capacity, width), BF16),
                pltpu.SemaphoreType.DMA((experts,)),
            ],
        ),
        out_shape=jax.ShapeDtypeStruct((experts, capacity, width), BF16),
        compiler_params=params(16),
        cost_estimate=cost(12 * experts * capacity * width, 9 << 20),
    )(place, grads, gain, notes, *in_hbm(*backs))


def shards(tokens, routes, positives, expert_out, router, norm_gain, loss_scale):
    experts, capacity, width = expert_out.shape[2:]
    rows = tokens.shape[0]
    slots = experts * capacity
    outer = lax.axis_size("u")
    mine = lax.axis_index("expert").astype(I32)
    mine_at = mine[None]
    wide = outer * experts
    part = width // experts
    group = PAIR_DEV * experts
    pairs = group * outer * CORES
    scale = 4.0 / math.sqrt(width)
    gain = norm_gain[None, :]
    columns = outer * experts * ROWS_DEV

    received = exchange(expert_out.reshape(experts, capacity, width), "expert").reshape(slots, width)
    gates, slot = routing(tokens, routes, router, experts, capacity)
    lane = jnp.arange(columns, dtype=I32)
    spread_positive = jnp.where(
        (lane % (2 * group)) // ROWS_DEV == mine,
        jnp.where(lane % ROWS_DEV == 0, positives[0], positives[1]) * (lane % ROWS_DEV < PAIR_DEV),
        0,
    ).astype(F32)

    summed, offered, inverse = forward(tokens, received, slot, gates, gain, experts, outer)
    near = exchange(offered, ("u", "expert"))
    facts = jnp.concatenate(
        [jnp.zeros((rows, 2), F32), inverse, gates, slot.astype(F32), routes.astype(F32)], axis=1
    )
    facts = jnp.pad(facts, ((0, 0), (0, 128 - facts.shape[1])))
    facts, *backs = pack(mine_at, summed, received, slot, facts, experts, capacity)

    def move(after, turns):
        after, *ready = lax.optimization_barrier((after, *[backs[r] for r in turns]))
        for r, x in zip(turns, ready):
            backs[r] = lax.ppermute(x, "expert", [(i, (i + r) % experts) for i in range(experts)])
        return after

    def landed(value, turns):
        value, *done = lax.optimization_barrier((value, *[backs[r] for r in turns]))
        for r, x in zip(turns, done):
            backs[r] = x
        return value

    slot_ids = jnp.arange(slots, dtype=I32)[None, :]
    picks = [slot[:, k : k + 1] == slot_ids for k in range(2)]
    gate_slot = jnp.sum(
        jnp.where(picks[0], gates[:, 0:1], 0.0) + jnp.where(picks[1], gates[:, 1:2], 0.0), axis=0
    )
    taken = picks[0] | picks[1]
    inverse_slot = jnp.sum(jnp.where(taken, inverse, 0.0), axis=0)
    sequence = (jnp.arange(rows, dtype=I32) // SEQ).astype(F32)
    sequence_slot = jnp.sum(jnp.where(taken, sequence[:, None], 0.0), axis=0)
    notes = jnp.stack([gate_slot, inverse_slot, sequence_slot, spread_positive])
    notes = jnp.pad(notes, ((0, 4), (0, 0)))

    near, facts = lax.optimization_barrier((near, facts))
    far = swap_core(near)
    near, far = near.reshape(columns, part), far.reshape(columns, part)
    offered = pl.pallas_call(
        scores_kernel,
        in_specs=[VMEM] * 3,
        out_specs=HBM,
        out_shape=pltpu.HBM((experts, 2 * group + 8, columns), F32),
        scratch_shapes=[pltpu.VMEM((2 * group + 8, columns), F32), pltpu.SemaphoreType.DMA((experts,))],
        compiler_params=params(2),
    )(near, far, notes)
    offered = move(offered, TURNS[0])
    gathered = exchange(offered, "expert")
    devices = outer * CORES
    offered, kept = pl.pallas_call(
        functools.partial(totals_kernel, scale),
        in_specs=[VMEM],
        out_specs=[HBM] * 2,
        out_shape=[pltpu.HBM((devices, 8, 128), F32), pltpu.HBM((3 * group, columns), F32)],
        scratch_shapes=[
            pltpu.VMEM((3 * group, columns), F32),
            pltpu.VMEM((devices, 8, 128), F32),
            pltpu.SemaphoreType.DMA(()),
            pltpu.SemaphoreType.DMA(()),
        ],
        compiler_params=params(2),
    )(gathered)
    offered = move(offered, TURNS[1])
    heard = exchange(offered, ("u", "c"))
    heard = landed(heard, TURNS[0])
    offered, loss = pl.pallas_call(
        functools.partial(gradient_kernel, scale),
        in_specs=[SMEM] + [VMEM] * 4,
        out_specs=[HBM, VMEM],
        out_shape=[pltpu.HBM((experts, 2 * group, part), F32), jax.ShapeDtypeStruct((1, 1), F32)],
        scratch_shapes=[pltpu.VMEM((2 * group, part), F32), pltpu.SemaphoreType.DMA((experts,))],
        compiler_params=params(2),
    )((loss_scale / pairs)[None], heard, kept, near, far)
    offered = move(offered, TURNS[2])
    grads = exchange(offered, "expert")
    grads = landed(grads, TURNS[1])

    router_part, state, weighted = pl.pallas_call(
        router_kernel,
        in_specs=[VMEM] * 2 + [HBM] * 4,
        out_specs=[VMEM, HBM, HBM],
        out_shape=[
            jax.ShapeDtypeStruct((width * experts // 128, 128), F32),
            pltpu.HBM((rows, 128), F32),
            pltpu.HBM((rows // SEQ, width), F32),
        ],
        scratch_shapes=[
            pltpu.VMEM((experts, rows, part), F32),
            pltpu.VMEM((experts, slots, part), BF16),
            pltpu.VMEM((experts, rows, part), BF16),
            pltpu.VMEM((rows, 128), F32),
            pltpu.VMEM((rows, 128), F32),
            pltpu.VMEM((rows // SEQ, width), F32),
            pltpu.SemaphoreType.DMA((3, experts)),
            pltpu.SemaphoreType.DMA(()),
            pltpu.SemaphoreType.DMA((2,)),
        ],
        compiler_params=params(16),
    )(grads, gain, *in_hbm(summed, received, tokens, facts))
    router_part = router_part + swap_core(router_part)
    router_part = exchange(router_part.reshape(wide, -1, 128), ("u", "expert"))
    held = lax.dynamic_slice_in_dim(gathered[:, 2 * group : 2 * group + 3], mine * capacity, capacity, axis=2)
    held = jnp.pad(jnp.transpose(held, (0, 2, 1)), ((0, 0), (0, 0), (0, 5)))
    expert_grad = expert_rows(mine_at, grads, gain, held, backs)
    router_part, expert_grad = lax.optimization_barrier((router_part, expert_grad))
    router_sum = jnp.sum(router_part, axis=0)
    turned = jnp.pad(router.T, ((0, 128 - experts), (0, 0)))
    token_grad = token_rows(summed, weighted, state, turned, experts)
    router_all = exchange(jnp.broadcast_to(router_sum[None], (wide,) + router_sum.shape), ("u", "expert"))
    router_all, token_grad = lax.optimization_barrier((router_all, token_grad))
    router_grad = router_all.reshape(-1, experts, 128).transpose(1, 0, 2).reshape(experts, width).T
    return token_grad, expert_grad.reshape(1, 1, experts, capacity, width), router_grad, loss[0, 0] / pairs


def solution(mesh):
    outer = mesh.shape["dp"] // CORES
    fine = Mesh(mesh.devices.reshape(outer, CORES, mesh.shape["expert"]), ("u", "c", "expert"))
    everywhere = ("u", "c", "expert")
    return jax.shard_map(
        shards,
        mesh=fine,
        in_specs=(
            P(everywhere, None),
            P(everywhere, None),
            P(everywhere),
            P(("u", "c"), "expert", None, None, None),
            P(),
            P(),
            P(),
        ),
        out_specs=(P(everywhere, None), P(("u", "c"), "expert", None, None, None), P(), P()),
        check_vma=False,
    )
```

```python
import functools
import math

import jax
import jax.numpy as jnp
from jax import lax
from jax.experimental import pallas as pl
from jax.experimental.pallas import tpu as pltpu
from jax.sharding import Mesh, PartitionSpec as P

PAIR_DEV = 2
SEQ = 48
EPS = 1e-05
CORES = 2
ROWS_DEV = 2 * PAIR_DEV
F32 = jnp.float32
BF16 = jnp.bfloat16
I32 = jnp.int32
VMEM = pl.BlockSpec(memory_space=pltpu.VMEM)
SMEM = pl.BlockSpec(memory_space=pltpu.SMEM)
HBM = pl.BlockSpec(memory_space=pltpu.HBM)
NT = (((1,), (1,)), ((), ()))
TURNS = ((1, 7), (4, 3), (5, 2, 6))


def iota(shape, dim):
    return lax.broadcasted_iota(I32, shape, dim)


def params(mib):
    return pltpu.CompilerParams(vmem_limit_bytes=mib << 20)


def cost(flops, moved):
    return pl.CostEstimate(flops=flops, bytes_accessed=moved, transcendentals=0)


def fold(x):
    total = x[:, :128]
    for k in range(1, x.shape[1] // 128):
        total = total + x[:, 128 * k : 128 * (k + 1)]
    return total


def in_hbm(*arrays):
    return [pltpu.with_memory_space_constraint(x, pltpu.HBM) for x in arrays]


def copy_all(copies):
    for copy in copies:
        copy.start()
    for copy in copies:
        copy.wait()


def to_each(source, target, sems):
    copy_all([pltpu.make_async_copy(source, target.at[i], sems.at[i]) for i in range(target.shape[0])])


def swap_core(x):
    return lax.ppermute(x, "c", [(0, 1), (1, 0)])


def exchange(x, axes):
    return lax.all_to_all(x, axes, split_axis=0, concat_axis=0, tiled=True)


def spread(x, axes, size):
    return exchange(jnp.broadcast_to(x[None], (size,) + x.shape), axes)


def routing(tokens, routes, router, experts, capacity):
    logits = jnp.dot(tokens, router, preferred_element_type=F32)
    lanes = jnp.arange(experts, dtype=I32)[None, None, :]
    one_hot = (routes[:, :, None] == lanes).astype(F32)
    chosen = jnp.sum(one_hot * logits[:, None, :], axis=2)
    gates = jax.nn.softmax(chosen, axis=1)
    rows = routes.shape[0]
    hits = jnp.sum(one_hot, axis=1)
    order = jnp.arange(rows, dtype=I32)
    earlier = (order[None, :] < order[:, None]).astype(BF16)
    before = jnp.dot(earlier, hits.astype(BF16), preferred_element_type=F32)
    rank = jnp.sum(one_hot * before[:, None, :], axis=2).astype(I32)
    return gates, routes * capacity + rank


def forward_kernel(
    steps, outer, tok, rec, slot, gate, gain, summed, offered, inverse, held, square, sliced, row_sem, slice_sem
):
    step = pl.program_id(0)
    part = tok.shape[1]

    def keep(e):
        start = pl.multiple_of(e * part, part)
        return pltpu.make_async_copy(held.at[e], summed.at[:, pl.ds(start, part)], row_sem.at[e])

    def offer(u):
        return pltpu.make_async_copy(sliced, offered.at[pl.ds(u * steps, steps)], slice_sem.at[u])

    rows, slots = tok.shape[0], rec.shape[0]
    ids = iota((rows, slots), 1)
    first = (slot[:, 0:1] == ids).astype(BF16)
    second = (slot[:, 1:2] == ids).astype(BF16)

    @pl.when(step == 0)
    def _():
        square[...] = jnp.zeros_like(square)

    for k in range(part // 256):
        cols = slice(256 * k, 256 * (k + 1))
        block = rec[:, cols]
        x = (
            tok[:, cols].astype(F32)
            + gate[:, 0:1] * jnp.dot(first, block, preferred_element_type=F32)
            + gate[:, 1:2] * jnp.dot(second, block, preferred_element_type=F32)
        )
        held[step, :, cols] = x
        square[...] += fold(x * x)
    keep(step).start()

    @pl.when(step == steps - 1)
    def _():
        mean = jnp.sum(square[...], axis=1, keepdims=True) / (steps * part)
        scale = lax.rsqrt(mean + EPS)
        inverse[...] = scale
        count = rows // SEQ
        for e in range(steps):
            x = held[e] * scale
            x = jnp.sum(x.reshape(count, SEQ, part), axis=1) / SEQ
            sliced[e] = (x * gain[:, part * e : part * (e + 1)]).astype(BF16)
        for u in range(outer):
            offer(u).start()
        for e in range(steps):
            keep(e).wait()
        for u in range(outer):
            offer(u).wait()


def forward(tokens, received, slot, gates, gain, experts, outer):
    rows, width = tokens.shape
    slots = received.shape[0]
    part = width // experts
    whole = lambda shape: pl.BlockSpec(shape, lambda i: (0,) * len(shape))
    return pl.pallas_call(
        functools.partial(forward_kernel, experts, outer),
        grid=(experts,),
        in_specs=[
            pl.BlockSpec((rows, part), lambda i: (0, i)),
            pl.BlockSpec((slots, part), lambda i: (0, i)),
            whole((rows, 2)),
            whole((rows, 2)),
            whole((1, width)),
        ],
        out_specs=[HBM, HBM, whole((rows, 1))],
        out_shape=[
            pltpu.HBM((rows, width), F32),
            pltpu.HBM((outer * experts, rows // SEQ, part), BF16),
            jax.ShapeDtypeStruct((rows, 1), F32),
        ],
        scratch_shapes=[
            pltpu.VMEM((experts, rows, part), F32),
            pltpu.VMEM((rows, 128), F32),
            pltpu.VMEM((experts, rows // SEQ, part), BF16),
            pltpu.SemaphoreType.DMA((experts,)),
            pltpu.SemaphoreType.DMA((outer,)),
        ],
        compiler_params=params(14),
        cost_estimate=cost(4 * rows * slots * width, 10 << 20),
    )(tokens, received, slot, gates, gain)


def pack_kernel(turns, place, x, turned, *rest):
    *outs, packed, sems = rest
    step, steps = pl.program_id(0), packed.shape[0]
    rows, part = x.shape
    capacity = outs[0].shape[0]
    slots = steps * capacity

    def leave(e, i):
        start = pl.multiple_of(e * part, part)
        return pltpu.make_async_copy(
            packed.at[e, pl.ds(i * capacity, capacity)], outs[i].at[:, pl.ds(start, part)], sems.at[e, i]
        )

    first = jnp.concatenate([iota((capacity, rows), 0) + r * capacity for r in turns], axis=0)
    target = lax.rem(first + place[0] * capacity, slots)
    spot = ((turned[0:1, :] == target) | (turned[1:2, :] == target)).astype(BF16)
    for k in range(part // 256):
        cols = slice(256 * k, 256 * (k + 1))
        packed[step, :, cols] = jnp.dot(
            spot, x[:, cols].astype(BF16), preferred_element_type=F32
        ).astype(BF16)
    for i in range(len(outs)):
        leave(step, i).start()

    @pl.when(step == steps - 1)
    def _():
        for e in range(steps):
            for i in range(len(outs)):
                leave(e, i).wait()


def pack(place, summed, turned, turns, experts, capacity):
    rows, width = summed.shape
    part = width // experts
    return pl.pallas_call(
        functools.partial(pack_kernel, turns),
        grid=(experts,),
        in_specs=[
            SMEM,
            pl.BlockSpec((rows, part), lambda i: (0, i)),
            pl.BlockSpec((2, rows), lambda i: (0, 0)),
        ],
        out_specs=[HBM] * len(turns),
        out_shape=[pltpu.HBM((capacity, width), BF16)] * len(turns),
        scratch_shapes=[
            pltpu.VMEM((experts, len(turns) * capacity, part), BF16),
            pltpu.SemaphoreType.DMA((experts, len(turns))),
        ],
        compiler_params=params(12),
        cost_estimate=cost(2 * rows * len(turns) * capacity * width, 5 << 20),
    )(place, *in_hbm(summed), turned)


def overlap_kernel(steps, x, rec, slot, facts, out, dots):
    step = pl.program_id(0)
    rows, part = x.shape
    slots = rec.shape[0]
    ids = iota((rows, slots), 1)
    first = (slot[:, 0:1] == ids).astype(BF16)
    second = (slot[:, 1:2] == ids).astype(BF16)

    @pl.when(step == 0)
    def _():
        dots[...] = jnp.zeros_like(dots)

    for k in range(part // 256):
        cols = slice(256 * k, 256 * (k + 1))
        value, block = x[:, cols], rec[:, cols]
        dots[0] += fold(value * jnp.dot(first, block, preferred_element_type=F32))
        dots[1] += fold(value * jnp.dot(second, block, preferred_element_type=F32))

    @pl.when(step == steps - 1)
    def _():
        lane = iota((rows, 128), 1)
        known = facts[...]
        for k in range(2):
            known = jnp.where(lane == k, jnp.sum(dots[k], axis=1, keepdims=True), known)
        out[...] = known


def overlaps(summed, received, slot, facts, experts):
    rows, width = summed.shape
    slots = received.shape[0]
    part = width // experts
    whole = lambda shape: pl.BlockSpec(shape, lambda i: (0, 0))
    return pl.pallas_call(
        functools.partial(overlap_kernel, experts),
        grid=(experts,),
        in_specs=[
            pl.BlockSpec((rows, part), lambda i: (0, i)),
            pl.BlockSpec((slots, part), lambda i: (0, i)),
            whole((rows, 2)),
            whole((rows, 128)),
        ],
        out_specs=whole((rows, 128)),
        out_shape=jax.ShapeDtypeStruct((rows, 128), F32),
        scratch_shapes=[pltpu.VMEM((2, rows, 128), F32)],
        compiler_params=params(12),
        cost_estimate=cost(4 * rows * slots * width, 7 << 20),
    )(*in_hbm(summed, received), slot, facts)


def lanes_of(shape, dim):
    lane = iota(shape, dim)
    kind = lax.rem(lane, ROWS_DEV)
    return lane, kind, kind >= PAIR_DEV


def picker(group, kind, turned=False):
    wide = 2 * group
    shape, pair, row = ((wide, group), 1, 0) if turned else ((group, wide), 0, 1)
    a = iota(shape, pair)
    b = iota(shape, row)
    source = (a // PAIR_DEV) * ROWS_DEV + lax.rem(a, PAIR_DEV) + PAIR_DEV * kind
    return (source == b).astype(BF16)


def scores_kernel(near, far, notes, offered, whole, sems):
    experts, total, columns = offered.shape
    group = experts * PAIR_DEV
    wide = 2 * group
    own = near[pl.ds(pl.multiple_of(lax.axis_index("u") * wide, wide), wide), :]
    queries, records = [
        jnp.dot(picker(group, kind), own, preferred_element_type=F32).astype(BF16) for kind in (0, 1)
    ]
    at_record = lanes_of((group, columns), 1)[2]
    for k, side in enumerate((near, far)):
        every = side[...]
        by_query = lax.dot_general(queries, every, NT, preferred_element_type=F32)
        by_record = lax.dot_general(records, every, NT, preferred_element_type=F32)
        whole[group * k : group * (k + 1)] = jnp.where(at_record, by_query, by_record)
    whole[2 * group :] = notes[...]
    to_each(whole, offered, sems)


def totals_kernel(scale, gathered, offered, kept_out, kept, spread, kept_sem, sem):
    place, core = lax.axis_index("u"), lax.axis_index("c")
    experts, total, columns = gathered.shape
    group = experts * PAIR_DEV
    both = gathered[0]
    for e in range(1, experts):
        both = both + gathered[e]
    positive_lane = both[2 * group + 3 : 2 * group + 4, :]
    near, far = both[:group] * scale, both[group : 2 * group] * scale
    kept[0:group] = near
    kept[group : 2 * group] = far

    shape = (group, columns)
    lane, kind, at_record = lanes_of(shape, 1)
    pair = iota(shape, 0)
    within = lax.rem(lane, 2 * group)
    matching = (within // ROWS_DEV == pair // PAIR_DEV) & (kind == lax.rem(pair, PAIR_DEV))
    here = matching & (lane // (2 * group) == place)
    positive = jnp.sum(jnp.where(here, positive_lane, 0.0), axis=1, keepdims=True)

    low = jnp.float32(-jnp.inf)
    near_records = jnp.where(at_record, near, low)
    far_records = jnp.where(at_record, far, low)
    highest = jnp.maximum(
        jnp.max(near_records, axis=1, keepdims=True), jnp.max(far_records, axis=1, keepdims=True)
    )
    weight = jnp.sum(jnp.exp(near_records - highest), axis=1, keepdims=True) + jnp.sum(
        jnp.exp(far_records - highest), axis=1, keepdims=True
    )
    log_total = highest + jnp.log(weight)
    chosen = jnp.zeros((group, 1), F32)
    for side, where in ((near, core), (far, 1 - core)):
        name = column_names(lane, kind, group, where)
        hit = at_record & (name.astype(F32) == positive)
        chosen = chosen + jnp.sum(jnp.where(hit, side, 0.0), axis=1, keepdims=True)
    kept[2 * group : 3 * group, :128] = jnp.broadcast_to(log_total, (group, 128))
    kept[2 * group : 3 * group, 128:256] = jnp.broadcast_to(positive, (group, 128))
    saved = pltpu.make_async_copy(kept, kept_out, kept_sem)
    saved.start()
    row_loss = log_total - chosen

    total_lane = jnp.sum(jnp.where(here, log_total, 0.0), axis=0, keepdims=True)
    loss_lane = jnp.sum(jnp.where(here, row_loss, 0.0), axis=0, keepdims=True)
    own_lane = jnp.where(lane[0:1] // (2 * group) == place, positive_lane, 0.0)
    pieces = [x[:, 128 * k : 128 * (k + 1)] for x in (total_lane, own_lane) for k in range(columns // 128)]
    loss_pieces = [
        pltpu.roll(loss_lane, PAIR_DEV, 1)[:, 128 * k : 128 * (k + 1)] for k in range(columns // 128)
    ]
    pieces = [a + b for a, b in zip(pieces, loss_pieces)] + pieces[columns // 128 :]
    message = jnp.concatenate(pieces, axis=0)
    for d in range(spread.shape[0]):
        spread[d] = message
    copy_all([pltpu.make_async_copy(spread, offered, sem)])
    saved.wait()


def column_names(lane, kind, group, core):
    wide = 2 * group
    block = (lane // wide) * CORES + core
    return block * group + (lax.rem(lane, wide) // ROWS_DEV) * PAIR_DEV + lax.rem(kind, PAIR_DEV)


def gradient_kernel(scale, factor, heard, kept, near, far, offered, loss, whole, sems):
    place, core = lax.axis_index("u"), lax.axis_index("c")
    experts, wide, columns = offered.shape
    group = wide // 2
    outer_size = heard.shape[0] // CORES
    pieces = columns // 128
    shape = (group, columns)
    lane, kind, at_record = lanes_of(shape, 1)
    pair = iota(shape, 0)
    own_name = (place * CORES + core) * group + iota((group, 1), 0)
    own_total = kept[2 * group : 3 * group, 0:1]
    own_positive = kept[2 * group : 3 * group, 128:129]
    result = jnp.zeros((wide, columns), F32)
    losses = jnp.zeros((1, columns), F32)
    for k, (side, where) in enumerate(((near, core), (far, 1 - core))):
        told = heard[where]
        for u in range(1, outer_size):
            told = told + heard[u * CORES + where]
        total = jnp.concatenate([told[i : i + 1] for i in range(pieces)], axis=1)
        positive = jnp.concatenate([told[pieces + i : pieces + i + 1] for i in range(pieces)], axis=1)
        losses = losses + jnp.where(at_record[0:1], total, 0.0)
        value = kept[group * k : group * (k + 1), :]
        name = column_names(lane, kind, group, where).astype(F32)
        hit = jnp.where(name == own_positive, 1.0, 0.0)
        by_query = (jnp.exp(value - own_total) - hit) * factor[0]
        by_query = jnp.where(at_record, by_query, 0.0).astype(BF16)
        hit = jnp.where(positive == own_name.astype(F32), 1.0, 0.0)
        by_record = (jnp.exp(jnp.where(at_record, 0.0, value - total)) - hit) * factor[0]
        by_record = jnp.where(at_record, 0.0, by_record).astype(BF16)
        rows = jnp.dot(picker(group, 0, True), by_query, preferred_element_type=F32) + jnp.dot(
            picker(group, 1, True), by_record, preferred_element_type=F32
        )
        result = result + jnp.dot(rows.astype(BF16), side[...], preferred_element_type=F32)
    whole[...] = (result * scale).astype(BF16)
    to_each(whole, offered, sems)
    loss[...] = jnp.sum(losses, axis=1, keepdims=True)


def rows_of(grads, e, index):
    tile = grads[e, pl.ds(pl.multiple_of((index // 4) * 16, 16), 16), :].astype(F32)
    piece = lax.rem(index, 4)
    quarters = [tile[ROWS_DEV * k : ROWS_DEV * (k + 1)] for k in range(4)]
    half = jnp.where(piece < 2, quarters[0], quarters[2]), jnp.where(piece < 2, quarters[1], quarters[3])
    return jnp.where(lax.rem(piece, 2) == 0, half[0], half[1])


def split_bf16(x):
    high = x.astype(BF16)
    rest = x - high.astype(F32)
    mid = rest.astype(BF16)
    low = (rest - mid.astype(F32)).astype(BF16)
    return high, mid, low


def router_kernel(
    grads, gain, summed_in, rec_in, tok_in, facts_in, part_out, state_out, weighted_out,
    summed, rec, tok, facts, state, weighted, sems, facts_sem, out_sems
):
    experts, _, part = grads.shape
    rows = summed.shape[1]
    slots = rec.shape[1]
    count = rows // SEQ

    def load(e):
        cols = pl.ds(e * part, part)
        pairs = ((summed_in, summed), (rec_in, rec), (tok_in, tok))
        return [
            pltpu.make_async_copy(a.at[:, cols], b.at[e], sems.at[k, e]) for k, (a, b) in enumerate(pairs)
        ]

    known = pltpu.make_async_copy(facts_in, facts, facts_sem)
    loads = [load(e) for e in range(experts)]
    for k in (1, 0):
        for e in range(experts):
            loads[e][k].start()
    known.start()
    for e in range(experts):
        loads[e][2].start()

    w = []
    for e in range(experts):
        cols = slice(part * e, part * (e + 1))
        w.append(rows_of(grads, e, lax.axis_index("expert")) * (gain[:, cols] / SEQ))
        weighted[:, cols] = w[e]
    on_slots = jnp.zeros((16, slots), F32)
    for e in range(experts):
        lhs = jnp.concatenate(list(split_bf16(w[e])) + [jnp.zeros((count, part), BF16)], axis=0)
        loads[e][1].wait()
        on_slots = on_slots + lax.dot_general(lhs, rec[e], NT, preferred_element_type=F32)
    acc = [jnp.zeros((SEQ, 128), F32) for _ in range(count)]
    for e in range(experts):
        loads[e][0].wait()
        for q in range(count):
            acc[q] = acc[q] + fold(summed[e, SEQ * q : SEQ * (q + 1), :] * w[e][q : q + 1, :])
    known.wait()
    on_slots = on_slots[0:count] + on_slots[count : 2 * count] + on_slots[2 * count : 3 * count]
    ids = iota((SEQ, slots), 1)
    lanes = iota((SEQ, 128), 1)
    choices = []
    for q in range(count):
        at = slice(SEQ * q, SEQ * (q + 1))
        fact = facts[at, :]
        inv = fact[:, 2:3]
        shrink = inv * inv * inv * (jnp.sum(acc[q], axis=1, keepdims=True) / (experts * part))
        row = on_slots[q : q + 1, :]
        grad_gate = []
        for k in range(2):
            spot = fact[:, 5 + k : 6 + k].astype(I32)
            along = jnp.sum(jnp.where(spot == ids, row, 0.0), axis=1, keepdims=True)
            grad_gate.append(inv * along - shrink * fact[:, k : k + 1])
        gates = [fact[:, 3 + k : 4 + k] for k in range(2)]
        mean = gates[0] * grad_gate[0] + gates[1] * grad_gate[1]
        choice = jnp.zeros((SEQ, 128), F32)
        for k in range(2):
            chosen = gates[k] * (grad_gate[k] - mean)
            route = fact[:, 7 + k : 8 + k].astype(I32)
            choice = choice + jnp.where(route == lanes, chosen, 0.0)
        choices.append(choice)
        choice = jnp.where(lanes == experts, inv, choice)
        state[at] = jnp.where(lanes == experts + 1, shrink, choice)
    saved = [
        pltpu.make_async_copy(state, state_out, out_sems.at[0]),
        pltpu.make_async_copy(weighted, weighted_out, out_sems.at[1]),
    ]
    for copy in saved:
        copy.start()
    lhs = jnp.transpose(jnp.concatenate(choices, axis=0))[:experts].astype(BF16)
    tiles = part // 128
    for e in range(experts):
        loads[e][2].wait()
        block = jnp.dot(lhs, tok[e], preferred_element_type=F32)
        for k in range(tiles):
            at = experts * (tiles * e + k)
            part_out[at : at + experts, :] = block[:, 128 * k : 128 * (k + 1)]
    for copy in saved:
        copy.wait()


def token_kernel(experts, summed, weighted, state, router, out):
    rows = summed.shape[0]
    known = state[...]
    choice = jnp.where(iota(known.shape, 1) < experts, known, 0.0).astype(BF16)
    through = jnp.dot(choice, router[...], preferred_element_type=F32)
    for q in range(rows // SEQ):
        at = slice(SEQ * q, SEQ * (q + 1))
        inverse, shrink = known[at, experts : experts + 1], known[at, experts + 1 : experts + 2]
        x = inverse * weighted[q : q + 1, :] - shrink * summed[at]
        out[at] = (x + through[SEQ * q : SEQ * (q + 1)]).astype(BF16)


def token_rows(summed, weighted, state, router, experts):
    rows, width = summed.shape
    part = width // experts
    split = lambda count: pl.BlockSpec((count, part), lambda i: (0, i))
    return pl.pallas_call(
        functools.partial(token_kernel, experts),
        grid=(experts,),
        in_specs=[
            split(rows),
            split(weighted.shape[0]),
            pl.BlockSpec((rows, 128), lambda i: (0, 0)),
            split(128),
        ],
        out_specs=split(rows),
        out_shape=jax.ShapeDtypeStruct((rows, width), BF16),
        compiler_params=params(10),
        cost_estimate=cost(2 * rows * 128 * width, 5 << 20),
    )(*in_hbm(summed, weighted, state), router)


def expert_kernel(place, grads, gain, notes, *rest):
    *sources, out, backs, sems = rest
    experts = len(sources)
    _, _, part = grads.shape
    step = pl.program_id(0)
    source = lax.rem(place[0] + experts - step, experts)
    gate, inv, seq = notes[0, :, 0:1], notes[0, :, 1:2], notes[0, :, 2:3]
    capacity = gate.shape[0]
    loads = [pltpu.make_async_copy(sources[r], backs.at[r], sems.at[r]) for r in range(experts)]

    @pl.when(step == 0)
    def _():
        for load in loads:
            load.start()

    for r in range(experts):

        @pl.when(step == r)
        def _():
            loads[r].wait()
            back = backs.at[r]
            acc = jnp.zeros((capacity, 128), F32)
            rows = []
            for e in range(experts):
                cols = slice(part * e, part * (e + 1))
                w = rows_of(grads, e, source) * (gain[:, cols] / SEQ)
                x = jnp.broadcast_to(w[0:1], (capacity, part))
                for s in range(1, ROWS_DEV):
                    x = jnp.where(seq == s, w[s : s + 1], x)
                rows.append(w)
                acc = acc + fold(x * back[:, cols].astype(F32))
            shrink = inv * inv * inv * (jnp.sum(acc, axis=1, keepdims=True) / (experts * part))
            for e in range(experts):
                cols = slice(part * e, part * (e + 1))
                w = rows[e]
                x = jnp.broadcast_to(w[0:1], (capacity, part))
                for s in range(1, ROWS_DEV):
                    x = jnp.where(seq == s, w[s : s + 1], x)
                x = gate * (inv * x - shrink * back[:, cols].astype(F32))
                out[0, :, cols] = x.astype(BF16)


def expert_rows(place, grads, gain, notes, backs):
    experts, capacity = notes.shape[:2]
    width = gain.shape[1]
    whole = lambda shape: pl.BlockSpec(shape, lambda i, p: (0,) * len(shape))
    source = lambda i, p: (lax.rem(p[0] + experts - i, experts), 0, 0)
    return pl.pallas_call(
        expert_kernel,
        grid_spec=pltpu.PrefetchScalarGridSpec(
            num_scalar_prefetch=1,
            grid=(experts,),
            in_specs=[
                whole(grads.shape),
                whole((1, width)),
                pl.BlockSpec((1, capacity, notes.shape[2]), source),
            ]
            + [HBM] * experts,
            out_specs=pl.BlockSpec((1, capacity, width), source),
            scratch_shapes=[
                pltpu.VMEM((experts, capacity, width), BF16),
                pltpu.SemaphoreType.DMA((experts,)),
            ],
        ),
        out_shape=jax.ShapeDtypeStruct((experts, capacity, width), BF16),
        compiler_params=params(16),
        cost_estimate=cost(12 * experts * capacity * width, 9 << 20),
    )(place, grads, gain, notes, *in_hbm(*backs))


def shards(tokens, routes, positives, expert_out, router, norm_gain, loss_scale):
    experts, capacity, width = expert_out.shape[2:]
    rows = tokens.shape[0]
    slots = experts * capacity
    outer = lax.axis_size("u")
    mine = lax.axis_index("expert").astype(I32)
    mine_at = mine[None]
    wide = outer * experts
    part = width // experts
    group = PAIR_DEV * experts
    pairs = group * outer * CORES
    scale = 4.0 / math.sqrt(width)
    gain = norm_gain[None, :]
    columns = outer * experts * ROWS_DEV

    received = exchange(expert_out.reshape(experts, capacity, width), "expert").reshape(slots, width)
    gates, slot = routing(tokens, routes, router, experts, capacity)
    lane = jnp.arange(columns, dtype=I32)
    spread_positive = jnp.where(
        (lane % (2 * group)) // ROWS_DEV == mine,
        jnp.where(lane % ROWS_DEV == 0, positives[0], positives[1]) * (lane % ROWS_DEV < PAIR_DEV),
        0,
    ).astype(F32)

    summed, offered, inverse = forward(tokens, received, slot, gates, gain, experts, outer)
    near = exchange(offered, ("u", "expert"))
    facts = jnp.concatenate(
        [jnp.zeros((rows, 2), F32), inverse, gates, slot.astype(F32), routes.astype(F32)], axis=1
    )
    facts = jnp.pad(facts, ((0, 0), (0, 128 - facts.shape[1])))
    backs = list(pack(mine_at, summed, slot.T, tuple(range(experts)), experts, capacity))

    def move(after, turns):
        after, *ready = lax.optimization_barrier((after, *[backs[r] for r in turns]))
        for r, x in zip(turns, ready):
            backs[r] = lax.ppermute(x, "expert", [(i, (i + r) % experts) for i in range(experts)])
        return after

    move(slot, TURNS[0])

    def landed(value, turns):
        value, *done = lax.optimization_barrier((value, *[backs[r] for r in turns]))
        for r, x in zip(turns, done):
            backs[r] = x
        return value

    slot_ids = jnp.arange(slots, dtype=I32)[None, :]
    picks = [slot[:, k : k + 1] == slot_ids for k in range(2)]
    gate_slot = jnp.sum(
        jnp.where(picks[0], gates[:, 0:1], 0.0) + jnp.where(picks[1], gates[:, 1:2], 0.0), axis=0
    )
    taken = picks[0] | picks[1]
    inverse_slot = jnp.sum(jnp.where(taken, inverse, 0.0), axis=0)
    sequence = (jnp.arange(rows, dtype=I32) // SEQ).astype(F32)
    sequence_slot = jnp.sum(jnp.where(taken, sequence[:, None], 0.0), axis=0)
    notes = jnp.stack([gate_slot, inverse_slot, sequence_slot, spread_positive])
    notes = jnp.pad(notes, ((0, 4), (0, 0)))

    near, *backs = lax.optimization_barrier((near, *backs))
    far = swap_core(near)
    near, far = near.reshape(columns, part), far.reshape(columns, part)
    offered = pl.pallas_call(
        scores_kernel,
        in_specs=[VMEM] * 3,
        out_specs=HBM,
        out_shape=pltpu.HBM((experts, 2 * group + 8, columns), F32),
        scratch_shapes=[pltpu.VMEM((2 * group + 8, columns), F32), pltpu.SemaphoreType.DMA((experts,))],
        compiler_params=params(2),
    )(near, far, notes)
    offered = move(offered, TURNS[1] + TURNS[2])
    gathered = exchange(offered, "expert")
    devices = outer * CORES
    offered, kept = pl.pallas_call(
        functools.partial(totals_kernel, scale),
        in_specs=[VMEM],
        out_specs=[HBM] * 2,
        out_shape=[pltpu.HBM((devices, 8, 128), F32), pltpu.HBM((3 * group, columns), F32)],
        scratch_shapes=[
            pltpu.VMEM((3 * group, columns), F32),
            pltpu.VMEM((devices, 8, 128), F32),
            pltpu.SemaphoreType.DMA(()),
            pltpu.SemaphoreType.DMA(()),
        ],
        compiler_params=params(2),
    )(gathered)
    heard = exchange(offered, ("u", "c"))
    heard = landed(heard, TURNS[1])
    offered, facts = lax.optimization_barrier((offered, facts))
    facts = overlaps(summed, received, slot, facts, experts)
    heard, facts = lax.optimization_barrier((heard, facts))
    offered, loss = pl.pallas_call(
        functools.partial(gradient_kernel, scale),
        in_specs=[SMEM] + [VMEM] * 4,
        out_specs=[HBM, VMEM],
        out_shape=[pltpu.HBM((experts, 2 * group, part), BF16), jax.ShapeDtypeStruct((1, 1), F32)],
        scratch_shapes=[pltpu.VMEM((2 * group, part), BF16), pltpu.SemaphoreType.DMA((experts,))],
        compiler_params=params(2),
    )((loss_scale / pairs)[None], heard, kept, near, far)
    grads = exchange(offered, "expert")
    grads = landed(grads, TURNS[2])

    router_part, state, weighted = pl.pallas_call(
        router_kernel,
        in_specs=[VMEM] * 2 + [HBM] * 4,
        out_specs=[VMEM, HBM, HBM],
        out_shape=[
            jax.ShapeDtypeStruct((width * experts // 128, 128), F32),
            pltpu.HBM((rows, 128), F32),
            pltpu.HBM((rows // SEQ, width), F32),
        ],
        scratch_shapes=[
            pltpu.VMEM((experts, rows, part), F32),
            pltpu.VMEM((experts, slots, part), BF16),
            pltpu.VMEM((experts, rows, part), BF16),
            pltpu.VMEM((rows, 128), F32),
            pltpu.VMEM((rows, 128), F32),
            pltpu.VMEM((rows // SEQ, width), F32),
            pltpu.SemaphoreType.DMA((3, experts)),
            pltpu.SemaphoreType.DMA(()),
            pltpu.SemaphoreType.DMA((2,)),
        ],
        compiler_params=params(16),
    )(grads, gain, *in_hbm(summed, received, tokens, facts))
    router_part = exchange(router_part.reshape(outer, -1, 128), "u")
    router_part = jnp.sum(router_part, axis=0)
    router_part = spread(router_part, ("c", "expert"), CORES * experts)
    held = lax.dynamic_slice_in_dim(gathered[:, 2 * group : 2 * group + 3], mine * capacity, capacity, axis=2)
    held = jnp.pad(jnp.transpose(held, (0, 2, 1)), ((0, 0), (0, 0), (0, 5)))
    expert_grad = expert_rows(mine_at, grads, gain, held, backs)
    turned = jnp.pad(router.T, ((0, 128 - experts), (0, 0)))
    router_part, expert_grad = lax.optimization_barrier((router_part, expert_grad))
    router_part = jnp.sum(router_part, axis=0)
    token_grad = token_rows(summed, weighted, state, turned, experts)
    router_all = spread(router_part, "u", outer)
    router_all, token_grad = lax.optimization_barrier((router_all, token_grad))
    router_grad = router_all.reshape(-1, experts, 128).transpose(1, 0, 2).reshape(experts, width).T
    return token_grad, expert_grad.reshape(1, 1, experts, capacity, width), router_grad, loss[0, 0] / pairs


def solution(mesh):
    outer = mesh.shape["dp"] // CORES
    fine = Mesh(mesh.devices.reshape(outer, CORES, mesh.shape["expert"]), ("u", "c", "expert"))
    everywhere = ("u", "c", "expert")
    return jax.shard_map(
        shards,
        mesh=fine,
        in_specs=(
            P(everywhere, None),
            P(everywhere, None),
            P(everywhere),
            P(("u", "c"), "expert", None, None, None),
            P(),
            P(),
            P(),
        ),
        out_specs=(P(everywhere, None), P(("u", "c"), "expert", None, None, None), P(), P()),
        check_vma=False,
    )
```

```python
import functools
import math

import jax
import jax.numpy as jnp
from jax import lax
from jax.experimental import pallas as pl
from jax.experimental.pallas import tpu as pltpu
from jax.sharding import Mesh, PartitionSpec as P

PAIR_DEV = 2
SEQ = 48
EPS = 1e-05
CORES = 2
ROWS_DEV = 2 * PAIR_DEV
F32 = jnp.float32
BF16 = jnp.bfloat16
I32 = jnp.int32
VMEM = pl.BlockSpec(memory_space=pltpu.VMEM)
SMEM = pl.BlockSpec(memory_space=pltpu.SMEM)
HBM = pl.BlockSpec(memory_space=pltpu.HBM)
NT = (((1,), (1,)), ((), ()))
TURNS = ((1, 7), (4, 3), (5,), (2, 6))


def iota(shape, dim):
    return lax.broadcasted_iota(I32, shape, dim)


def params(mib):
    return pltpu.CompilerParams(vmem_limit_bytes=mib << 20)


def cost(flops, moved):
    return pl.CostEstimate(flops=flops, bytes_accessed=moved, transcendentals=0)


def fold(x):
    total = x[:, :128]
    for k in range(1, x.shape[1] // 128):
        total = total + x[:, 128 * k : 128 * (k + 1)]
    return total


def in_hbm(*arrays):
    return [pltpu.with_memory_space_constraint(x, pltpu.HBM) for x in arrays]


def copy_all(copies):
    for copy in copies:
        copy.start()
    for copy in copies:
        copy.wait()


def to_each(source, target, sems):
    copy_all([pltpu.make_async_copy(source, target.at[i], sems.at[i]) for i in range(target.shape[0])])


def swap_core(x):
    return lax.ppermute(x, "c", [(0, 1), (1, 0)])


def exchange(x, axes):
    return lax.all_to_all(x, axes, split_axis=0, concat_axis=0, tiled=True)


def spread(x, axes, size):
    return exchange(jnp.broadcast_to(x[None], (size,) + x.shape), axes)


def routing(tokens, routes, router, experts, capacity):
    logits = jnp.dot(tokens, router, preferred_element_type=F32)
    lanes = jnp.arange(experts, dtype=I32)[None, None, :]
    one_hot = (routes[:, :, None] == lanes).astype(F32)
    chosen = jnp.sum(one_hot * logits[:, None, :], axis=2)
    gates = jax.nn.softmax(chosen, axis=1)
    rows = routes.shape[0]
    hits = jnp.sum(one_hot, axis=1)
    order = jnp.arange(rows, dtype=I32)
    earlier = (order[None, :] < order[:, None]).astype(BF16)
    before = jnp.dot(earlier, hits.astype(BF16), preferred_element_type=F32)
    rank = jnp.sum(one_hot * before[:, None, :], axis=2).astype(I32)
    return gates, routes * capacity + rank


def one_hots(slot, slots):
    ids = iota((slot.shape[0], slots), 1)
    return jnp.concatenate([(slot[:, k : k + 1] == ids).astype(BF16) for k in range(2)], axis=0)


def forward_kernel(
    steps, tok, rec, slot, gate, gain, summed, sliced_out, inverse, held, square, picks, sliced, row_sem, slice_sem
):
    step = pl.program_id(0)
    rows, part = tok.shape

    def keep(e):
        start = pl.multiple_of(e * part, part)
        return pltpu.make_async_copy(held.at[e], summed.at[:, pl.ds(start, part)], row_sem.at[e])

    @pl.when(step == 0)
    def _():
        square[...] = jnp.zeros_like(square)
        picks[...] = one_hots(slot, rec.shape[0])

    for k in range(part // 256):
        cols = slice(256 * k, 256 * (k + 1))
        both = jnp.dot(picks[...], rec[:, cols], preferred_element_type=F32)
        x = tok[:, cols].astype(F32) + gate[:, 0:1] * both[:rows] + gate[:, 1:2] * both[rows:]
        held[step, :, cols] = x
        square[...] += fold(x * x)
    keep(step).start()

    @pl.when(step == steps - 1)
    def _():
        mean = jnp.sum(square[...], axis=1, keepdims=True) / (steps * part)
        scale = lax.rsqrt(mean + EPS)
        inverse[...] = scale
        count = rows // SEQ
        for e in range(steps):
            x = held[e] * scale
            x = jnp.sum(x.reshape(count, SEQ, part), axis=1) / SEQ
            sliced[e] = (x * gain[:, part * e : part * (e + 1)]).astype(BF16)
        offer = pltpu.make_async_copy(sliced, sliced_out, slice_sem)
        offer.start()
        for e in range(steps):
            keep(e).wait()
        offer.wait()


def forward(tokens, received, slot, gates, gain, experts):
    rows, width = tokens.shape
    slots = received.shape[0]
    part = width // experts
    whole = lambda shape: pl.BlockSpec(shape, lambda i: (0,) * len(shape))
    return pl.pallas_call(
        functools.partial(forward_kernel, experts),
        grid=(experts,),
        in_specs=[
            pl.BlockSpec((rows, part), lambda i: (0, i)),
            pl.BlockSpec((slots, part), lambda i: (0, i)),
            whole((rows, 2)),
            whole((rows, 2)),
            whole((1, width)),
        ],
        out_specs=[HBM, HBM, whole((rows, 1))],
        out_shape=[
            pltpu.HBM((rows, width), F32),
            pltpu.HBM((experts, rows // SEQ, part), BF16),
            jax.ShapeDtypeStruct((rows, 1), F32),
        ],
        scratch_shapes=[
            pltpu.VMEM((experts, rows, part), F32),
            pltpu.VMEM((rows, 128), F32),
            pltpu.VMEM((2 * rows, slots), BF16),
            pltpu.VMEM((experts, rows // SEQ, part), BF16),
            pltpu.SemaphoreType.DMA((experts,)),
            pltpu.SemaphoreType.DMA(()),
        ],
        compiler_params=params(14),
        cost_estimate=cost(4 * rows * slots * width, 10 << 20),
    )(tokens, received, slot, gates, gain)


def pack_kernel(place, x, turned, *rest):
    *outs, spot, packed, sems = rest
    step, steps = pl.program_id(0), packed.shape[0]
    rows, part = x.shape
    capacity = outs[0].shape[0]
    slots = spot.shape[0]

    def leave(e, i):
        start = pl.multiple_of(e * part, part)
        return pltpu.make_async_copy(
            packed.at[e, pl.ds(i * capacity, capacity)], outs[i].at[:, pl.ds(start, part)], sems.at[e, i]
        )

    @pl.when(step == 0)
    def _():
        target = lax.rem(iota((slots, rows), 0) + place[0] * capacity, slots)
        spot[...] = ((turned[0:1, :] == target) | (turned[1:2, :] == target)).astype(BF16)

    for k in range(part // 512):
        cols = slice(512 * k, 512 * (k + 1))
        packed[step, :, cols] = jnp.dot(
            spot[...], x[:, cols].astype(BF16), preferred_element_type=F32
        ).astype(BF16)
    for i in range(len(outs)):
        leave(step, i).start()

    @pl.when(step == steps - 1)
    def _():
        for e in range(steps):
            for i in range(len(outs)):
                leave(e, i).wait()


def pack(place, summed, turned, experts, capacity):
    rows, width = summed.shape
    steps = experts // 2
    part = width // steps
    slots = experts * capacity
    return pl.pallas_call(
        pack_kernel,
        grid=(steps,),
        in_specs=[
            SMEM,
            pl.BlockSpec((rows, part), lambda i: (0, i)),
            pl.BlockSpec((2, rows), lambda i: (0, 0)),
        ],
        out_specs=[HBM] * experts,
        out_shape=[pltpu.HBM((capacity, width), BF16)] * experts,
        scratch_shapes=[
            pltpu.VMEM((slots, rows), BF16),
            pltpu.VMEM((steps, slots, part), BF16),
            pltpu.SemaphoreType.DMA((steps, experts)),
        ],
        compiler_params=params(14),
        cost_estimate=cost(2 * rows * slots * width, 7 << 20),
    )(place, *in_hbm(summed), turned)


def overlap_kernel(steps, x, rec, slot, facts, out, fetched, picks, dots):
    step = pl.program_id(0)
    rows, part = x.shape

    @pl.when(step == 0)
    def _():
        dots[...] = jnp.zeros_like(dots)
        picks[...] = one_hots(slot, rec.shape[0])

    for k in range(part // 256):
        cols = slice(256 * k, 256 * (k + 1))
        both = jnp.dot(picks[...], rec[:, cols], preferred_element_type=F32)
        fetched[:, cols] = both.astype(BF16)
        value = x[:, cols]
        dots[:rows] += fold(value * both[:rows])
        dots[rows:] += fold(value * both[rows:])

    @pl.when(step == steps - 1)
    def _():
        lane = iota((rows, 128), 1)
        known = facts[...]
        for k in range(2):
            total = jnp.sum(dots[rows * k : rows * (k + 1)], axis=1, keepdims=True)
            known = jnp.where(lane == k, total, known)
        out[...] = known


def overlaps(summed, received, slot, facts, experts):
    rows, width = summed.shape
    slots = received.shape[0]
    part = width // experts
    whole = lambda shape: pl.BlockSpec(shape, lambda i: (0, 0))
    return pl.pallas_call(
        functools.partial(overlap_kernel, experts),
        grid=(experts,),
        in_specs=[
            pl.BlockSpec((rows, part), lambda i: (0, i)),
            pl.BlockSpec((slots, part), lambda i: (0, i)),
            whole((rows, 2)),
            whole((rows, 128)),
        ],
        out_specs=[whole((rows, 128)), pl.BlockSpec((2 * rows, part), lambda i: (0, i))],
        out_shape=[pltpu.HBM((rows, 128), F32), pltpu.HBM((2 * rows, width), BF16)],
        scratch_shapes=[pltpu.VMEM((2 * rows, slots), BF16), pltpu.VMEM((2 * rows, 128), F32)],
        compiler_params=params(12),
        cost_estimate=cost(4 * rows * slots * width, 10 << 20),
    )(*in_hbm(summed, received), slot, facts)


def lanes_of(shape, dim):
    lane = iota(shape, dim)
    kind = lax.rem(lane, ROWS_DEV)
    return lane, kind, kind >= PAIR_DEV


def picker(group, kind, turned=False):
    wide = 2 * group
    shape, pair, row = ((wide, group), 1, 0) if turned else ((group, wide), 0, 1)
    a = iota(shape, pair)
    b = iota(shape, row)
    source = (a // PAIR_DEV) * ROWS_DEV + lax.rem(a, PAIR_DEV) + PAIR_DEV * kind
    return (source == b).astype(BF16)


def scores_kernel(own, near, far, notes, offered, whole, sems):
    experts, total, columns = offered.shape
    group = experts * PAIR_DEV
    queries, records = [
        jnp.dot(picker(group, kind), own[...], preferred_element_type=F32).astype(BF16) for kind in (0, 1)
    ]
    at_record = lanes_of((group, columns), 1)[2]
    for k, side in enumerate((near, far)):
        every = side[...]
        by_query = lax.dot_general(queries, every, NT, preferred_element_type=F32)
        by_record = lax.dot_general(records, every, NT, preferred_element_type=F32)
        whole[group * k : group * (k + 1)] = jnp.where(at_record, by_query, by_record)
    whole[2 * group :] = notes[...]
    to_each(whole, offered, sems)


def totals_kernel(scale, gathered, offered, kept_out, kept, spread, kept_sem, sem):
    place, core = lax.axis_index("u"), lax.axis_index("c")
    experts, total, columns = gathered.shape
    group = experts * PAIR_DEV
    both = gathered[0]
    for e in range(1, experts):
        both = both + gathered[e]
    positive_lane = both[2 * group + 3 : 2 * group + 4, :]
    near, far = both[:group] * scale, both[group : 2 * group] * scale
    kept[0:group] = near
    kept[group : 2 * group] = far

    shape = (group, columns)
    lane, kind, at_record = lanes_of(shape, 1)
    pair = iota(shape, 0)
    within = lax.rem(lane, 2 * group)
    matching = (within // ROWS_DEV == pair // PAIR_DEV) & (kind == lax.rem(pair, PAIR_DEV))
    here = matching & (lane // (2 * group) == place)
    positive = jnp.sum(jnp.where(here, positive_lane, 0.0), axis=1, keepdims=True)

    low = jnp.float32(-jnp.inf)
    near_records = jnp.where(at_record, near, low)
    far_records = jnp.where(at_record, far, low)
    highest = jnp.maximum(
        jnp.max(near_records, axis=1, keepdims=True), jnp.max(far_records, axis=1, keepdims=True)
    )
    weight = jnp.sum(jnp.exp(near_records - highest), axis=1, keepdims=True) + jnp.sum(
        jnp.exp(far_records - highest), axis=1, keepdims=True
    )
    log_total = highest + jnp.log(weight)
    chosen = jnp.zeros((group, 1), F32)
    for side, where in ((near, core), (far, 1 - core)):
        name = column_names(lane, kind, group, where)
        hit = at_record & (name.astype(F32) == positive)
        chosen = chosen + jnp.sum(jnp.where(hit, side, 0.0), axis=1, keepdims=True)
    kept[2 * group : 3 * group, :128] = jnp.broadcast_to(log_total, (group, 128))
    kept[2 * group : 3 * group, 128:256] = jnp.broadcast_to(positive, (group, 128))
    saved = pltpu.make_async_copy(kept, kept_out, kept_sem)
    saved.start()
    row_loss = log_total - chosen

    total_lane = jnp.sum(jnp.where(here, log_total, 0.0), axis=0, keepdims=True)
    loss_lane = jnp.sum(jnp.where(here, row_loss, 0.0), axis=0, keepdims=True)
    own_lane = jnp.where(lane[0:1] // (2 * group) == place, positive_lane, 0.0)
    pieces = [x[:, 128 * k : 128 * (k + 1)] for x in (total_lane, own_lane) for k in range(columns // 128)]
    loss_pieces = [
        pltpu.roll(loss_lane, PAIR_DEV, 1)[:, 128 * k : 128 * (k + 1)] for k in range(columns // 128)
    ]
    pieces = [a + b for a, b in zip(pieces, loss_pieces)] + pieces[columns // 128 :]
    message = jnp.concatenate(pieces, axis=0)
    for d in range(spread.shape[0]):
        spread[d] = message
    copy_all([pltpu.make_async_copy(spread, offered, sem)])
    saved.wait()


def column_names(lane, kind, group, core):
    wide = 2 * group
    block = (lane // wide) * CORES + core
    return block * group + (lax.rem(lane, wide) // ROWS_DEV) * PAIR_DEV + lax.rem(kind, PAIR_DEV)


def gradient_kernel(scale, factor, heard, kept, near, far, offered, loss, whole, sems):
    place, core = lax.axis_index("u"), lax.axis_index("c")
    experts, wide, columns = offered.shape
    group = wide // 2
    outer_size = heard.shape[0] // CORES
    pieces = columns // 128
    shape = (group, columns)
    lane, kind, at_record = lanes_of(shape, 1)
    pair = iota(shape, 0)
    own_name = (place * CORES + core) * group + iota((group, 1), 0)
    own_total = kept[2 * group : 3 * group, 0:1]
    own_positive = kept[2 * group : 3 * group, 128:129]
    result = jnp.zeros((wide, columns), F32)
    losses = jnp.zeros((1, columns), F32)
    for k, (side, where) in enumerate(((near, core), (far, 1 - core))):
        told = heard[where]
        for u in range(1, outer_size):
            told = told + heard[u * CORES + where]
        total = jnp.concatenate([told[i : i + 1] for i in range(pieces)], axis=1)
        positive = jnp.concatenate([told[pieces + i : pieces + i + 1] for i in range(pieces)], axis=1)
        losses = losses + jnp.where(at_record[0:1], total, 0.0)
        value = kept[group * k : group * (k + 1), :]
        name = column_names(lane, kind, group, where).astype(F32)
        hit = jnp.where(name == own_positive, 1.0, 0.0)
        by_query = (jnp.exp(value - own_total) - hit) * factor[0]
        by_query = jnp.where(at_record, by_query, 0.0).astype(BF16)
        hit = jnp.where(positive == own_name.astype(F32), 1.0, 0.0)
        by_record = (jnp.exp(jnp.where(at_record, 0.0, value - total)) - hit) * factor[0]
        by_record = jnp.where(at_record, 0.0, by_record).astype(BF16)
        rows = jnp.dot(picker(group, 0, True), by_query, preferred_element_type=F32) + jnp.dot(
            picker(group, 1, True), by_record, preferred_element_type=F32
        )
        result = result + jnp.dot(rows.astype(BF16), side[...], preferred_element_type=F32)
    whole[...] = (result * scale).astype(BF16)
    to_each(whole, offered, sems)
    loss[...] = jnp.sum(losses, axis=1, keepdims=True)


def rows_of(grads, e, index):
    tile = grads[e, pl.ds(pl.multiple_of((index // 4) * 16, 16), 16), :].astype(F32)
    piece = lax.rem(index, 4)
    quarters = [tile[ROWS_DEV * k : ROWS_DEV * (k + 1)] for k in range(4)]
    half = jnp.where(piece < 2, quarters[0], quarters[2]), jnp.where(piece < 2, quarters[1], quarters[3])
    return jnp.where(lax.rem(piece, 2) == 0, half[0], half[1])


def router_kernel(
    grads, gain, summed_in, fetched_in, tok_in, facts_in, part_out, state_out, weighted_out,
    summed, fetched, tok, facts, state, weighted, acc, sems, facts_sem, out_sems
):
    experts, _, part = grads.shape
    rows = summed.shape[1]
    count = rows // SEQ
    sources = ((summed_in, summed), (fetched_in, fetched), (tok_in, tok))

    def load(e):
        cols = pl.ds(e * part, part)
        return [
            pltpu.make_async_copy(a.at[:, cols], b.at[e], sems.at[k, e]) for k, (a, b) in enumerate(sources)
        ]

    known = pltpu.make_async_copy(facts_in, facts, facts_sem)
    loads = [load(e) for e in range(experts)]
    for e in range(experts):
        loads[e][0].start()
        loads[e][1].start()
    known.start()
    for e in range(experts):
        loads[e][2].start()

    for e in range(experts):
        cols = slice(part * e, part * (e + 1))
        w = rows_of(grads, e, lax.axis_index("expert")) * (gain[:, cols] / SEQ)
        weighted[:, cols] = w
        loads[e][0].wait()
        loads[e][1].wait()
        for q in range(count):
            row = w[q : q + 1, :]
            at = [slice(rows * k + SEQ * q, rows * k + SEQ * (q + 1)) for k in range(2)]
            terms = [summed[e, at[0], :], fetched[e, at[0], :].astype(F32), fetched[e, at[1], :].astype(F32)]
            for k, term in enumerate(terms):
                total = fold(term * row)
                spot = slice(SEQ * q, SEQ * (q + 1))
                acc[k, spot] = total if e == 0 else acc[k, spot] + total
    known.wait()
    lanes = iota((SEQ, 128), 1)
    choices = []
    for q in range(count):
        at = slice(SEQ * q, SEQ * (q + 1))
        fact = facts[at, :]
        inv = fact[:, 2:3]
        shrink = inv * inv * inv * (jnp.sum(acc[0, at], axis=1, keepdims=True) / (experts * part))
        grad_gate = []
        for k in range(2):
            along = jnp.sum(acc[1 + k, at], axis=1, keepdims=True)
            grad_gate.append(inv * along - shrink * fact[:, k : k + 1])
        gates = [fact[:, 3 + k : 4 + k] for k in range(2)]
        mean = gates[0] * grad_gate[0] + gates[1] * grad_gate[1]
        choice = jnp.zeros((SEQ, 128), F32)
        for k in range(2):
            chosen = gates[k] * (grad_gate[k] - mean)
            route = fact[:, 5 + k : 6 + k].astype(I32)
            choice = choice + jnp.where(route == lanes, chosen, 0.0)
        choices.append(choice)
        choice = jnp.where(lanes == experts, inv, choice)
        state[at] = jnp.where(lanes == experts + 1, shrink, choice)
    saved = [
        pltpu.make_async_copy(state, state_out, out_sems.at[0]),
        pltpu.make_async_copy(weighted, weighted_out, out_sems.at[1]),
    ]
    for copy in saved:
        copy.start()
    lhs = jnp.transpose(jnp.concatenate(choices, axis=0))[:experts].astype(BF16)
    tiles = part // 128
    for e in range(experts):
        loads[e][2].wait()
        block = jnp.dot(lhs, tok[e], preferred_element_type=F32)
        for k in range(tiles):
            at = experts * (tiles * e + k)
            part_out[at : at + experts, :] = block[:, 128 * k : 128 * (k + 1)]
    for copy in saved:
        copy.wait()


def token_kernel(experts, summed, weighted, state, router, out):
    rows = summed.shape[0]
    known = state[...]
    choice = jnp.where(iota(known.shape, 1) < experts, known, 0.0).astype(BF16)
    through = jnp.dot(choice, router[...], preferred_element_type=F32)
    for q in range(rows // SEQ):
        at = slice(SEQ * q, SEQ * (q + 1))
        inverse, shrink = known[at, experts : experts + 1], known[at, experts + 1 : experts + 2]
        x = inverse * weighted[q : q + 1, :] - shrink * summed[at]
        out[at] = (x + through[SEQ * q : SEQ * (q + 1)]).astype(BF16)


def token_rows(summed, weighted, state, router, experts):
    rows, width = summed.shape
    part = width // experts
    split = lambda count: pl.BlockSpec((count, part), lambda i: (0, i))
    return pl.pallas_call(
        functools.partial(token_kernel, experts),
        grid=(experts,),
        in_specs=[
            split(rows),
            split(weighted.shape[0]),
            pl.BlockSpec((rows, 128), lambda i: (0, 0)),
            split(128),
        ],
        out_specs=split(rows),
        out_shape=jax.ShapeDtypeStruct((rows, width), BF16),
        compiler_params=params(10),
        cost_estimate=cost(2 * rows * 128 * width, 5 << 20),
    )(*in_hbm(summed, weighted, state), router)


def expert_kernel(place, grads, gain, notes, *rest):
    *sources, out, backs, sems = rest
    experts = len(sources)
    _, _, part = grads.shape
    step = pl.program_id(0)
    source = lax.rem(place[0] + experts - step, experts)
    gate, inv, seq = notes[0, :, 0:1], notes[0, :, 1:2], notes[0, :, 2:3]
    capacity = gate.shape[0]
    loads = [pltpu.make_async_copy(sources[r], backs.at[r], sems.at[r]) for r in range(experts)]

    @pl.when(step == 0)
    def _():
        for load in loads:
            load.start()

    for r in range(experts):

        @pl.when(step == r)
        def _():
            loads[r].wait()
            back = backs.at[r]
            acc = jnp.zeros((capacity, 128), F32)
            rows = []
            for e in range(experts):
                cols = slice(part * e, part * (e + 1))
                w = rows_of(grads, e, source) * (gain[:, cols] / SEQ)
                x = jnp.broadcast_to(w[0:1], (capacity, part))
                for s in range(1, ROWS_DEV):
                    x = jnp.where(seq == s, w[s : s + 1], x)
                rows.append(w)
                acc = acc + fold(x * back[:, cols].astype(F32))
            shrink = inv * inv * inv * (jnp.sum(acc, axis=1, keepdims=True) / (experts * part))
            for e in range(experts):
                cols = slice(part * e, part * (e + 1))
                w = rows[e]
                x = jnp.broadcast_to(w[0:1], (capacity, part))
                for s in range(1, ROWS_DEV):
                    x = jnp.where(seq == s, w[s : s + 1], x)
                x = gate * (inv * x - shrink * back[:, cols].astype(F32))
                out[0, :, cols] = x.astype(BF16)


def expert_rows(place, grads, gain, notes, backs):
    experts, capacity = notes.shape[:2]
    width = gain.shape[1]
    whole = lambda shape: pl.BlockSpec(shape, lambda i, p: (0,) * len(shape))
    source = lambda i, p: (lax.rem(p[0] + experts - i, experts), 0, 0)
    return pl.pallas_call(
        expert_kernel,
        grid_spec=pltpu.PrefetchScalarGridSpec(
            num_scalar_prefetch=1,
            grid=(experts,),
            in_specs=[
                whole(grads.shape),
                whole((1, width)),
                pl.BlockSpec((1, capacity, notes.shape[2]), source),
            ]
            + [HBM] * experts,
            out_specs=pl.BlockSpec((1, capacity, width), source),
            scratch_shapes=[
                pltpu.VMEM((experts, capacity, width), BF16),
                pltpu.SemaphoreType.DMA((experts,)),
            ],
        ),
        out_shape=jax.ShapeDtypeStruct((experts, capacity, width), BF16),
        compiler_params=params(16),
        cost_estimate=cost(12 * experts * capacity * width, 9 << 20),
    )(place, grads, gain, notes, *in_hbm(*backs))


def shards(tokens, routes, positives, expert_out, router, norm_gain, loss_scale):
    experts, capacity, width = expert_out.shape[2:]
    rows = tokens.shape[0]
    slots = experts * capacity
    outer = lax.axis_size("u")
    mine = lax.axis_index("expert").astype(I32)
    mine_at = mine[None]
    part = width // experts
    group = PAIR_DEV * experts
    pairs = group * outer * CORES
    scale = 4.0 / math.sqrt(width)
    gain = norm_gain[None, :]
    columns = outer * experts * ROWS_DEV

    received = exchange(expert_out.reshape(experts, capacity, width), "expert").reshape(slots, width)
    gates, slot = routing(tokens, routes, router, experts, capacity)
    lane = jnp.arange(columns, dtype=I32)
    spread_positive = jnp.where(
        (lane % (2 * group)) // ROWS_DEV == mine,
        jnp.where(lane % ROWS_DEV == 0, positives[0], positives[1]) * (lane % ROWS_DEV < PAIR_DEV),
        0,
    ).astype(F32)

    summed, sliced, inverse = forward(tokens, received, slot, gates, gain, experts)
    own = exchange(sliced, "expert").reshape(2 * group, part)
    facts = jnp.concatenate(
        [jnp.zeros((rows, 2), F32), inverse, gates, routes.astype(F32)], axis=1
    )
    facts = jnp.pad(facts, ((0, 0), (0, 128 - facts.shape[1])))
    backs = list(pack(mine_at, summed, slot.T, experts, capacity))

    def move(after, turns):
        after, *ready = lax.optimization_barrier((after, *[backs[r] for r in turns]))
        for r, x in zip(turns, ready):
            backs[r] = lax.ppermute(x, "expert", [(i, (i + r) % experts) for i in range(experts)])
        return after


    def landed(value, turns):
        value, *done = lax.optimization_barrier((value, *[backs[r] for r in turns]))
        for r, x in zip(turns, done):
            backs[r] = x
        return value

    slot_ids = jnp.arange(slots, dtype=I32)[None, :]
    picks = [slot[:, k : k + 1] == slot_ids for k in range(2)]
    gate_slot = jnp.sum(
        jnp.where(picks[0], gates[:, 0:1], 0.0) + jnp.where(picks[1], gates[:, 1:2], 0.0), axis=0
    )
    taken = picks[0] | picks[1]
    inverse_slot = jnp.sum(jnp.where(taken, inverse, 0.0), axis=0)
    sequence = (jnp.arange(rows, dtype=I32) // SEQ).astype(F32)
    sequence_slot = jnp.sum(jnp.where(taken, sequence[:, None], 0.0), axis=0)
    notes = jnp.stack([gate_slot, inverse_slot, sequence_slot, spread_positive])
    notes = jnp.pad(notes, ((0, 4), (0, 0)))

    own, *backs = lax.optimization_barrier((own, *backs))
    own = move(own, TURNS[0])
    near = spread(own, "u", outer)
    far = swap_core(near)
    near, far = near.reshape(columns, part), far.reshape(columns, part)
    offered = pl.pallas_call(
        scores_kernel,
        in_specs=[VMEM] * 4,
        out_specs=HBM,
        out_shape=pltpu.HBM((experts, 2 * group + 8, columns), F32),
        scratch_shapes=[pltpu.VMEM((2 * group + 8, columns), F32), pltpu.SemaphoreType.DMA((experts,))],
        compiler_params=params(2),
    )(own, near, far, notes)
    offered = landed(offered, TURNS[0])
    offered = move(offered, TURNS[1])
    gathered = exchange(offered, "expert")
    devices = outer * CORES
    offered, kept = pl.pallas_call(
        functools.partial(totals_kernel, scale),
        in_specs=[VMEM],
        out_specs=[HBM] * 2,
        out_shape=[pltpu.HBM((devices, 8, 128), F32), pltpu.HBM((3 * group, columns), F32)],
        scratch_shapes=[
            pltpu.VMEM((3 * group, columns), F32),
            pltpu.VMEM((devices, 8, 128), F32),
            pltpu.SemaphoreType.DMA(()),
            pltpu.SemaphoreType.DMA(()),
        ],
        compiler_params=params(2),
    )(gathered)
    offered = move(offered, TURNS[2])
    heard = exchange(offered, ("u", "c"))
    heard = landed(heard, TURNS[1])
    facts, fetched = overlaps(summed, received, slot, facts, experts)
    heard, facts = lax.optimization_barrier((heard, facts))
    offered, loss = pl.pallas_call(
        functools.partial(gradient_kernel, scale),
        in_specs=[SMEM] + [VMEM] * 4,
        out_specs=[HBM, VMEM],
        out_shape=[pltpu.HBM((experts, 2 * group, part), BF16), jax.ShapeDtypeStruct((1, 1), F32)],
        scratch_shapes=[pltpu.VMEM((2 * group, part), BF16), pltpu.SemaphoreType.DMA((experts,))],
        compiler_params=params(2),
    )((loss_scale / pairs)[None], heard, kept, near, far)
    offered = move(offered, TURNS[3])
    grads = exchange(offered, "expert")
    grads = landed(grads, TURNS[2])

    router_part, state, weighted = pl.pallas_call(
        router_kernel,
        in_specs=[VMEM] * 2 + [HBM] * 4,
        out_specs=[VMEM, HBM, HBM],
        out_shape=[
            jax.ShapeDtypeStruct((width * experts // 128, 128), F32),
            pltpu.HBM((rows, 128), F32),
            pltpu.HBM((rows // SEQ, width), F32),
        ],
        scratch_shapes=[
            pltpu.VMEM((experts, rows, part), F32),
            pltpu.VMEM((experts, 2 * rows, part), BF16),
            pltpu.VMEM((experts, rows, part), BF16),
            pltpu.VMEM((rows, 128), F32),
            pltpu.VMEM((rows, 128), F32),
            pltpu.VMEM((rows // SEQ, width), F32),
            pltpu.VMEM((3, rows, 128), F32),
            pltpu.SemaphoreType.DMA((3, experts)),
            pltpu.SemaphoreType.DMA(()),
            pltpu.SemaphoreType.DMA((2,)),
        ],
        compiler_params=params(16),
    )(grads, gain, *in_hbm(summed, fetched, tokens, facts))
    router_part = exchange(router_part.reshape(outer, -1, 128), "u")
    router_part = jnp.sum(router_part, axis=0)
    router_part = spread(router_part, ("c", "expert"), CORES * experts)
    held = lax.dynamic_slice_in_dim(gathered[:, 2 * group : 2 * group + 3], mine * capacity, capacity, axis=2)
    held = jnp.pad(jnp.transpose(held, (0, 2, 1)), ((0, 0), (0, 0), (0, 5)))
    expert_grad = expert_rows(mine_at, grads, gain, held, backs)
    turned = jnp.pad(router.T, ((0, 128 - experts), (0, 0)))
    router_part, expert_grad = lax.optimization_barrier((router_part, expert_grad))
    router_part = jnp.sum(router_part, axis=0)
    token_grad = token_rows(summed, weighted, state, turned, experts)
    router_all = spread(router_part, "u", outer)
    router_all, token_grad = lax.optimization_barrier((router_all, token_grad))
    router_grad = router_all.reshape(-1, experts, 128).transpose(1, 0, 2).reshape(experts, width).T
    return token_grad, expert_grad.reshape(1, 1, experts, capacity, width), router_grad, loss[0, 0] / pairs


def solution(mesh):
    outer = mesh.shape["dp"] // CORES
    fine = Mesh(mesh.devices.reshape(outer, CORES, mesh.shape["expert"]), ("u", "c", "expert"))
    everywhere = ("u", "c", "expert")
    return jax.shard_map(
        shards,
        mesh=fine,
        in_specs=(
            P(everywhere, None),
            P(everywhere, None),
            P(everywhere),
            P(("u", "c"), "expert", None, None, None),
            P(),
            P(),
            P(),
        ),
        out_specs=(P(everywhere, None), P(("u", "c"), "expert", None, None, None), P(), P()),
        check_vma=False,
    )
```

```python
import functools
import math

import jax
import jax.numpy as jnp
from jax import lax
from jax.experimental import pallas as pl
from jax.experimental.pallas import tpu as pltpu
from jax.sharding import Mesh, PartitionSpec as P

PAIR_DEV = 2
SEQ = 48
EPS = 1e-05
CORES = 2
ROWS_DEV = 2 * PAIR_DEV
F32 = jnp.float32
BF16 = jnp.bfloat16
I32 = jnp.int32
VMEM = pl.BlockSpec(memory_space=pltpu.VMEM)
SMEM = pl.BlockSpec(memory_space=pltpu.SMEM)
HBM = pl.BlockSpec(memory_space=pltpu.HBM)
NT = (((1,), (1,)), ((), ()))
TURNS = ((4, 1, 7), (3, 5), (2, 6))
SHARED = 6


def iota(shape, dim):
    return lax.broadcasted_iota(I32, shape, dim)


def params(mib):
    return pltpu.CompilerParams(vmem_limit_bytes=mib << 20)


def cost(flops, moved):
    return pl.CostEstimate(flops=flops, bytes_accessed=moved, transcendentals=0)


def fold(x):
    total = x[:, :128]
    for k in range(1, x.shape[1] // 128):
        total = total + x[:, 128 * k : 128 * (k + 1)]
    return total


def in_hbm(*arrays):
    return [pltpu.with_memory_space_constraint(x, pltpu.HBM) for x in arrays]


def copy_all(copies):
    for copy in copies:
        copy.start()
    for copy in copies:
        copy.wait()


def to_each(source, target, sems):
    copy_all([pltpu.make_async_copy(source, target.at[i], sems.at[i]) for i in range(target.shape[0])])


def swap_core(x):
    return lax.ppermute(x, "c", [(0, 1), (1, 0)])


def exchange(x, axes):
    return lax.all_to_all(x, axes, split_axis=0, concat_axis=0, tiled=True)


def spread(x, axes, size):
    return exchange(jnp.broadcast_to(x[None], (size,) + x.shape), axes)


def routing(tokens, routes, router, experts, capacity):
    logits = jnp.dot(tokens, router, preferred_element_type=F32)
    lanes = jnp.arange(experts, dtype=I32)[None, None, :]
    one_hot = (routes[:, :, None] == lanes).astype(F32)
    chosen = jnp.sum(one_hot * logits[:, None, :], axis=2)
    gates = jax.nn.softmax(chosen, axis=1)
    rows = routes.shape[0]
    hits = jnp.sum(one_hot, axis=1)
    order = jnp.arange(rows, dtype=I32)
    earlier = (order[None, :] < order[:, None]).astype(BF16)
    before = jnp.dot(earlier, hits.astype(BF16), preferred_element_type=F32)
    rank = jnp.sum(one_hot * before[:, None, :], axis=2).astype(I32)
    return gates, routes * capacity + rank


def one_hots(slot, slots):
    ids = iota((slot.shape[0], slots), 1)
    return jnp.concatenate([(slot[:, k : k + 1] == ids).astype(BF16) for k in range(2)], axis=0)


def forward_kernel(
    steps, tok, rec, slot, gate, gain, summed, sliced_out, rows_out, inverse,
    held, square, picks, sliced, rounded, row_sem, slice_sem, rounded_sem
):
    step = pl.program_id(0)
    rows, part = tok.shape

    def keep(e):
        start = pl.multiple_of(e * part, part)
        return pltpu.make_async_copy(held.at[e], summed.at[:, pl.ds(start, part)], row_sem.at[e])

    shared = rounded.shape[0]

    def share(e):
        start = pl.multiple_of(e * part, part)
        return pltpu.make_async_copy(rounded.at[e], rows_out.at[:, pl.ds(start, part)], rounded_sem.at[e])

    @pl.when(step == 0)
    def _():
        square[...] = jnp.zeros_like(square)
        picks[...] = one_hots(slot, rec.shape[0])

    for k in range(part // 256):
        cols = slice(256 * k, 256 * (k + 1))
        both = jnp.dot(picks[...], rec[:, cols], preferred_element_type=F32)
        x = tok[:, cols].astype(F32) + gate[:, 0:1] * both[:rows] + gate[:, 1:2] * both[rows:]
        held[step, :, cols] = x
        square[...] += fold(x * x)
    keep(step).start()

    @pl.when(step < shared)
    def _():
        rounded[step] = held[step].astype(BF16)
        share(step).start()

    @pl.when(step == steps - 1)
    def _():
        mean = jnp.sum(square[...], axis=1, keepdims=True) / (steps * part)
        scale = lax.rsqrt(mean + EPS)
        inverse[...] = scale
        count = rows // SEQ
        for e in range(steps):
            x = held[e] * scale
            x = jnp.sum(x.reshape(count, SEQ, part), axis=1) / SEQ
            sliced[e] = (x * gain[:, part * e : part * (e + 1)]).astype(BF16)
        offer = pltpu.make_async_copy(sliced, sliced_out, slice_sem)
        offer.start()
        for e in range(steps):
            keep(e).wait()
        for e in range(shared):
            share(e).wait()
        offer.wait()


def forward(tokens, received, slot, gates, gain, experts):
    rows, width = tokens.shape
    slots = received.shape[0]
    part = width // experts
    whole = lambda shape: pl.BlockSpec(shape, lambda i: (0,) * len(shape))
    return pl.pallas_call(
        functools.partial(forward_kernel, experts),
        grid=(experts,),
        in_specs=[
            pl.BlockSpec((rows, part), lambda i: (0, i)),
            pl.BlockSpec((slots, part), lambda i: (0, i)),
            whole((rows, 2)),
            whole((rows, 2)),
            whole((1, width)),
        ],
        out_specs=[HBM, HBM, HBM, whole((rows, 1))],
        out_shape=[
            pltpu.HBM((rows, width), F32),
            pltpu.HBM((experts, rows // SEQ, part), BF16),
            pltpu.HBM((rows, SHARED * part), BF16),
            jax.ShapeDtypeStruct((rows, 1), F32),
        ],
        scratch_shapes=[
            pltpu.VMEM((experts, rows, part), F32),
            pltpu.VMEM((rows, 128), F32),
            pltpu.VMEM((2 * rows, slots), BF16),
            pltpu.VMEM((experts, rows // SEQ, part), BF16),
            pltpu.VMEM((SHARED, rows, part), BF16),
            pltpu.SemaphoreType.DMA((experts,)),
            pltpu.SemaphoreType.DMA(()),
            pltpu.SemaphoreType.DMA((SHARED,)),
        ],
        compiler_params=params(16),
        cost_estimate=cost(4 * rows * slots * width, 10 << 20),
    )(tokens, received, slot, gates, gain)


def pack_kernel(place, x, turned, *rest):
    *outs, spot, packed, sems = rest
    step, steps = pl.program_id(0), packed.shape[0]
    rows, part = x.shape
    capacity = outs[0].shape[0]
    slots = spot.shape[0]

    def leave(e, i):
        start = pl.multiple_of(e * part, part)
        return pltpu.make_async_copy(
            packed.at[e, pl.ds(i * capacity, capacity)], outs[i].at[:, pl.ds(start, part)], sems.at[e, i]
        )

    @pl.when(step == 0)
    def _():
        target = lax.rem(iota((slots, rows), 0) + place[0] * capacity, slots)
        spot[...] = ((turned[0:1, :] == target) | (turned[1:2, :] == target)).astype(BF16)

    for k in range(part // 512):
        cols = slice(512 * k, 512 * (k + 1))
        packed[step, :, cols] = jnp.dot(
            spot[...], x[:, cols].astype(BF16), preferred_element_type=F32
        ).astype(BF16)
    for i in range(len(outs)):
        leave(step, i).start()

    @pl.when(step == steps - 1)
    def _():
        for e in range(steps):
            for i in range(len(outs)):
                leave(e, i).wait()


def pack(place, summed, turned, experts, capacity):
    rows, width = summed.shape
    part = width // experts
    steps = experts - SHARED
    slots = experts * capacity
    return pl.pallas_call(
        pack_kernel,
        grid=(steps,),
        in_specs=[
            SMEM,
            pl.BlockSpec((rows, part), lambda i: (0, i + SHARED)),
            pl.BlockSpec((2, rows), lambda i: (0, 0)),
        ],
        out_specs=[HBM] * experts,
        out_shape=[pltpu.HBM((capacity, steps * part), BF16)] * experts,
        scratch_shapes=[
            pltpu.VMEM((slots, rows), BF16),
            pltpu.VMEM((steps, slots, part), BF16),
            pltpu.SemaphoreType.DMA((steps, experts)),
        ],
        compiler_params=params(14),
        cost_estimate=cost(2 * rows * slots * steps * part, 2 << 20),
    )(place, *in_hbm(summed), turned)


def overlap_kernel(steps, x, rec, slot, facts, out, fetched, picks, dots):
    step = pl.program_id(0)
    rows, part = x.shape

    @pl.when(step == 0)
    def _():
        dots[...] = jnp.zeros_like(dots)
        picks[...] = one_hots(slot, rec.shape[0])

    for k in range(part // 256):
        cols = slice(256 * k, 256 * (k + 1))
        both = jnp.dot(picks[...], rec[:, cols], preferred_element_type=F32)
        fetched[:, cols] = both.astype(BF16)
        value = x[:, cols]
        dots[:rows] += fold(value * both[:rows])
        dots[rows:] += fold(value * both[rows:])

    @pl.when(step == steps - 1)
    def _():
        lane = iota((rows, 128), 1)
        known = facts[...]
        for k in range(2):
            total = jnp.sum(dots[rows * k : rows * (k + 1)], axis=1, keepdims=True)
            known = jnp.where(lane == k, total, known)
        out[...] = known


def overlaps(summed, received, slot, facts, experts):
    rows, width = summed.shape
    slots = received.shape[0]
    part = width // experts
    whole = lambda shape: pl.BlockSpec(shape, lambda i: (0, 0))
    return pl.pallas_call(
        functools.partial(overlap_kernel, experts),
        grid=(experts,),
        in_specs=[
            pl.BlockSpec((rows, part), lambda i: (0, i)),
            pl.BlockSpec((slots, part), lambda i: (0, i)),
            whole((rows, 2)),
            whole((rows, 128)),
        ],
        out_specs=[whole((rows, 128)), pl.BlockSpec((2 * rows, part), lambda i: (0, i))],
        out_shape=[pltpu.HBM((rows, 128), F32), pltpu.HBM((2 * rows, width), BF16)],
        scratch_shapes=[pltpu.VMEM((2 * rows, slots), BF16), pltpu.VMEM((2 * rows, 128), F32)],
        compiler_params=params(12),
        cost_estimate=cost(4 * rows * slots * width, 10 << 20),
    )(*in_hbm(summed, received), slot, facts)


def lanes_of(shape, dim):
    lane = iota(shape, dim)
    kind = lax.rem(lane, ROWS_DEV)
    return lane, kind, kind >= PAIR_DEV


def picker(group, kind, turned=False):
    wide = 2 * group
    shape, pair, row = ((wide, group), 1, 0) if turned else ((group, wide), 0, 1)
    a = iota(shape, pair)
    b = iota(shape, row)
    source = (a // PAIR_DEV) * ROWS_DEV + lax.rem(a, PAIR_DEV) + PAIR_DEV * kind
    return (source == b).astype(BF16)


def scores_kernel(own, near, far, notes, offered, whole, sems):
    experts, total, columns = offered.shape
    group = experts * PAIR_DEV
    queries, records = [
        jnp.dot(picker(group, kind), own[...], preferred_element_type=F32).astype(BF16) for kind in (0, 1)
    ]
    at_record = lanes_of((group, columns), 1)[2]
    for k, side in enumerate((near, far)):
        every = side[...]
        by_query = lax.dot_general(queries, every, NT, preferred_element_type=F32)
        by_record = lax.dot_general(records, every, NT, preferred_element_type=F32)
        whole[group * k : group * (k + 1)] = jnp.where(at_record, by_query, by_record)
    whole[2 * group :] = notes[...]
    to_each(whole, offered, sems)


def totals_kernel(scale, gathered, offered, kept_out, kept, spread, kept_sem, sem):
    place, core = lax.axis_index("u"), lax.axis_index("c")
    experts, total, columns = gathered.shape
    group = experts * PAIR_DEV
    both = gathered[0]
    for e in range(1, experts):
        both = both + gathered[e]
    positive_lane = both[2 * group + 3 : 2 * group + 4, :]
    near, far = both[:group] * scale, both[group : 2 * group] * scale
    kept[0:group] = near
    kept[group : 2 * group] = far

    shape = (group, columns)
    lane, kind, at_record = lanes_of(shape, 1)
    pair = iota(shape, 0)
    within = lax.rem(lane, 2 * group)
    matching = (within // ROWS_DEV == pair // PAIR_DEV) & (kind == lax.rem(pair, PAIR_DEV))
    here = matching & (lane // (2 * group) == place)
    positive = jnp.sum(jnp.where(here, positive_lane, 0.0), axis=1, keepdims=True)

    low = jnp.float32(-jnp.inf)
    near_records = jnp.where(at_record, near, low)
    far_records = jnp.where(at_record, far, low)
    highest = jnp.maximum(
        jnp.max(near_records, axis=1, keepdims=True), jnp.max(far_records, axis=1, keepdims=True)
    )
    weight = jnp.sum(jnp.exp(near_records - highest), axis=1, keepdims=True) + jnp.sum(
        jnp.exp(far_records - highest), axis=1, keepdims=True
    )
    log_total = highest + jnp.log(weight)
    chosen = jnp.zeros((group, 1), F32)
    for side, where in ((near, core), (far, 1 - core)):
        name = column_names(lane, kind, group, where)
        hit = at_record & (name.astype(F32) == positive)
        chosen = chosen + jnp.sum(jnp.where(hit, side, 0.0), axis=1, keepdims=True)
    kept[2 * group : 3 * group, :128] = jnp.broadcast_to(log_total, (group, 128))
    kept[2 * group : 3 * group, 128:256] = jnp.broadcast_to(positive, (group, 128))
    saved = pltpu.make_async_copy(kept, kept_out, kept_sem)
    saved.start()
    row_loss = log_total - chosen

    total_lane = jnp.sum(jnp.where(here, log_total, 0.0), axis=0, keepdims=True)
    loss_lane = jnp.sum(jnp.where(here, row_loss, 0.0), axis=0, keepdims=True)
    own_lane = jnp.where(lane[0:1] // (2 * group) == place, positive_lane, 0.0)
    pieces = [x[:, 128 * k : 128 * (k + 1)] for x in (total_lane, own_lane) for k in range(columns // 128)]
    loss_pieces = [
        pltpu.roll(loss_lane, PAIR_DEV, 1)[:, 128 * k : 128 * (k + 1)] for k in range(columns // 128)
    ]
    pieces = [a + b for a, b in zip(pieces, loss_pieces)] + pieces[columns // 128 :]
    message = jnp.concatenate(pieces, axis=0)
    for d in range(spread.shape[0]):
        spread[d] = message
    copy_all([pltpu.make_async_copy(spread, offered, sem)])
    saved.wait()


def column_names(lane, kind, group, core):
    wide = 2 * group
    block = (lane // wide) * CORES + core
    return block * group + (lax.rem(lane, wide) // ROWS_DEV) * PAIR_DEV + lax.rem(kind, PAIR_DEV)


def gradient_kernel(scale, factor, heard, kept, near, far, offered, loss, whole, sems):
    place, core = lax.axis_index("u"), lax.axis_index("c")
    experts, wide, columns = offered.shape
    group = wide // 2
    outer_size = heard.shape[0] // CORES
    pieces = columns // 128
    shape = (group, columns)
    lane, kind, at_record = lanes_of(shape, 1)
    pair = iota(shape, 0)
    own_name = (place * CORES + core) * group + iota((group, 1), 0)
    own_total = kept[2 * group : 3 * group, 0:1]
    own_positive = kept[2 * group : 3 * group, 128:129]
    result = jnp.zeros((wide, columns), F32)
    losses = jnp.zeros((1, columns), F32)
    for k, (side, where) in enumerate(((near, core), (far, 1 - core))):
        told = heard[where]
        for u in range(1, outer_size):
            told = told + heard[u * CORES + where]
        total = jnp.concatenate([told[i : i + 1] for i in range(pieces)], axis=1)
        positive = jnp.concatenate([told[pieces + i : pieces + i + 1] for i in range(pieces)], axis=1)
        losses = losses + jnp.where(at_record[0:1], total, 0.0)
        value = kept[group * k : group * (k + 1), :]
        name = column_names(lane, kind, group, where).astype(F32)
        hit = jnp.where(name == own_positive, 1.0, 0.0)
        by_query = (jnp.exp(value - own_total) - hit) * factor[0]
        by_query = jnp.where(at_record, by_query, 0.0).astype(BF16)
        hit = jnp.where(positive == own_name.astype(F32), 1.0, 0.0)
        by_record = (jnp.exp(jnp.where(at_record, 0.0, value - total)) - hit) * factor[0]
        by_record = jnp.where(at_record, 0.0, by_record).astype(BF16)
        rows = jnp.dot(picker(group, 0, True), by_query, preferred_element_type=F32) + jnp.dot(
            picker(group, 1, True), by_record, preferred_element_type=F32
        )
        result = result + jnp.dot(rows.astype(BF16), side[...], preferred_element_type=F32)
    whole[...] = (result * scale).astype(BF16)
    to_each(whole, offered, sems)
    loss[...] = jnp.sum(losses, axis=1, keepdims=True)


def rows_of(grads, e, index):
    tile = grads[e, pl.ds(pl.multiple_of((index // 4) * 16, 16), 16), :].astype(F32)
    piece = lax.rem(index, 4)
    quarters = [tile[ROWS_DEV * k : ROWS_DEV * (k + 1)] for k in range(4)]
    half = jnp.where(piece < 2, quarters[0], quarters[2]), jnp.where(piece < 2, quarters[1], quarters[3])
    return jnp.where(lax.rem(piece, 2) == 0, half[0], half[1])


def router_kernel(
    grads, gain, summed_in, fetched_in, tok_in, facts_in, part_out, state_out, weighted_out,
    summed, fetched, tok, facts, state, weighted, acc, sems, facts_sem, out_sems
):
    experts, _, part = grads.shape
    rows = summed.shape[1]
    count = rows // SEQ
    sources = ((summed_in, summed), (fetched_in, fetched), (tok_in, tok))

    def load(e):
        cols = pl.ds(e * part, part)
        return [
            pltpu.make_async_copy(a.at[:, cols], b.at[e], sems.at[k, e]) for k, (a, b) in enumerate(sources)
        ]

    known = pltpu.make_async_copy(facts_in, facts, facts_sem)
    loads = [load(e) for e in range(experts)]
    for e in range(experts):
        loads[e][0].start()
        loads[e][1].start()
    known.start()
    for e in range(experts):
        loads[e][2].start()

    for e in range(experts):
        cols = slice(part * e, part * (e + 1))
        w = rows_of(grads, e, lax.axis_index("expert")) * (gain[:, cols] / SEQ)
        weighted[:, cols] = w
        loads[e][0].wait()
        loads[e][1].wait()
        for q in range(count):
            row = w[q : q + 1, :]
            at = [slice(rows * k + SEQ * q, rows * k + SEQ * (q + 1)) for k in range(2)]
            terms = [summed[e, at[0], :], fetched[e, at[0], :].astype(F32), fetched[e, at[1], :].astype(F32)]
            for k, term in enumerate(terms):
                total = fold(term * row)
                spot = slice(SEQ * q, SEQ * (q + 1))
                acc[k, spot] = total if e == 0 else acc[k, spot] + total
    known.wait()
    lanes = iota((SEQ, 128), 1)
    choices = []
    for q in range(count):
        at = slice(SEQ * q, SEQ * (q + 1))
        fact = facts[at, :]
        inv = fact[:, 2:3]
        shrink = inv * inv * inv * (jnp.sum(acc[0, at], axis=1, keepdims=True) / (experts * part))
        grad_gate = []
        for k in range(2):
            along = jnp.sum(acc[1 + k, at], axis=1, keepdims=True)
            grad_gate.append(inv * along - shrink * fact[:, k : k + 1])
        gates = [fact[:, 3 + k : 4 + k] for k in range(2)]
        mean = gates[0] * grad_gate[0] + gates[1] * grad_gate[1]
        choice = jnp.zeros((SEQ, 128), F32)
        for k in range(2):
            chosen = gates[k] * (grad_gate[k] - mean)
            route = fact[:, 5 + k : 6 + k].astype(I32)
            choice = choice + jnp.where(route == lanes, chosen, 0.0)
        choices.append(choice)
        choice = jnp.where(lanes == experts, inv, choice)
        state[at] = jnp.where(lanes == experts + 1, shrink, choice)
    saved = [
        pltpu.make_async_copy(state, state_out, out_sems.at[0]),
        pltpu.make_async_copy(weighted, weighted_out, out_sems.at[1]),
    ]
    for copy in saved:
        copy.start()
    lhs = jnp.transpose(jnp.concatenate(choices, axis=0))[:experts].astype(BF16)
    tiles = part // 128
    for e in range(experts):
        loads[e][2].wait()
        block = jnp.dot(lhs, tok[e], preferred_element_type=F32)
        for k in range(tiles):
            at = experts * (tiles * e + k)
            part_out[at : at + experts, :] = block[:, 128 * k : 128 * (k + 1)]
    for copy in saved:
        copy.wait()


def token_kernel(experts, summed, weighted, state, router, out):
    rows = summed.shape[0]
    known = state[...]
    choice = jnp.where(iota(known.shape, 1) < experts, known, 0.0).astype(BF16)
    through = jnp.dot(choice, router[...], preferred_element_type=F32)
    for q in range(rows // SEQ):
        at = slice(SEQ * q, SEQ * (q + 1))
        inverse, shrink = known[at, experts : experts + 1], known[at, experts + 1 : experts + 2]
        x = inverse * weighted[q : q + 1, :] - shrink * summed[at]
        out[at] = (x + through[SEQ * q : SEQ * (q + 1)]).astype(BF16)


def token_rows(summed, weighted, state, router, experts):
    rows, width = summed.shape
    part = width // experts
    split = lambda count: pl.BlockSpec((count, part), lambda i: (0, i))
    return pl.pallas_call(
        functools.partial(token_kernel, experts),
        grid=(experts,),
        in_specs=[
            split(rows),
            split(weighted.shape[0]),
            pl.BlockSpec((rows, 128), lambda i: (0, 0)),
            split(128),
        ],
        out_specs=split(rows),
        out_shape=jax.ShapeDtypeStruct((rows, width), BF16),
        compiler_params=params(10),
        cost_estimate=cost(2 * rows * 128 * width, 5 << 20),
    )(*in_hbm(summed, weighted, state), router)


def expert_kernel(place, grads, gain, notes, shared_in, *rest):
    *sources, out, backs, shared, row, sems, shared_sems = rest
    experts = len(sources)
    _, _, part = grads.shape
    step = pl.program_id(0)
    rows = shared.shape[1]
    capacity = row.shape[0]
    split = shared.shape[2] // part
    gate, inv, token = notes[0, :, 0:1], notes[0, :, 1:2], notes[0, :, 2:3]

    def origin(r):
        return lax.rem(place[0] + experts - r, experts)

    def load(r):
        start = pl.multiple_of(origin(r) * rows, rows)
        return [
            pltpu.make_async_copy(shared_in.at[pl.ds(start, rows)], shared.at[r], shared_sems.at[r]),
            pltpu.make_async_copy(sources[r], backs.at[r], sems.at[r]),
        ]

    @pl.when(step == 0)
    def _():
        for r in range(experts):
            for copy in load(r):
                copy.start()

    for r in range(experts):

        @pl.when(step == r)
        def _():
            for copy in load(r):
                copy.wait()

    pick = (token.astype(I32) == iota((capacity, rows), 1)).astype(BF16)
    acc = jnp.zeros((capacity, 128), F32)

    def gradient_rows(e):
        cols = slice(part * e, part * (e + 1))
        w = rows_of(grads, e, origin(step)) * (gain[:, cols] / SEQ)
        x = jnp.broadcast_to(w[0:1], (capacity, part))
        for s in range(1, ROWS_DEV):
            x = jnp.where(token >= s * SEQ, w[s : s + 1], x)
        return x

    for e in range(experts):
        cols = slice(part * e, part * (e + 1))
        if e < split:
            back = jnp.dot(pick, shared[step, :, cols], preferred_element_type=F32)
        else:
            back = backs[step, :, part * (e - split) : part * (e - split + 1)].astype(F32)
        row[:, cols] = back
        acc = acc + fold(gradient_rows(e) * back)
    shrink = inv * inv * inv * (jnp.sum(acc, axis=1, keepdims=True) / (experts * part))
    keep, drop = gate * inv, gate * shrink
    for e in range(experts):
        cols = slice(part * e, part * (e + 1))
        out[0, :, cols] = (keep * gradient_rows(e) - drop * row[:, cols]).astype(BF16)


def expert_rows(place, grads, gain, notes, shared, backs):
    experts, capacity = notes.shape[:2]
    width = gain.shape[1]
    rows = shared.shape[0] // experts
    whole = lambda shape: pl.BlockSpec(shape, lambda i, p: (0,) * len(shape))
    source = lambda i, p: (lax.rem(p[0] + experts - i, experts), 0, 0)
    return pl.pallas_call(
        expert_kernel,
        grid_spec=pltpu.PrefetchScalarGridSpec(
            num_scalar_prefetch=1,
            grid=(experts,),
            in_specs=[
                whole(grads.shape),
                whole((1, width)),
                pl.BlockSpec((1, capacity, notes.shape[2]), source),
            ]
            + [HBM] * (experts + 1),
            out_specs=pl.BlockSpec((1, capacity, width), source),
            scratch_shapes=[
                pltpu.VMEM((experts,) + backs[0].shape, BF16),
                pltpu.VMEM((experts, rows, shared.shape[1]), BF16),
                pltpu.VMEM((capacity, width), F32),
                pltpu.SemaphoreType.DMA((experts,)),
                pltpu.SemaphoreType.DMA((experts,)),
            ],
        ),
        out_shape=jax.ShapeDtypeStruct((experts, capacity, width), BF16),
        compiler_params=params(24),
        cost_estimate=cost(12 * experts * capacity * width, 15 << 20),
    )(place, grads, gain, notes, *in_hbm(shared, *backs))


def shards(tokens, routes, positives, expert_out, router, norm_gain, loss_scale):
    experts, capacity, width = expert_out.shape[2:]
    rows = tokens.shape[0]
    slots = experts * capacity
    outer = lax.axis_size("u")
    mine = lax.axis_index("expert").astype(I32)
    mine_at = mine[None]
    part = width // experts
    group = PAIR_DEV * experts
    pairs = group * outer * CORES
    scale = 4.0 / math.sqrt(width)
    gain = norm_gain[None, :]
    columns = outer * experts * ROWS_DEV

    received = exchange(expert_out.reshape(experts, capacity, width), "expert").reshape(slots, width)
    gates, slot = routing(tokens, routes, router, experts, capacity)
    lane = jnp.arange(columns, dtype=I32)
    spread_positive = jnp.where(
        (lane % (2 * group)) // ROWS_DEV == mine,
        jnp.where(lane % ROWS_DEV == 0, positives[0], positives[1]) * (lane % ROWS_DEV < PAIR_DEV),
        0,
    ).astype(F32)

    summed, sliced, rounded, inverse = forward(tokens, received, slot, gates, gain, experts)
    shared = lax.all_gather(rounded, "expert", axis=0, tiled=True)
    own = exchange(sliced, "expert").reshape(2 * group, part)
    facts = jnp.concatenate(
        [jnp.zeros((rows, 2), F32), inverse, gates, routes.astype(F32)], axis=1
    )
    facts = jnp.pad(facts, ((0, 0), (0, 128 - facts.shape[1])))
    backs = list(pack(mine_at, summed, slot.T, experts, capacity))

    def move(after, turns):
        after, *ready = lax.optimization_barrier((after, *[backs[r] for r in turns]))
        for r, x in zip(turns, ready):
            backs[r] = lax.ppermute(x, "expert", [(i, (i + r) % experts) for i in range(experts)])
        return after


    def landed(value, turns):
        value, *done = lax.optimization_barrier((value, *[backs[r] for r in turns]))
        for r, x in zip(turns, done):
            backs[r] = x
        return value

    slot_ids = jnp.arange(slots, dtype=I32)[None, :]
    picks = [slot[:, k : k + 1] == slot_ids for k in range(2)]
    gate_slot = jnp.sum(
        jnp.where(picks[0], gates[:, 0:1], 0.0) + jnp.where(picks[1], gates[:, 1:2], 0.0), axis=0
    )
    taken = picks[0] | picks[1]
    inverse_slot = jnp.sum(jnp.where(taken, inverse, 0.0), axis=0)
    order = jnp.arange(rows, dtype=I32).astype(F32)
    token_slot = jnp.sum(jnp.where(taken, order[:, None], 0.0), axis=0)
    notes = jnp.stack([gate_slot, inverse_slot, token_slot, spread_positive])
    notes = jnp.pad(notes, ((0, 4), (0, 0)))

    own, *backs = lax.optimization_barrier((own, *backs))
    near = spread(own, "u", outer)
    facts, fetched = overlaps(summed, received, slot, facts, experts)
    near, facts, fetched = lax.optimization_barrier((near, facts, fetched))
    far = swap_core(near)
    near, far = near.reshape(columns, part), far.reshape(columns, part)
    offered = pl.pallas_call(
        scores_kernel,
        in_specs=[VMEM] * 4,
        out_specs=HBM,
        out_shape=pltpu.HBM((experts, 2 * group + 8, columns), F32),
        scratch_shapes=[pltpu.VMEM((2 * group + 8, columns), F32), pltpu.SemaphoreType.DMA((experts,))],
        compiler_params=params(2),
    )(own, near, far, notes)
    offered = move(offered, TURNS[0])
    gathered = exchange(offered, "expert")
    gathered = landed(gathered, TURNS[0])
    devices = outer * CORES
    offered, kept = pl.pallas_call(
        functools.partial(totals_kernel, scale),
        in_specs=[VMEM],
        out_specs=[HBM] * 2,
        out_shape=[pltpu.HBM((devices, 8, 128), F32), pltpu.HBM((3 * group, columns), F32)],
        scratch_shapes=[
            pltpu.VMEM((3 * group, columns), F32),
            pltpu.VMEM((devices, 8, 128), F32),
            pltpu.SemaphoreType.DMA(()),
            pltpu.SemaphoreType.DMA(()),
        ],
        compiler_params=params(2),
    )(gathered)
    offered = move(offered, TURNS[1])
    heard = exchange(offered, ("u", "c"))
    heard = landed(heard, TURNS[1])
    offered, loss = pl.pallas_call(
        functools.partial(gradient_kernel, scale),
        in_specs=[SMEM] + [VMEM] * 4,
        out_specs=[HBM, VMEM],
        out_shape=[pltpu.HBM((experts, 2 * group, part), BF16), jax.ShapeDtypeStruct((1, 1), F32)],
        scratch_shapes=[pltpu.VMEM((2 * group, part), BF16), pltpu.SemaphoreType.DMA((experts,))],
        compiler_params=params(2),
    )((loss_scale / pairs)[None], heard, kept, near, far)
    offered = move(offered, TURNS[2])
    grads = exchange(offered, "expert")
    grads = landed(grads, TURNS[2])

    router_part, state, weighted = pl.pallas_call(
        router_kernel,
        in_specs=[VMEM] * 2 + [HBM] * 4,
        out_specs=[VMEM, HBM, HBM],
        out_shape=[
            jax.ShapeDtypeStruct((width * experts // 128, 128), F32),
            pltpu.HBM((rows, 128), F32),
            pltpu.HBM((rows // SEQ, width), F32),
        ],
        scratch_shapes=[
            pltpu.VMEM((experts, rows, part), F32),
            pltpu.VMEM((experts, 2 * rows, part), BF16),
            pltpu.VMEM((experts, rows, part), BF16),
            pltpu.VMEM((rows, 128), F32),
            pltpu.VMEM((rows, 128), F32),
            pltpu.VMEM((rows // SEQ, width), F32),
            pltpu.VMEM((3, rows, 128), F32),
            pltpu.SemaphoreType.DMA((3, experts)),
            pltpu.SemaphoreType.DMA(()),
            pltpu.SemaphoreType.DMA((2,)),
        ],
        compiler_params=params(16),
    )(grads, gain, *in_hbm(summed, fetched, tokens, facts))
    router_part = exchange(router_part.reshape(outer, -1, 128), "u")
    router_part = jnp.sum(router_part, axis=0)
    router_part = spread(router_part, ("c", "expert"), CORES * experts)
    held = lax.dynamic_slice_in_dim(gathered[:, 2 * group : 2 * group + 3], mine * capacity, capacity, axis=2)
    held = jnp.pad(jnp.transpose(held, (0, 2, 1)), ((0, 0), (0, 0), (0, 5)))
    turned = jnp.pad(router.T, ((0, 128 - experts), (0, 0)))
    token_grad = token_rows(summed, weighted, state, turned, experts)
    router_part, token_grad = lax.optimization_barrier((router_part, token_grad))
    router_part = jnp.sum(router_part, axis=0)
    router_all = spread(router_part, "u", outer)
    expert_grad = expert_rows(mine_at, grads, gain, held, shared, backs)
    router_all, expert_grad = lax.optimization_barrier((router_all, expert_grad))
    router_grad = router_all.reshape(-1, experts, 128).transpose(1, 0, 2).reshape(experts, width).T
    return token_grad, expert_grad.reshape(1, 1, experts, capacity, width), router_grad, loss[0, 0] / pairs


def solution(mesh):
    outer = mesh.shape["dp"] // CORES
    fine = Mesh(mesh.devices.reshape(outer, CORES, mesh.shape["expert"]), ("u", "c", "expert"))
    everywhere = ("u", "c", "expert")
    return jax.shard_map(
        shards,
        mesh=fine,
        in_specs=(
            P(everywhere, None),
            P(everywhere, None),
            P(everywhere),
            P(("u", "c"), "expert", None, None, None),
            P(),
            P(),
            P(),
        ),
        out_specs=(P(everywhere, None), P(("u", "c"), "expert", None, None, None), P(), P()),
        check_vma=False,
    )
```

```python
import functools
import math

import jax
import jax.numpy as jnp
from jax import lax
from jax.experimental import pallas as pl
from jax.experimental.pallas import tpu as pltpu
from jax.sharding import Mesh, PartitionSpec as P

PAIR_DEV = 2
SEQ = 48
EPS = 1e-05
CORES = 2
ROWS_DEV = 2 * PAIR_DEV
F32 = jnp.float32
BF16 = jnp.bfloat16
I32 = jnp.int32
VMEM = pl.BlockSpec(memory_space=pltpu.VMEM)
SMEM = pl.BlockSpec(memory_space=pltpu.SMEM)
HBM = pl.BlockSpec(memory_space=pltpu.HBM)
NT = (((1,), (1,)), ((), ()))
TURNS = ((4, 1, 7), (3, 5), (2, 6))


def iota(shape, dim):
    return lax.broadcasted_iota(I32, shape, dim)


def params(mib):
    return pltpu.CompilerParams(vmem_limit_bytes=mib << 20)


def cost(flops, moved):
    return pl.CostEstimate(flops=flops, bytes_accessed=moved, transcendentals=0)


def fold(x):
    total = x[:, :128]
    for k in range(1, x.shape[1] // 128):
        total = total + x[:, 128 * k : 128 * (k + 1)]
    return total


def in_hbm(*arrays):
    return [pltpu.with_memory_space_constraint(x, pltpu.HBM) for x in arrays]


def copy_all(copies):
    for copy in copies:
        copy.start()
    for copy in copies:
        copy.wait()


def to_each(source, target, sems):
    copy_all([pltpu.make_async_copy(source, target.at[i], sems.at[i]) for i in range(target.shape[0])])


def swap_core(x):
    return lax.ppermute(x, "c", [(0, 1), (1, 0)])


def exchange(x, axes):
    return lax.all_to_all(x, axes, split_axis=0, concat_axis=0, tiled=True)


def spread(x, axes, size):
    return exchange(jnp.broadcast_to(x[None], (size,) + x.shape), axes)


def routing(tokens, routes, router, experts, capacity):
    logits = jnp.dot(tokens, router, preferred_element_type=F32)
    lanes = jnp.arange(experts, dtype=I32)[None, None, :]
    one_hot = (routes[:, :, None] == lanes).astype(F32)
    chosen = jnp.sum(one_hot * logits[:, None, :], axis=2)
    gates = jax.nn.softmax(chosen, axis=1)
    rows = routes.shape[0]
    hits = jnp.sum(one_hot, axis=1)
    order = jnp.arange(rows, dtype=I32)
    earlier = (order[None, :] < order[:, None]).astype(BF16)
    before = jnp.dot(earlier, hits.astype(BF16), preferred_element_type=F32)
    rank = jnp.sum(one_hot * before[:, None, :], axis=2).astype(I32)
    return gates, routes * capacity + rank


def one_hots(slot, slots):
    ids = iota((slot.shape[0], slots), 1)
    return jnp.concatenate([(slot[:, k : k + 1] == ids).astype(BF16) for k in range(2)], axis=0)


def forward_kernel(
    steps, tok, rec, slot, gate, gain, summed, sliced_out, inverse, held, square, picks, sliced, row_sem, slice_sem
):
    step = pl.program_id(0)
    rows, part = tok.shape

    def keep(e):
        start = pl.multiple_of(e * part, part)
        return pltpu.make_async_copy(held.at[e], summed.at[:, pl.ds(start, part)], row_sem.at[e])

    @pl.when(step == 0)
    def _():
        square[...] = jnp.zeros_like(square)
        picks[...] = one_hots(slot, rec.shape[0])

    for k in range(part // 256):
        cols = slice(256 * k, 256 * (k + 1))
        both = jnp.dot(picks[...], rec[:, cols], preferred_element_type=F32)
        x = tok[:, cols].astype(F32) + gate[:, 0:1] * both[:rows] + gate[:, 1:2] * both[rows:]
        held[step, :, cols] = x
        square[...] += fold(x * x)
    keep(step).start()

    @pl.when(step == steps - 1)
    def _():
        mean = jnp.sum(square[...], axis=1, keepdims=True) / (steps * part)
        scale = lax.rsqrt(mean + EPS)
        inverse[...] = scale
        count = rows // SEQ
        for e in range(steps):
            x = held[e] * scale
            x = jnp.sum(x.reshape(count, SEQ, part), axis=1) / SEQ
            sliced[e] = (x * gain[:, part * e : part * (e + 1)]).astype(BF16)
        offer = pltpu.make_async_copy(sliced, sliced_out, slice_sem)
        offer.start()
        for e in range(steps):
            keep(e).wait()
        offer.wait()


def forward(tokens, received, slot, gates, gain, experts):
    rows, width = tokens.shape
    slots = received.shape[0]
    part = width // experts
    whole = lambda shape: pl.BlockSpec(shape, lambda i: (0,) * len(shape))
    return pl.pallas_call(
        functools.partial(forward_kernel, experts),
        grid=(experts,),
        in_specs=[
            pl.BlockSpec((rows, part), lambda i: (0, i)),
            pl.BlockSpec((slots, part), lambda i: (0, i)),
            whole((rows, 2)),
            whole((rows, 2)),
            whole((1, width)),
        ],
        out_specs=[HBM, HBM, whole((rows, 1))],
        out_shape=[
            pltpu.HBM((rows, width), F32),
            pltpu.HBM((experts, rows // SEQ, part), BF16),
            jax.ShapeDtypeStruct((rows, 1), F32),
        ],
        scratch_shapes=[
            pltpu.VMEM((experts, rows, part), F32),
            pltpu.VMEM((rows, 128), F32),
            pltpu.VMEM((2 * rows, slots), BF16),
            pltpu.VMEM((experts, rows // SEQ, part), BF16),
            pltpu.SemaphoreType.DMA((experts,)),
            pltpu.SemaphoreType.DMA(()),
        ],
        compiler_params=params(14),
        cost_estimate=cost(4 * rows * slots * width, 10 << 20),
    )(tokens, received, slot, gates, gain)


def pack_kernel(place, x, turned, *rest):
    *outs, spot, packed, sems = rest
    step, steps = pl.program_id(0), packed.shape[0]
    rows, part = x.shape
    capacity = outs[0].shape[0]
    slots = spot.shape[0]

    def leave(e, i):
        start = pl.multiple_of(e * part, part)
        return pltpu.make_async_copy(
            packed.at[e, pl.ds(i * capacity, capacity)], outs[i].at[:, pl.ds(start, part)], sems.at[e, i]
        )

    @pl.when(step == 0)
    def _():
        target = lax.rem(iota((slots, rows), 0) + place[0] * capacity, slots)
        spot[...] = ((turned[0:1, :] == target) | (turned[1:2, :] == target)).astype(BF16)

    for k in range(part // 512):
        cols = slice(512 * k, 512 * (k + 1))
        packed[step, :, cols] = jnp.dot(
            spot[...], x[:, cols].astype(BF16), preferred_element_type=F32
        ).astype(BF16)
    for i in range(len(outs)):
        leave(step, i).start()

    @pl.when(step == steps - 1)
    def _():
        for e in range(steps):
            for i in range(len(outs)):
                leave(e, i).wait()


def pack(place, summed, turned, experts, capacity):
    rows, width = summed.shape
    steps = experts // 2
    part = width // steps
    slots = experts * capacity
    return pl.pallas_call(
        pack_kernel,
        grid=(steps,),
        in_specs=[
            SMEM,
            pl.BlockSpec((rows, part), lambda i: (0, i)),
            pl.BlockSpec((2, rows), lambda i: (0, 0)),
        ],
        out_specs=[HBM] * experts,
        out_shape=[pltpu.HBM((capacity, width), BF16)] * experts,
        scratch_shapes=[
            pltpu.VMEM((slots, rows), BF16),
            pltpu.VMEM((steps, slots, part), BF16),
            pltpu.SemaphoreType.DMA((steps, experts)),
        ],
        compiler_params=params(14),
        cost_estimate=cost(2 * rows * slots * width, 7 << 20),
    )(place, *in_hbm(summed), turned)


def overlap_kernel(steps, x, rec, slot, facts, out, fetched, picks, dots):
    step = pl.program_id(0)
    rows, part = x.shape

    @pl.when(step == 0)
    def _():
        dots[...] = jnp.zeros_like(dots)
        picks[...] = one_hots(slot, rec.shape[0])

    for k in range(part // 256):
        cols = slice(256 * k, 256 * (k + 1))
        both = jnp.dot(picks[...], rec[:, cols], preferred_element_type=F32)
        fetched[:, cols] = both.astype(BF16)
        value = x[:, cols]
        dots[:rows] += fold(value * both[:rows])
        dots[rows:] += fold(value * both[rows:])

    @pl.when(step == steps - 1)
    def _():
        lane = iota((rows, 128), 1)
        known = facts[...]
        for k in range(2):
            total = jnp.sum(dots[rows * k : rows * (k + 1)], axis=1, keepdims=True)
            known = jnp.where(lane == k, total, known)
        out[...] = known


def overlaps(summed, received, slot, facts, experts):
    rows, width = summed.shape
    slots = received.shape[0]
    part = width // experts
    whole = lambda shape: pl.BlockSpec(shape, lambda i: (0, 0))
    return pl.pallas_call(
        functools.partial(overlap_kernel, experts),
        grid=(experts,),
        in_specs=[
            pl.BlockSpec((rows, part), lambda i: (0, i)),
            pl.BlockSpec((slots, part), lambda i: (0, i)),
            whole((rows, 2)),
            whole((rows, 128)),
        ],
        out_specs=[whole((rows, 128)), pl.BlockSpec((2 * rows, part), lambda i: (0, i))],
        out_shape=[pltpu.HBM((rows, 128), F32), pltpu.HBM((2 * rows, width), BF16)],
        scratch_shapes=[pltpu.VMEM((2 * rows, slots), BF16), pltpu.VMEM((2 * rows, 128), F32)],
        compiler_params=params(12),
        cost_estimate=cost(4 * rows * slots * width, 10 << 20),
    )(*in_hbm(summed, received), slot, facts)


def lanes_of(shape, dim):
    lane = iota(shape, dim)
    kind = lax.rem(lane, ROWS_DEV)
    return lane, kind, kind >= PAIR_DEV


def picker(group, kind, turned=False):
    wide = 2 * group
    shape, pair, row = ((wide, group), 1, 0) if turned else ((group, wide), 0, 1)
    a = iota(shape, pair)
    b = iota(shape, row)
    source = (a // PAIR_DEV) * ROWS_DEV + lax.rem(a, PAIR_DEV) + PAIR_DEV * kind
    return (source == b).astype(BF16)


def scores_kernel(own, near, far, notes, offered, whole, sems):
    experts, total, columns = offered.shape
    group = experts * PAIR_DEV
    queries, records = [
        jnp.dot(picker(group, kind), own[...], preferred_element_type=F32).astype(BF16) for kind in (0, 1)
    ]
    at_record = lanes_of((group, columns), 1)[2]
    for k, side in enumerate((near, far)):
        every = side[...]
        by_query = lax.dot_general(queries, every, NT, preferred_element_type=F32)
        by_record = lax.dot_general(records, every, NT, preferred_element_type=F32)
        whole[group * k : group * (k + 1)] = jnp.where(at_record, by_query, by_record)
    whole[2 * group :] = notes[...]
    to_each(whole, offered, sems)


def totals_kernel(scale, gathered, offered, kept_out, kept, spread, kept_sem, sem):
    place, core = lax.axis_index("u"), lax.axis_index("c")
    experts, total, columns = gathered.shape
    group = experts * PAIR_DEV
    both = gathered[0]
    for e in range(1, experts):
        both = both + gathered[e]
    positive_lane = both[2 * group + 3 : 2 * group + 4, :]
    near, far = both[:group] * scale, both[group : 2 * group] * scale
    kept[0:group] = near
    kept[group : 2 * group] = far

    shape = (group, columns)
    lane, kind, at_record = lanes_of(shape, 1)
    pair = iota(shape, 0)
    within = lax.rem(lane, 2 * group)
    matching = (within // ROWS_DEV == pair // PAIR_DEV) & (kind == lax.rem(pair, PAIR_DEV))
    here = matching & (lane // (2 * group) == place)
    positive = jnp.sum(jnp.where(here, positive_lane, 0.0), axis=1, keepdims=True)

    low = jnp.float32(-jnp.inf)
    near_records = jnp.where(at_record, near, low)
    far_records = jnp.where(at_record, far, low)
    highest = jnp.maximum(
        jnp.max(near_records, axis=1, keepdims=True), jnp.max(far_records, axis=1, keepdims=True)
    )
    weight = jnp.sum(jnp.exp(near_records - highest), axis=1, keepdims=True) + jnp.sum(
        jnp.exp(far_records - highest), axis=1, keepdims=True
    )
    log_total = highest + jnp.log(weight)
    chosen = jnp.zeros((group, 1), F32)
    for side, where in ((near, core), (far, 1 - core)):
        name = column_names(lane, kind, group, where)
        hit = at_record & (name.astype(F32) == positive)
        chosen = chosen + jnp.sum(jnp.where(hit, side, 0.0), axis=1, keepdims=True)
    kept[2 * group : 3 * group, :128] = jnp.broadcast_to(log_total, (group, 128))
    kept[2 * group : 3 * group, 128:256] = jnp.broadcast_to(positive, (group, 128))
    saved = pltpu.make_async_copy(kept, kept_out, kept_sem)
    saved.start()
    row_loss = log_total - chosen

    total_lane = jnp.sum(jnp.where(here, log_total, 0.0), axis=0, keepdims=True)
    loss_lane = jnp.sum(jnp.where(here, row_loss, 0.0), axis=0, keepdims=True)
    own_lane = jnp.where(lane[0:1] // (2 * group) == place, positive_lane, 0.0)
    pieces = [x[:, 128 * k : 128 * (k + 1)] for x in (total_lane, own_lane) for k in range(columns // 128)]
    loss_pieces = [
        pltpu.roll(loss_lane, PAIR_DEV, 1)[:, 128 * k : 128 * (k + 1)] for k in range(columns // 128)
    ]
    pieces = [a + b for a, b in zip(pieces, loss_pieces)] + pieces[columns // 128 :]
    message = jnp.concatenate(pieces, axis=0)
    for d in range(spread.shape[0]):
        spread[d] = message
    copy_all([pltpu.make_async_copy(spread, offered, sem)])
    saved.wait()


def column_names(lane, kind, group, core):
    wide = 2 * group
    block = (lane // wide) * CORES + core
    return block * group + (lax.rem(lane, wide) // ROWS_DEV) * PAIR_DEV + lax.rem(kind, PAIR_DEV)


def gradient_kernel(scale, factor, heard, kept, near, far, offered, loss, whole, sems):
    place, core = lax.axis_index("u"), lax.axis_index("c")
    experts, wide, columns = offered.shape
    group = wide // 2
    outer_size = heard.shape[0] // CORES
    pieces = columns // 128
    shape = (group, columns)
    lane, kind, at_record = lanes_of(shape, 1)
    pair = iota(shape, 0)
    own_name = (place * CORES + core) * group + iota((group, 1), 0)
    own_total = kept[2 * group : 3 * group, 0:1]
    own_positive = kept[2 * group : 3 * group, 128:129]
    result = jnp.zeros((wide, columns), F32)
    losses = jnp.zeros((1, columns), F32)
    for k, (side, where) in enumerate(((near, core), (far, 1 - core))):
        told = heard[where]
        for u in range(1, outer_size):
            told = told + heard[u * CORES + where]
        total = jnp.concatenate([told[i : i + 1] for i in range(pieces)], axis=1)
        positive = jnp.concatenate([told[pieces + i : pieces + i + 1] for i in range(pieces)], axis=1)
        losses = losses + jnp.where(at_record[0:1], total, 0.0)
        value = kept[group * k : group * (k + 1), :]
        name = column_names(lane, kind, group, where).astype(F32)
        hit = jnp.where(name == own_positive, 1.0, 0.0)
        by_query = (jnp.exp(value - own_total) - hit) * factor[0]
        by_query = jnp.where(at_record, by_query, 0.0).astype(BF16)
        hit = jnp.where(positive == own_name.astype(F32), 1.0, 0.0)
        by_record = (jnp.exp(jnp.where(at_record, 0.0, value - total)) - hit) * factor[0]
        by_record = jnp.where(at_record, 0.0, by_record).astype(BF16)
        rows = jnp.dot(picker(group, 0, True), by_query, preferred_element_type=F32) + jnp.dot(
            picker(group, 1, True), by_record, preferred_element_type=F32
        )
        result = result + jnp.dot(rows.astype(BF16), side[...], preferred_element_type=F32)
    whole[...] = (result * scale).astype(BF16)
    to_each(whole, offered, sems)
    loss[...] = jnp.sum(losses, axis=1, keepdims=True)


def rows_of(grads, e, index):
    tile = grads[e, pl.ds(pl.multiple_of((index // 4) * 16, 16), 16), :].astype(F32)
    piece = lax.rem(index, 4)
    quarters = [tile[ROWS_DEV * k : ROWS_DEV * (k + 1)] for k in range(4)]
    half = jnp.where(piece < 2, quarters[0], quarters[2]), jnp.where(piece < 2, quarters[1], quarters[3])
    return jnp.where(lax.rem(piece, 2) == 0, half[0], half[1])


def router_kernel(
    grads, gain, summed_in, fetched_in, tok_in, facts_in, part_out, state_out, weighted_out,
    summed, fetched, tok, facts, state, weighted, acc, sems, facts_sem, out_sems
):
    experts, _, part = grads.shape
    rows = summed.shape[1]
    count = rows // SEQ
    sources = ((summed_in, summed), (fetched_in, fetched), (tok_in, tok))

    def load(e):
        cols = pl.ds(e * part, part)
        return [
            pltpu.make_async_copy(a.at[:, cols], b.at[e], sems.at[k, e]) for k, (a, b) in enumerate(sources)
        ]

    known = pltpu.make_async_copy(facts_in, facts, facts_sem)
    loads = [load(e) for e in range(experts)]
    for e in range(experts):
        loads[e][0].start()
        loads[e][1].start()
    known.start()
    for e in range(experts):
        loads[e][2].start()

    for e in range(experts):
        cols = slice(part * e, part * (e + 1))
        w = rows_of(grads, e, lax.axis_index("expert")) * (gain[:, cols] / SEQ)
        weighted[:, cols] = w
        loads[e][0].wait()
        loads[e][1].wait()
        for q in range(count):
            row = w[q : q + 1, :]
            at = [slice(rows * k + SEQ * q, rows * k + SEQ * (q + 1)) for k in range(2)]
            terms = [summed[e, at[0], :], fetched[e, at[0], :].astype(F32), fetched[e, at[1], :].astype(F32)]
            for k, term in enumerate(terms):
                total = fold(term * row)
                spot = slice(SEQ * q, SEQ * (q + 1))
                acc[k, spot] = total if e == 0 else acc[k, spot] + total
    known.wait()
    lanes = iota((SEQ, 128), 1)
    choices = []
    for q in range(count):
        at = slice(SEQ * q, SEQ * (q + 1))
        fact = facts[at, :]
        inv = fact[:, 2:3]
        shrink = inv * inv * inv * (jnp.sum(acc[0, at], axis=1, keepdims=True) / (experts * part))
        grad_gate = []
        for k in range(2):
            along = jnp.sum(acc[1 + k, at], axis=1, keepdims=True)
            grad_gate.append(inv * along - shrink * fact[:, k : k + 1])
        gates = [fact[:, 3 + k : 4 + k] for k in range(2)]
        mean = gates[0] * grad_gate[0] + gates[1] * grad_gate[1]
        choice = jnp.zeros((SEQ, 128), F32)
        for k in range(2):
            chosen = gates[k] * (grad_gate[k] - mean)
            route = fact[:, 5 + k : 6 + k].astype(I32)
            choice = choice + jnp.where(route == lanes, chosen, 0.0)
        choices.append(choice)
        choice = jnp.where(lanes == experts, inv, choice)
        state[at] = jnp.where(lanes == experts + 1, shrink, choice)
    saved = [
        pltpu.make_async_copy(state, state_out, out_sems.at[0]),
        pltpu.make_async_copy(weighted, weighted_out, out_sems.at[1]),
    ]
    for copy in saved:
        copy.start()
    lhs = jnp.transpose(jnp.concatenate(choices, axis=0))[:experts].astype(BF16)
    tiles = part // 128
    for e in range(experts):
        loads[e][2].wait()
        block = jnp.dot(lhs, tok[e], preferred_element_type=F32)
        for k in range(tiles):
            at = experts * (tiles * e + k)
            part_out[at : at + experts, :] = block[:, 128 * k : 128 * (k + 1)]
    for copy in saved:
        copy.wait()


def token_kernel(experts, summed, weighted, state, router, out):
    rows = summed.shape[0]
    known = state[...]
    choice = jnp.where(iota(known.shape, 1) < experts, known, 0.0).astype(BF16)
    through = jnp.dot(choice, router[...], preferred_element_type=F32)
    for q in range(rows // SEQ):
        at = slice(SEQ * q, SEQ * (q + 1))
        inverse, shrink = known[at, experts : experts + 1], known[at, experts + 1 : experts + 2]
        x = inverse * weighted[q : q + 1, :] - shrink * summed[at]
        out[at] = (x + through[SEQ * q : SEQ * (q + 1)]).astype(BF16)


def token_rows(summed, weighted, state, router, experts):
    rows, width = summed.shape
    part = width // experts
    split = lambda count: pl.BlockSpec((count, part), lambda i: (0, i))
    return pl.pallas_call(
        functools.partial(token_kernel, experts),
        grid=(experts,),
        in_specs=[
            split(rows),
            split(weighted.shape[0]),
            pl.BlockSpec((rows, 128), lambda i: (0, 0)),
            split(128),
        ],
        out_specs=split(rows),
        out_shape=jax.ShapeDtypeStruct((rows, width), BF16),
        compiler_params=params(10),
        cost_estimate=cost(2 * rows * 128 * width, 5 << 20),
    )(*in_hbm(summed, weighted, state), router)


def expert_kernel(place, grads, gain, notes, *rest):
    *sources, out, backs, sems = rest
    experts = len(sources)
    _, _, part = grads.shape
    step = pl.program_id(0)
    source = lax.rem(place[0] + experts - step, experts)
    gate, inv, seq = notes[0, :, 0:1], notes[0, :, 1:2], notes[0, :, 2:3]
    capacity = gate.shape[0]
    loads = [pltpu.make_async_copy(sources[r], backs.at[r], sems.at[r]) for r in range(experts)]

    @pl.when(step == 0)
    def _():
        for load in loads:
            load.start()

    for r in range(experts):

        @pl.when(step == r)
        def _():
            loads[r].wait()
            back = backs.at[r]
            acc = jnp.zeros((capacity, 128), F32)
            rows = []
            for e in range(experts):
                cols = slice(part * e, part * (e + 1))
                w = rows_of(grads, e, source) * (gain[:, cols] / SEQ)
                x = jnp.broadcast_to(w[0:1], (capacity, part))
                for s in range(1, ROWS_DEV):
                    x = jnp.where(seq == s, w[s : s + 1], x)
                rows.append(w)
                acc = acc + fold(x * back[:, cols].astype(F32))
            shrink = inv * inv * inv * (jnp.sum(acc, axis=1, keepdims=True) / (experts * part))
            for e in range(experts):
                cols = slice(part * e, part * (e + 1))
                w = rows[e]
                x = jnp.broadcast_to(w[0:1], (capacity, part))
                for s in range(1, ROWS_DEV):
                    x = jnp.where(seq == s, w[s : s + 1], x)
                x = gate * (inv * x - shrink * back[:, cols].astype(F32))
                out[0, :, cols] = x.astype(BF16)


def expert_rows(place, grads, gain, notes, backs):
    experts, capacity = notes.shape[:2]
    width = gain.shape[1]
    whole = lambda shape: pl.BlockSpec(shape, lambda i, p: (0,) * len(shape))
    source = lambda i, p: (lax.rem(p[0] + experts - i, experts), 0, 0)
    return pl.pallas_call(
        expert_kernel,
        grid_spec=pltpu.PrefetchScalarGridSpec(
            num_scalar_prefetch=1,
            grid=(experts,),
            in_specs=[
                whole(grads.shape),
                whole((1, width)),
                pl.BlockSpec((1, capacity, notes.shape[2]), source),
            ]
            + [HBM] * experts,
            out_specs=pl.BlockSpec((1, capacity, width), source),
            scratch_shapes=[
                pltpu.VMEM((experts, capacity, width), BF16),
                pltpu.SemaphoreType.DMA((experts,)),
            ],
        ),
        out_shape=jax.ShapeDtypeStruct((experts, capacity, width), BF16),
        compiler_params=params(16),
        cost_estimate=cost(12 * experts * capacity * width, 9 << 20),
    )(place, grads, gain, notes, *in_hbm(*backs))


def shards(tokens, routes, positives, expert_out, router, norm_gain, loss_scale):
    experts, capacity, width = expert_out.shape[2:]
    rows = tokens.shape[0]
    slots = experts * capacity
    outer = lax.axis_size("u")
    mine = lax.axis_index("expert").astype(I32)
    mine_at = mine[None]
    part = width // experts
    group = PAIR_DEV * experts
    pairs = group * outer * CORES
    scale = 4.0 / math.sqrt(width)
    gain = norm_gain[None, :]
    columns = outer * experts * ROWS_DEV

    received = exchange(expert_out.reshape(experts, capacity, width), "expert").reshape(slots, width)
    gates, slot = routing(tokens, routes, router, experts, capacity)
    lane = jnp.arange(columns, dtype=I32)
    spread_positive = jnp.where(
        (lane % (2 * group)) // ROWS_DEV == mine,
        jnp.where(lane % ROWS_DEV == 0, positives[0], positives[1]) * (lane % ROWS_DEV < PAIR_DEV),
        0,
    ).astype(F32)

    summed, sliced, inverse = forward(tokens, received, slot, gates, gain, experts)
    own = exchange(sliced, "expert").reshape(2 * group, part)
    facts = jnp.concatenate(
        [jnp.zeros((rows, 2), F32), inverse, gates, routes.astype(F32)], axis=1
    )
    facts = jnp.pad(facts, ((0, 0), (0, 128 - facts.shape[1])))
    backs = list(pack(mine_at, summed, slot.T, experts, capacity))

    def move(after, turns):
        after, *ready = lax.optimization_barrier((after, *[backs[r] for r in turns]))
        for r, x in zip(turns, ready):
            backs[r] = lax.ppermute(x, "expert", [(i, (i + r) % experts) for i in range(experts)])
        return after


    def landed(value, turns):
        value, *done = lax.optimization_barrier((value, *[backs[r] for r in turns]))
        for r, x in zip(turns, done):
            backs[r] = x
        return value

    slot_ids = jnp.arange(slots, dtype=I32)[None, :]
    picks = [slot[:, k : k + 1] == slot_ids for k in range(2)]
    gate_slot = jnp.sum(
        jnp.where(picks[0], gates[:, 0:1], 0.0) + jnp.where(picks[1], gates[:, 1:2], 0.0), axis=0
    )
    taken = picks[0] | picks[1]
    inverse_slot = jnp.sum(jnp.where(taken, inverse, 0.0), axis=0)
    sequence = (jnp.arange(rows, dtype=I32) // SEQ).astype(F32)
    sequence_slot = jnp.sum(jnp.where(taken, sequence[:, None], 0.0), axis=0)
    notes = jnp.stack([gate_slot, inverse_slot, sequence_slot, spread_positive])
    notes = jnp.pad(notes, ((0, 4), (0, 0)))

    own, *backs = lax.optimization_barrier((own, *backs))
    near = spread(own, "u", outer)
    facts, fetched = overlaps(summed, received, slot, facts, experts)
    near, facts, fetched = lax.optimization_barrier((near, facts, fetched))
    far = swap_core(near)
    near, far = near.reshape(columns, part), far.reshape(columns, part)
    offered = pl.pallas_call(
        scores_kernel,
        in_specs=[VMEM] * 4,
        out_specs=HBM,
        out_shape=pltpu.HBM((experts, 2 * group + 8, columns), F32),
        scratch_shapes=[pltpu.VMEM((2 * group + 8, columns), F32), pltpu.SemaphoreType.DMA((experts,))],
        compiler_params=params(2),
    )(own, near, far, notes)
    offered = move(offered, TURNS[0])
    gathered = exchange(offered, "expert")
    devices = outer * CORES
    offered, kept = pl.pallas_call(
        functools.partial(totals_kernel, scale),
        in_specs=[VMEM],
        out_specs=[HBM] * 2,
        out_shape=[pltpu.HBM((devices, 8, 128), F32), pltpu.HBM((3 * group, columns), F32)],
        scratch_shapes=[
            pltpu.VMEM((3 * group, columns), F32),
            pltpu.VMEM((devices, 8, 128), F32),
            pltpu.SemaphoreType.DMA(()),
            pltpu.SemaphoreType.DMA(()),
        ],
        compiler_params=params(2),
    )(gathered)
    offered = move(offered, TURNS[1])
    heard = exchange(offered, ("u", "c"))
    heard = landed(heard, TURNS[0][:1])
    offered, loss = pl.pallas_call(
        functools.partial(gradient_kernel, scale),
        in_specs=[SMEM] + [VMEM] * 4,
        out_specs=[HBM, VMEM],
        out_shape=[pltpu.HBM((experts, 2 * group, part), BF16), jax.ShapeDtypeStruct((1, 1), F32)],
        scratch_shapes=[pltpu.VMEM((2 * group, part), BF16), pltpu.SemaphoreType.DMA((experts,))],
        compiler_params=params(2),
    )((loss_scale / pairs)[None], heard, kept, near, far)
    offered = move(offered, TURNS[2])
    grads = exchange(offered, "expert")
    grads = landed(grads, TURNS[0][1:])

    router_part, state, weighted = pl.pallas_call(
        router_kernel,
        in_specs=[VMEM] * 2 + [HBM] * 4,
        out_specs=[VMEM, HBM, HBM],
        out_shape=[
            jax.ShapeDtypeStruct((width * experts // 128, 128), F32),
            pltpu.HBM((rows, 128), F32),
            pltpu.HBM((rows // SEQ, width), F32),
        ],
        scratch_shapes=[
            pltpu.VMEM((experts, rows, part), F32),
            pltpu.VMEM((experts, 2 * rows, part), BF16),
            pltpu.VMEM((experts, rows, part), BF16),
            pltpu.VMEM((rows, 128), F32),
            pltpu.VMEM((rows, 128), F32),
            pltpu.VMEM((rows // SEQ, width), F32),
            pltpu.VMEM((3, rows, 128), F32),
            pltpu.SemaphoreType.DMA((3, experts)),
            pltpu.SemaphoreType.DMA(()),
            pltpu.SemaphoreType.DMA((2,)),
        ],
        compiler_params=params(16),
    )(grads, gain, *in_hbm(summed, fetched, tokens, facts))
    router_part = exchange(router_part.reshape(outer, -1, 128), "u")
    router_part = landed(router_part, TURNS[1])
    router_part = jnp.sum(router_part, axis=0)
    router_part = spread(router_part, ("c", "expert"), CORES * experts)
    held = lax.dynamic_slice_in_dim(gathered[:, 2 * group : 2 * group + 3], mine * capacity, capacity, axis=2)
    held = jnp.pad(jnp.transpose(held, (0, 2, 1)), ((0, 0), (0, 0), (0, 5)))
    turned = jnp.pad(router.T, ((0, 128 - experts), (0, 0)))
    token_grad = token_rows(summed, weighted, state, turned, experts)
    router_part, token_grad = lax.optimization_barrier((router_part, token_grad))
    router_part = jnp.sum(router_part, axis=0)
    router_all = spread(router_part, "u", outer)
    expert_grad = expert_rows(mine_at, grads, gain, held, backs)
    router_all, expert_grad = lax.optimization_barrier((router_all, expert_grad))
    router_grad = router_all.reshape(-1, experts, 128).transpose(1, 0, 2).reshape(experts, width).T
    return token_grad, expert_grad.reshape(1, 1, experts, capacity, width), router_grad, loss[0, 0] / pairs


def solution(mesh):
    outer = mesh.shape["dp"] // CORES
    fine = Mesh(mesh.devices.reshape(outer, CORES, mesh.shape["expert"]), ("u", "c", "expert"))
    everywhere = ("u", "c", "expert")
    return jax.shard_map(
        shards,
        mesh=fine,
        in_specs=(
            P(everywhere, None),
            P(everywhere, None),
            P(everywhere),
            P(("u", "c"), "expert", None, None, None),
            P(),
            P(),
            P(),
        ),
        out_specs=(P(everywhere, None), P(("u", "c"), "expert", None, None, None), P(), P()),
        check_vma=False,
    )
```

```python
import functools
import math

import jax
import jax.numpy as jnp
from jax import lax
from jax.experimental import pallas as pl
from jax.experimental.pallas import tpu as pltpu
from jax.sharding import Mesh, PartitionSpec as P

PAIR_DEV = 2
SEQ = 48
EPS = 1e-05
CORES = 2
ROWS_DEV = 2 * PAIR_DEV
F32 = jnp.float32
BF16 = jnp.bfloat16
I32 = jnp.int32
VMEM = pl.BlockSpec(memory_space=pltpu.VMEM)
SMEM = pl.BlockSpec(memory_space=pltpu.SMEM)
HBM = pl.BlockSpec(memory_space=pltpu.HBM)
NT = (((1,), (1,)), ((), ()))
TURNS = ((4, 1, 7), (3, 5), (2, 6))


def iota(shape, dim):
    return lax.broadcasted_iota(I32, shape, dim)


def params(mib):
    return pltpu.CompilerParams(vmem_limit_bytes=mib << 20)


def cost(flops, moved):
    return pl.CostEstimate(flops=flops, bytes_accessed=moved, transcendentals=0)


def fold(x):
    total = x[:, :128]
    for k in range(1, x.shape[1] // 128):
        total = total + x[:, 128 * k : 128 * (k + 1)]
    return total


def in_hbm(*arrays):
    return [pltpu.with_memory_space_constraint(x, pltpu.HBM) for x in arrays]


def copy_all(copies):
    for copy in copies:
        copy.start()
    for copy in copies:
        copy.wait()


def to_each(source, target, sems):
    copy_all([pltpu.make_async_copy(source, target.at[i], sems.at[i]) for i in range(target.shape[0])])


def swap_core(x):
    return lax.ppermute(x, "c", [(0, 1), (1, 0)])


def exchange(x, axes):
    return lax.all_to_all(x, axes, split_axis=0, concat_axis=0, tiled=True)


def spread(x, axes, size):
    return exchange(jnp.broadcast_to(x[None], (size,) + x.shape), axes)


def routing(tokens, routes, router, experts, capacity):
    logits = jnp.dot(tokens, router, preferred_element_type=F32)
    lanes = jnp.arange(experts, dtype=I32)[None, None, :]
    one_hot = (routes[:, :, None] == lanes).astype(F32)
    chosen = jnp.sum(one_hot * logits[:, None, :], axis=2)
    gates = jax.nn.softmax(chosen, axis=1)
    rows = routes.shape[0]
    hits = jnp.sum(one_hot, axis=1)
    order = jnp.arange(rows, dtype=I32)
    earlier = (order[None, :] < order[:, None]).astype(BF16)
    before = jnp.dot(earlier, hits.astype(BF16), preferred_element_type=F32)
    rank = jnp.sum(one_hot * before[:, None, :], axis=2).astype(I32)
    return gates, routes * capacity + rank


def one_hots(slot, slots):
    ids = iota((slot.shape[0], slots), 1)
    return jnp.concatenate([(slot[:, k : k + 1] == ids).astype(BF16) for k in range(2)], axis=0)


def forward_kernel(
    steps, tok, rec, slot, gate, gain, summed, sliced_out, inverse, held, square, picks, sliced, row_sem, slice_sem
):
    step = pl.program_id(0)
    rows, part = tok.shape

    def keep(e):
        start = pl.multiple_of(e * part, part)
        return pltpu.make_async_copy(held.at[e], summed.at[:, pl.ds(start, part)], row_sem.at[e])

    @pl.when(step == 0)
    def _():
        square[...] = jnp.zeros_like(square)
        picks[...] = one_hots(slot, rec.shape[0])

    for k in range(part // 256):
        cols = slice(256 * k, 256 * (k + 1))
        both = jnp.dot(picks[...], rec[:, cols], preferred_element_type=F32)
        x = tok[:, cols].astype(F32) + gate[:, 0:1] * both[:rows] + gate[:, 1:2] * both[rows:]
        held[step, :, cols] = x
        square[...] += fold(x * x)
    keep(step).start()

    @pl.when(step == steps - 1)
    def _():
        mean = jnp.sum(square[...], axis=1, keepdims=True) / (steps * part)
        scale = lax.rsqrt(mean + EPS)
        inverse[...] = scale
        count = rows // SEQ
        for e in range(steps):
            x = held[e] * scale
            x = jnp.sum(x.reshape(count, SEQ, part), axis=1) / SEQ
            sliced[e] = (x * gain[:, part * e : part * (e + 1)]).astype(BF16)
        offer = pltpu.make_async_copy(sliced, sliced_out, slice_sem)
        offer.start()
        for e in range(steps):
            keep(e).wait()
        offer.wait()


def forward(tokens, received, slot, gates, gain, experts):
    rows, width = tokens.shape
    slots = received.shape[0]
    part = width // experts
    whole = lambda shape: pl.BlockSpec(shape, lambda i: (0,) * len(shape))
    return pl.pallas_call(
        functools.partial(forward_kernel, experts),
        grid=(experts,),
        in_specs=[
            pl.BlockSpec((rows, part), lambda i: (0, i)),
            pl.BlockSpec((slots, part), lambda i: (0, i)),
            whole((rows, 2)),
            whole((rows, 2)),
            whole((1, width)),
        ],
        out_specs=[HBM, HBM, whole((rows, 1))],
        out_shape=[
            pltpu.HBM((rows, width), F32),
            pltpu.HBM((experts, rows // SEQ, part), BF16),
            jax.ShapeDtypeStruct((rows, 1), F32),
        ],
        scratch_shapes=[
            pltpu.VMEM((experts, rows, part), F32),
            pltpu.VMEM((rows, 128), F32),
            pltpu.VMEM((2 * rows, slots), BF16),
            pltpu.VMEM((experts, rows // SEQ, part), BF16),
            pltpu.SemaphoreType.DMA((experts,)),
            pltpu.SemaphoreType.DMA(()),
        ],
        compiler_params=params(14),
        cost_estimate=cost(4 * rows * slots * width, 10 << 20),
    )(tokens, received, slot, gates, gain)


def pack_kernel(place, x, turned, *rest):
    *outs, spot, packed, sems = rest
    step, steps = pl.program_id(0), packed.shape[0]
    rows, part = x.shape
    capacity = outs[0].shape[0]
    slots = spot.shape[0]

    def leave(e, i):
        start = pl.multiple_of(e * part, part)
        return pltpu.make_async_copy(
            packed.at[e, pl.ds(i * capacity, capacity)], outs[i].at[:, pl.ds(start, part)], sems.at[e, i]
        )

    @pl.when(step == 0)
    def _():
        target = lax.rem(iota((slots, rows), 0) + place[0] * capacity, slots)
        spot[...] = ((turned[0:1, :] == target) | (turned[1:2, :] == target)).astype(BF16)

    for k in range(part // 512):
        cols = slice(512 * k, 512 * (k + 1))
        packed[step, :, cols] = jnp.dot(
            spot[...], x[:, cols].astype(BF16), preferred_element_type=F32
        ).astype(BF16)
    for i in range(len(outs)):
        leave(step, i).start()

    @pl.when(step == steps - 1)
    def _():
        for e in range(steps):
            for i in range(len(outs)):
                leave(e, i).wait()


def pack(place, summed, turned, experts, capacity):
    rows, width = summed.shape
    steps = experts // 2
    part = width // steps
    slots = experts * capacity
    return pl.pallas_call(
        pack_kernel,
        grid=(steps,),
        in_specs=[
            SMEM,
            pl.BlockSpec((rows, part), lambda i: (0, i)),
            pl.BlockSpec((2, rows), lambda i: (0, 0)),
        ],
        out_specs=[HBM] * experts,
        out_shape=[pltpu.HBM((capacity, width), BF16)] * experts,
        scratch_shapes=[
            pltpu.VMEM((slots, rows), BF16),
            pltpu.VMEM((steps, slots, part), BF16),
            pltpu.SemaphoreType.DMA((steps, experts)),
        ],
        compiler_params=params(14),
        cost_estimate=cost(2 * rows * slots * width, 7 << 20),
    )(place, *in_hbm(summed), turned)


def overlap_kernel(steps, x, rec, slot, facts, out, fetched, picks, dots):
    step = pl.program_id(0)
    rows, part = x.shape

    @pl.when(step == 0)
    def _():
        dots[...] = jnp.zeros_like(dots)
        picks[...] = one_hots(slot, rec.shape[0])

    for k in range(part // 256):
        cols = slice(256 * k, 256 * (k + 1))
        both = jnp.dot(picks[...], rec[:, cols], preferred_element_type=F32)
        fetched[:, cols] = both.astype(BF16)
        value = x[:, cols]
        dots[:rows] += fold(value * both[:rows])
        dots[rows:] += fold(value * both[rows:])

    @pl.when(step == steps - 1)
    def _():
        lane = iota((rows, 128), 1)
        known = facts[...]
        for k in range(2):
            total = jnp.sum(dots[rows * k : rows * (k + 1)], axis=1, keepdims=True)
            known = jnp.where(lane == k, total, known)
        out[...] = known


def overlaps(summed, received, slot, facts, experts):
    rows, width = summed.shape
    slots = received.shape[0]
    part = width // experts
    whole = lambda shape: pl.BlockSpec(shape, lambda i: (0, 0))
    return pl.pallas_call(
        functools.partial(overlap_kernel, experts),
        grid=(experts,),
        in_specs=[
            pl.BlockSpec((rows, part), lambda i: (0, i)),
            pl.BlockSpec((slots, part), lambda i: (0, i)),
            whole((rows, 2)),
            whole((rows, 128)),
        ],
        out_specs=[whole((rows, 128)), pl.BlockSpec((2 * rows, part), lambda i: (0, i))],
        out_shape=[pltpu.HBM((rows, 128), F32), pltpu.HBM((2 * rows, width), BF16)],
        scratch_shapes=[pltpu.VMEM((2 * rows, slots), BF16), pltpu.VMEM((2 * rows, 128), F32)],
        compiler_params=params(12),
        cost_estimate=cost(4 * rows * slots * width, 10 << 20),
    )(*in_hbm(summed, received), slot, facts)


def lanes_of(shape, dim):
    lane = iota(shape, dim)
    kind = lax.rem(lane, ROWS_DEV)
    return lane, kind, kind >= PAIR_DEV


def picker(group, kind, turned=False):
    wide = 2 * group
    shape, pair, row = ((wide, group), 1, 0) if turned else ((group, wide), 0, 1)
    a = iota(shape, pair)
    b = iota(shape, row)
    source = (a // PAIR_DEV) * ROWS_DEV + lax.rem(a, PAIR_DEV) + PAIR_DEV * kind
    return (source == b).astype(BF16)


def scores_kernel(own, near, far, notes, offered, whole, sems):
    experts, total, columns = offered.shape
    group = experts * PAIR_DEV
    queries, records = [
        jnp.dot(picker(group, kind), own[...], preferred_element_type=F32).astype(BF16) for kind in (0, 1)
    ]
    at_record = lanes_of((group, columns), 1)[2]
    for k, side in enumerate((near, far)):
        every = side[...]
        by_query = lax.dot_general(queries, every, NT, preferred_element_type=F32)
        by_record = lax.dot_general(records, every, NT, preferred_element_type=F32)
        whole[group * k : group * (k + 1)] = jnp.where(at_record, by_query, by_record)
    whole[2 * group :] = notes[...]
    to_each(whole, offered, sems)


def totals_kernel(scale, gathered, offered, kept_out, kept, spread, kept_sem, sem):
    place, core = lax.axis_index("u"), lax.axis_index("c")
    experts, total, columns = gathered.shape
    group = experts * PAIR_DEV
    both = gathered[0]
    for e in range(1, experts):
        both = both + gathered[e]
    positive_lane = both[2 * group + 3 : 2 * group + 4, :]
    near, far = both[:group] * scale, both[group : 2 * group] * scale
    kept[0:group] = near
    kept[group : 2 * group] = far

    shape = (group, columns)
    lane, kind, at_record = lanes_of(shape, 1)
    pair = iota(shape, 0)
    within = lax.rem(lane, 2 * group)
    matching = (within // ROWS_DEV == pair // PAIR_DEV) & (kind == lax.rem(pair, PAIR_DEV))
    here = matching & (lane // (2 * group) == place)
    positive = jnp.sum(jnp.where(here, positive_lane, 0.0), axis=1, keepdims=True)

    low = jnp.float32(-jnp.inf)
    near_records = jnp.where(at_record, near, low)
    far_records = jnp.where(at_record, far, low)
    highest = jnp.maximum(
        jnp.max(near_records, axis=1, keepdims=True), jnp.max(far_records, axis=1, keepdims=True)
    )
    weight = jnp.sum(jnp.exp(near_records - highest), axis=1, keepdims=True) + jnp.sum(
        jnp.exp(far_records - highest), axis=1, keepdims=True
    )
    log_total = highest + jnp.log(weight)
    chosen = jnp.zeros((group, 1), F32)
    for side, where in ((near, core), (far, 1 - core)):
        name = column_names(lane, kind, group, where)
        hit = at_record & (name.astype(F32) == positive)
        chosen = chosen + jnp.sum(jnp.where(hit, side, 0.0), axis=1, keepdims=True)
    kept[2 * group : 3 * group, :128] = jnp.broadcast_to(log_total, (group, 128))
    kept[2 * group : 3 * group, 128:256] = jnp.broadcast_to(positive, (group, 128))
    saved = pltpu.make_async_copy(kept, kept_out, kept_sem)
    saved.start()
    row_loss = log_total - chosen

    total_lane = jnp.sum(jnp.where(here, log_total, 0.0), axis=0, keepdims=True)
    loss_lane = jnp.sum(jnp.where(here, row_loss, 0.0), axis=0, keepdims=True)
    own_lane = jnp.where(lane[0:1] // (2 * group) == place, positive_lane, 0.0)
    pieces = [x[:, 128 * k : 128 * (k + 1)] for x in (total_lane, own_lane) for k in range(columns // 128)]
    loss_pieces = [
        pltpu.roll(loss_lane, PAIR_DEV, 1)[:, 128 * k : 128 * (k + 1)] for k in range(columns // 128)
    ]
    pieces = [a + b for a, b in zip(pieces, loss_pieces)] + pieces[columns // 128 :]
    message = jnp.concatenate(pieces, axis=0)
    for d in range(spread.shape[0]):
        spread[d] = message
    copy_all([pltpu.make_async_copy(spread, offered, sem)])
    saved.wait()


def column_names(lane, kind, group, core):
    wide = 2 * group
    block = (lane // wide) * CORES + core
    return block * group + (lax.rem(lane, wide) // ROWS_DEV) * PAIR_DEV + lax.rem(kind, PAIR_DEV)


def gradient_kernel(scale, factor, heard, kept, near, far, offered, loss, whole, sems):
    place, core = lax.axis_index("u"), lax.axis_index("c")
    experts, wide, columns = offered.shape
    group = wide // 2
    outer_size = heard.shape[0] // CORES
    pieces = columns // 128
    shape = (group, columns)
    lane, kind, at_record = lanes_of(shape, 1)
    pair = iota(shape, 0)
    own_name = (place * CORES + core) * group + iota((group, 1), 0)
    own_total = kept[2 * group : 3 * group, 0:1]
    own_positive = kept[2 * group : 3 * group, 128:129]
    result = jnp.zeros((wide, columns), F32)
    losses = jnp.zeros((1, columns), F32)
    for k, (side, where) in enumerate(((near, core), (far, 1 - core))):
        told = heard[where]
        for u in range(1, outer_size):
            told = told + heard[u * CORES + where]
        total = jnp.concatenate([told[i : i + 1] for i in range(pieces)], axis=1)
        positive = jnp.concatenate([told[pieces + i : pieces + i + 1] for i in range(pieces)], axis=1)
        losses = losses + jnp.where(at_record[0:1], total, 0.0)
        value = kept[group * k : group * (k + 1), :]
        name = column_names(lane, kind, group, where).astype(F32)
        hit = jnp.where(name == own_positive, 1.0, 0.0)
        by_query = (jnp.exp(value - own_total) - hit) * factor[0]
        by_query = jnp.where(at_record, by_query, 0.0).astype(BF16)
        hit = jnp.where(positive == own_name.astype(F32), 1.0, 0.0)
        by_record = (jnp.exp(jnp.where(at_record, 0.0, value - total)) - hit) * factor[0]
        by_record = jnp.where(at_record, 0.0, by_record).astype(BF16)
        rows = jnp.dot(picker(group, 0, True), by_query, preferred_element_type=F32) + jnp.dot(
            picker(group, 1, True), by_record, preferred_element_type=F32
        )
        result = result + jnp.dot(rows.astype(BF16), side[...], preferred_element_type=F32)
    whole[...] = (result * scale).astype(BF16)
    to_each(whole, offered, sems)
    loss[...] = jnp.sum(losses, axis=1, keepdims=True)


def rows_of(grads, e, index):
    tile = grads[e, pl.ds(pl.multiple_of((index // 4) * 16, 16), 16), :].astype(F32)
    piece = lax.rem(index, 4)
    quarters = [tile[ROWS_DEV * k : ROWS_DEV * (k + 1)] for k in range(4)]
    half = jnp.where(piece < 2, quarters[0], quarters[2]), jnp.where(piece < 2, quarters[1], quarters[3])
    return jnp.where(lax.rem(piece, 2) == 0, half[0], half[1])


def router_kernel(
    grads, gain, summed_in, fetched_in, tok_in, facts_in, part_out, state_out, weighted_out,
    summed, fetched, tok, facts, state, weighted, acc, sems, facts_sem, out_sems
):
    experts, _, part = grads.shape
    rows = summed.shape[1]
    count = rows // SEQ
    sources = ((summed_in, summed), (fetched_in, fetched), (tok_in, tok))

    def load(e):
        cols = pl.ds(e * part, part)
        return [
            pltpu.make_async_copy(a.at[:, cols], b.at[e], sems.at[k, e]) for k, (a, b) in enumerate(sources)
        ]

    known = pltpu.make_async_copy(facts_in, facts, facts_sem)
    loads = [load(e) for e in range(experts)]
    for e in range(experts):
        loads[e][0].start()
        loads[e][1].start()
    known.start()
    for e in range(experts):
        loads[e][2].start()

    for e in range(experts):
        cols = slice(part * e, part * (e + 1))
        w = rows_of(grads, e, lax.axis_index("expert")) * (gain[:, cols] / SEQ)
        weighted[:, cols] = w
        loads[e][0].wait()
        loads[e][1].wait()
        for q in range(count):
            row = w[q : q + 1, :]
            at = [slice(rows * k + SEQ * q, rows * k + SEQ * (q + 1)) for k in range(2)]
            terms = [summed[e, at[0], :], fetched[e, at[0], :].astype(F32), fetched[e, at[1], :].astype(F32)]
            for k, term in enumerate(terms):
                total = fold(term * row)
                spot = slice(SEQ * q, SEQ * (q + 1))
                acc[k, spot] = total if e == 0 else acc[k, spot] + total
    known.wait()
    lanes = iota((SEQ, 128), 1)
    choices = []
    for q in range(count):
        at = slice(SEQ * q, SEQ * (q + 1))
        fact = facts[at, :]
        inv = fact[:, 2:3]
        shrink = inv * inv * inv * (jnp.sum(acc[0, at], axis=1, keepdims=True) / (experts * part))
        grad_gate = []
        for k in range(2):
            along = jnp.sum(acc[1 + k, at], axis=1, keepdims=True)
            grad_gate.append(inv * along - shrink * fact[:, k : k + 1])
        gates = [fact[:, 3 + k : 4 + k] for k in range(2)]
        mean = gates[0] * grad_gate[0] + gates[1] * grad_gate[1]
        choice = jnp.zeros((SEQ, 128), F32)
        for k in range(2):
            chosen = gates[k] * (grad_gate[k] - mean)
            route = fact[:, 5 + k : 6 + k].astype(I32)
            choice = choice + jnp.where(route == lanes, chosen, 0.0)
        choices.append(choice)
        choice = jnp.where(lanes == experts, inv, choice)
        state[at] = jnp.where(lanes == experts + 1, shrink, choice)
    saved = [
        pltpu.make_async_copy(state, state_out, out_sems.at[0]),
        pltpu.make_async_copy(weighted, weighted_out, out_sems.at[1]),
    ]
    for copy in saved:
        copy.start()
    lhs = jnp.transpose(jnp.concatenate(choices, axis=0))[:experts].astype(BF16)
    tiles = part // 128
    for e in range(experts):
        loads[e][2].wait()
        block = jnp.dot(lhs, tok[e], preferred_element_type=F32)
        for k in range(tiles):
            at = experts * (tiles * e + k)
            part_out[at : at + experts, :] = block[:, 128 * k : 128 * (k + 1)]
    for copy in saved:
        copy.wait()


def token_kernel(experts, summed, weighted, state, router, out):
    rows = summed.shape[0]
    known = state[...]
    choice = jnp.where(iota(known.shape, 1) < experts, known, 0.0).astype(BF16)
    through = jnp.dot(choice, router[...], preferred_element_type=F32)
    for q in range(rows // SEQ):
        at = slice(SEQ * q, SEQ * (q + 1))
        inverse, shrink = known[at, experts : experts + 1], known[at, experts + 1 : experts + 2]
        x = inverse * weighted[q : q + 1, :] - shrink * summed[at]
        out[at] = (x + through[SEQ * q : SEQ * (q + 1)]).astype(BF16)


def token_rows(summed, weighted, state, router, experts):
    rows, width = summed.shape
    part = width // experts
    split = lambda count: pl.BlockSpec((count, part), lambda i: (0, i))
    return pl.pallas_call(
        functools.partial(token_kernel, experts),
        grid=(experts,),
        in_specs=[
            split(rows),
            split(weighted.shape[0]),
            pl.BlockSpec((rows, 128), lambda i: (0, 0)),
            split(128),
        ],
        out_specs=split(rows),
        out_shape=jax.ShapeDtypeStruct((rows, width), BF16),
        compiler_params=params(10),
        cost_estimate=cost(2 * rows * 128 * width, 5 << 20),
    )(*in_hbm(summed, weighted, state), router)


def expert_kernel(place, grads, gain, notes, *rest):
    *sources, out, backs, sems = rest
    experts = len(sources)
    _, _, part = grads.shape
    step = pl.program_id(0)
    source = lax.rem(place[0] + experts - step, experts)
    gate, inv, seq = notes[0, :, 0:1], notes[0, :, 1:2], notes[0, :, 2:3]
    capacity = gate.shape[0]
    loads = [pltpu.make_async_copy(sources[r], backs.at[r], sems.at[r]) for r in range(experts)]

    @pl.when(step == 0)
    def _():
        for load in loads:
            load.start()

    for r in range(experts):

        @pl.when(step == r)
        def _():
            loads[r].wait()
            back = backs.at[r]
            acc = jnp.zeros((capacity, 128), F32)
            rows = []
            for e in range(experts):
                cols = slice(part * e, part * (e + 1))
                w = rows_of(grads, e, source) * (gain[:, cols] / SEQ)
                x = jnp.broadcast_to(w[0:1], (capacity, part))
                for s in range(1, ROWS_DEV):
                    x = jnp.where(seq == s, w[s : s + 1], x)
                rows.append(w)
                acc = acc + fold(x * back[:, cols].astype(F32))
            shrink = inv * inv * inv * (jnp.sum(acc, axis=1, keepdims=True) / (experts * part))
            for e in range(experts):
                cols = slice(part * e, part * (e + 1))
                w = rows[e]
                x = jnp.broadcast_to(w[0:1], (capacity, part))
                for s in range(1, ROWS_DEV):
                    x = jnp.where(seq == s, w[s : s + 1], x)
                x = gate * (inv * x - shrink * back[:, cols].astype(F32))
                out[0, :, cols] = x.astype(BF16)


def expert_rows(place, grads, gain, notes, backs):
    experts, capacity = notes.shape[:2]
    width = gain.shape[1]
    whole = lambda shape: pl.BlockSpec(shape, lambda i, p: (0,) * len(shape))
    source = lambda i, p: (lax.rem(p[0] + experts - i, experts), 0, 0)
    return pl.pallas_call(
        expert_kernel,
        grid_spec=pltpu.PrefetchScalarGridSpec(
            num_scalar_prefetch=1,
            grid=(experts,),
            in_specs=[
                whole(grads.shape),
                whole((1, width)),
                pl.BlockSpec((1, capacity, notes.shape[2]), source),
            ]
            + [HBM] * experts,
            out_specs=pl.BlockSpec((1, capacity, width), source),
            scratch_shapes=[
                pltpu.VMEM((experts, capacity, width), BF16),
                pltpu.SemaphoreType.DMA((experts,)),
            ],
        ),
        out_shape=jax.ShapeDtypeStruct((experts, capacity, width), BF16),
        compiler_params=params(16),
        cost_estimate=cost(12 * experts * capacity * width, 9 << 20),
    )(place, grads, gain, notes, *in_hbm(*backs))


def shards(tokens, routes, positives, expert_out, router, norm_gain, loss_scale):
    experts, capacity, width = expert_out.shape[2:]
    rows = tokens.shape[0]
    slots = experts * capacity
    outer = lax.axis_size("u")
    mine = lax.axis_index("expert").astype(I32)
    mine_at = mine[None]
    part = width // experts
    group = PAIR_DEV * experts
    pairs = group * outer * CORES
    scale = 4.0 / math.sqrt(width)
    gain = norm_gain[None, :]
    columns = outer * experts * ROWS_DEV

    received = exchange(expert_out.reshape(experts, capacity, width), "expert").reshape(slots, width)
    gates, slot = routing(tokens, routes, router, experts, capacity)
    lane = jnp.arange(columns, dtype=I32)
    spread_positive = jnp.where(
        (lane % (2 * group)) // ROWS_DEV == mine,
        jnp.where(lane % ROWS_DEV == 0, positives[0], positives[1]) * (lane % ROWS_DEV < PAIR_DEV),
        0,
    ).astype(F32)

    summed, sliced, inverse = forward(tokens, received, slot, gates, gain, experts)
    own = exchange(sliced, "expert").reshape(2 * group, part)
    facts = jnp.concatenate(
        [jnp.zeros((rows, 2), F32), inverse, gates, routes.astype(F32)], axis=1
    )
    facts = jnp.pad(facts, ((0, 0), (0, 128 - facts.shape[1])))
    backs = list(pack(mine_at, summed, slot.T, experts, capacity))

    def move(after, turns):
        after, *ready = lax.optimization_barrier((after, *[backs[r] for r in turns]))
        for r, x in zip(turns, ready):
            backs[r] = lax.ppermute(x, "expert", [(i, (i + r) % experts) for i in range(experts)])
        return after


    def landed(value, turns):
        value, *done = lax.optimization_barrier((value, *[backs[r] for r in turns]))
        for r, x in zip(turns, done):
            backs[r] = x
        return value

    slot_ids = jnp.arange(slots, dtype=I32)[None, :]
    picks = [slot[:, k : k + 1] == slot_ids for k in range(2)]
    gate_slot = jnp.sum(
        jnp.where(picks[0], gates[:, 0:1], 0.0) + jnp.where(picks[1], gates[:, 1:2], 0.0), axis=0
    )
    taken = picks[0] | picks[1]
    inverse_slot = jnp.sum(jnp.where(taken, inverse, 0.0), axis=0)
    sequence = (jnp.arange(rows, dtype=I32) // SEQ).astype(F32)
    sequence_slot = jnp.sum(jnp.where(taken, sequence[:, None], 0.0), axis=0)
    notes = jnp.stack([gate_slot, inverse_slot, sequence_slot, spread_positive])
    notes = jnp.pad(notes, ((0, 4), (0, 0)))

    own, *backs = lax.optimization_barrier((own, *backs))
    near = spread(own, "u", outer)
    facts, fetched = overlaps(summed, received, slot, facts, experts)
    near, facts, fetched = lax.optimization_barrier((near, facts, fetched))
    far = swap_core(near)
    near, far = near.reshape(columns, part), far.reshape(columns, part)
    offered = pl.pallas_call(
        scores_kernel,
        in_specs=[VMEM] * 4,
        out_specs=HBM,
        out_shape=pltpu.HBM((experts, 2 * group + 8, columns), F32),
        scratch_shapes=[pltpu.VMEM((2 * group + 8, columns), F32), pltpu.SemaphoreType.DMA((experts,))],
        compiler_params=params(2),
    )(own, near, far, notes)
    offered = move(offered, TURNS[0])
    gathered = exchange(offered, "expert")
    devices = outer * CORES
    offered, kept = pl.pallas_call(
        functools.partial(totals_kernel, scale),
        in_specs=[VMEM],
        out_specs=[HBM] * 2,
        out_shape=[pltpu.HBM((devices, 8, 128), F32), pltpu.HBM((3 * group, columns), F32)],
        scratch_shapes=[
            pltpu.VMEM((3 * group, columns), F32),
            pltpu.VMEM((devices, 8, 128), F32),
            pltpu.SemaphoreType.DMA(()),
            pltpu.SemaphoreType.DMA(()),
        ],
        compiler_params=params(2),
    )(gathered)
    offered = move(offered, TURNS[1])
    heard = exchange(offered, ("u", "c"))
    heard = landed(heard, TURNS[0][:1])
    offered, loss = pl.pallas_call(
        functools.partial(gradient_kernel, scale),
        in_specs=[SMEM] + [VMEM] * 4,
        out_specs=[HBM, VMEM],
        out_shape=[pltpu.HBM((experts, 2 * group, part), BF16), jax.ShapeDtypeStruct((1, 1), F32)],
        scratch_shapes=[pltpu.VMEM((2 * group, part), BF16), pltpu.SemaphoreType.DMA((experts,))],
        compiler_params=params(2),
    )((loss_scale / pairs)[None], heard, kept, near, far)
    offered = move(offered, TURNS[2])
    grads = exchange(offered, "expert")
    grads = landed(grads, TURNS[0][1:])

    router_part, state, weighted = pl.pallas_call(
        router_kernel,
        in_specs=[VMEM] * 2 + [HBM] * 4,
        out_specs=[VMEM, HBM, HBM],
        out_shape=[
            jax.ShapeDtypeStruct((width * experts // 128, 128), F32),
            pltpu.HBM((rows, 128), F32),
            pltpu.HBM((rows // SEQ, width), F32),
        ],
        scratch_shapes=[
            pltpu.VMEM((experts, rows, part), F32),
            pltpu.VMEM((experts, 2 * rows, part), BF16),
            pltpu.VMEM((experts, rows, part), BF16),
            pltpu.VMEM((rows, 128), F32),
            pltpu.VMEM((rows, 128), F32),
            pltpu.VMEM((rows // SEQ, width), F32),
            pltpu.VMEM((3, rows, 128), F32),
            pltpu.SemaphoreType.DMA((3, experts)),
            pltpu.SemaphoreType.DMA(()),
            pltpu.SemaphoreType.DMA((2,)),
        ],
        compiler_params=params(16),
    )(grads, gain, *in_hbm(summed, fetched, tokens, facts))
    router_part = exchange(router_part.reshape(outer, -1, 128), "u")
    turned = jnp.pad(router.T, ((0, 128 - experts), (0, 0)))
    token_grad = token_rows(summed, weighted, state, turned, experts)
    router_part, token_grad = lax.optimization_barrier((router_part, token_grad))
    router_part = landed(router_part, TURNS[1])
    router_part = jnp.sum(router_part, axis=0)
    router_part = spread(router_part, ("c", "expert"), CORES * experts)
    held = lax.dynamic_slice_in_dim(gathered[:, 2 * group : 2 * group + 3], mine * capacity, capacity, axis=2)
    held = jnp.pad(jnp.transpose(held, (0, 2, 1)), ((0, 0), (0, 0), (0, 5)))
    expert_grad = expert_rows(mine_at, grads, gain, held, backs)
    router_part, expert_grad = lax.optimization_barrier((router_part, expert_grad))
    router_part = jnp.sum(router_part, axis=0)
    router_all = spread(router_part, "u", outer)
    router_grad = router_all.reshape(-1, experts, 128).transpose(1, 0, 2).reshape(experts, width).T
    return token_grad, expert_grad.reshape(1, 1, experts, capacity, width), router_grad, loss[0, 0] / pairs


def solution(mesh):
    outer = mesh.shape["dp"] // CORES
    fine = Mesh(mesh.devices.reshape(outer, CORES, mesh.shape["expert"]), ("u", "c", "expert"))
    everywhere = ("u", "c", "expert")
    return jax.shard_map(
        shards,
        mesh=fine,
        in_specs=(
            P(everywhere, None),
            P(everywhere, None),
            P(everywhere),
            P(("u", "c"), "expert", None, None, None),
            P(),
            P(),
            P(),
        ),
        out_specs=(P(everywhere, None), P(("u", "c"), "expert", None, None, None), P(), P()),
        check_vma=False,
    )
```

```python
import functools
import math

import jax
import jax.numpy as jnp
from jax import lax
from jax.experimental import pallas as pl
from jax.experimental.pallas import tpu as pltpu
from jax.sharding import Mesh, PartitionSpec as P

PAIR_DEV = 2
SEQ = 48
EPS = 1e-05
CORES = 2
ROWS_DEV = 2 * PAIR_DEV
F32 = jnp.float32
BF16 = jnp.bfloat16
I32 = jnp.int32
VMEM = pl.BlockSpec(memory_space=pltpu.VMEM)
SMEM = pl.BlockSpec(memory_space=pltpu.SMEM)
HBM = pl.BlockSpec(memory_space=pltpu.HBM)
NT = (((1,), (1,)), ((), ()))
TURNS = ((4, 1, 7), (3, 5), (2, 6))


def iota(shape, dim):
    return lax.broadcasted_iota(I32, shape, dim)


def params(mib):
    return pltpu.CompilerParams(vmem_limit_bytes=mib << 20)


def cost(flops, moved):
    return pl.CostEstimate(flops=flops, bytes_accessed=moved, transcendentals=0)


def fold(x):
    total = x[:, :128]
    for k in range(1, x.shape[1] // 128):
        total = total + x[:, 128 * k : 128 * (k + 1)]
    return total


def in_hbm(*arrays):
    return [pltpu.with_memory_space_constraint(x, pltpu.HBM) for x in arrays]


def copy_all(copies):
    for copy in copies:
        copy.start()
    for copy in copies:
        copy.wait()


def to_each(source, target, sems):
    copy_all([pltpu.make_async_copy(source, target.at[i], sems.at[i]) for i in range(target.shape[0])])


def swap_core(x):
    return lax.ppermute(x, "c", [(0, 1), (1, 0)])


def exchange(x, axes):
    return lax.all_to_all(x, axes, split_axis=0, concat_axis=0, tiled=True)


def spread(x, axes, size):
    return exchange(jnp.broadcast_to(x[None], (size,) + x.shape), axes)


def routing(tokens, routes, router, experts, capacity):
    logits = jnp.dot(tokens, router, preferred_element_type=F32)
    lanes = jnp.arange(experts, dtype=I32)[None, None, :]
    one_hot = (routes[:, :, None] == lanes).astype(F32)
    chosen = jnp.sum(one_hot * logits[:, None, :], axis=2)
    gates = jax.nn.softmax(chosen, axis=1)
    rows = routes.shape[0]
    hits = jnp.sum(one_hot, axis=1)
    order = jnp.arange(rows, dtype=I32)
    earlier = (order[None, :] < order[:, None]).astype(BF16)
    before = jnp.dot(earlier, hits.astype(BF16), preferred_element_type=F32)
    rank = jnp.sum(one_hot * before[:, None, :], axis=2).astype(I32)
    return gates, routes * capacity + rank


def one_hots(slot, slots):
    ids = iota((slot.shape[0], slots), 1)
    return jnp.concatenate([(slot[:, k : k + 1] == ids).astype(BF16) for k in range(2)], axis=0)


def forward_kernel(
    steps, tok, rec, slot, gate, gain, summed, sliced_out, inverse, held, square, picks, sliced, row_sem, slice_sem
):
    step = pl.program_id(0)
    rows, part = tok.shape

    def keep(e):
        start = pl.multiple_of(e * part, part)
        return pltpu.make_async_copy(held.at[e], summed.at[:, pl.ds(start, part)], row_sem.at[e])

    @pl.when(step == 0)
    def _():
        square[...] = jnp.zeros_like(square)
        picks[...] = one_hots(slot, rec.shape[0])

    for k in range(part // 256):
        cols = slice(256 * k, 256 * (k + 1))
        both = jnp.dot(picks[...], rec[:, cols], preferred_element_type=F32)
        x = tok[:, cols].astype(F32) + gate[:, 0:1] * both[:rows] + gate[:, 1:2] * both[rows:]
        held[step, :, cols] = x
        square[...] += fold(x * x)
    keep(step).start()

    @pl.when(step == steps - 1)
    def _():
        mean = jnp.sum(square[...], axis=1, keepdims=True) / (steps * part)
        scale = lax.rsqrt(mean + EPS)
        inverse[...] = scale
        count = rows // SEQ
        for e in range(steps):
            x = held[e] * scale
            x = jnp.sum(x.reshape(count, SEQ, part), axis=1) / SEQ
            sliced[e] = (x * gain[:, part * e : part * (e + 1)]).astype(BF16)
        offer = pltpu.make_async_copy(sliced, sliced_out, slice_sem)
        offer.start()
        for e in range(steps):
            keep(e).wait()
        offer.wait()


def forward(tokens, received, slot, gates, gain, experts):
    rows, width = tokens.shape
    slots = received.shape[0]
    part = width // experts
    whole = lambda shape: pl.BlockSpec(shape, lambda i: (0,) * len(shape))
    return pl.pallas_call(
        functools.partial(forward_kernel, experts),
        grid=(experts,),
        in_specs=[
            pl.BlockSpec((rows, part), lambda i: (0, i)),
            pl.BlockSpec((slots, part), lambda i: (0, i)),
            whole((rows, 2)),
            whole((rows, 2)),
            whole((1, width)),
        ],
        out_specs=[HBM, HBM, whole((rows, 1))],
        out_shape=[
            pltpu.HBM((rows, width), F32),
            pltpu.HBM((experts, rows // SEQ, part), BF16),
            jax.ShapeDtypeStruct((rows, 1), F32),
        ],
        scratch_shapes=[
            pltpu.VMEM((experts, rows, part), F32),
            pltpu.VMEM((rows, 128), F32),
            pltpu.VMEM((2 * rows, slots), BF16),
            pltpu.VMEM((experts, rows // SEQ, part), BF16),
            pltpu.SemaphoreType.DMA((experts,)),
            pltpu.SemaphoreType.DMA(()),
        ],
        compiler_params=params(14),
        cost_estimate=cost(4 * rows * slots * width, 10 << 20),
    )(tokens, received, slot, gates, gain)


def pack_kernel(place, x, turned, *rest):
    *outs, spot, packed, sems = rest
    step, steps = pl.program_id(0), packed.shape[0]
    rows, part = x.shape
    capacity = outs[0].shape[0]
    slots = spot.shape[0]

    def leave(e, i):
        start = pl.multiple_of(e * part, part)
        return pltpu.make_async_copy(
            packed.at[e, pl.ds(i * capacity, capacity)], outs[i].at[:, pl.ds(start, part)], sems.at[e, i]
        )

    @pl.when(step == 0)
    def _():
        target = lax.rem(iota((slots, rows), 0) + place[0] * capacity, slots)
        spot[...] = ((turned[0:1, :] == target) | (turned[1:2, :] == target)).astype(BF16)

    for k in range(part // 512):
        cols = slice(512 * k, 512 * (k + 1))
        packed[step, :, cols] = jnp.dot(
            spot[...], x[:, cols].astype(BF16), preferred_element_type=F32
        ).astype(BF16)
    for i in range(len(outs)):
        leave(step, i).start()

    @pl.when(step == steps - 1)
    def _():
        for e in range(steps):
            for i in range(len(outs)):
                leave(e, i).wait()


def pack(place, summed, turned, experts, capacity):
    rows, width = summed.shape
    steps = experts // 2
    part = width // steps
    slots = experts * capacity
    return pl.pallas_call(
        pack_kernel,
        grid=(steps,),
        in_specs=[
            SMEM,
            pl.BlockSpec((rows, part), lambda i: (0, i)),
            pl.BlockSpec((2, rows), lambda i: (0, 0)),
        ],
        out_specs=[HBM] * experts,
        out_shape=[pltpu.HBM((capacity, width), BF16)] * experts,
        scratch_shapes=[
            pltpu.VMEM((slots, rows), BF16),
            pltpu.VMEM((steps, slots, part), BF16),
            pltpu.SemaphoreType.DMA((steps, experts)),
        ],
        compiler_params=params(14),
        cost_estimate=cost(2 * rows * slots * width, 7 << 20),
    )(place, *in_hbm(summed), turned)


def overlap_kernel(steps, x, rec, slot, facts, out, fetched, picks, dots):
    step = pl.program_id(0)
    rows, part = x.shape

    @pl.when(step == 0)
    def _():
        dots[...] = jnp.zeros_like(dots)
        picks[...] = one_hots(slot, rec.shape[0])

    for k in range(part // 256):
        cols = slice(256 * k, 256 * (k + 1))
        both = jnp.dot(picks[...], rec[:, cols], preferred_element_type=F32)
        fetched[:, cols] = both.astype(BF16)
        value = x[:, cols]
        dots[:rows] += fold(value * both[:rows])
        dots[rows:] += fold(value * both[rows:])

    @pl.when(step == steps - 1)
    def _():
        lane = iota((rows, 128), 1)
        known = facts[...]
        for k in range(2):
            total = jnp.sum(dots[rows * k : rows * (k + 1)], axis=1, keepdims=True)
            known = jnp.where(lane == k, total, known)
        out[...] = known


def overlaps(summed, received, slot, facts, experts):
    rows, width = summed.shape
    slots = received.shape[0]
    part = width // experts
    whole = lambda shape: pl.BlockSpec(shape, lambda i: (0, 0))
    return pl.pallas_call(
        functools.partial(overlap_kernel, experts),
        grid=(experts,),
        in_specs=[
            pl.BlockSpec((rows, part), lambda i: (0, i)),
            pl.BlockSpec((slots, part), lambda i: (0, i)),
            whole((rows, 2)),
            whole((rows, 128)),
        ],
        out_specs=[whole((rows, 128)), pl.BlockSpec((2 * rows, part), lambda i: (0, i))],
        out_shape=[pltpu.HBM((rows, 128), F32), pltpu.HBM((2 * rows, width), BF16)],
        scratch_shapes=[pltpu.VMEM((2 * rows, slots), BF16), pltpu.VMEM((2 * rows, 128), F32)],
        compiler_params=params(12),
        cost_estimate=cost(4 * rows * slots * width, 10 << 20),
    )(*in_hbm(summed, received), slot, facts)


def lanes_of(shape, dim):
    lane = iota(shape, dim)
    kind = lax.rem(lane, ROWS_DEV)
    return lane, kind, kind >= PAIR_DEV


def picker(group, kind, turned=False):
    wide = 2 * group
    shape, pair, row = ((wide, group), 1, 0) if turned else ((group, wide), 0, 1)
    a = iota(shape, pair)
    b = iota(shape, row)
    source = (a // PAIR_DEV) * ROWS_DEV + lax.rem(a, PAIR_DEV) + PAIR_DEV * kind
    return (source == b).astype(BF16)


def scores_kernel(own, near, far, notes, offered, whole, sems):
    experts, total, columns = offered.shape
    group = experts * PAIR_DEV
    queries, records = [
        jnp.dot(picker(group, kind), own[...], preferred_element_type=F32).astype(BF16) for kind in (0, 1)
    ]
    at_record = lanes_of((group, columns), 1)[2]
    for k, side in enumerate((near, far)):
        every = side[...]
        by_query = lax.dot_general(queries, every, NT, preferred_element_type=F32)
        by_record = lax.dot_general(records, every, NT, preferred_element_type=F32)
        whole[group * k : group * (k + 1)] = jnp.where(at_record, by_query, by_record)
    whole[2 * group :] = notes[...]
    to_each(whole, offered, sems)


def totals_kernel(scale, gathered, offered, kept_out, kept, spread, kept_sem, sem):
    place, core = lax.axis_index("u"), lax.axis_index("c")
    experts, total, columns = gathered.shape
    group = experts * PAIR_DEV
    both = gathered[0]
    for e in range(1, experts):
        both = both + gathered[e]
    positive_lane = both[2 * group + 3 : 2 * group + 4, :]
    near, far = both[:group] * scale, both[group : 2 * group] * scale
    kept[0:group] = near
    kept[group : 2 * group] = far

    shape = (group, columns)
    lane, kind, at_record = lanes_of(shape, 1)
    pair = iota(shape, 0)
    within = lax.rem(lane, 2 * group)
    matching = (within // ROWS_DEV == pair // PAIR_DEV) & (kind == lax.rem(pair, PAIR_DEV))
    here = matching & (lane // (2 * group) == place)
    positive = jnp.sum(jnp.where(here, positive_lane, 0.0), axis=1, keepdims=True)

    low = jnp.float32(-jnp.inf)
    near_records = jnp.where(at_record, near, low)
    far_records = jnp.where(at_record, far, low)
    highest = jnp.maximum(
        jnp.max(near_records, axis=1, keepdims=True), jnp.max(far_records, axis=1, keepdims=True)
    )
    weight = jnp.sum(jnp.exp(near_records - highest), axis=1, keepdims=True) + jnp.sum(
        jnp.exp(far_records - highest), axis=1, keepdims=True
    )
    log_total = highest + jnp.log(weight)
    chosen = jnp.zeros((group, 1), F32)
    for side, where in ((near, core), (far, 1 - core)):
        name = column_names(lane, kind, group, where)
        hit = at_record & (name.astype(F32) == positive)
        chosen = chosen + jnp.sum(jnp.where(hit, side, 0.0), axis=1, keepdims=True)
    kept[2 * group : 3 * group, :128] = jnp.broadcast_to(log_total, (group, 128))
    kept[2 * group : 3 * group, 128:256] = jnp.broadcast_to(positive, (group, 128))
    saved = pltpu.make_async_copy(kept, kept_out, kept_sem)
    saved.start()
    row_loss = log_total - chosen

    total_lane = jnp.sum(jnp.where(here, log_total, 0.0), axis=0, keepdims=True)
    loss_lane = jnp.sum(jnp.where(here, row_loss, 0.0), axis=0, keepdims=True)
    own_lane = jnp.where(lane[0:1] // (2 * group) == place, positive_lane, 0.0)
    pieces = [x[:, 128 * k : 128 * (k + 1)] for x in (total_lane, own_lane) for k in range(columns // 128)]
    loss_pieces = [
        pltpu.roll(loss_lane, PAIR_DEV, 1)[:, 128 * k : 128 * (k + 1)] for k in range(columns // 128)
    ]
    pieces = [a + b for a, b in zip(pieces, loss_pieces)] + pieces[columns // 128 :]
    message = jnp.concatenate(pieces, axis=0)
    for d in range(spread.shape[0]):
        spread[d] = message
    copy_all([pltpu.make_async_copy(spread, offered, sem)])
    saved.wait()


def column_names(lane, kind, group, core):
    wide = 2 * group
    block = (lane // wide) * CORES + core
    return block * group + (lax.rem(lane, wide) // ROWS_DEV) * PAIR_DEV + lax.rem(kind, PAIR_DEV)


def gradient_kernel(scale, factor, heard, kept, near, far, offered, loss, whole, sems):
    place, core = lax.axis_index("u"), lax.axis_index("c")
    experts, wide, columns = offered.shape
    group = wide // 2
    outer_size = heard.shape[0] // CORES
    pieces = columns // 128
    shape = (group, columns)
    lane, kind, at_record = lanes_of(shape, 1)
    pair = iota(shape, 0)
    own_name = (place * CORES + core) * group + iota((group, 1), 0)
    own_total = kept[2 * group : 3 * group, 0:1]
    own_positive = kept[2 * group : 3 * group, 128:129]
    result = jnp.zeros((wide, columns), F32)
    losses = jnp.zeros((1, columns), F32)
    for k, (side, where) in enumerate(((near, core), (far, 1 - core))):
        told = heard[where]
        for u in range(1, outer_size):
            told = told + heard[u * CORES + where]
        total = jnp.concatenate([told[i : i + 1] for i in range(pieces)], axis=1)
        positive = jnp.concatenate([told[pieces + i : pieces + i + 1] for i in range(pieces)], axis=1)
        losses = losses + jnp.where(at_record[0:1], total, 0.0)
        value = kept[group * k : group * (k + 1), :]
        name = column_names(lane, kind, group, where).astype(F32)
        hit = jnp.where(name == own_positive, 1.0, 0.0)
        by_query = (jnp.exp(value - own_total) - hit) * factor[0]
        by_query = jnp.where(at_record, by_query, 0.0).astype(BF16)
        hit = jnp.where(positive == own_name.astype(F32), 1.0, 0.0)
        by_record = (jnp.exp(jnp.where(at_record, 0.0, value - total)) - hit) * factor[0]
        by_record = jnp.where(at_record, 0.0, by_record).astype(BF16)
        rows = jnp.dot(picker(group, 0, True), by_query, preferred_element_type=F32) + jnp.dot(
            picker(group, 1, True), by_record, preferred_element_type=F32
        )
        result = result + jnp.dot(rows.astype(BF16), side[...], preferred_element_type=F32)
    whole[...] = (result * scale).astype(BF16)
    to_each(whole, offered, sems)
    loss[...] = jnp.sum(losses, axis=1, keepdims=True)


def rows_of(grads, e, index):
    tile = grads[e, pl.ds(pl.multiple_of((index // 4) * 16, 16), 16), :].astype(F32)
    piece = lax.rem(index, 4)
    quarters = [tile[ROWS_DEV * k : ROWS_DEV * (k + 1)] for k in range(4)]
    half = jnp.where(piece < 2, quarters[0], quarters[2]), jnp.where(piece < 2, quarters[1], quarters[3])
    return jnp.where(lax.rem(piece, 2) == 0, half[0], half[1])


def router_kernel(
    grads, gain, summed_in, fetched_in, tok_in, facts_in, part_out, state_out, weighted_out,
    summed, fetched, tok, facts, state, weighted, acc, sems, facts_sem, out_sems
):
    experts, _, part = grads.shape
    rows = summed.shape[1]
    count = rows // SEQ
    sources = ((summed_in, summed), (fetched_in, fetched), (tok_in, tok))

    def load(e):
        cols = pl.ds(e * part, part)
        return [
            pltpu.make_async_copy(a.at[:, cols], b.at[e], sems.at[k, e]) for k, (a, b) in enumerate(sources)
        ]

    known = pltpu.make_async_copy(facts_in, facts, facts_sem)
    loads = [load(e) for e in range(experts)]
    for e in range(experts):
        loads[e][0].start()
        loads[e][1].start()
    known.start()
    for e in range(experts):
        loads[e][2].start()

    for e in range(experts):
        cols = slice(part * e, part * (e + 1))
        w = rows_of(grads, e, lax.axis_index("expert")) * (gain[:, cols] / SEQ)
        weighted[:, cols] = w
        loads[e][0].wait()
        loads[e][1].wait()
        for q in range(count):
            row = w[q : q + 1, :]
            at = [slice(rows * k + SEQ * q, rows * k + SEQ * (q + 1)) for k in range(2)]
            terms = [summed[e, at[0], :], fetched[e, at[0], :].astype(F32), fetched[e, at[1], :].astype(F32)]
            for k, term in enumerate(terms):
                total = fold(term * row)
                spot = slice(SEQ * q, SEQ * (q + 1))
                acc[k, spot] = total if e == 0 else acc[k, spot] + total
    known.wait()
    lanes = iota((SEQ, 128), 1)
    choices = []
    for q in range(count):
        at = slice(SEQ * q, SEQ * (q + 1))
        fact = facts[at, :]
        inv = fact[:, 2:3]
        shrink = inv * inv * inv * (jnp.sum(acc[0, at], axis=1, keepdims=True) / (experts * part))
        grad_gate = []
        for k in range(2):
            along = jnp.sum(acc[1 + k, at], axis=1, keepdims=True)
            grad_gate.append(inv * along - shrink * fact[:, k : k + 1])
        gates = [fact[:, 3 + k : 4 + k] for k in range(2)]
        mean = gates[0] * grad_gate[0] + gates[1] * grad_gate[1]
        choice = jnp.zeros((SEQ, 128), F32)
        for k in range(2):
            chosen = gates[k] * (grad_gate[k] - mean)
            route = fact[:, 5 + k : 6 + k].astype(I32)
            choice = choice + jnp.where(route == lanes, chosen, 0.0)
        choices.append(choice)
        choice = jnp.where(lanes == experts, inv, choice)
        state[at] = jnp.where(lanes == experts + 1, shrink, choice)
    saved = [
        pltpu.make_async_copy(state, state_out, out_sems.at[0]),
        pltpu.make_async_copy(weighted, weighted_out, out_sems.at[1]),
    ]
    for copy in saved:
        copy.start()
    lhs = jnp.transpose(jnp.concatenate(choices, axis=0))[:experts].astype(BF16)
    tiles = part // 128
    for e in range(experts):
        loads[e][2].wait()
        block = jnp.dot(lhs, tok[e], preferred_element_type=F32)
        for k in range(tiles):
            at = experts * (tiles * e + k)
            part_out[at : at + experts, :] = block[:, 128 * k : 128 * (k + 1)]
    for copy in saved:
        copy.wait()


def token_kernel(experts, summed, weighted, state, router, out):
    rows = summed.shape[0]
    known = state[...]
    choice = jnp.where(iota(known.shape, 1) < experts, known, 0.0).astype(BF16)
    through = jnp.dot(choice, router[...], preferred_element_type=F32)
    for q in range(rows // SEQ):
        at = slice(SEQ * q, SEQ * (q + 1))
        inverse, shrink = known[at, experts : experts + 1], known[at, experts + 1 : experts + 2]
        x = inverse * weighted[q : q + 1, :] - shrink * summed[at]
        out[at] = (x + through[SEQ * q : SEQ * (q + 1)]).astype(BF16)


def token_rows(summed, weighted, state, router, experts):
    rows, width = summed.shape
    part = width // experts
    split = lambda count: pl.BlockSpec((count, part), lambda i: (0, i))
    return pl.pallas_call(
        functools.partial(token_kernel, experts),
        grid=(experts,),
        in_specs=[
            split(rows),
            split(weighted.shape[0]),
            pl.BlockSpec((rows, 128), lambda i: (0, 0)),
            split(128),
        ],
        out_specs=split(rows),
        out_shape=jax.ShapeDtypeStruct((rows, width), BF16),
        compiler_params=params(10),
        cost_estimate=cost(2 * rows * 128 * width, 5 << 20),
    )(*in_hbm(summed, weighted, state), router)


def expert_kernel(count, source, grads, gain, notes, *rest):
    sources, (out, backs, sems) = rest[:count], rest[-3:]
    experts, _, part = grads.shape
    step = pl.program_id(0)
    gate, inv, seq = notes[0, :, 0:1], notes[0, :, 1:2], notes[0, :, 2:3]
    capacity = gate.shape[0]
    loads = [pltpu.make_async_copy(sources[r], backs.at[r], sems.at[r]) for r in range(count)]

    @pl.when(step == 0)
    def _():
        for load in loads:
            load.start()

    for r in range(count):

        @pl.when(step == r)
        def _():
            loads[r].wait()

    def gradient_rows(e):
        w = rows_of(grads, e, source[step]) * (gain[:, part * e : part * (e + 1)] / SEQ)
        x = jnp.broadcast_to(w[0:1], (capacity, part))
        for s in range(1, ROWS_DEV):
            x = jnp.where(seq == s, w[s : s + 1], x)
        return x

    acc = jnp.zeros((capacity, 128), F32)
    for e in range(experts):
        back = backs[step, :, part * e : part * (e + 1)].astype(F32)
        acc = acc + fold(gradient_rows(e) * back)
    shrink = inv * inv * inv * (jnp.sum(acc, axis=1, keepdims=True) / (experts * part))
    keep, drop = gate * inv, gate * shrink
    for e in range(experts):
        cols = slice(part * e, part * (e + 1))
        out[0, :, cols] = (keep * gradient_rows(e) - drop * backs[step, :, cols].astype(F32)).astype(BF16)


def expert_rows(source, grads, gain, notes, backs, before=None):
    experts, capacity = notes.shape[:2]
    width = gain.shape[1]
    count = len(backs)
    whole = lambda shape: pl.BlockSpec(shape, lambda i, p: (0,) * len(shape))
    block = lambda i, p: (p[i], 0, 0)
    kept = [] if before is None else [before]
    return pl.pallas_call(
        functools.partial(expert_kernel, count),
        grid_spec=pltpu.PrefetchScalarGridSpec(
            num_scalar_prefetch=1,
            grid=(count,),
            in_specs=[
                whole(grads.shape),
                whole((1, width)),
                pl.BlockSpec((1, capacity, notes.shape[2]), block),
            ]
            + [HBM] * (count + len(kept)),
            out_specs=pl.BlockSpec((1, capacity, width), block),
            scratch_shapes=[
                pltpu.VMEM((count, capacity, width), BF16),
                pltpu.SemaphoreType.DMA((count,)),
            ],
        ),
        out_shape=jax.ShapeDtypeStruct((experts, capacity, width), BF16),
        input_output_aliases={4 + count: 0} if kept else {},
        compiler_params=params(16),
        cost_estimate=cost(12 * count * capacity * width, count << 20),
    )(source, grads, gain, notes, *in_hbm(*backs), *kept)


def shards(tokens, routes, positives, expert_out, router, norm_gain, loss_scale):
    experts, capacity, width = expert_out.shape[2:]
    rows = tokens.shape[0]
    slots = experts * capacity
    outer = lax.axis_size("u")
    mine = lax.axis_index("expert").astype(I32)
    mine_at = mine[None]
    part = width // experts
    group = PAIR_DEV * experts
    pairs = group * outer * CORES
    scale = 4.0 / math.sqrt(width)
    gain = norm_gain[None, :]
    columns = outer * experts * ROWS_DEV

    received = exchange(expert_out.reshape(experts, capacity, width), "expert").reshape(slots, width)
    gates, slot = routing(tokens, routes, router, experts, capacity)
    lane = jnp.arange(columns, dtype=I32)
    spread_positive = jnp.where(
        (lane % (2 * group)) // ROWS_DEV == mine,
        jnp.where(lane % ROWS_DEV == 0, positives[0], positives[1]) * (lane % ROWS_DEV < PAIR_DEV),
        0,
    ).astype(F32)

    summed, sliced, inverse = forward(tokens, received, slot, gates, gain, experts)
    own = exchange(sliced, "expert").reshape(2 * group, part)
    facts = jnp.concatenate(
        [jnp.zeros((rows, 2), F32), inverse, gates, routes.astype(F32)], axis=1
    )
    facts = jnp.pad(facts, ((0, 0), (0, 128 - facts.shape[1])))
    backs = list(pack(mine_at, summed, slot.T, experts, capacity))

    def move(after, turns):
        after, *ready = lax.optimization_barrier((after, *[backs[r] for r in turns]))
        for r, x in zip(turns, ready):
            backs[r] = lax.ppermute(x, "expert", [(i, (i + r) % experts) for i in range(experts)])
        return after


    def landed(value, turns):
        value, *done = lax.optimization_barrier((value, *[backs[r] for r in turns]))
        for r, x in zip(turns, done):
            backs[r] = x
        return value

    slot_ids = jnp.arange(slots, dtype=I32)[None, :]
    picks = [slot[:, k : k + 1] == slot_ids for k in range(2)]
    gate_slot = jnp.sum(
        jnp.where(picks[0], gates[:, 0:1], 0.0) + jnp.where(picks[1], gates[:, 1:2], 0.0), axis=0
    )
    taken = picks[0] | picks[1]
    inverse_slot = jnp.sum(jnp.where(taken, inverse, 0.0), axis=0)
    sequence = (jnp.arange(rows, dtype=I32) // SEQ).astype(F32)
    sequence_slot = jnp.sum(jnp.where(taken, sequence[:, None], 0.0), axis=0)
    notes = jnp.stack([gate_slot, inverse_slot, sequence_slot, spread_positive])
    notes = jnp.pad(notes, ((0, 4), (0, 0)))

    own, *backs = lax.optimization_barrier((own, *backs))
    near = spread(own, "u", outer)
    facts, fetched = overlaps(summed, received, slot, facts, experts)
    near, facts, fetched = lax.optimization_barrier((near, facts, fetched))
    far = swap_core(near)
    near, far = near.reshape(columns, part), far.reshape(columns, part)
    offered = pl.pallas_call(
        scores_kernel,
        in_specs=[VMEM] * 4,
        out_specs=HBM,
        out_shape=pltpu.HBM((experts, 2 * group + 8, columns), F32),
        scratch_shapes=[pltpu.VMEM((2 * group + 8, columns), F32), pltpu.SemaphoreType.DMA((experts,))],
        compiler_params=params(2),
    )(own, near, far, notes)
    offered = move(offered, TURNS[0])
    gathered = exchange(offered, "expert")
    devices = outer * CORES
    offered, kept = pl.pallas_call(
        functools.partial(totals_kernel, scale),
        in_specs=[VMEM],
        out_specs=[HBM] * 2,
        out_shape=[pltpu.HBM((devices, 8, 128), F32), pltpu.HBM((3 * group, columns), F32)],
        scratch_shapes=[
            pltpu.VMEM((3 * group, columns), F32),
            pltpu.VMEM((devices, 8, 128), F32),
            pltpu.SemaphoreType.DMA(()),
            pltpu.SemaphoreType.DMA(()),
        ],
        compiler_params=params(2),
    )(gathered)
    heard = exchange(offered, ("u", "c"))
    heard = landed(heard, TURNS[0][:1])
    offered, loss = pl.pallas_call(
        functools.partial(gradient_kernel, scale),
        in_specs=[SMEM] + [VMEM] * 4,
        out_specs=[HBM, VMEM],
        out_shape=[pltpu.HBM((experts, 2 * group, part), BF16), jax.ShapeDtypeStruct((1, 1), F32)],
        scratch_shapes=[pltpu.VMEM((2 * group, part), BF16), pltpu.SemaphoreType.DMA((experts,))],
        compiler_params=params(2),
    )((loss_scale / pairs)[None], heard, kept, near, far)
    offered = move(offered, TURNS[1])
    grads = exchange(offered, "expert")
    grads = landed(grads, TURNS[0][1:])

    router_part, state, weighted = pl.pallas_call(
        router_kernel,
        in_specs=[VMEM] * 2 + [HBM] * 4,
        out_specs=[VMEM, HBM, HBM],
        out_shape=[
            jax.ShapeDtypeStruct((width * experts // 128, 128), F32),
            pltpu.HBM((rows, 128), F32),
            pltpu.HBM((rows // SEQ, width), F32),
        ],
        scratch_shapes=[
            pltpu.VMEM((experts, rows, part), F32),
            pltpu.VMEM((experts, 2 * rows, part), BF16),
            pltpu.VMEM((experts, rows, part), BF16),
            pltpu.VMEM((rows, 128), F32),
            pltpu.VMEM((rows, 128), F32),
            pltpu.VMEM((rows // SEQ, width), F32),
            pltpu.VMEM((3, rows, 128), F32),
            pltpu.SemaphoreType.DMA((3, experts)),
            pltpu.SemaphoreType.DMA(()),
            pltpu.SemaphoreType.DMA((2,)),
        ],
        compiler_params=params(16),
    )(grads, gain, *in_hbm(summed, fetched, tokens, facts))
    router_part = move(router_part, TURNS[2])
    router_part = exchange(router_part.reshape(outer, -1, 128), "u")
    router_part = jnp.sum(router_part, axis=0)
    router_part = spread(router_part, ("c", "expert"), CORES * experts)
    held = lax.dynamic_slice_in_dim(gathered[:, 2 * group : 2 * group + 3], mine * capacity, capacity, axis=2)
    held = jnp.pad(jnp.transpose(held, (0, 2, 1)), ((0, 0), (0, 0), (0, 5)))
    turned = jnp.pad(router.T, ((0, 128 - experts), (0, 0)))
    token_grad = token_rows(summed, weighted, state, turned, experts)
    parts = [(0,) + TURNS[0] + TURNS[1], TURNS[2]]
    places = [(mine + experts - jnp.array(turns, I32)) % experts for turns in parts]
    expert_grad = expert_rows(places[0], grads, gain, held, [backs[r] for r in parts[0]])
    router_part, token_grad, expert_grad = lax.optimization_barrier((router_part, token_grad, expert_grad))
    router_part = jnp.sum(router_part, axis=0)
    router_all = spread(router_part, "u", outer)
    expert_grad = expert_rows(places[1], grads, gain, held, [backs[r] for r in parts[1]], expert_grad)
    router_all, expert_grad = lax.optimization_barrier((router_all, expert_grad))
    router_grad = router_all.reshape(-1, experts, 128).transpose(1, 0, 2).reshape(experts, width).T
    return token_grad, expert_grad.reshape(1, 1, experts, capacity, width), router_grad, loss[0, 0] / pairs


def solution(mesh):
    outer = mesh.shape["dp"] // CORES
    fine = Mesh(mesh.devices.reshape(outer, CORES, mesh.shape["expert"]), ("u", "c", "expert"))
    everywhere = ("u", "c", "expert")
    return jax.shard_map(
        shards,
        mesh=fine,
        in_specs=(
            P(everywhere, None),
            P(everywhere, None),
            P(everywhere),
            P(("u", "c"), "expert", None, None, None),
            P(),
            P(),
            P(),
        ),
        out_specs=(P(everywhere, None), P(("u", "c"), "expert", None, None, None), P(), P()),
        check_vma=False,
    )
```

```python
import functools
import math

import jax
import jax.numpy as jnp
from jax import lax
from jax.experimental import pallas as pl
from jax.experimental.pallas import tpu as pltpu
from jax.sharding import Mesh, PartitionSpec as P

PAIR_DEV = 2
SEQ = 48
EPS = 1e-05
CORES = 2
ROWS_DEV = 2 * PAIR_DEV
F32 = jnp.float32
BF16 = jnp.bfloat16
I32 = jnp.int32
VMEM = pl.BlockSpec(memory_space=pltpu.VMEM)
SMEM = pl.BlockSpec(memory_space=pltpu.SMEM)
HBM = pl.BlockSpec(memory_space=pltpu.HBM)
NT = (((1,), (1,)), ((), ()))
TURNS = ((1, 3, 2), (5, 7), (4, 6))
HALVES, RING = 2, 4


def iota(shape, dim):
    return lax.broadcasted_iota(I32, shape, dim)


def params(mib):
    return pltpu.CompilerParams(vmem_limit_bytes=mib << 20)


def cost(flops, moved):
    return pl.CostEstimate(flops=flops, bytes_accessed=moved, transcendentals=0)


def fold(x):
    total = x[:, :128]
    for k in range(1, x.shape[1] // 128):
        total = total + x[:, 128 * k : 128 * (k + 1)]
    return total


def in_hbm(*arrays):
    return [pltpu.with_memory_space_constraint(x, pltpu.HBM) for x in arrays]


def shifted(index, halves, along):
    return lax.rem(index // RING + halves, HALVES) * RING + lax.rem(lax.rem(index, RING) + along, RING)


def copy_all(copies):
    for copy in copies:
        copy.start()
    for copy in copies:
        copy.wait()


def to_each(source, target, sems):
    copy_all([pltpu.make_async_copy(source, target.at[i], sems.at[i]) for i in range(target.shape[0])])


def swap_core(x):
    return lax.ppermute(x, "c", [(0, 1), (1, 0)])


def exchange(x, axes):
    return lax.all_to_all(x, axes, split_axis=0, concat_axis=0, tiled=True)


def spread(x, axes, size):
    return exchange(jnp.broadcast_to(x[None], (size,) + x.shape), axes)


def routing(tokens, routes, router, experts, capacity):
    logits = jnp.dot(tokens, router, preferred_element_type=F32)
    lanes = jnp.arange(experts, dtype=I32)[None, None, :]
    one_hot = (routes[:, :, None] == lanes).astype(F32)
    chosen = jnp.sum(one_hot * logits[:, None, :], axis=2)
    gates = jax.nn.softmax(chosen, axis=1)
    rows = routes.shape[0]
    hits = jnp.sum(one_hot, axis=1)
    order = jnp.arange(rows, dtype=I32)
    earlier = (order[None, :] < order[:, None]).astype(BF16)
    before = jnp.dot(earlier, hits.astype(BF16), preferred_element_type=F32)
    rank = jnp.sum(one_hot * before[:, None, :], axis=2).astype(I32)
    return gates, routes * capacity + rank


def one_hots(slot, slots):
    ids = iota((slot.shape[0], slots), 1)
    return jnp.concatenate([(slot[:, k : k + 1] == ids).astype(BF16) for k in range(2)], axis=0)


def forward_kernel(
    steps, tok, rec, slot, gate, gain, summed, sliced_out, inverse, held, square, picks, sliced, row_sem, slice_sem
):
    step = pl.program_id(0)
    rows, part = tok.shape

    def keep(e):
        start = pl.multiple_of(e * part, part)
        return pltpu.make_async_copy(held.at[e], summed.at[:, pl.ds(start, part)], row_sem.at[e])

    @pl.when(step == 0)
    def _():
        square[...] = jnp.zeros_like(square)
        picks[...] = one_hots(slot, rec.shape[0])

    for k in range(part // 256):
        cols = slice(256 * k, 256 * (k + 1))
        both = jnp.dot(picks[...], rec[:, cols], preferred_element_type=F32)
        x = tok[:, cols].astype(F32) + gate[:, 0:1] * both[:rows] + gate[:, 1:2] * both[rows:]
        held[step, :, cols] = x
        square[...] += fold(x * x)
    keep(step).start()

    @pl.when(step == steps - 1)
    def _():
        mean = jnp.sum(square[...], axis=1, keepdims=True) / (steps * part)
        scale = lax.rsqrt(mean + EPS)
        inverse[...] = scale
        count = rows // SEQ
        for e in range(steps):
            x = held[e] * scale
            x = jnp.sum(x.reshape(count, SEQ, part), axis=1) / SEQ
            sliced[e] = (x * gain[:, part * e : part * (e + 1)]).astype(BF16)
        offer = pltpu.make_async_copy(sliced, sliced_out, slice_sem)
        offer.start()
        for e in range(steps):
            keep(e).wait()
        offer.wait()


def forward(tokens, received, slot, gates, gain, experts):
    rows, width = tokens.shape
    slots = received.shape[0]
    part = width // experts
    whole = lambda shape: pl.BlockSpec(shape, lambda i: (0,) * len(shape))
    return pl.pallas_call(
        functools.partial(forward_kernel, experts),
        grid=(experts,),
        in_specs=[
            pl.BlockSpec((rows, part), lambda i: (0, i)),
            pl.BlockSpec((slots, part), lambda i: (0, i)),
            whole((rows, 2)),
            whole((rows, 2)),
            whole((1, width)),
        ],
        out_specs=[HBM, HBM, whole((rows, 1))],
        out_shape=[
            pltpu.HBM((rows, width), F32),
            pltpu.HBM((experts, rows // SEQ, part), BF16),
            jax.ShapeDtypeStruct((rows, 1), F32),
        ],
        scratch_shapes=[
            pltpu.VMEM((experts, rows, part), F32),
            pltpu.VMEM((rows, 128), F32),
            pltpu.VMEM((2 * rows, slots), BF16),
            pltpu.VMEM((experts, rows // SEQ, part), BF16),
            pltpu.SemaphoreType.DMA((experts,)),
            pltpu.SemaphoreType.DMA(()),
        ],
        compiler_params=params(14),
        cost_estimate=cost(4 * rows * slots * width, 10 << 20),
    )(tokens, received, slot, gates, gain)


def pack_kernel(place, x, turned, *rest):
    *outs, spot, packed, sems = rest
    step, steps = pl.program_id(0), packed.shape[0]
    rows, part = x.shape
    capacity = outs[0].shape[0]
    slots = spot.shape[0]

    def leave(e, i):
        start = pl.multiple_of(e * part, part)
        return pltpu.make_async_copy(
            packed.at[e, pl.ds(i * capacity, capacity)], outs[i].at[:, pl.ds(start, part)], sems.at[e, i]
        )

    @pl.when(step == 0)
    def _():
        row = iota((slots, 1), 0)
        chunk = row // capacity
        target = shifted(place[0], chunk // RING, lax.rem(chunk, RING)) * capacity + lax.rem(row, capacity)
        spot[...] = ((turned[0:1, :] == target) | (turned[1:2, :] == target)).astype(BF16)

    for k in range(part // 512):
        cols = slice(512 * k, 512 * (k + 1))
        packed[step, :, cols] = jnp.dot(
            spot[...], x[:, cols].astype(BF16), preferred_element_type=F32
        ).astype(BF16)
    for i in range(len(outs)):
        leave(step, i).start()

    @pl.when(step == steps - 1)
    def _():
        for e in range(steps):
            for i in range(len(outs)):
                leave(e, i).wait()


def pack(place, summed, turned, experts, capacity):
    rows, width = summed.shape
    steps = experts // 2
    part = width // steps
    slots = experts * capacity
    return pl.pallas_call(
        pack_kernel,
        grid=(steps,),
        in_specs=[
            SMEM,
            pl.BlockSpec((rows, part), lambda i: (0, i)),
            pl.BlockSpec((2, rows), lambda i: (0, 0)),
        ],
        out_specs=[HBM] * experts,
        out_shape=[pltpu.HBM((capacity, width), BF16)] * experts,
        scratch_shapes=[
            pltpu.VMEM((slots, rows), BF16),
            pltpu.VMEM((steps, slots, part), BF16),
            pltpu.SemaphoreType.DMA((steps, experts)),
        ],
        compiler_params=params(14),
        cost_estimate=cost(2 * rows * slots * width, 7 << 20),
    )(place, *in_hbm(summed), turned)


def overlap_kernel(steps, x, rec, slot, facts, out, fetched, picks, dots):
    step = pl.program_id(0)
    rows, part = x.shape

    @pl.when(step == 0)
    def _():
        dots[...] = jnp.zeros_like(dots)
        picks[...] = one_hots(slot, rec.shape[0])

    for k in range(part // 256):
        cols = slice(256 * k, 256 * (k + 1))
        both = jnp.dot(picks[...], rec[:, cols], preferred_element_type=F32)
        fetched[:, cols] = both.astype(BF16)
        value = x[:, cols]
        dots[:rows] += fold(value * both[:rows])
        dots[rows:] += fold(value * both[rows:])

    @pl.when(step == steps - 1)
    def _():
        lane = iota((rows, 128), 1)
        known = facts[...]
        for k in range(2):
            total = jnp.sum(dots[rows * k : rows * (k + 1)], axis=1, keepdims=True)
            known = jnp.where(lane == k, total, known)
        out[...] = known


def overlaps(summed, received, slot, facts, experts):
    rows, width = summed.shape
    slots = received.shape[0]
    part = width // experts
    whole = lambda shape: pl.BlockSpec(shape, lambda i: (0, 0))
    return pl.pallas_call(
        functools.partial(overlap_kernel, experts),
        grid=(experts,),
        in_specs=[
            pl.BlockSpec((rows, part), lambda i: (0, i)),
            pl.BlockSpec((slots, part), lambda i: (0, i)),
            whole((rows, 2)),
            whole((rows, 128)),
        ],
        out_specs=[whole((rows, 128)), pl.BlockSpec((2 * rows, part), lambda i: (0, i))],
        out_shape=[pltpu.HBM((rows, 128), F32), pltpu.HBM((2 * rows, width), BF16)],
        scratch_shapes=[pltpu.VMEM((2 * rows, slots), BF16), pltpu.VMEM((2 * rows, 128), F32)],
        compiler_params=params(12),
        cost_estimate=cost(4 * rows * slots * width, 10 << 20),
    )(*in_hbm(summed, received), slot, facts)


def lanes_of(shape, dim):
    lane = iota(shape, dim)
    kind = lax.rem(lane, ROWS_DEV)
    return lane, kind, kind >= PAIR_DEV


def picker(group, kind, turned=False):
    wide = 2 * group
    shape, pair, row = ((wide, group), 1, 0) if turned else ((group, wide), 0, 1)
    a = iota(shape, pair)
    b = iota(shape, row)
    source = (a // PAIR_DEV) * ROWS_DEV + lax.rem(a, PAIR_DEV) + PAIR_DEV * kind
    return (source == b).astype(BF16)


def scores_kernel(own, near, far, notes, offered, whole, sems):
    experts, total, columns = offered.shape
    group = experts * PAIR_DEV
    queries, records = [
        jnp.dot(picker(group, kind), own[...], preferred_element_type=F32).astype(BF16) for kind in (0, 1)
    ]
    at_record = lanes_of((group, columns), 1)[2]
    for k, side in enumerate((near, far)):
        every = side[...]
        by_query = lax.dot_general(queries, every, NT, preferred_element_type=F32)
        by_record = lax.dot_general(records, every, NT, preferred_element_type=F32)
        whole[group * k : group * (k + 1)] = jnp.where(at_record, by_query, by_record)
    whole[2 * group :] = notes[...]
    to_each(whole, offered, sems)


def totals_kernel(scale, gathered, offered, kept_out, kept, spread, kept_sem, sem):
    place, core = lax.axis_index("u"), lax.axis_index("c")
    experts, total, columns = gathered.shape
    group = experts * PAIR_DEV
    both = gathered[0]
    for e in range(1, experts):
        both = both + gathered[e]
    positive_lane = both[2 * group + 3 : 2 * group + 4, :]
    near, far = both[:group] * scale, both[group : 2 * group] * scale
    kept[0:group] = near
    kept[group : 2 * group] = far

    shape = (group, columns)
    lane, kind, at_record = lanes_of(shape, 1)
    pair = iota(shape, 0)
    within = lax.rem(lane, 2 * group)
    matching = (within // ROWS_DEV == pair // PAIR_DEV) & (kind == lax.rem(pair, PAIR_DEV))
    here = matching & (lane // (2 * group) == place)
    positive = jnp.sum(jnp.where(here, positive_lane, 0.0), axis=1, keepdims=True)

    low = jnp.float32(-jnp.inf)
    near_records = jnp.where(at_record, near, low)
    far_records = jnp.where(at_record, far, low)
    highest = jnp.maximum(
        jnp.max(near_records, axis=1, keepdims=True), jnp.max(far_records, axis=1, keepdims=True)
    )
    weight = jnp.sum(jnp.exp(near_records - highest), axis=1, keepdims=True) + jnp.sum(
        jnp.exp(far_records - highest), axis=1, keepdims=True
    )
    log_total = highest + jnp.log(weight)
    chosen = jnp.zeros((group, 1), F32)
    for side, where in ((near, core), (far, 1 - core)):
        name = column_names(lane, kind, group, where)
        hit = at_record & (name.astype(F32) == positive)
        chosen = chosen + jnp.sum(jnp.where(hit, side, 0.0), axis=1, keepdims=True)
    kept[2 * group : 3 * group, :128] = jnp.broadcast_to(log_total, (group, 128))
    kept[2 * group : 3 * group, 128:256] = jnp.broadcast_to(positive, (group, 128))
    saved = pltpu.make_async_copy(kept, kept_out, kept_sem)
    saved.start()
    row_loss = log_total - chosen

    total_lane = jnp.sum(jnp.where(here, log_total, 0.0), axis=0, keepdims=True)
    loss_lane = jnp.sum(jnp.where(here, row_loss, 0.0), axis=0, keepdims=True)
    own_lane = jnp.where(lane[0:1] // (2 * group) == place, positive_lane, 0.0)
    pieces = [x[:, 128 * k : 128 * (k + 1)] for x in (total_lane, own_lane) for k in range(columns // 128)]
    loss_pieces = [
        pltpu.roll(loss_lane, PAIR_DEV, 1)[:, 128 * k : 128 * (k + 1)] for k in range(columns // 128)
    ]
    pieces = [a + b for a, b in zip(pieces, loss_pieces)] + pieces[columns // 128 :]
    message = jnp.concatenate(pieces, axis=0)
    for d in range(spread.shape[0]):
        spread[d] = message
    copy_all([pltpu.make_async_copy(spread, offered, sem)])
    saved.wait()


def column_names(lane, kind, group, core):
    wide = 2 * group
    block = (lane // wide) * CORES + core
    return block * group + (lax.rem(lane, wide) // ROWS_DEV) * PAIR_DEV + lax.rem(kind, PAIR_DEV)


def gradient_kernel(scale, factor, heard, kept, near, far, offered, loss, whole, sems):
    place, core = lax.axis_index("u"), lax.axis_index("c")
    experts, wide, columns = offered.shape
    group = wide // 2
    outer_size = heard.shape[0] // CORES
    pieces = columns // 128
    shape = (group, columns)
    lane, kind, at_record = lanes_of(shape, 1)
    pair = iota(shape, 0)
    own_name = (place * CORES + core) * group + iota((group, 1), 0)
    own_total = kept[2 * group : 3 * group, 0:1]
    own_positive = kept[2 * group : 3 * group, 128:129]
    result = jnp.zeros((wide, columns), F32)
    losses = jnp.zeros((1, columns), F32)
    for k, (side, where) in enumerate(((near, core), (far, 1 - core))):
        told = heard[where]
        for u in range(1, outer_size):
            told = told + heard[u * CORES + where]
        total = jnp.concatenate([told[i : i + 1] for i in range(pieces)], axis=1)
        positive = jnp.concatenate([told[pieces + i : pieces + i + 1] for i in range(pieces)], axis=1)
        losses = losses + jnp.where(at_record[0:1], total, 0.0)
        value = kept[group * k : group * (k + 1), :]
        name = column_names(lane, kind, group, where).astype(F32)
        hit = jnp.where(name == own_positive, 1.0, 0.0)
        by_query = (jnp.exp(value - own_total) - hit) * factor[0]
        by_query = jnp.where(at_record, by_query, 0.0).astype(BF16)
        hit = jnp.where(positive == own_name.astype(F32), 1.0, 0.0)
        by_record = (jnp.exp(jnp.where(at_record, 0.0, value - total)) - hit) * factor[0]
        by_record = jnp.where(at_record, 0.0, by_record).astype(BF16)
        rows = jnp.dot(picker(group, 0, True), by_query, preferred_element_type=F32) + jnp.dot(
            picker(group, 1, True), by_record, preferred_element_type=F32
        )
        result = result + jnp.dot(rows.astype(BF16), side[...], preferred_element_type=F32)
    whole[...] = (result * scale).astype(BF16)
    to_each(whole, offered, sems)
    loss[...] = jnp.sum(losses, axis=1, keepdims=True)


def rows_of(grads, e, index):
    tile = grads[e, pl.ds(pl.multiple_of((index // 4) * 16, 16), 16), :].astype(F32)
    piece = lax.rem(index, 4)
    quarters = [tile[ROWS_DEV * k : ROWS_DEV * (k + 1)] for k in range(4)]
    half = jnp.where(piece < 2, quarters[0], quarters[2]), jnp.where(piece < 2, quarters[1], quarters[3])
    return jnp.where(lax.rem(piece, 2) == 0, half[0], half[1])


def router_kernel(
    grads, gain, summed_in, fetched_in, tok_in, facts_in, part_out, state_out, weighted_out,
    summed, fetched, tok, facts, state, weighted, acc, sems, facts_sem, out_sems
):
    experts, _, part = grads.shape
    rows = summed.shape[1]
    count = rows // SEQ
    sources = ((summed_in, summed), (fetched_in, fetched), (tok_in, tok))

    def load(e):
        cols = pl.ds(e * part, part)
        return [
            pltpu.make_async_copy(a.at[:, cols], b.at[e], sems.at[k, e]) for k, (a, b) in enumerate(sources)
        ]

    known = pltpu.make_async_copy(facts_in, facts, facts_sem)
    loads = [load(e) for e in range(experts)]
    for e in range(experts):
        loads[e][0].start()
        loads[e][1].start()
    known.start()
    for e in range(experts):
        loads[e][2].start()

    for e in range(experts):
        cols = slice(part * e, part * (e + 1))
        w = rows_of(grads, e, lax.axis_index("expert")) * (gain[:, cols] / SEQ)
        weighted[:, cols] = w
        loads[e][0].wait()
        loads[e][1].wait()
        for q in range(count):
            row = w[q : q + 1, :]
            at = [slice(rows * k + SEQ * q, rows * k + SEQ * (q + 1)) for k in range(2)]
            terms = [summed[e, at[0], :], fetched[e, at[0], :].astype(F32), fetched[e, at[1], :].astype(F32)]
            for k, term in enumerate(terms):
                total = fold(term * row)
                spot = slice(SEQ * q, SEQ * (q + 1))
                acc[k, spot] = total if e == 0 else acc[k, spot] + total
    known.wait()
    lanes = iota((SEQ, 128), 1)
    choices = []
    for q in range(count):
        at = slice(SEQ * q, SEQ * (q + 1))
        fact = facts[at, :]
        inv = fact[:, 2:3]
        shrink = inv * inv * inv * (jnp.sum(acc[0, at], axis=1, keepdims=True) / (experts * part))
        grad_gate = []
        for k in range(2):
            along = jnp.sum(acc[1 + k, at], axis=1, keepdims=True)
            grad_gate.append(inv * along - shrink * fact[:, k : k + 1])
        gates = [fact[:, 3 + k : 4 + k] for k in range(2)]
        mean = gates[0] * grad_gate[0] + gates[1] * grad_gate[1]
        choice = jnp.zeros((SEQ, 128), F32)
        for k in range(2):
            chosen = gates[k] * (grad_gate[k] - mean)
            route = fact[:, 5 + k : 6 + k].astype(I32)
            choice = choice + jnp.where(route == lanes, chosen, 0.0)
        choices.append(choice)
        choice = jnp.where(lanes == experts, inv, choice)
        state[at] = jnp.where(lanes == experts + 1, shrink, choice)
    saved = [
        pltpu.make_async_copy(state, state_out, out_sems.at[0]),
        pltpu.make_async_copy(weighted, weighted_out, out_sems.at[1]),
    ]
    for copy in saved:
        copy.start()
    lhs = jnp.transpose(jnp.concatenate(choices, axis=0))[:experts].astype(BF16)
    tiles = part // 128
    for e in range(experts):
        loads[e][2].wait()
        block = jnp.dot(lhs, tok[e], preferred_element_type=F32)
        for k in range(tiles):
            at = experts * (tiles * e + k)
            part_out[at : at + experts, :] = block[:, 128 * k : 128 * (k + 1)]
    for copy in saved:
        copy.wait()


def token_kernel(experts, summed, weighted, state, router, out):
    rows = summed.shape[0]
    known = state[...]
    choice = jnp.where(iota(known.shape, 1) < experts, known, 0.0).astype(BF16)
    through = jnp.dot(choice, router[...], preferred_element_type=F32)
    for q in range(rows // SEQ):
        at = slice(SEQ * q, SEQ * (q + 1))
        inverse, shrink = known[at, experts : experts + 1], known[at, experts + 1 : experts + 2]
        x = inverse * weighted[q : q + 1, :] - shrink * summed[at]
        out[at] = (x + through[SEQ * q : SEQ * (q + 1)]).astype(BF16)


def token_rows(summed, weighted, state, router, experts):
    rows, width = summed.shape
    part = width // experts
    split = lambda count: pl.BlockSpec((count, part), lambda i: (0, i))
    return pl.pallas_call(
        functools.partial(token_kernel, experts),
        grid=(experts,),
        in_specs=[
            split(rows),
            split(weighted.shape[0]),
            pl.BlockSpec((rows, 128), lambda i: (0, 0)),
            split(128),
        ],
        out_specs=split(rows),
        out_shape=jax.ShapeDtypeStruct((rows, width), BF16),
        compiler_params=params(10),
        cost_estimate=cost(2 * rows * 128 * width, 5 << 20),
    )(*in_hbm(summed, weighted, state), router)


def expert_kernel(count, source, grads, gain, notes, *rest):
    sources, (out, backs, sems) = rest[:count], rest[-3:]
    experts, _, part = grads.shape
    step = pl.program_id(0)
    gate, inv, seq = notes[0, :, 0:1], notes[0, :, 1:2], notes[0, :, 2:3]
    capacity = gate.shape[0]
    loads = [pltpu.make_async_copy(sources[r], backs.at[r], sems.at[r]) for r in range(count)]

    @pl.when(step == 0)
    def _():
        for load in loads:
            load.start()

    for r in range(count):

        @pl.when(step == r)
        def _():
            loads[r].wait()

    def gradient_rows(e):
        w = rows_of(grads, e, source[step]) * (gain[:, part * e : part * (e + 1)] / SEQ)
        x = jnp.broadcast_to(w[0:1], (capacity, part))
        for s in range(1, ROWS_DEV):
            x = jnp.where(seq == s, w[s : s + 1], x)
        return x

    acc = jnp.zeros((capacity, 128), F32)
    for e in range(experts):
        back = backs[step, :, part * e : part * (e + 1)].astype(F32)
        acc = acc + fold(gradient_rows(e) * back)
    shrink = inv * inv * inv * (jnp.sum(acc, axis=1, keepdims=True) / (experts * part))
    keep, drop = gate * inv, gate * shrink
    for e in range(experts):
        cols = slice(part * e, part * (e + 1))
        out[0, :, cols] = (keep * gradient_rows(e) - drop * backs[step, :, cols].astype(F32)).astype(BF16)


def expert_rows(source, grads, gain, notes, backs, before=None):
    experts, capacity = notes.shape[:2]
    width = gain.shape[1]
    count = len(backs)
    whole = lambda shape: pl.BlockSpec(shape, lambda i, p: (0,) * len(shape))
    block = lambda i, p: (p[i], 0, 0)
    kept = [] if before is None else [before]
    return pl.pallas_call(
        functools.partial(expert_kernel, count),
        grid_spec=pltpu.PrefetchScalarGridSpec(
            num_scalar_prefetch=1,
            grid=(count,),
            in_specs=[
                whole(grads.shape),
                whole((1, width)),
                pl.BlockSpec((1, capacity, notes.shape[2]), block),
            ]
            + [HBM] * (count + len(kept)),
            out_specs=pl.BlockSpec((1, capacity, width), block),
            scratch_shapes=[
                pltpu.VMEM((count, capacity, width), BF16),
                pltpu.SemaphoreType.DMA((count,)),
            ],
        ),
        out_shape=jax.ShapeDtypeStruct((experts, capacity, width), BF16),
        input_output_aliases={4 + count: 0} if kept else {},
        compiler_params=params(16),
        cost_estimate=cost(12 * count * capacity * width, count << 20),
    )(source, grads, gain, notes, *in_hbm(*backs), *kept)


def shards(tokens, routes, positives, expert_out, router, norm_gain, loss_scale):
    experts, capacity, width = expert_out.shape[2:]
    rows = tokens.shape[0]
    slots = experts * capacity
    outer = lax.axis_size("u")
    mine = lax.axis_index("expert").astype(I32)
    mine_at = mine[None]
    part = width // experts
    group = PAIR_DEV * experts
    pairs = group * outer * CORES
    scale = 4.0 / math.sqrt(width)
    gain = norm_gain[None, :]
    columns = outer * experts * ROWS_DEV

    received = exchange(expert_out.reshape(experts, capacity, width), "expert").reshape(slots, width)
    gates, slot = routing(tokens, routes, router, experts, capacity)
    lane = jnp.arange(columns, dtype=I32)
    spread_positive = jnp.where(
        (lane % (2 * group)) // ROWS_DEV == mine,
        jnp.where(lane % ROWS_DEV == 0, positives[0], positives[1]) * (lane % ROWS_DEV < PAIR_DEV),
        0,
    ).astype(F32)

    summed, sliced, inverse = forward(tokens, received, slot, gates, gain, experts)
    own = exchange(sliced, "expert").reshape(2 * group, part)
    facts = jnp.concatenate(
        [jnp.zeros((rows, 2), F32), inverse, gates, routes.astype(F32)], axis=1
    )
    facts = jnp.pad(facts, ((0, 0), (0, 128 - facts.shape[1])))
    backs = list(pack(mine_at, summed, slot.T, experts, capacity))

    def move(after, turns):
        after, *ready = lax.optimization_barrier((after, *[backs[r] for r in turns]))
        for r, x in zip(turns, ready):
            pairs = [(i, (i // RING + r // RING) % HALVES * RING + (i + r) % RING) for i in range(experts)]
            backs[r] = lax.ppermute(x, "expert", pairs)
        return after


    def landed(value, turns):
        value, *done = lax.optimization_barrier((value, *[backs[r] for r in turns]))
        for r, x in zip(turns, done):
            backs[r] = x
        return value

    slot_ids = jnp.arange(slots, dtype=I32)[None, :]
    picks = [slot[:, k : k + 1] == slot_ids for k in range(2)]
    gate_slot = jnp.sum(
        jnp.where(picks[0], gates[:, 0:1], 0.0) + jnp.where(picks[1], gates[:, 1:2], 0.0), axis=0
    )
    taken = picks[0] | picks[1]
    inverse_slot = jnp.sum(jnp.where(taken, inverse, 0.0), axis=0)
    sequence = (jnp.arange(rows, dtype=I32) // SEQ).astype(F32)
    sequence_slot = jnp.sum(jnp.where(taken, sequence[:, None], 0.0), axis=0)
    notes = jnp.stack([gate_slot, inverse_slot, sequence_slot, spread_positive])
    notes = jnp.pad(notes, ((0, 4), (0, 0)))

    own, *backs = lax.optimization_barrier((own, *backs))
    near = spread(own, "u", outer)
    facts, fetched = overlaps(summed, received, slot, facts, experts)
    near, facts, fetched = lax.optimization_barrier((near, facts, fetched))
    far = swap_core(near)
    near, far = near.reshape(columns, part), far.reshape(columns, part)
    offered = pl.pallas_call(
        scores_kernel,
        in_specs=[VMEM] * 4,
        out_specs=HBM,
        out_shape=pltpu.HBM((experts, 2 * group + 8, columns), F32),
        scratch_shapes=[pltpu.VMEM((2 * group + 8, columns), F32), pltpu.SemaphoreType.DMA((experts,))],
        compiler_params=params(2),
    )(own, near, far, notes)
    offered = move(offered, TURNS[0])
    gathered = exchange(offered, "expert")
    devices = outer * CORES
    offered, kept = pl.pallas_call(
        functools.partial(totals_kernel, scale),
        in_specs=[VMEM],
        out_specs=[HBM] * 2,
        out_shape=[pltpu.HBM((devices, 8, 128), F32), pltpu.HBM((3 * group, columns), F32)],
        scratch_shapes=[
            pltpu.VMEM((3 * group, columns), F32),
            pltpu.VMEM((devices, 8, 128), F32),
            pltpu.SemaphoreType.DMA(()),
            pltpu.SemaphoreType.DMA(()),
        ],
        compiler_params=params(2),
    )(gathered)
    heard = exchange(offered, ("u", "c"))
    heard = landed(heard, TURNS[0][:1])
    offered, loss = pl.pallas_call(
        functools.partial(gradient_kernel, scale),
        in_specs=[SMEM] + [VMEM] * 4,
        out_specs=[HBM, VMEM],
        out_shape=[pltpu.HBM((experts, 2 * group, part), BF16), jax.ShapeDtypeStruct((1, 1), F32)],
        scratch_shapes=[pltpu.VMEM((2 * group, part), BF16), pltpu.SemaphoreType.DMA((experts,))],
        compiler_params=params(2),
    )((loss_scale / pairs)[None], heard, kept, near, far)
    offered = move(offered, TURNS[1])
    grads = exchange(offered, "expert")
    grads = landed(grads, TURNS[0][1:])

    router_part, state, weighted = pl.pallas_call(
        router_kernel,
        in_specs=[VMEM] * 2 + [HBM] * 4,
        out_specs=[VMEM, HBM, HBM],
        out_shape=[
            jax.ShapeDtypeStruct((width * experts // 128, 128), F32),
            pltpu.HBM((rows, 128), F32),
            pltpu.HBM((rows // SEQ, width), F32),
        ],
        scratch_shapes=[
            pltpu.VMEM((experts, rows, part), F32),
            pltpu.VMEM((experts, 2 * rows, part), BF16),
            pltpu.VMEM((experts, rows, part), BF16),
            pltpu.VMEM((rows, 128), F32),
            pltpu.VMEM((rows, 128), F32),
            pltpu.VMEM((rows // SEQ, width), F32),
            pltpu.VMEM((3, rows, 128), F32),
            pltpu.SemaphoreType.DMA((3, experts)),
            pltpu.SemaphoreType.DMA(()),
            pltpu.SemaphoreType.DMA((2,)),
        ],
        compiler_params=params(16),
    )(grads, gain, *in_hbm(summed, fetched, tokens, facts))
    router_part = move(router_part, TURNS[2])
    router_part = exchange(router_part.reshape(outer, -1, 128), "u")
    router_part = jnp.sum(router_part, axis=0)
    router_part = spread(router_part, ("c", "expert"), CORES * experts)
    held = lax.dynamic_slice_in_dim(gathered[:, 2 * group : 2 * group + 3], mine * capacity, capacity, axis=2)
    held = jnp.pad(jnp.transpose(held, (0, 2, 1)), ((0, 0), (0, 0), (0, 5)))
    turned = jnp.pad(router.T, ((0, 128 - experts), (0, 0)))
    token_grad = token_rows(summed, weighted, state, turned, experts)
    parts = [(0,) + TURNS[0] + TURNS[1], TURNS[2]]
    places = [
        jnp.stack([shifted(mine, (HALVES - r // RING) % HALVES, (RING - r % RING) % RING) for r in turns])
        for turns in parts
    ]
    expert_grad = expert_rows(places[0], grads, gain, held, [backs[r] for r in parts[0]])
    router_part, token_grad, expert_grad = lax.optimization_barrier((router_part, token_grad, expert_grad))
    router_part = jnp.sum(router_part, axis=0)
    router_all = spread(router_part, "u", outer)
    expert_grad = expert_rows(places[1], grads, gain, held, [backs[r] for r in parts[1]], expert_grad)
    router_all, expert_grad = lax.optimization_barrier((router_all, expert_grad))
    router_grad = router_all.reshape(-1, experts, 128).transpose(1, 0, 2).reshape(experts, width).T
    return token_grad, expert_grad.reshape(1, 1, experts, capacity, width), router_grad, loss[0, 0] / pairs


def solution(mesh):
    outer = mesh.shape["dp"] // CORES
    fine = Mesh(mesh.devices.reshape(outer, CORES, mesh.shape["expert"]), ("u", "c", "expert"))
    everywhere = ("u", "c", "expert")
    return jax.shard_map(
        shards,
        mesh=fine,
        in_specs=(
            P(everywhere, None),
            P(everywhere, None),
            P(everywhere),
            P(("u", "c"), "expert", None, None, None),
            P(),
            P(),
            P(),
        ),
        out_specs=(P(everywhere, None), P(("u", "c"), "expert", None, None, None), P(), P()),
        check_vma=False,
    )
```

```python
import functools
import math

import jax
import jax.numpy as jnp
from jax import lax
from jax.experimental import pallas as pl
from jax.experimental.pallas import tpu as pltpu
from jax.sharding import Mesh, PartitionSpec as P

PAIR_DEV = 2
SEQ = 48
EPS = 1e-05
CORES = 2
ROWS_DEV = 2 * PAIR_DEV
F32 = jnp.float32
BF16 = jnp.bfloat16
I32 = jnp.int32
VMEM = pl.BlockSpec(memory_space=pltpu.VMEM)
SMEM = pl.BlockSpec(memory_space=pltpu.SMEM)
HBM = pl.BlockSpec(memory_space=pltpu.HBM)
NT = (((1,), (1,)), ((), ()))
TURNS = ((1, 3, 2), (5, 7), (4, 6))
HALVES, RING = 2, 4


def iota(shape, dim):
    return lax.broadcasted_iota(I32, shape, dim)


def params(mib):
    return pltpu.CompilerParams(vmem_limit_bytes=mib << 20)


def cost(flops, moved):
    return pl.CostEstimate(flops=flops, bytes_accessed=moved, transcendentals=0)


def fold(x):
    total = x[:, :128]
    for k in range(1, x.shape[1] // 128):
        total = total + x[:, 128 * k : 128 * (k + 1)]
    return total


def in_hbm(*arrays):
    return [pltpu.with_memory_space_constraint(x, pltpu.HBM) for x in arrays]


def shifted(index, halves, along):
    return lax.rem(index // RING + halves, HALVES) * RING + lax.rem(lax.rem(index, RING) + along, RING)


def copy_all(copies):
    for copy in copies:
        copy.start()
    for copy in copies:
        copy.wait()


def to_each(source, target, sems):
    copy_all([pltpu.make_async_copy(source, target.at[i], sems.at[i]) for i in range(target.shape[0])])


def swap_core(x):
    return lax.ppermute(x, "c", [(0, 1), (1, 0)])


def exchange(x, axes):
    return lax.all_to_all(x, axes, split_axis=0, concat_axis=0, tiled=True)


def spread(x, axes, size):
    return exchange(jnp.broadcast_to(x[None], (size,) + x.shape), axes)


def routing(tokens, routes, router, experts, capacity):
    logits = jnp.dot(tokens, router, preferred_element_type=F32)
    lanes = jnp.arange(experts, dtype=I32)[None, None, :]
    one_hot = (routes[:, :, None] == lanes).astype(F32)
    chosen = jnp.sum(one_hot * logits[:, None, :], axis=2)
    gates = jax.nn.softmax(chosen, axis=1)
    rows = routes.shape[0]
    hits = jnp.sum(one_hot, axis=1)
    order = jnp.arange(rows, dtype=I32)
    earlier = (order[None, :] < order[:, None]).astype(BF16)
    before = jnp.dot(earlier, hits.astype(BF16), preferred_element_type=F32)
    rank = jnp.sum(one_hot * before[:, None, :], axis=2).astype(I32)
    return gates, routes * capacity + rank


def one_hots(slot, slots):
    ids = iota((slot.shape[0], slots), 1)
    return jnp.concatenate([(slot[:, k : k + 1] == ids).astype(BF16) for k in range(2)], axis=0)


def forward_kernel(
    steps, tok, rec, slot, gate, gain, summed, sliced_out, inverse, held, square, picks, sliced, row_sem, slice_sem
):
    step = pl.program_id(0)
    rows, part = tok.shape

    def keep(e):
        start = pl.multiple_of(e * part, part)
        return pltpu.make_async_copy(held.at[e], summed.at[:, pl.ds(start, part)], row_sem.at[e])

    @pl.when(step == 0)
    def _():
        square[...] = jnp.zeros_like(square)
        picks[...] = one_hots(slot, rec.shape[0])

    for k in range(part // 256):
        cols = slice(256 * k, 256 * (k + 1))
        both = jnp.dot(picks[...], rec[:, cols], preferred_element_type=F32)
        x = tok[:, cols].astype(F32) + gate[:, 0:1] * both[:rows] + gate[:, 1:2] * both[rows:]
        held[step, :, cols] = x
        square[...] += fold(x * x)
    keep(step).start()

    @pl.when(step == steps - 1)
    def _():
        mean = jnp.sum(square[...], axis=1, keepdims=True) / (steps * part)
        scale = lax.rsqrt(mean + EPS)
        inverse[...] = scale
        count = rows // SEQ
        for e in range(steps):
            x = held[e] * scale
            x = jnp.sum(x.reshape(count, SEQ, part), axis=1) / SEQ
            sliced[e] = (x * gain[:, part * e : part * (e + 1)]).astype(BF16)
        offer = pltpu.make_async_copy(sliced, sliced_out, slice_sem)
        offer.start()
        for e in range(steps):
            keep(e).wait()
        offer.wait()


def forward(tokens, received, slot, gates, gain, experts):
    rows, width = tokens.shape
    slots = received.shape[0]
    part = width // experts
    whole = lambda shape: pl.BlockSpec(shape, lambda i: (0,) * len(shape))
    return pl.pallas_call(
        functools.partial(forward_kernel, experts),
        grid=(experts,),
        in_specs=[
            pl.BlockSpec((rows, part), lambda i: (0, i)),
            pl.BlockSpec((slots, part), lambda i: (0, i)),
            whole((rows, 2)),
            whole((rows, 2)),
            whole((1, width)),
        ],
        out_specs=[HBM, HBM, whole((rows, 1))],
        out_shape=[
            pltpu.HBM((rows, width), F32),
            pltpu.HBM((experts, rows // SEQ, part), BF16),
            jax.ShapeDtypeStruct((rows, 1), F32),
        ],
        scratch_shapes=[
            pltpu.VMEM((experts, rows, part), F32),
            pltpu.VMEM((rows, 128), F32),
            pltpu.VMEM((2 * rows, slots), BF16),
            pltpu.VMEM((experts, rows // SEQ, part), BF16),
            pltpu.SemaphoreType.DMA((experts,)),
            pltpu.SemaphoreType.DMA(()),
        ],
        compiler_params=params(14),
        cost_estimate=cost(4 * rows * slots * width, 10 << 20),
    )(tokens, received, slot, gates, gain)


def pack_kernel(place, x, turned, *rest):
    *outs, spot, packed, sems = rest
    step, steps = pl.program_id(0), packed.shape[0]
    rows, part = x.shape
    capacity = outs[0].shape[0]
    slots = spot.shape[0]

    def leave(e, i):
        start = pl.multiple_of(e * part, part)
        return pltpu.make_async_copy(
            packed.at[e, pl.ds(i * capacity, capacity)], outs[i].at[:, pl.ds(start, part)], sems.at[e, i]
        )

    @pl.when(step == 0)
    def _():
        row = iota((slots, 1), 0)
        chunk = row // capacity
        target = shifted(place[0], chunk // RING, lax.rem(chunk, RING)) * capacity + lax.rem(row, capacity)
        spot[...] = ((turned[0:1, :] == target) | (turned[1:2, :] == target)).astype(BF16)

    for k in range(part // 512):
        cols = slice(512 * k, 512 * (k + 1))
        packed[step, :, cols] = jnp.dot(
            spot[...], x[:, cols].astype(BF16), preferred_element_type=F32
        ).astype(BF16)
    for i in range(len(outs)):
        leave(step, i).start()

    @pl.when(step == steps - 1)
    def _():
        for e in range(steps):
            for i in range(len(outs)):
                leave(e, i).wait()


def pack(place, summed, turned, experts, capacity):
    rows, width = summed.shape
    steps = experts // 2
    part = width // steps
    slots = experts * capacity
    return pl.pallas_call(
        pack_kernel,
        grid=(steps,),
        in_specs=[
            SMEM,
            pl.BlockSpec((rows, part), lambda i: (0, i)),
            pl.BlockSpec((2, rows), lambda i: (0, 0)),
        ],
        out_specs=[HBM] * experts,
        out_shape=[pltpu.HBM((capacity, width), BF16)] * experts,
        scratch_shapes=[
            pltpu.VMEM((slots, rows), BF16),
            pltpu.VMEM((steps, slots, part), BF16),
            pltpu.SemaphoreType.DMA((steps, experts)),
        ],
        compiler_params=params(14),
        cost_estimate=cost(2 * rows * slots * width, 7 << 20),
    )(place, *in_hbm(summed), turned)


def overlap_kernel(steps, x, rec, slot, facts, out, fetched, picks, dots):
    step = pl.program_id(0)
    rows, part = x.shape

    @pl.when(step == 0)
    def _():
        dots[...] = jnp.zeros_like(dots)
        picks[...] = one_hots(slot, rec.shape[0])

    for k in range(part // 256):
        cols = slice(256 * k, 256 * (k + 1))
        both = jnp.dot(picks[...], rec[:, cols], preferred_element_type=F32)
        fetched[:, cols] = both.astype(BF16)
        value = x[:, cols]
        dots[:rows] += fold(value * both[:rows])
        dots[rows:] += fold(value * both[rows:])

    @pl.when(step == steps - 1)
    def _():
        lane = iota((rows, 128), 1)
        known = facts[...]
        for k in range(2):
            total = jnp.sum(dots[rows * k : rows * (k + 1)], axis=1, keepdims=True)
            known = jnp.where(lane == k, total, known)
        out[...] = known


def overlaps(summed, received, slot, facts, experts):
    rows, width = summed.shape
    slots = received.shape[0]
    part = width // experts
    whole = lambda shape: pl.BlockSpec(shape, lambda i: (0, 0))
    return pl.pallas_call(
        functools.partial(overlap_kernel, experts),
        grid=(experts,),
        in_specs=[
            pl.BlockSpec((rows, part), lambda i: (0, i)),
            pl.BlockSpec((slots, part), lambda i: (0, i)),
            whole((rows, 2)),
            whole((rows, 128)),
        ],
        out_specs=[whole((rows, 128)), pl.BlockSpec((2 * rows, part), lambda i: (0, i))],
        out_shape=[pltpu.HBM((rows, 128), F32), pltpu.HBM((2 * rows, width), BF16)],
        scratch_shapes=[pltpu.VMEM((2 * rows, slots), BF16), pltpu.VMEM((2 * rows, 128), F32)],
        compiler_params=params(12),
        cost_estimate=cost(4 * rows * slots * width, 10 << 20),
    )(*in_hbm(summed, received), slot, facts)


def lanes_of(shape, dim):
    lane = iota(shape, dim)
    kind = lax.rem(lane, ROWS_DEV)
    return lane, kind, kind >= PAIR_DEV


def picker(group, kind, turned=False):
    wide = 2 * group
    shape, pair, row = ((wide, group), 1, 0) if turned else ((group, wide), 0, 1)
    a = iota(shape, pair)
    b = iota(shape, row)
    source = (a // PAIR_DEV) * ROWS_DEV + lax.rem(a, PAIR_DEV) + PAIR_DEV * kind
    return (source == b).astype(BF16)


def scores_kernel(own, near, far, notes, offered, whole, sems):
    experts, total, columns = offered.shape
    group = experts * PAIR_DEV
    queries, records = [
        jnp.dot(picker(group, kind), own[...], preferred_element_type=F32).astype(BF16) for kind in (0, 1)
    ]
    at_record = lanes_of((group, columns), 1)[2]
    for k, side in enumerate((near, far)):
        every = side[...]
        by_query = lax.dot_general(queries, every, NT, preferred_element_type=F32)
        by_record = lax.dot_general(records, every, NT, preferred_element_type=F32)
        whole[group * k : group * (k + 1)] = jnp.where(at_record, by_query, by_record)
    whole[2 * group :] = notes[...]
    to_each(whole, offered, sems)


def totals_kernel(scale, gathered, offered, kept_out, kept, spread, kept_sem, sem):
    place, core = lax.axis_index("u"), lax.axis_index("c")
    experts, total, columns = gathered.shape
    group = experts * PAIR_DEV
    both = gathered[0]
    for e in range(1, experts):
        both = both + gathered[e]
    positive_lane = both[2 * group + 3 : 2 * group + 4, :]
    near, far = both[:group] * scale, both[group : 2 * group] * scale
    kept[0:group] = near
    kept[group : 2 * group] = far

    shape = (group, columns)
    lane, kind, at_record = lanes_of(shape, 1)
    pair = iota(shape, 0)
    within = lax.rem(lane, 2 * group)
    matching = (within // ROWS_DEV == pair // PAIR_DEV) & (kind == lax.rem(pair, PAIR_DEV))
    here = matching & (lane // (2 * group) == place)
    positive = jnp.sum(jnp.where(here, positive_lane, 0.0), axis=1, keepdims=True)

    low = jnp.float32(-jnp.inf)
    near_records = jnp.where(at_record, near, low)
    far_records = jnp.where(at_record, far, low)
    highest = jnp.maximum(
        jnp.max(near_records, axis=1, keepdims=True), jnp.max(far_records, axis=1, keepdims=True)
    )
    weight = jnp.sum(jnp.exp(near_records - highest), axis=1, keepdims=True) + jnp.sum(
        jnp.exp(far_records - highest), axis=1, keepdims=True
    )
    log_total = highest + jnp.log(weight)
    chosen = jnp.zeros((group, 1), F32)
    for side, where in ((near, core), (far, 1 - core)):
        name = column_names(lane, kind, group, where)
        hit = at_record & (name.astype(F32) == positive)
        chosen = chosen + jnp.sum(jnp.where(hit, side, 0.0), axis=1, keepdims=True)
    kept[2 * group : 3 * group, :128] = jnp.broadcast_to(log_total, (group, 128))
    kept[2 * group : 3 * group, 128:256] = jnp.broadcast_to(positive, (group, 128))
    saved = pltpu.make_async_copy(kept, kept_out, kept_sem)
    saved.start()
    row_loss = log_total - chosen

    total_lane = jnp.sum(jnp.where(here, log_total, 0.0), axis=0, keepdims=True)
    loss_lane = jnp.sum(jnp.where(here, row_loss, 0.0), axis=0, keepdims=True)
    own_lane = jnp.where(lane[0:1] // (2 * group) == place, positive_lane, 0.0)
    pieces = [x[:, 128 * k : 128 * (k + 1)] for x in (total_lane, own_lane) for k in range(columns // 128)]
    loss_pieces = [
        pltpu.roll(loss_lane, PAIR_DEV, 1)[:, 128 * k : 128 * (k + 1)] for k in range(columns // 128)
    ]
    pieces = [a + b for a, b in zip(pieces, loss_pieces)] + pieces[columns // 128 :]
    message = jnp.concatenate(pieces, axis=0)
    for d in range(spread.shape[0]):
        spread[d] = message
    copy_all([pltpu.make_async_copy(spread, offered, sem)])
    saved.wait()


def column_names(lane, kind, group, core):
    wide = 2 * group
    block = (lane // wide) * CORES + core
    return block * group + (lax.rem(lane, wide) // ROWS_DEV) * PAIR_DEV + lax.rem(kind, PAIR_DEV)


def gradient_kernel(scale, factor, heard, kept, near, far, offered, loss, whole, sems):
    place, core = lax.axis_index("u"), lax.axis_index("c")
    experts, wide, columns = offered.shape
    group = wide // 2
    outer_size = heard.shape[0] // CORES
    pieces = columns // 128
    shape = (group, columns)
    lane, kind, at_record = lanes_of(shape, 1)
    pair = iota(shape, 0)
    own_name = (place * CORES + core) * group + iota((group, 1), 0)
    own_total = kept[2 * group : 3 * group, 0:1]
    own_positive = kept[2 * group : 3 * group, 128:129]
    result = jnp.zeros((wide, columns), F32)
    losses = jnp.zeros((1, columns), F32)
    for k, (side, where) in enumerate(((near, core), (far, 1 - core))):
        told = heard[where]
        for u in range(1, outer_size):
            told = told + heard[u * CORES + where]
        total = jnp.concatenate([told[i : i + 1] for i in range(pieces)], axis=1)
        positive = jnp.concatenate([told[pieces + i : pieces + i + 1] for i in range(pieces)], axis=1)
        losses = losses + jnp.where(at_record[0:1], total, 0.0)
        value = kept[group * k : group * (k + 1), :]
        name = column_names(lane, kind, group, where).astype(F32)
        hit = jnp.where(name == own_positive, 1.0, 0.0)
        by_query = (jnp.exp(value - own_total) - hit) * factor[0]
        by_query = jnp.where(at_record, by_query, 0.0).astype(BF16)
        hit = jnp.where(positive == own_name.astype(F32), 1.0, 0.0)
        by_record = (jnp.exp(jnp.where(at_record, 0.0, value - total)) - hit) * factor[0]
        by_record = jnp.where(at_record, 0.0, by_record).astype(BF16)
        rows = jnp.dot(picker(group, 0, True), by_query, preferred_element_type=F32) + jnp.dot(
            picker(group, 1, True), by_record, preferred_element_type=F32
        )
        result = result + jnp.dot(rows.astype(BF16), side[...], preferred_element_type=F32)
    whole[...] = (result * scale).astype(BF16)
    to_each(whole, offered, sems)
    loss[...] = jnp.sum(losses, axis=1, keepdims=True)


def rows_of(grads, e, index):
    tile = grads[e, pl.ds(pl.multiple_of((index // 4) * 16, 16), 16), :].astype(F32)
    piece = lax.rem(index, 4)
    quarters = [tile[ROWS_DEV * k : ROWS_DEV * (k + 1)] for k in range(4)]
    half = jnp.where(piece < 2, quarters[0], quarters[2]), jnp.where(piece < 2, quarters[1], quarters[3])
    return jnp.where(lax.rem(piece, 2) == 0, half[0], half[1])


def router_kernel(
    grads, gain, summed_in, fetched_in, tok_in, facts_in, part_out, state_out, weighted_out,
    summed, fetched, tok, facts, state, weighted, acc, sems, facts_sem, out_sems
):
    experts, _, part = grads.shape
    rows = summed.shape[1]
    count = rows // SEQ
    sources = ((summed_in, summed), (fetched_in, fetched), (tok_in, tok))

    def load(e):
        cols = pl.ds(e * part, part)
        return [
            pltpu.make_async_copy(a.at[:, cols], b.at[e], sems.at[k, e]) for k, (a, b) in enumerate(sources)
        ]

    known = pltpu.make_async_copy(facts_in, facts, facts_sem)
    loads = [load(e) for e in range(experts)]
    for e in range(experts):
        loads[e][0].start()
        loads[e][1].start()
    known.start()
    for e in range(experts):
        loads[e][2].start()

    for e in range(experts):
        cols = slice(part * e, part * (e + 1))
        w = rows_of(grads, e, lax.axis_index("expert")) * (gain[:, cols] / SEQ)
        weighted[:, cols] = w
        loads[e][0].wait()
        loads[e][1].wait()
        for q in range(count):
            row = w[q : q + 1, :]
            at = [slice(rows * k + SEQ * q, rows * k + SEQ * (q + 1)) for k in range(2)]
            terms = [summed[e, at[0], :], fetched[e, at[0], :].astype(F32), fetched[e, at[1], :].astype(F32)]
            for k, term in enumerate(terms):
                total = fold(term * row)
                spot = slice(SEQ * q, SEQ * (q + 1))
                acc[k, spot] = total if e == 0 else acc[k, spot] + total
    known.wait()
    lanes = iota((SEQ, 128), 1)
    choices = []
    for q in range(count):
        at = slice(SEQ * q, SEQ * (q + 1))
        fact = facts[at, :]
        inv = fact[:, 2:3]
        shrink = inv * inv * inv * (jnp.sum(acc[0, at], axis=1, keepdims=True) / (experts * part))
        grad_gate = []
        for k in range(2):
            along = jnp.sum(acc[1 + k, at], axis=1, keepdims=True)
            grad_gate.append(inv * along - shrink * fact[:, k : k + 1])
        gates = [fact[:, 3 + k : 4 + k] for k in range(2)]
        mean = gates[0] * grad_gate[0] + gates[1] * grad_gate[1]
        choice = jnp.zeros((SEQ, 128), F32)
        for k in range(2):
            chosen = gates[k] * (grad_gate[k] - mean)
            route = fact[:, 5 + k : 6 + k].astype(I32)
            choice = choice + jnp.where(route == lanes, chosen, 0.0)
        choices.append(choice)
        choice = jnp.where(lanes == experts, inv, choice)
        state[at] = jnp.where(lanes == experts + 1, shrink, choice)
    saved = [
        pltpu.make_async_copy(state, state_out, out_sems.at[0]),
        pltpu.make_async_copy(weighted, weighted_out, out_sems.at[1]),
    ]
    for copy in saved:
        copy.start()
    lhs = jnp.transpose(jnp.concatenate(choices, axis=0))[:experts].astype(BF16)
    tiles = part // 128
    for e in range(experts):
        loads[e][2].wait()
        block = jnp.dot(lhs, tok[e], preferred_element_type=F32)
        for k in range(tiles):
            at = experts * (tiles * e + k)
            part_out[at : at + experts, :] = block[:, 128 * k : 128 * (k + 1)]
    for copy in saved:
        copy.wait()


def token_kernel(experts, summed, weighted, state, router, out):
    rows = summed.shape[0]
    known = state[...]
    choice = jnp.where(iota(known.shape, 1) < experts, known, 0.0).astype(BF16)
    through = jnp.dot(choice, router[...], preferred_element_type=F32)
    for q in range(rows // SEQ):
        at = slice(SEQ * q, SEQ * (q + 1))
        inverse, shrink = known[at, experts : experts + 1], known[at, experts + 1 : experts + 2]
        x = inverse * weighted[q : q + 1, :] - shrink * summed[at]
        out[at] = (x + through[SEQ * q : SEQ * (q + 1)]).astype(BF16)


def token_rows(summed, weighted, state, router, experts):
    rows, width = summed.shape
    part = width // experts
    split = lambda count: pl.BlockSpec((count, part), lambda i: (0, i))
    return pl.pallas_call(
        functools.partial(token_kernel, experts),
        grid=(experts,),
        in_specs=[
            split(rows),
            split(weighted.shape[0]),
            pl.BlockSpec((rows, 128), lambda i: (0, 0)),
            split(128),
        ],
        out_specs=split(rows),
        out_shape=jax.ShapeDtypeStruct((rows, width), BF16),
        compiler_params=params(10),
        cost_estimate=cost(2 * rows * 128 * width, 5 << 20),
    )(*in_hbm(summed, weighted, state), router)


def expert_kernel(count, source, grads, gain, notes, *rest):
    sources, (out, backs, sems) = rest[:count], rest[-3:]
    experts, _, part = grads.shape
    step = pl.program_id(0)
    gate, inv, seq = notes[0, :, 0:1], notes[0, :, 1:2], notes[0, :, 2:3]
    capacity = gate.shape[0]
    loads = [pltpu.make_async_copy(sources[r], backs.at[r], sems.at[r]) for r in range(count)]

    @pl.when(step == 0)
    def _():
        for load in loads:
            load.start()

    for r in range(count):

        @pl.when(step == r)
        def _():
            loads[r].wait()

    def gradient_rows(e):
        w = rows_of(grads, e, source[step]) * (gain[:, part * e : part * (e + 1)] / SEQ)
        x = jnp.broadcast_to(w[0:1], (capacity, part))
        for s in range(1, ROWS_DEV):
            x = jnp.where(seq == s, w[s : s + 1], x)
        return x

    acc = jnp.zeros((capacity, 128), F32)
    for e in range(experts):
        back = backs[step, :, part * e : part * (e + 1)].astype(F32)
        acc = acc + fold(gradient_rows(e) * back)
    shrink = inv * inv * inv * (jnp.sum(acc, axis=1, keepdims=True) / (experts * part))
    keep, drop = gate * inv, gate * shrink
    for e in range(experts):
        cols = slice(part * e, part * (e + 1))
        out[0, :, cols] = (keep * gradient_rows(e) - drop * backs[step, :, cols].astype(F32)).astype(BF16)


def expert_rows(source, grads, gain, notes, backs, before=None):
    experts, capacity = notes.shape[:2]
    width = gain.shape[1]
    count = len(backs)
    whole = lambda shape: pl.BlockSpec(shape, lambda i, p: (0,) * len(shape))
    block = lambda i, p: (p[i], 0, 0)
    kept = [] if before is None else [before]
    return pl.pallas_call(
        functools.partial(expert_kernel, count),
        grid_spec=pltpu.PrefetchScalarGridSpec(
            num_scalar_prefetch=1,
            grid=(count,),
            in_specs=[
                whole(grads.shape),
                whole((1, width)),
                pl.BlockSpec((1, capacity, notes.shape[2]), block),
            ]
            + [HBM] * (count + len(kept)),
            out_specs=pl.BlockSpec((1, capacity, width), block),
            scratch_shapes=[
                pltpu.VMEM((count, capacity, width), BF16),
                pltpu.SemaphoreType.DMA((count,)),
            ],
        ),
        out_shape=jax.ShapeDtypeStruct((experts, capacity, width), BF16),
        input_output_aliases={4 + count: 0} if kept else {},
        compiler_params=params(16),
        cost_estimate=cost(12 * count * capacity * width, count << 20),
    )(source, grads, gain, notes, *in_hbm(*backs), *kept)


def shards(tokens, routes, positives, expert_out, router, norm_gain, loss_scale):
    experts, capacity, width = expert_out.shape[2:]
    rows = tokens.shape[0]
    slots = experts * capacity
    outer = lax.axis_size("u")
    mine = lax.axis_index("expert").astype(I32)
    mine_at = mine[None]
    part = width // experts
    group = PAIR_DEV * experts
    pairs = group * outer * CORES
    scale = 4.0 / math.sqrt(width)
    gain = norm_gain[None, :]
    columns = outer * experts * ROWS_DEV

    received = exchange(expert_out.reshape(experts, capacity, width), "expert").reshape(slots, width)
    gates, slot = routing(tokens, routes, router, experts, capacity)
    lane = jnp.arange(columns, dtype=I32)
    spread_positive = jnp.where(
        (lane % (2 * group)) // ROWS_DEV == mine,
        jnp.where(lane % ROWS_DEV == 0, positives[0], positives[1]) * (lane % ROWS_DEV < PAIR_DEV),
        0,
    ).astype(F32)

    summed, sliced, inverse = forward(tokens, received, slot, gates, gain, experts)
    own = exchange(sliced, "expert").reshape(2 * group, part)
    facts = jnp.concatenate(
        [jnp.zeros((rows, 2), F32), inverse, gates, routes.astype(F32)], axis=1
    )
    facts = jnp.pad(facts, ((0, 0), (0, 128 - facts.shape[1])))
    backs = list(pack(mine_at, summed, slot.T, experts, capacity))

    def move(after, turns):
        after, *ready = lax.optimization_barrier((after, *[backs[r] for r in turns]))
        for r, x in zip(turns, ready):
            pairs = [(i, (i // RING + r // RING) % HALVES * RING + (i + r) % RING) for i in range(experts)]
            backs[r] = lax.ppermute(x, "expert", pairs)
        return after


    def landed(value, turns):
        value, *done = lax.optimization_barrier((value, *[backs[r] for r in turns]))
        for r, x in zip(turns, done):
            backs[r] = x
        return value

    slot_ids = jnp.arange(slots, dtype=I32)[None, :]
    picks = [slot[:, k : k + 1] == slot_ids for k in range(2)]
    gate_slot = jnp.sum(
        jnp.where(picks[0], gates[:, 0:1], 0.0) + jnp.where(picks[1], gates[:, 1:2], 0.0), axis=0
    )
    taken = picks[0] | picks[1]
    inverse_slot = jnp.sum(jnp.where(taken, inverse, 0.0), axis=0)
    sequence = (jnp.arange(rows, dtype=I32) // SEQ).astype(F32)
    sequence_slot = jnp.sum(jnp.where(taken, sequence[:, None], 0.0), axis=0)
    notes = jnp.stack([gate_slot, inverse_slot, sequence_slot, spread_positive])
    notes = jnp.pad(notes, ((0, 4), (0, 0)))

    own, *backs = lax.optimization_barrier((own, *backs))
    near = spread(own, "u", outer)
    facts, fetched = overlaps(summed, received, slot, facts, experts)
    near, facts, fetched = lax.optimization_barrier((near, facts, fetched))
    far = swap_core(near)
    near, far = near.reshape(columns, part), far.reshape(columns, part)
    offered = pl.pallas_call(
        scores_kernel,
        in_specs=[VMEM] * 4,
        out_specs=HBM,
        out_shape=pltpu.HBM((experts, 2 * group + 8, columns), F32),
        scratch_shapes=[pltpu.VMEM((2 * group + 8, columns), F32), pltpu.SemaphoreType.DMA((experts,))],
        compiler_params=params(2),
    )(own, near, far, notes)
    offered = move(offered, TURNS[0])
    gathered = exchange(offered, "expert")
    devices = outer * CORES
    offered, kept = pl.pallas_call(
        functools.partial(totals_kernel, scale),
        in_specs=[VMEM],
        out_specs=[HBM] * 2,
        out_shape=[pltpu.HBM((devices, 8, 128), F32), pltpu.HBM((3 * group, columns), F32)],
        scratch_shapes=[
            pltpu.VMEM((3 * group, columns), F32),
            pltpu.VMEM((devices, 8, 128), F32),
            pltpu.SemaphoreType.DMA(()),
            pltpu.SemaphoreType.DMA(()),
        ],
        compiler_params=params(2),
    )(gathered)
    heard = exchange(offered, ("u", "c"))
    heard = landed(heard, TURNS[0][:1])
    offered, loss = pl.pallas_call(
        functools.partial(gradient_kernel, scale),
        in_specs=[SMEM] + [VMEM] * 4,
        out_specs=[HBM, VMEM],
        out_shape=[pltpu.HBM((experts, 2 * group, part), BF16), jax.ShapeDtypeStruct((1, 1), F32)],
        scratch_shapes=[pltpu.VMEM((2 * group, part), BF16), pltpu.SemaphoreType.DMA((experts,))],
        compiler_params=params(2),
    )((loss_scale / pairs)[None], heard, kept, near, far)
    offered = move(offered, TURNS[1])
    grads = exchange(offered, "expert")
    grads = landed(grads, TURNS[0][1:])

    router_part, state, weighted = pl.pallas_call(
        router_kernel,
        in_specs=[VMEM] * 2 + [HBM] * 4,
        out_specs=[VMEM, HBM, HBM],
        out_shape=[
            jax.ShapeDtypeStruct((width * experts // 128, 128), F32),
            pltpu.HBM((rows, 128), F32),
            pltpu.HBM((rows // SEQ, width), F32),
        ],
        scratch_shapes=[
            pltpu.VMEM((experts, rows, part), F32),
            pltpu.VMEM((experts, 2 * rows, part), BF16),
            pltpu.VMEM((experts, rows, part), BF16),
            pltpu.VMEM((rows, 128), F32),
            pltpu.VMEM((rows, 128), F32),
            pltpu.VMEM((rows // SEQ, width), F32),
            pltpu.VMEM((3, rows, 128), F32),
            pltpu.SemaphoreType.DMA((3, experts)),
            pltpu.SemaphoreType.DMA(()),
            pltpu.SemaphoreType.DMA((2,)),
        ],
        compiler_params=params(16),
    )(grads, gain, *in_hbm(summed, fetched, tokens, facts))
    router_part = move(router_part, TURNS[2])
    router_part = exchange(router_part.reshape(outer, -1, 128), "u")
    turned = jnp.pad(router.T, ((0, 128 - experts), (0, 0)))
    token_grad = token_rows(summed, weighted, state, turned, experts)
    router_part, token_grad = lax.optimization_barrier((router_part, token_grad))
    router_part = jnp.sum(router_part, axis=0)
    router_part = spread(router_part, ("c", "expert"), CORES * experts)
    held = lax.dynamic_slice_in_dim(gathered[:, 2 * group : 2 * group + 3], mine * capacity, capacity, axis=2)
    held = jnp.pad(jnp.transpose(held, (0, 2, 1)), ((0, 0), (0, 0), (0, 5)))
    parts = [(0,) + TURNS[0] + TURNS[1], TURNS[2]]
    places = [
        jnp.stack([shifted(mine, (HALVES - r // RING) % HALVES, (RING - r % RING) % RING) for r in turns])
        for turns in parts
    ]
    expert_grad = expert_rows(places[0], grads, gain, held, [backs[r] for r in parts[0]])
    router_part, expert_grad = lax.optimization_barrier((router_part, expert_grad))
    router_part = jnp.sum(router_part, axis=0)
    router_all = spread(router_part, "u", outer)
    expert_grad = expert_rows(places[1], grads, gain, held, [backs[r] for r in parts[1]], expert_grad)
    router_all, expert_grad = lax.optimization_barrier((router_all, expert_grad))
    router_grad = router_all.reshape(-1, experts, 128).transpose(1, 0, 2).reshape(experts, width).T
    return token_grad, expert_grad.reshape(1, 1, experts, capacity, width), router_grad, loss[0, 0] / pairs


def solution(mesh):
    outer = mesh.shape["dp"] // CORES
    fine = Mesh(mesh.devices.reshape(outer, CORES, mesh.shape["expert"]), ("u", "c", "expert"))
    everywhere = ("u", "c", "expert")
    return jax.shard_map(
        shards,
        mesh=fine,
        in_specs=(
            P(everywhere, None),
            P(everywhere, None),
            P(everywhere),
            P(("u", "c"), "expert", None, None, None),
            P(),
            P(),
            P(),
        ),
        out_specs=(P(everywhere, None), P(("u", "c"), "expert", None, None, None), P(), P()),
        check_vma=False,
    )
```

```python
import functools
import math

import jax
import jax.numpy as jnp
from jax import lax
from jax.experimental import pallas as pl
from jax.experimental.pallas import tpu as pltpu
from jax.sharding import Mesh, PartitionSpec as P

PAIR_DEV = 2
SEQ = 48
EPS = 1e-05
CORES = 2
ROWS_DEV = 2 * PAIR_DEV
F32 = jnp.float32
BF16 = jnp.bfloat16
I32 = jnp.int32
VMEM = pl.BlockSpec(memory_space=pltpu.VMEM)
SMEM = pl.BlockSpec(memory_space=pltpu.SMEM)
HBM = pl.BlockSpec(memory_space=pltpu.HBM)
NT = (((1,), (1,)), ((), ()))
TURNS = ((4, 1, 3, 2), (5, 7), (6,))
HALVES, RING = 2, 4


def iota(shape, dim):
    return lax.broadcasted_iota(I32, shape, dim)


def params(mib):
    return pltpu.CompilerParams(vmem_limit_bytes=mib << 20)


def cost(flops, moved):
    return pl.CostEstimate(flops=flops, bytes_accessed=moved, transcendentals=0)


def fold(x):
    total = x[:, :128]
    for k in range(1, x.shape[1] // 128):
        total = total + x[:, 128 * k : 128 * (k + 1)]
    return total


def in_hbm(*arrays):
    return [pltpu.with_memory_space_constraint(x, pltpu.HBM) for x in arrays]


def shifted(index, halves, along):
    return lax.rem(index // RING + halves, HALVES) * RING + lax.rem(lax.rem(index, RING) + along, RING)


def copy_all(copies):
    for copy in copies:
        copy.start()
    for copy in copies:
        copy.wait()


def to_each(source, target, sems):
    copy_all([pltpu.make_async_copy(source, target.at[i], sems.at[i]) for i in range(target.shape[0])])


def swap_core(x):
    return lax.ppermute(x, "c", [(0, 1), (1, 0)])


def exchange(x, axes):
    return lax.all_to_all(x, axes, split_axis=0, concat_axis=0, tiled=True)


def spread(x, axes, size):
    return exchange(jnp.broadcast_to(x[None], (size,) + x.shape), axes)


def routing(tokens, routes, router, experts, capacity):
    logits = jnp.dot(tokens, router, preferred_element_type=F32)
    lanes = jnp.arange(experts, dtype=I32)[None, None, :]
    one_hot = (routes[:, :, None] == lanes).astype(F32)
    chosen = jnp.sum(one_hot * logits[:, None, :], axis=2)
    gates = jax.nn.softmax(chosen, axis=1)
    rows = routes.shape[0]
    hits = jnp.sum(one_hot, axis=1)
    order = jnp.arange(rows, dtype=I32)
    earlier = (order[None, :] < order[:, None]).astype(BF16)
    before = jnp.dot(earlier, hits.astype(BF16), preferred_element_type=F32)
    rank = jnp.sum(one_hot * before[:, None, :], axis=2).astype(I32)
    return gates, routes * capacity + rank


def one_hots(slot, slots):
    ids = iota((slot.shape[0], slots), 1)
    return jnp.concatenate([(slot[:, k : k + 1] == ids).astype(BF16) for k in range(2)], axis=0)


def forward_kernel(
    steps, tok, rec, slot, gate, gain, summed, sliced_out, inverse, held, square, picks, sliced, row_sem, slice_sem
):
    step = pl.program_id(0)
    rows, part = tok.shape

    def keep(e):
        start = pl.multiple_of(e * part, part)
        return pltpu.make_async_copy(held.at[e], summed.at[:, pl.ds(start, part)], row_sem.at[e])

    @pl.when(step == 0)
    def _():
        square[...] = jnp.zeros_like(square)
        picks[...] = one_hots(slot, rec.shape[0])

    for k in range(part // 256):
        cols = slice(256 * k, 256 * (k + 1))
        both = jnp.dot(picks[...], rec[:, cols], preferred_element_type=F32)
        x = tok[:, cols].astype(F32) + gate[:, 0:1] * both[:rows] + gate[:, 1:2] * both[rows:]
        held[step, :, cols] = x
        square[...] += fold(x * x)
    keep(step).start()

    @pl.when(step == steps - 1)
    def _():
        mean = jnp.sum(square[...], axis=1, keepdims=True) / (steps * part)
        scale = lax.rsqrt(mean + EPS)
        inverse[...] = scale
        count = rows // SEQ
        for e in range(steps):
            x = held[e] * scale
            x = jnp.sum(x.reshape(count, SEQ, part), axis=1) / SEQ
            sliced[e] = (x * gain[:, part * e : part * (e + 1)]).astype(BF16)
        offer = pltpu.make_async_copy(sliced, sliced_out, slice_sem)
        offer.start()
        for e in range(steps):
            keep(e).wait()
        offer.wait()


def forward(tokens, received, slot, gates, gain, experts):
    rows, width = tokens.shape
    slots = received.shape[0]
    part = width // experts
    whole = lambda shape: pl.BlockSpec(shape, lambda i: (0,) * len(shape))
    return pl.pallas_call(
        functools.partial(forward_kernel, experts),
        grid=(experts,),
        in_specs=[
            pl.BlockSpec((rows, part), lambda i: (0, i)),
            pl.BlockSpec((slots, part), lambda i: (0, i)),
            whole((rows, 2)),
            whole((rows, 2)),
            whole((1, width)),
        ],
        out_specs=[HBM, HBM, whole((rows, 1))],
        out_shape=[
            pltpu.HBM((rows, width), F32),
            pltpu.HBM((experts, rows // SEQ, part), BF16),
            jax.ShapeDtypeStruct((rows, 1), F32),
        ],
        scratch_shapes=[
            pltpu.VMEM((experts, rows, part), F32),
            pltpu.VMEM((rows, 128), F32),
            pltpu.VMEM((2 * rows, slots), BF16),
            pltpu.VMEM((experts, rows // SEQ, part), BF16),
            pltpu.SemaphoreType.DMA((experts,)),
            pltpu.SemaphoreType.DMA(()),
        ],
        compiler_params=params(14),
        cost_estimate=cost(4 * rows * slots * width, 10 << 20),
    )(tokens, received, slot, gates, gain)


def pack_kernel(place, x, turned, *rest):
    *outs, spot, packed, sems = rest
    step, steps = pl.program_id(0), packed.shape[0]
    rows, part = x.shape
    capacity = outs[0].shape[0]
    slots = spot.shape[0]

    def leave(e, i):
        start = pl.multiple_of(e * part, part)
        return pltpu.make_async_copy(
            packed.at[e, pl.ds(i * capacity, capacity)], outs[i].at[:, pl.ds(start, part)], sems.at[e, i]
        )

    @pl.when(step == 0)
    def _():
        row = iota((slots, 1), 0)
        chunk = row // capacity
        target = shifted(place[0], chunk // RING, lax.rem(chunk, RING)) * capacity + lax.rem(row, capacity)
        spot[...] = ((turned[0:1, :] == target) | (turned[1:2, :] == target)).astype(BF16)

    for k in range(part // 512):
        cols = slice(512 * k, 512 * (k + 1))
        packed[step, :, cols] = jnp.dot(
            spot[...], x[:, cols].astype(BF16), preferred_element_type=F32
        ).astype(BF16)
    for i in range(len(outs)):
        leave(step, i).start()

    @pl.when(step == steps - 1)
    def _():
        for e in range(steps):
            for i in range(len(outs)):
                leave(e, i).wait()


def pack(place, summed, turned, experts, capacity):
    rows, width = summed.shape
    steps = experts // 2
    part = width // steps
    slots = experts * capacity
    return pl.pallas_call(
        pack_kernel,
        grid=(steps,),
        in_specs=[
            SMEM,
            pl.BlockSpec((rows, part), lambda i: (0, i)),
            pl.BlockSpec((2, rows), lambda i: (0, 0)),
        ],
        out_specs=[HBM] * experts,
        out_shape=[pltpu.HBM((capacity, width), BF16)] * experts,
        scratch_shapes=[
            pltpu.VMEM((slots, rows), BF16),
            pltpu.VMEM((steps, slots, part), BF16),
            pltpu.SemaphoreType.DMA((steps, experts)),
        ],
        compiler_params=params(14),
        cost_estimate=cost(2 * rows * slots * width, 7 << 20),
    )(place, *in_hbm(summed), turned)


def overlap_kernel(steps, x, rec, slot, facts, out, fetched, picks, dots):
    step = pl.program_id(0)
    rows, part = x.shape

    @pl.when(step == 0)
    def _():
        dots[...] = jnp.zeros_like(dots)
        picks[...] = one_hots(slot, rec.shape[0])

    for k in range(part // 256):
        cols = slice(256 * k, 256 * (k + 1))
        both = jnp.dot(picks[...], rec[:, cols], preferred_element_type=F32)
        fetched[:, cols] = both.astype(BF16)
        value = x[:, cols]
        dots[:rows] += fold(value * both[:rows])
        dots[rows:] += fold(value * both[rows:])

    @pl.when(step == steps - 1)
    def _():
        lane = iota((rows, 128), 1)
        known = facts[...]
        for k in range(2):
            total = jnp.sum(dots[rows * k : rows * (k + 1)], axis=1, keepdims=True)
            known = jnp.where(lane == k, total, known)
        out[...] = known


def overlaps(summed, received, slot, facts, experts):
    rows, width = summed.shape
    slots = received.shape[0]
    part = width // experts
    whole = lambda shape: pl.BlockSpec(shape, lambda i: (0, 0))
    return pl.pallas_call(
        functools.partial(overlap_kernel, experts),
        grid=(experts,),
        in_specs=[
            pl.BlockSpec((rows, part), lambda i: (0, i)),
            pl.BlockSpec((slots, part), lambda i: (0, i)),
            whole((rows, 2)),
            whole((rows, 128)),
        ],
        out_specs=[whole((rows, 128)), pl.BlockSpec((2 * rows, part), lambda i: (0, i))],
        out_shape=[pltpu.HBM((rows, 128), F32), pltpu.HBM((2 * rows, width), BF16)],
        scratch_shapes=[pltpu.VMEM((2 * rows, slots), BF16), pltpu.VMEM((2 * rows, 128), F32)],
        compiler_params=params(12),
        cost_estimate=cost(4 * rows * slots * width, 10 << 20),
    )(*in_hbm(summed, received), slot, facts)


def lanes_of(shape, dim):
    lane = iota(shape, dim)
    kind = lax.rem(lane, ROWS_DEV)
    return lane, kind, kind >= PAIR_DEV


def picker(group, kind, turned=False):
    wide = 2 * group
    shape, pair, row = ((wide, group), 1, 0) if turned else ((group, wide), 0, 1)
    a = iota(shape, pair)
    b = iota(shape, row)
    source = (a // PAIR_DEV) * ROWS_DEV + lax.rem(a, PAIR_DEV) + PAIR_DEV * kind
    return (source == b).astype(BF16)


def scores_kernel(own, near, far, notes, offered, whole, sems):
    experts, total, columns = offered.shape
    group = experts * PAIR_DEV
    queries, records = [
        jnp.dot(picker(group, kind), own[...], preferred_element_type=F32).astype(BF16) for kind in (0, 1)
    ]
    at_record = lanes_of((group, columns), 1)[2]
    for k, side in enumerate((near, far)):
        every = side[...]
        by_query = lax.dot_general(queries, every, NT, preferred_element_type=F32)
        by_record = lax.dot_general(records, every, NT, preferred_element_type=F32)
        whole[group * k : group * (k + 1)] = jnp.where(at_record, by_query, by_record)
    whole[2 * group :] = notes[...]
    to_each(whole, offered, sems)


def totals_kernel(scale, gathered, offered, kept_out, kept, spread, kept_sem, sem):
    place, core = lax.axis_index("u"), lax.axis_index("c")
    experts, total, columns = gathered.shape
    group = experts * PAIR_DEV
    both = gathered[0]
    for e in range(1, experts):
        both = both + gathered[e]
    positive_lane = both[2 * group + 3 : 2 * group + 4, :]
    near, far = both[:group] * scale, both[group : 2 * group] * scale
    kept[0:group] = near
    kept[group : 2 * group] = far

    shape = (group, columns)
    lane, kind, at_record = lanes_of(shape, 1)
    pair = iota(shape, 0)
    within = lax.rem(lane, 2 * group)
    matching = (within // ROWS_DEV == pair // PAIR_DEV) & (kind == lax.rem(pair, PAIR_DEV))
    here = matching & (lane // (2 * group) == place)
    positive = jnp.sum(jnp.where(here, positive_lane, 0.0), axis=1, keepdims=True)

    low = jnp.float32(-jnp.inf)
    near_records = jnp.where(at_record, near, low)
    far_records = jnp.where(at_record, far, low)
    highest = jnp.maximum(
        jnp.max(near_records, axis=1, keepdims=True), jnp.max(far_records, axis=1, keepdims=True)
    )
    weight = jnp.sum(jnp.exp(near_records - highest), axis=1, keepdims=True) + jnp.sum(
        jnp.exp(far_records - highest), axis=1, keepdims=True
    )
    log_total = highest + jnp.log(weight)
    chosen = jnp.zeros((group, 1), F32)
    for side, where in ((near, core), (far, 1 - core)):
        name = column_names(lane, kind, group, where)
        hit = at_record & (name.astype(F32) == positive)
        chosen = chosen + jnp.sum(jnp.where(hit, side, 0.0), axis=1, keepdims=True)
    kept[2 * group : 3 * group, :128] = jnp.broadcast_to(log_total, (group, 128))
    kept[2 * group : 3 * group, 128:256] = jnp.broadcast_to(positive, (group, 128))
    saved = pltpu.make_async_copy(kept, kept_out, kept_sem)
    saved.start()
    row_loss = log_total - chosen

    total_lane = jnp.sum(jnp.where(here, log_total, 0.0), axis=0, keepdims=True)
    loss_lane = jnp.sum(jnp.where(here, row_loss, 0.0), axis=0, keepdims=True)
    own_lane = jnp.where(lane[0:1] // (2 * group) == place, positive_lane, 0.0)
    pieces = [x[:, 128 * k : 128 * (k + 1)] for x in (total_lane, own_lane) for k in range(columns // 128)]
    loss_pieces = [
        pltpu.roll(loss_lane, PAIR_DEV, 1)[:, 128 * k : 128 * (k + 1)] for k in range(columns // 128)
    ]
    pieces = [a + b for a, b in zip(pieces, loss_pieces)] + pieces[columns // 128 :]
    message = jnp.concatenate(pieces, axis=0)
    for d in range(spread.shape[0]):
        spread[d] = message
    copy_all([pltpu.make_async_copy(spread, offered, sem)])
    saved.wait()


def column_names(lane, kind, group, core):
    wide = 2 * group
    block = (lane // wide) * CORES + core
    return block * group + (lax.rem(lane, wide) // ROWS_DEV) * PAIR_DEV + lax.rem(kind, PAIR_DEV)


def gradient_kernel(scale, factor, heard, kept, near, far, offered, loss, whole, sems):
    place, core = lax.axis_index("u"), lax.axis_index("c")
    experts, wide, columns = offered.shape
    group = wide // 2
    outer_size = heard.shape[0] // CORES
    pieces = columns // 128
    shape = (group, columns)
    lane, kind, at_record = lanes_of(shape, 1)
    pair = iota(shape, 0)
    own_name = (place * CORES + core) * group + iota((group, 1), 0)
    own_total = kept[2 * group : 3 * group, 0:1]
    own_positive = kept[2 * group : 3 * group, 128:129]
    result = jnp.zeros((wide, columns), F32)
    losses = jnp.zeros((1, columns), F32)
    for k, (side, where) in enumerate(((near, core), (far, 1 - core))):
        told = heard[where]
        for u in range(1, outer_size):
            told = told + heard[u * CORES + where]
        total = jnp.concatenate([told[i : i + 1] for i in range(pieces)], axis=1)
        positive = jnp.concatenate([told[pieces + i : pieces + i + 1] for i in range(pieces)], axis=1)
        losses = losses + jnp.where(at_record[0:1], total, 0.0)
        value = kept[group * k : group * (k + 1), :]
        name = column_names(lane, kind, group, where).astype(F32)
        hit = jnp.where(name == own_positive, 1.0, 0.0)
        by_query = (jnp.exp(value - own_total) - hit) * factor[0]
        by_query = jnp.where(at_record, by_query, 0.0).astype(BF16)
        hit = jnp.where(positive == own_name.astype(F32), 1.0, 0.0)
        by_record = (jnp.exp(jnp.where(at_record, 0.0, value - total)) - hit) * factor[0]
        by_record = jnp.where(at_record, 0.0, by_record).astype(BF16)
        rows = jnp.dot(picker(group, 0, True), by_query, preferred_element_type=F32) + jnp.dot(
            picker(group, 1, True), by_record, preferred_element_type=F32
        )
        result = result + jnp.dot(rows.astype(BF16), side[...], preferred_element_type=F32)
    whole[...] = (result * scale).astype(BF16)
    to_each(whole, offered, sems)
    loss[...] = jnp.sum(losses, axis=1, keepdims=True)


def rows_of(grads, e, index):
    tile = grads[e, pl.ds(pl.multiple_of((index // 4) * 16, 16), 16), :].astype(F32)
    piece = lax.rem(index, 4)
    quarters = [tile[ROWS_DEV * k : ROWS_DEV * (k + 1)] for k in range(4)]
    half = jnp.where(piece < 2, quarters[0], quarters[2]), jnp.where(piece < 2, quarters[1], quarters[3])
    return jnp.where(lax.rem(piece, 2) == 0, half[0], half[1])


def router_kernel(
    grads, gain, summed_in, fetched_in, tok_in, facts_in, part_out, state_out, weighted_out,
    summed, fetched, tok, facts, state, weighted, acc, sems, facts_sem, out_sems
):
    experts, _, part = grads.shape
    rows = summed.shape[1]
    count = rows // SEQ
    sources = ((summed_in, summed), (fetched_in, fetched), (tok_in, tok))

    def load(e):
        cols = pl.ds(e * part, part)
        return [
            pltpu.make_async_copy(a.at[:, cols], b.at[e], sems.at[k, e]) for k, (a, b) in enumerate(sources)
        ]

    known = pltpu.make_async_copy(facts_in, facts, facts_sem)
    loads = [load(e) for e in range(experts)]
    for e in range(experts):
        loads[e][0].start()
        loads[e][1].start()
    known.start()
    for e in range(experts):
        loads[e][2].start()

    for e in range(experts):
        cols = slice(part * e, part * (e + 1))
        w = rows_of(grads, e, lax.axis_index("expert")) * (gain[:, cols] / SEQ)
        weighted[:, cols] = w
        loads[e][0].wait()
        loads[e][1].wait()
        for q in range(count):
            row = w[q : q + 1, :]
            at = [slice(rows * k + SEQ * q, rows * k + SEQ * (q + 1)) for k in range(2)]
            terms = [summed[e, at[0], :], fetched[e, at[0], :].astype(F32), fetched[e, at[1], :].astype(F32)]
            for k, term in enumerate(terms):
                total = fold(term * row)
                spot = slice(SEQ * q, SEQ * (q + 1))
                acc[k, spot] = total if e == 0 else acc[k, spot] + total
    known.wait()
    lanes = iota((SEQ, 128), 1)
    choices = []
    for q in range(count):
        at = slice(SEQ * q, SEQ * (q + 1))
        fact = facts[at, :]
        inv = fact[:, 2:3]
        shrink = inv * inv * inv * (jnp.sum(acc[0, at], axis=1, keepdims=True) / (experts * part))
        grad_gate = []
        for k in range(2):
            along = jnp.sum(acc[1 + k, at], axis=1, keepdims=True)
            grad_gate.append(inv * along - shrink * fact[:, k : k + 1])
        gates = [fact[:, 3 + k : 4 + k] for k in range(2)]
        mean = gates[0] * grad_gate[0] + gates[1] * grad_gate[1]
        choice = jnp.zeros((SEQ, 128), F32)
        for k in range(2):
            chosen = gates[k] * (grad_gate[k] - mean)
            route = fact[:, 5 + k : 6 + k].astype(I32)
            choice = choice + jnp.where(route == lanes, chosen, 0.0)
        choices.append(choice)
        choice = jnp.where(lanes == experts, inv, choice)
        state[at] = jnp.where(lanes == experts + 1, shrink, choice)
    saved = [
        pltpu.make_async_copy(state, state_out, out_sems.at[0]),
        pltpu.make_async_copy(weighted, weighted_out, out_sems.at[1]),
    ]
    for copy in saved:
        copy.start()
    lhs = jnp.transpose(jnp.concatenate(choices, axis=0))[:experts].astype(BF16)
    tiles = part // 128
    for e in range(experts):
        loads[e][2].wait()
        block = jnp.dot(lhs, tok[e], preferred_element_type=F32)
        for k in range(tiles):
            at = experts * (tiles * e + k)
            part_out[at : at + experts, :] = block[:, 128 * k : 128 * (k + 1)]
    for copy in saved:
        copy.wait()


def token_kernel(experts, summed, weighted, state, router, out):
    rows = summed.shape[0]
    known = state[...]
    choice = jnp.where(iota(known.shape, 1) < experts, known, 0.0).astype(BF16)
    through = jnp.dot(choice, router[...], preferred_element_type=F32)
    for q in range(rows // SEQ):
        at = slice(SEQ * q, SEQ * (q + 1))
        inverse, shrink = known[at, experts : experts + 1], known[at, experts + 1 : experts + 2]
        x = inverse * weighted[q : q + 1, :] - shrink * summed[at]
        out[at] = (x + through[SEQ * q : SEQ * (q + 1)]).astype(BF16)


def token_rows(summed, weighted, state, router, experts):
    rows, width = summed.shape
    part = width // experts
    split = lambda count: pl.BlockSpec((count, part), lambda i: (0, i))
    return pl.pallas_call(
        functools.partial(token_kernel, experts),
        grid=(experts,),
        in_specs=[
            split(rows),
            split(weighted.shape[0]),
            pl.BlockSpec((rows, 128), lambda i: (0, 0)),
            split(128),
        ],
        out_specs=split(rows),
        out_shape=jax.ShapeDtypeStruct((rows, width), BF16),
        compiler_params=params(10),
        cost_estimate=cost(2 * rows * 128 * width, 5 << 20),
    )(*in_hbm(summed, weighted, state), router)


def expert_kernel(count, source, grads, gain, notes, *rest):
    sources, (out, backs, sems) = rest[:count], rest[-3:]
    experts, _, part = grads.shape
    step = pl.program_id(0)
    gate, inv, seq = notes[0, :, 0:1], notes[0, :, 1:2], notes[0, :, 2:3]
    capacity = gate.shape[0]
    loads = [pltpu.make_async_copy(sources[r], backs.at[r], sems.at[r]) for r in range(count)]

    @pl.when(step == 0)
    def _():
        for load in loads:
            load.start()

    for r in range(count):

        @pl.when(step == r)
        def _():
            loads[r].wait()

    def gradient_rows(e):
        w = rows_of(grads, e, source[step]) * (gain[:, part * e : part * (e + 1)] / SEQ)
        x = jnp.broadcast_to(w[0:1], (capacity, part))
        for s in range(1, ROWS_DEV):
            x = jnp.where(seq == s, w[s : s + 1], x)
        return x

    acc = jnp.zeros((capacity, 128), F32)
    for e in range(experts):
        back = backs[step, :, part * e : part * (e + 1)].astype(F32)
        acc = acc + fold(gradient_rows(e) * back)
    shrink = inv * inv * inv * (jnp.sum(acc, axis=1, keepdims=True) / (experts * part))
    keep, drop = gate * inv, gate * shrink
    for e in range(experts):
        cols = slice(part * e, part * (e + 1))
        out[0, :, cols] = (keep * gradient_rows(e) - drop * backs[step, :, cols].astype(F32)).astype(BF16)


def expert_rows(source, grads, gain, notes, backs, before=None):
    experts, capacity = notes.shape[:2]
    width = gain.shape[1]
    count = len(backs)
    whole = lambda shape: pl.BlockSpec(shape, lambda i, p: (0,) * len(shape))
    block = lambda i, p: (p[i], 0, 0)
    kept = [] if before is None else [before]
    return pl.pallas_call(
        functools.partial(expert_kernel, count),
        grid_spec=pltpu.PrefetchScalarGridSpec(
            num_scalar_prefetch=1,
            grid=(count,),
            in_specs=[
                whole(grads.shape),
                whole((1, width)),
                pl.BlockSpec((1, capacity, notes.shape[2]), block),
            ]
            + [HBM] * (count + len(kept)),
            out_specs=pl.BlockSpec((1, capacity, width), block),
            scratch_shapes=[
                pltpu.VMEM((count, capacity, width), BF16),
                pltpu.SemaphoreType.DMA((count,)),
            ],
        ),
        out_shape=jax.ShapeDtypeStruct((experts, capacity, width), BF16),
        input_output_aliases={4 + count: 0} if kept else {},
        compiler_params=params(16),
        cost_estimate=cost(12 * count * capacity * width, count << 20),
    )(source, grads, gain, notes, *in_hbm(*backs), *kept)


def shards(tokens, routes, positives, expert_out, router, norm_gain, loss_scale):
    experts, capacity, width = expert_out.shape[2:]
    rows = tokens.shape[0]
    slots = experts * capacity
    outer = lax.axis_size("u")
    mine = lax.axis_index("expert").astype(I32)
    mine_at = mine[None]
    part = width // experts
    group = PAIR_DEV * experts
    pairs = group * outer * CORES
    scale = 4.0 / math.sqrt(width)
    gain = norm_gain[None, :]
    columns = outer * experts * ROWS_DEV

    received = exchange(expert_out.reshape(experts, capacity, width), "expert").reshape(slots, width)
    gates, slot = routing(tokens, routes, router, experts, capacity)
    lane = jnp.arange(columns, dtype=I32)
    spread_positive = jnp.where(
        (lane % (2 * group)) // ROWS_DEV == mine,
        jnp.where(lane % ROWS_DEV == 0, positives[0], positives[1]) * (lane % ROWS_DEV < PAIR_DEV),
        0,
    ).astype(F32)

    summed, sliced, inverse = forward(tokens, received, slot, gates, gain, experts)
    own = exchange(sliced, "expert").reshape(2 * group, part)
    facts = jnp.concatenate(
        [jnp.zeros((rows, 2), F32), inverse, gates, routes.astype(F32)], axis=1
    )
    facts = jnp.pad(facts, ((0, 0), (0, 128 - facts.shape[1])))
    backs = list(pack(mine_at, summed, slot.T, experts, capacity))

    def move(after, turns):
        after, *ready = lax.optimization_barrier((after, *[backs[r] for r in turns]))
        for r, x in zip(turns, ready):
            pairs = [(i, (i // RING + r // RING) % HALVES * RING + (i + r) % RING) for i in range(experts)]
            backs[r] = lax.ppermute(x, "expert", pairs)
        return after


    def landed(value, turns):
        value, *done = lax.optimization_barrier((value, *[backs[r] for r in turns]))
        for r, x in zip(turns, done):
            backs[r] = x
        return value

    slot_ids = jnp.arange(slots, dtype=I32)[None, :]
    picks = [slot[:, k : k + 1] == slot_ids for k in range(2)]
    gate_slot = jnp.sum(
        jnp.where(picks[0], gates[:, 0:1], 0.0) + jnp.where(picks[1], gates[:, 1:2], 0.0), axis=0
    )
    taken = picks[0] | picks[1]
    inverse_slot = jnp.sum(jnp.where(taken, inverse, 0.0), axis=0)
    sequence = (jnp.arange(rows, dtype=I32) // SEQ).astype(F32)
    sequence_slot = jnp.sum(jnp.where(taken, sequence[:, None], 0.0), axis=0)
    notes = jnp.stack([gate_slot, inverse_slot, sequence_slot, spread_positive])
    notes = jnp.pad(notes, ((0, 4), (0, 0)))

    own, *backs = lax.optimization_barrier((own, *backs))
    near = spread(own, "u", outer)
    facts, fetched = overlaps(summed, received, slot, facts, experts)
    near, facts, fetched = lax.optimization_barrier((near, facts, fetched))
    far = swap_core(near)
    near, far = near.reshape(columns, part), far.reshape(columns, part)
    offered = pl.pallas_call(
        scores_kernel,
        in_specs=[VMEM] * 4,
        out_specs=HBM,
        out_shape=pltpu.HBM((experts, 2 * group + 8, columns), F32),
        scratch_shapes=[pltpu.VMEM((2 * group + 8, columns), F32), pltpu.SemaphoreType.DMA((experts,))],
        compiler_params=params(2),
    )(own, near, far, notes)
    offered = move(offered, TURNS[0])
    gathered = exchange(offered, "expert")
    devices = outer * CORES
    offered, kept = pl.pallas_call(
        functools.partial(totals_kernel, scale),
        in_specs=[VMEM],
        out_specs=[HBM] * 2,
        out_shape=[pltpu.HBM((devices, 8, 128), F32), pltpu.HBM((3 * group, columns), F32)],
        scratch_shapes=[
            pltpu.VMEM((3 * group, columns), F32),
            pltpu.VMEM((devices, 8, 128), F32),
            pltpu.SemaphoreType.DMA(()),
            pltpu.SemaphoreType.DMA(()),
        ],
        compiler_params=params(2),
    )(gathered)
    heard = exchange(offered, ("u", "c"))
    heard = landed(heard, TURNS[0][:1])
    offered, loss = pl.pallas_call(
        functools.partial(gradient_kernel, scale),
        in_specs=[SMEM] + [VMEM] * 4,
        out_specs=[HBM, VMEM],
        out_shape=[pltpu.HBM((experts, 2 * group, part), BF16), jax.ShapeDtypeStruct((1, 1), F32)],
        scratch_shapes=[pltpu.VMEM((2 * group, part), BF16), pltpu.SemaphoreType.DMA((experts,))],
        compiler_params=params(2),
    )((loss_scale / pairs)[None], heard, kept, near, far)
    offered = move(offered, TURNS[1])
    grads = exchange(offered, "expert")
    grads = landed(grads, TURNS[0][1:])

    router_part, state, weighted = pl.pallas_call(
        router_kernel,
        in_specs=[VMEM] * 2 + [HBM] * 4,
        out_specs=[VMEM, HBM, HBM],
        out_shape=[
            jax.ShapeDtypeStruct((width * experts // 128, 128), F32),
            pltpu.HBM((rows, 128), F32),
            pltpu.HBM((rows // SEQ, width), F32),
        ],
        scratch_shapes=[
            pltpu.VMEM((experts, rows, part), F32),
            pltpu.VMEM((experts, 2 * rows, part), BF16),
            pltpu.VMEM((experts, rows, part), BF16),
            pltpu.VMEM((rows, 128), F32),
            pltpu.VMEM((rows, 128), F32),
            pltpu.VMEM((rows // SEQ, width), F32),
            pltpu.VMEM((3, rows, 128), F32),
            pltpu.SemaphoreType.DMA((3, experts)),
            pltpu.SemaphoreType.DMA(()),
            pltpu.SemaphoreType.DMA((2,)),
        ],
        compiler_params=params(16),
    )(grads, gain, *in_hbm(summed, fetched, tokens, facts))
    router_part = move(router_part, TURNS[2])
    router_part = exchange(router_part.reshape(outer, -1, 128), "u")
    turned = jnp.pad(router.T, ((0, 128 - experts), (0, 0)))
    token_grad = token_rows(summed, weighted, state, turned, experts)
    router_part, token_grad = lax.optimization_barrier((router_part, token_grad))
    router_part = jnp.sum(router_part, axis=0)
    router_part = spread(router_part, ("c", "expert"), CORES * experts)
    held = lax.dynamic_slice_in_dim(gathered[:, 2 * group : 2 * group + 3], mine * capacity, capacity, axis=2)
    held = jnp.pad(jnp.transpose(held, (0, 2, 1)), ((0, 0), (0, 0), (0, 5)))
    parts = [(0,) + TURNS[0] + TURNS[1], TURNS[2]]
    places = [
        jnp.stack([shifted(mine, (HALVES - r // RING) % HALVES, (RING - r % RING) % RING) for r in turns])
        for turns in parts
    ]
    expert_grad = expert_rows(places[0], grads, gain, held, [backs[r] for r in parts[0]])
    router_part, expert_grad = lax.optimization_barrier((router_part, expert_grad))
    router_part = jnp.sum(router_part, axis=0)
    router_all = spread(router_part, "u", outer)
    expert_grad = expert_rows(places[1], grads, gain, held, [backs[r] for r in parts[1]], expert_grad)
    router_all, expert_grad = lax.optimization_barrier((router_all, expert_grad))
    router_grad = router_all.reshape(-1, experts, 128).transpose(1, 0, 2).reshape(experts, width).T
    return token_grad, expert_grad.reshape(1, 1, experts, capacity, width), router_grad, loss[0, 0] / pairs


def solution(mesh):
    outer = mesh.shape["dp"] // CORES
    fine = Mesh(mesh.devices.reshape(outer, CORES, mesh.shape["expert"]), ("u", "c", "expert"))
    everywhere = ("u", "c", "expert")
    return jax.shard_map(
        shards,
        mesh=fine,
        in_specs=(
            P(everywhere, None),
            P(everywhere, None),
            P(everywhere),
            P(("u", "c"), "expert", None, None, None),
            P(),
            P(),
            P(),
        ),
        out_specs=(P(everywhere, None), P(("u", "c"), "expert", None, None, None), P(), P()),
        check_vma=False,
    )
```

```python
import functools
import math

import jax
import jax.numpy as jnp
from jax import lax
from jax.experimental import pallas as pl
from jax.experimental.pallas import tpu as pltpu
from jax.sharding import Mesh, PartitionSpec as P

PAIR_DEV = 2
SEQ = 48
EPS = 1e-05
CORES = 2
ROWS_DEV = 2 * PAIR_DEV
F32 = jnp.float32
BF16 = jnp.bfloat16
I32 = jnp.int32
VMEM = pl.BlockSpec(memory_space=pltpu.VMEM)
SMEM = pl.BlockSpec(memory_space=pltpu.SMEM)
HBM = pl.BlockSpec(memory_space=pltpu.HBM)
NT = (((1,), (1,)), ((), ()))
TURNS = ((4, 1, 3, 2), (5, 6), (7,))
HALVES, RING = 2, 4


def iota(shape, dim):
    return lax.broadcasted_iota(I32, shape, dim)


def params(mib):
    return pltpu.CompilerParams(vmem_limit_bytes=mib << 20)


def cost(flops, moved):
    return pl.CostEstimate(flops=flops, bytes_accessed=moved, transcendentals=0)


def fold(x):
    total = x[:, :128]
    for k in range(1, x.shape[1] // 128):
        total = total + x[:, 128 * k : 128 * (k + 1)]
    return total


def in_hbm(*arrays):
    return [pltpu.with_memory_space_constraint(x, pltpu.HBM) for x in arrays]


def shifted(index, halves, along):
    return lax.rem(index // RING + halves, HALVES) * RING + lax.rem(lax.rem(index, RING) + along, RING)


def copy_all(copies):
    for copy in copies:
        copy.start()
    for copy in copies:
        copy.wait()


def to_each(source, target, sems):
    copy_all([pltpu.make_async_copy(source, target.at[i], sems.at[i]) for i in range(target.shape[0])])


def swap_core(x):
    return lax.ppermute(x, "c", [(0, 1), (1, 0)])


def exchange(x, axes):
    return lax.all_to_all(x, axes, split_axis=0, concat_axis=0, tiled=True)


def spread(x, axes, size):
    return exchange(jnp.broadcast_to(x[None], (size,) + x.shape), axes)


def routing(tokens, routes, router, experts, capacity):
    logits = jnp.dot(tokens, router, preferred_element_type=F32)
    lanes = jnp.arange(experts, dtype=I32)[None, None, :]
    one_hot = (routes[:, :, None] == lanes).astype(F32)
    chosen = jnp.sum(one_hot * logits[:, None, :], axis=2)
    gates = jax.nn.softmax(chosen, axis=1)
    rows = routes.shape[0]
    hits = jnp.sum(one_hot, axis=1)
    order = jnp.arange(rows, dtype=I32)
    earlier = (order[None, :] < order[:, None]).astype(BF16)
    before = jnp.dot(earlier, hits.astype(BF16), preferred_element_type=F32)
    rank = jnp.sum(one_hot * before[:, None, :], axis=2).astype(I32)
    return gates, routes * capacity + rank


def one_hots(slot, slots):
    ids = iota((slot.shape[0], slots), 1)
    return jnp.concatenate([(slot[:, k : k + 1] == ids).astype(BF16) for k in range(2)], axis=0)


def forward_kernel(
    steps, tok, rec, slot, gate, gain, summed, sliced_out, inverse, held, square, picks, sliced, row_sem, slice_sem
):
    step = pl.program_id(0)
    rows, part = tok.shape

    def keep(e):
        start = pl.multiple_of(e * part, part)
        return pltpu.make_async_copy(held.at[e], summed.at[:, pl.ds(start, part)], row_sem.at[e])

    @pl.when(step == 0)
    def _():
        square[...] = jnp.zeros_like(square)
        picks[...] = one_hots(slot, rec.shape[0])

    for k in range(part // 256):
        cols = slice(256 * k, 256 * (k + 1))
        both = jnp.dot(picks[...], rec[:, cols], preferred_element_type=F32)
        x = tok[:, cols].astype(F32) + gate[:, 0:1] * both[:rows] + gate[:, 1:2] * both[rows:]
        held[step, :, cols] = x
        square[...] += fold(x * x)
    keep(step).start()

    @pl.when(step == steps - 1)
    def _():
        mean = jnp.sum(square[...], axis=1, keepdims=True) / (steps * part)
        scale = lax.rsqrt(mean + EPS)
        inverse[...] = scale
        count = rows // SEQ
        for e in range(steps):
            x = held[e] * scale
            x = jnp.sum(x.reshape(count, SEQ, part), axis=1) / SEQ
            sliced[e] = (x * gain[:, part * e : part * (e + 1)]).astype(BF16)
        offer = pltpu.make_async_copy(sliced, sliced_out, slice_sem)
        offer.start()
        for e in range(steps):
            keep(e).wait()
        offer.wait()


def forward(tokens, received, slot, gates, gain, experts):
    rows, width = tokens.shape
    slots = received.shape[0]
    part = width // experts
    whole = lambda shape: pl.BlockSpec(shape, lambda i: (0,) * len(shape))
    return pl.pallas_call(
        functools.partial(forward_kernel, experts),
        grid=(experts,),
        in_specs=[
            pl.BlockSpec((rows, part), lambda i: (0, i)),
            pl.BlockSpec((slots, part), lambda i: (0, i)),
            whole((rows, 2)),
            whole((rows, 2)),
            whole((1, width)),
        ],
        out_specs=[HBM, HBM, whole((rows, 1))],
        out_shape=[
            pltpu.HBM((rows, width), F32),
            pltpu.HBM((experts, rows // SEQ, part), BF16),
            jax.ShapeDtypeStruct((rows, 1), F32),
        ],
        scratch_shapes=[
            pltpu.VMEM((experts, rows, part), F32),
            pltpu.VMEM((rows, 128), F32),
            pltpu.VMEM((2 * rows, slots), BF16),
            pltpu.VMEM((experts, rows // SEQ, part), BF16),
            pltpu.SemaphoreType.DMA((experts,)),
            pltpu.SemaphoreType.DMA(()),
        ],
        compiler_params=params(14),
        cost_estimate=cost(4 * rows * slots * width, 10 << 20),
    )(tokens, received, slot, gates, gain)


def pack_kernel(place, x, turned, *rest):
    *outs, spot, packed, sems = rest
    step, steps = pl.program_id(0), packed.shape[0]
    rows, part = x.shape
    capacity = outs[0].shape[0]
    slots = spot.shape[0]

    def leave(e, i):
        start = pl.multiple_of(e * part, part)
        return pltpu.make_async_copy(
            packed.at[e, pl.ds(i * capacity, capacity)], outs[i].at[:, pl.ds(start, part)], sems.at[e, i]
        )

    @pl.when(step == 0)
    def _():
        row = iota((slots, 1), 0)
        chunk = row // capacity
        target = shifted(place[0], chunk // RING, lax.rem(chunk, RING)) * capacity + lax.rem(row, capacity)
        spot[...] = ((turned[0:1, :] == target) | (turned[1:2, :] == target)).astype(BF16)

    for k in range(part // 512):
        cols = slice(512 * k, 512 * (k + 1))
        packed[step, :, cols] = jnp.dot(
            spot[...], x[:, cols].astype(BF16), preferred_element_type=F32
        ).astype(BF16)
    for i in range(len(outs)):
        leave(step, i).start()

    @pl.when(step == steps - 1)
    def _():
        for e in range(steps):
            for i in range(len(outs)):
                leave(e, i).wait()


def pack(place, summed, turned, experts, capacity):
    rows, width = summed.shape
    steps = experts // 2
    part = width // steps
    slots = experts * capacity
    return pl.pallas_call(
        pack_kernel,
        grid=(steps,),
        in_specs=[
            SMEM,
            pl.BlockSpec((rows, part), lambda i: (0, i)),
            pl.BlockSpec((2, rows), lambda i: (0, 0)),
        ],
        out_specs=[HBM] * experts,
        out_shape=[pltpu.HBM((capacity, width), BF16)] * experts,
        scratch_shapes=[
            pltpu.VMEM((slots, rows), BF16),
            pltpu.VMEM((steps, slots, part), BF16),
            pltpu.SemaphoreType.DMA((steps, experts)),
        ],
        compiler_params=params(14),
        cost_estimate=cost(2 * rows * slots * width, 7 << 20),
    )(place, *in_hbm(summed), turned)


def overlap_kernel(steps, x, rec, slot, facts, out, fetched, picks, dots):
    step = pl.program_id(0)
    rows, part = x.shape

    @pl.when(step == 0)
    def _():
        dots[...] = jnp.zeros_like(dots)
        picks[...] = one_hots(slot, rec.shape[0])

    for k in range(part // 256):
        cols = slice(256 * k, 256 * (k + 1))
        both = jnp.dot(picks[...], rec[:, cols], preferred_element_type=F32)
        fetched[:, cols] = both.astype(BF16)
        value = x[:, cols]
        dots[:rows] += fold(value * both[:rows])
        dots[rows:] += fold(value * both[rows:])

    @pl.when(step == steps - 1)
    def _():
        lane = iota((rows, 128), 1)
        known = facts[...]
        for k in range(2):
            total = jnp.sum(dots[rows * k : rows * (k + 1)], axis=1, keepdims=True)
            known = jnp.where(lane == k, total, known)
        out[...] = known


def overlaps(summed, received, slot, facts, experts):
    rows, width = summed.shape
    slots = received.shape[0]
    part = width // experts
    whole = lambda shape: pl.BlockSpec(shape, lambda i: (0, 0))
    return pl.pallas_call(
        functools.partial(overlap_kernel, experts),
        grid=(experts,),
        in_specs=[
            pl.BlockSpec((rows, part), lambda i: (0, i)),
            pl.BlockSpec((slots, part), lambda i: (0, i)),
            whole((rows, 2)),
            whole((rows, 128)),
        ],
        out_specs=[whole((rows, 128)), pl.BlockSpec((2 * rows, part), lambda i: (0, i))],
        out_shape=[pltpu.HBM((rows, 128), F32), pltpu.HBM((2 * rows, width), BF16)],
        scratch_shapes=[pltpu.VMEM((2 * rows, slots), BF16), pltpu.VMEM((2 * rows, 128), F32)],
        compiler_params=params(12),
        cost_estimate=cost(4 * rows * slots * width, 10 << 20),
    )(*in_hbm(summed, received), slot, facts)


def lanes_of(shape, dim):
    lane = iota(shape, dim)
    kind = lax.rem(lane, ROWS_DEV)
    return lane, kind, kind >= PAIR_DEV


def picker(group, kind, turned=False):
    wide = 2 * group
    shape, pair, row = ((wide, group), 1, 0) if turned else ((group, wide), 0, 1)
    a = iota(shape, pair)
    b = iota(shape, row)
    source = (a // PAIR_DEV) * ROWS_DEV + lax.rem(a, PAIR_DEV) + PAIR_DEV * kind
    return (source == b).astype(BF16)


def scores_kernel(own, near, far, notes, offered, whole, sems):
    experts, total, columns = offered.shape
    group = experts * PAIR_DEV
    queries, records = [
        jnp.dot(picker(group, kind), own[...], preferred_element_type=F32).astype(BF16) for kind in (0, 1)
    ]
    at_record = lanes_of((group, columns), 1)[2]
    for k, side in enumerate((near, far)):
        every = side[...]
        by_query = lax.dot_general(queries, every, NT, preferred_element_type=F32)
        by_record = lax.dot_general(records, every, NT, preferred_element_type=F32)
        whole[group * k : group * (k + 1)] = jnp.where(at_record, by_query, by_record)
    whole[2 * group :] = notes[...]
    to_each(whole, offered, sems)


def totals_kernel(scale, gathered, offered, kept_out, kept, spread, kept_sem, sem):
    place, core = lax.axis_index("u"), lax.axis_index("c")
    experts, total, columns = gathered.shape
    group = experts * PAIR_DEV
    both = gathered[0]
    for e in range(1, experts):
        both = both + gathered[e]
    positive_lane = both[2 * group + 3 : 2 * group + 4, :]
    near, far = both[:group] * scale, both[group : 2 * group] * scale
    kept[0:group] = near
    kept[group : 2 * group] = far

    shape = (group, columns)
    lane, kind, at_record = lanes_of(shape, 1)
    pair = iota(shape, 0)
    within = lax.rem(lane, 2 * group)
    matching = (within // ROWS_DEV == pair // PAIR_DEV) & (kind == lax.rem(pair, PAIR_DEV))
    here = matching & (lane // (2 * group) == place)
    positive = jnp.sum(jnp.where(here, positive_lane, 0.0), axis=1, keepdims=True)

    low = jnp.float32(-jnp.inf)
    near_records = jnp.where(at_record, near, low)
    far_records = jnp.where(at_record, far, low)
    highest = jnp.maximum(
        jnp.max(near_records, axis=1, keepdims=True), jnp.max(far_records, axis=1, keepdims=True)
    )
    weight = jnp.sum(jnp.exp(near_records - highest), axis=1, keepdims=True) + jnp.sum(
        jnp.exp(far_records - highest), axis=1, keepdims=True
    )
    log_total = highest + jnp.log(weight)
    chosen = jnp.zeros((group, 1), F32)
    for side, where in ((near, core), (far, 1 - core)):
        name = column_names(lane, kind, group, where)
        hit = at_record & (name.astype(F32) == positive)
        chosen = chosen + jnp.sum(jnp.where(hit, side, 0.0), axis=1, keepdims=True)
    kept[2 * group : 3 * group, :128] = jnp.broadcast_to(log_total, (group, 128))
    kept[2 * group : 3 * group, 128:256] = jnp.broadcast_to(positive, (group, 128))
    saved = pltpu.make_async_copy(kept, kept_out, kept_sem)
    saved.start()
    row_loss = log_total - chosen

    total_lane = jnp.sum(jnp.where(here, log_total, 0.0), axis=0, keepdims=True)
    loss_lane = jnp.sum(jnp.where(here, row_loss, 0.0), axis=0, keepdims=True)
    own_lane = jnp.where(lane[0:1] // (2 * group) == place, positive_lane, 0.0)
    pieces = [x[:, 128 * k : 128 * (k + 1)] for x in (total_lane, own_lane) for k in range(columns // 128)]
    loss_pieces = [
        pltpu.roll(loss_lane, PAIR_DEV, 1)[:, 128 * k : 128 * (k + 1)] for k in range(columns // 128)
    ]
    pieces = [a + b for a, b in zip(pieces, loss_pieces)] + pieces[columns // 128 :]
    message = jnp.concatenate(pieces, axis=0)
    for d in range(spread.shape[0]):
        spread[d] = message
    copy_all([pltpu.make_async_copy(spread, offered, sem)])
    saved.wait()


def column_names(lane, kind, group, core):
    wide = 2 * group
    block = (lane // wide) * CORES + core
    return block * group + (lax.rem(lane, wide) // ROWS_DEV) * PAIR_DEV + lax.rem(kind, PAIR_DEV)


def gradient_kernel(scale, factor, heard, kept, near, far, offered, loss, whole, sems):
    place, core = lax.axis_index("u"), lax.axis_index("c")
    experts, wide, columns = offered.shape
    group = wide // 2
    outer_size = heard.shape[0] // CORES
    pieces = columns // 128
    shape = (group, columns)
    lane, kind, at_record = lanes_of(shape, 1)
    pair = iota(shape, 0)
    own_name = (place * CORES + core) * group + iota((group, 1), 0)
    own_total = kept[2 * group : 3 * group, 0:1]
    own_positive = kept[2 * group : 3 * group, 128:129]
    result = jnp.zeros((wide, columns), F32)
    losses = jnp.zeros((1, columns), F32)
    for k, (side, where) in enumerate(((near, core), (far, 1 - core))):
        told = heard[where]
        for u in range(1, outer_size):
            told = told + heard[u * CORES + where]
        total = jnp.concatenate([told[i : i + 1] for i in range(pieces)], axis=1)
        positive = jnp.concatenate([told[pieces + i : pieces + i + 1] for i in range(pieces)], axis=1)
        losses = losses + jnp.where(at_record[0:1], total, 0.0)
        value = kept[group * k : group * (k + 1), :]
        name = column_names(lane, kind, group, where).astype(F32)
        hit = jnp.where(name == own_positive, 1.0, 0.0)
        by_query = (jnp.exp(value - own_total) - hit) * factor[0]
        by_query = jnp.where(at_record, by_query, 0.0).astype(BF16)
        hit = jnp.where(positive == own_name.astype(F32), 1.0, 0.0)
        by_record = (jnp.exp(jnp.where(at_record, 0.0, value - total)) - hit) * factor[0]
        by_record = jnp.where(at_record, 0.0, by_record).astype(BF16)
        rows = jnp.dot(picker(group, 0, True), by_query, preferred_element_type=F32) + jnp.dot(
            picker(group, 1, True), by_record, preferred_element_type=F32
        )
        result = result + jnp.dot(rows.astype(BF16), side[...], preferred_element_type=F32)
    whole[...] = (result * scale).astype(BF16)
    to_each(whole, offered, sems)
    loss[...] = jnp.sum(losses, axis=1, keepdims=True)


def rows_of(grads, e, index):
    tile = grads[e, pl.ds(pl.multiple_of((index // 4) * 16, 16), 16), :].astype(F32)
    piece = lax.rem(index, 4)
    quarters = [tile[ROWS_DEV * k : ROWS_DEV * (k + 1)] for k in range(4)]
    half = jnp.where(piece < 2, quarters[0], quarters[2]), jnp.where(piece < 2, quarters[1], quarters[3])
    return jnp.where(lax.rem(piece, 2) == 0, half[0], half[1])


def router_kernel(
    grads, gain, summed_in, fetched_in, tok_in, facts_in, part_out, state_out, weighted_out,
    summed, fetched, tok, facts, state, weighted, acc, sems, facts_sem, out_sems
):
    experts, _, part = grads.shape
    rows = summed.shape[1]
    count = rows // SEQ
    sources = ((summed_in, summed), (fetched_in, fetched), (tok_in, tok))

    def load(e):
        cols = pl.ds(e * part, part)
        return [
            pltpu.make_async_copy(a.at[:, cols], b.at[e], sems.at[k, e]) for k, (a, b) in enumerate(sources)
        ]

    known = pltpu.make_async_copy(facts_in, facts, facts_sem)
    loads = [load(e) for e in range(experts)]
    for e in range(experts):
        loads[e][0].start()
        loads[e][1].start()
    known.start()
    for e in range(experts):
        loads[e][2].start()

    for e in range(experts):
        cols = slice(part * e, part * (e + 1))
        w = rows_of(grads, e, lax.axis_index("expert")) * (gain[:, cols] / SEQ)
        weighted[:, cols] = w
        loads[e][0].wait()
        loads[e][1].wait()
        for q in range(count):
            row = w[q : q + 1, :]
            at = [slice(rows * k + SEQ * q, rows * k + SEQ * (q + 1)) for k in range(2)]
            terms = [summed[e, at[0], :], fetched[e, at[0], :].astype(F32), fetched[e, at[1], :].astype(F32)]
            for k, term in enumerate(terms):
                total = fold(term * row)
                spot = slice(SEQ * q, SEQ * (q + 1))
                acc[k, spot] = total if e == 0 else acc[k, spot] + total
    known.wait()
    lanes = iota((SEQ, 128), 1)
    choices = []
    for q in range(count):
        at = slice(SEQ * q, SEQ * (q + 1))
        fact = facts[at, :]
        inv = fact[:, 2:3]
        shrink = inv * inv * inv * (jnp.sum(acc[0, at], axis=1, keepdims=True) / (experts * part))
        grad_gate = []
        for k in range(2):
            along = jnp.sum(acc[1 + k, at], axis=1, keepdims=True)
            grad_gate.append(inv * along - shrink * fact[:, k : k + 1])
        gates = [fact[:, 3 + k : 4 + k] for k in range(2)]
        mean = gates[0] * grad_gate[0] + gates[1] * grad_gate[1]
        choice = jnp.zeros((SEQ, 128), F32)
        for k in range(2):
            chosen = gates[k] * (grad_gate[k] - mean)
            route = fact[:, 5 + k : 6 + k].astype(I32)
            choice = choice + jnp.where(route == lanes, chosen, 0.0)
        choices.append(choice)
        choice = jnp.where(lanes == experts, inv, choice)
        state[at] = jnp.where(lanes == experts + 1, shrink, choice)
    saved = [
        pltpu.make_async_copy(state, state_out, out_sems.at[0]),
        pltpu.make_async_copy(weighted, weighted_out, out_sems.at[1]),
    ]
    for copy in saved:
        copy.start()
    lhs = jnp.transpose(jnp.concatenate(choices, axis=0))[:experts].astype(BF16)
    tiles = part // 128
    for e in range(experts):
        loads[e][2].wait()
        block = jnp.dot(lhs, tok[e], preferred_element_type=F32)
        for k in range(tiles):
            at = experts * (tiles * e + k)
            part_out[at : at + experts, :] = block[:, 128 * k : 128 * (k + 1)]
    for copy in saved:
        copy.wait()


def token_kernel(experts, summed, weighted, state, router, out):
    rows = summed.shape[0]
    known = state[...]
    choice = jnp.where(iota(known.shape, 1) < experts, known, 0.0).astype(BF16)
    through = jnp.dot(choice, router[...], preferred_element_type=F32)
    for q in range(rows // SEQ):
        at = slice(SEQ * q, SEQ * (q + 1))
        inverse, shrink = known[at, experts : experts + 1], known[at, experts + 1 : experts + 2]
        x = inverse * weighted[q : q + 1, :] - shrink * summed[at]
        out[at] = (x + through[SEQ * q : SEQ * (q + 1)]).astype(BF16)


def token_rows(summed, weighted, state, router, experts):
    rows, width = summed.shape
    part = width // experts
    split = lambda count: pl.BlockSpec((count, part), lambda i: (0, i))
    return pl.pallas_call(
        functools.partial(token_kernel, experts),
        grid=(experts,),
        in_specs=[
            split(rows),
            split(weighted.shape[0]),
            pl.BlockSpec((rows, 128), lambda i: (0, 0)),
            split(128),
        ],
        out_specs=split(rows),
        out_shape=jax.ShapeDtypeStruct((rows, width), BF16),
        compiler_params=params(10),
        cost_estimate=cost(2 * rows * 128 * width, 5 << 20),
    )(*in_hbm(summed, weighted, state), router)


def expert_kernel(count, source, grads, gain, notes, *rest):
    sources, (out, backs, sems) = rest[:count], rest[-3:]
    experts, _, part = grads.shape
    step = pl.program_id(0)
    gate, inv, seq = notes[0, :, 0:1], notes[0, :, 1:2], notes[0, :, 2:3]
    capacity = gate.shape[0]
    loads = [pltpu.make_async_copy(sources[r], backs.at[r], sems.at[r]) for r in range(count)]

    @pl.when(step == 0)
    def _():
        for load in loads:
            load.start()

    for r in range(count):

        @pl.when(step == r)
        def _():
            loads[r].wait()

    def gradient_rows(e):
        w = rows_of(grads, e, source[step]) * (gain[:, part * e : part * (e + 1)] / SEQ)
        x = jnp.broadcast_to(w[0:1], (capacity, part))
        for s in range(1, ROWS_DEV):
            x = jnp.where(seq == s, w[s : s + 1], x)
        return x

    acc = jnp.zeros((capacity, 128), F32)
    for e in range(experts):
        back = backs[step, :, part * e : part * (e + 1)].astype(F32)
        acc = acc + fold(gradient_rows(e) * back)
    shrink = inv * inv * inv * (jnp.sum(acc, axis=1, keepdims=True) / (experts * part))
    keep, drop = gate * inv, gate * shrink
    for e in range(experts):
        cols = slice(part * e, part * (e + 1))
        out[0, :, cols] = (keep * gradient_rows(e) - drop * backs[step, :, cols].astype(F32)).astype(BF16)


def expert_rows(source, grads, gain, notes, backs, before=None):
    experts, capacity = notes.shape[:2]
    width = gain.shape[1]
    count = len(backs)
    whole = lambda shape: pl.BlockSpec(shape, lambda i, p: (0,) * len(shape))
    block = lambda i, p: (p[i], 0, 0)
    kept = [] if before is None else [before]
    return pl.pallas_call(
        functools.partial(expert_kernel, count),
        grid_spec=pltpu.PrefetchScalarGridSpec(
            num_scalar_prefetch=1,
            grid=(count,),
            in_specs=[
                whole(grads.shape),
                whole((1, width)),
                pl.BlockSpec((1, capacity, notes.shape[2]), block),
            ]
            + [HBM] * (count + len(kept)),
            out_specs=pl.BlockSpec((1, capacity, width), block),
            scratch_shapes=[
                pltpu.VMEM((count, capacity, width), BF16),
                pltpu.SemaphoreType.DMA((count,)),
            ],
        ),
        out_shape=jax.ShapeDtypeStruct((experts, capacity, width), BF16),
        input_output_aliases={4 + count: 0} if kept else {},
        compiler_params=params(16),
        cost_estimate=cost(12 * count * capacity * width, count << 20),
    )(source, grads, gain, notes, *in_hbm(*backs), *kept)


def shards(tokens, routes, positives, expert_out, router, norm_gain, loss_scale):
    experts, capacity, width = expert_out.shape[2:]
    rows = tokens.shape[0]
    slots = experts * capacity
    outer = lax.axis_size("u")
    mine = lax.axis_index("expert").astype(I32)
    mine_at = mine[None]
    part = width // experts
    group = PAIR_DEV * experts
    pairs = group * outer * CORES
    scale = 4.0 / math.sqrt(width)
    gain = norm_gain[None, :]
    columns = outer * experts * ROWS_DEV

    received = exchange(expert_out.reshape(experts, capacity, width), "expert").reshape(slots, width)
    gates, slot = routing(tokens, routes, router, experts, capacity)
    lane = jnp.arange(columns, dtype=I32)
    spread_positive = jnp.where(
        (lane % (2 * group)) // ROWS_DEV == mine,
        jnp.where(lane % ROWS_DEV == 0, positives[0], positives[1]) * (lane % ROWS_DEV < PAIR_DEV),
        0,
    ).astype(F32)

    summed, sliced, inverse = forward(tokens, received, slot, gates, gain, experts)
    own = exchange(sliced, "expert").reshape(2 * group, part)
    facts = jnp.concatenate(
        [jnp.zeros((rows, 2), F32), inverse, gates, routes.astype(F32)], axis=1
    )
    facts = jnp.pad(facts, ((0, 0), (0, 128 - facts.shape[1])))
    backs = list(pack(mine_at, summed, slot.T, experts, capacity))

    def move(after, turns):
        after, *ready = lax.optimization_barrier((after, *[backs[r] for r in turns]))
        for r, x in zip(turns, ready):
            pairs = [(i, (i // RING + r // RING) % HALVES * RING + (i + r) % RING) for i in range(experts)]
            backs[r] = lax.ppermute(x, "expert", pairs)
        return after


    def landed(value, turns):
        value, *done = lax.optimization_barrier((value, *[backs[r] for r in turns]))
        for r, x in zip(turns, done):
            backs[r] = x
        return value

    slot_ids = jnp.arange(slots, dtype=I32)[None, :]
    picks = [slot[:, k : k + 1] == slot_ids for k in range(2)]
    gate_slot = jnp.sum(
        jnp.where(picks[0], gates[:, 0:1], 0.0) + jnp.where(picks[1], gates[:, 1:2], 0.0), axis=0
    )
    taken = picks[0] | picks[1]
    inverse_slot = jnp.sum(jnp.where(taken, inverse, 0.0), axis=0)
    sequence = (jnp.arange(rows, dtype=I32) // SEQ).astype(F32)
    sequence_slot = jnp.sum(jnp.where(taken, sequence[:, None], 0.0), axis=0)
    notes = jnp.stack([gate_slot, inverse_slot, sequence_slot, spread_positive])
    notes = jnp.pad(notes, ((0, 4), (0, 0)))

    own, *backs = lax.optimization_barrier((own, *backs))
    near = spread(own, "u", outer)
    facts, fetched = overlaps(summed, received, slot, facts, experts)
    near, facts, fetched = lax.optimization_barrier((near, facts, fetched))
    far = swap_core(near)
    near, far = near.reshape(columns, part), far.reshape(columns, part)
    offered = pl.pallas_call(
        scores_kernel,
        in_specs=[VMEM] * 4,
        out_specs=HBM,
        out_shape=pltpu.HBM((experts, 2 * group + 8, columns), F32),
        scratch_shapes=[pltpu.VMEM((2 * group + 8, columns), F32), pltpu.SemaphoreType.DMA((experts,))],
        compiler_params=params(2),
    )(own, near, far, notes)
    offered = move(offered, TURNS[0])
    gathered = exchange(offered, "expert")
    devices = outer * CORES
    offered, kept = pl.pallas_call(
        functools.partial(totals_kernel, scale),
        in_specs=[VMEM],
        out_specs=[HBM] * 2,
        out_shape=[pltpu.HBM((devices, 8, 128), F32), pltpu.HBM((3 * group, columns), F32)],
        scratch_shapes=[
            pltpu.VMEM((3 * group, columns), F32),
            pltpu.VMEM((devices, 8, 128), F32),
            pltpu.SemaphoreType.DMA(()),
            pltpu.SemaphoreType.DMA(()),
        ],
        compiler_params=params(2),
    )(gathered)
    heard = exchange(offered, ("u", "c"))
    heard = landed(heard, TURNS[0][:1])
    offered, loss = pl.pallas_call(
        functools.partial(gradient_kernel, scale),
        in_specs=[SMEM] + [VMEM] * 4,
        out_specs=[HBM, VMEM],
        out_shape=[pltpu.HBM((experts, 2 * group, part), BF16), jax.ShapeDtypeStruct((1, 1), F32)],
        scratch_shapes=[pltpu.VMEM((2 * group, part), BF16), pltpu.SemaphoreType.DMA((experts,))],
        compiler_params=params(2),
    )((loss_scale / pairs)[None], heard, kept, near, far)
    offered = move(offered, TURNS[1])
    grads = exchange(offered, "expert")
    grads = landed(grads, TURNS[0][1:])

    router_part, state, weighted = pl.pallas_call(
        router_kernel,
        in_specs=[VMEM] * 2 + [HBM] * 4,
        out_specs=[VMEM, HBM, HBM],
        out_shape=[
            jax.ShapeDtypeStruct((width * experts // 128, 128), F32),
            pltpu.HBM((rows, 128), F32),
            pltpu.HBM((rows // SEQ, width), F32),
        ],
        scratch_shapes=[
            pltpu.VMEM((experts, rows, part), F32),
            pltpu.VMEM((experts, 2 * rows, part), BF16),
            pltpu.VMEM((experts, rows, part), BF16),
            pltpu.VMEM((rows, 128), F32),
            pltpu.VMEM((rows, 128), F32),
            pltpu.VMEM((rows // SEQ, width), F32),
            pltpu.VMEM((3, rows, 128), F32),
            pltpu.SemaphoreType.DMA((3, experts)),
            pltpu.SemaphoreType.DMA(()),
            pltpu.SemaphoreType.DMA((2,)),
        ],
        compiler_params=params(16),
    )(grads, gain, *in_hbm(summed, fetched, tokens, facts))
    router_part = move(router_part, TURNS[2])
    router_part = exchange(router_part.reshape(outer, -1, 128), "u")
    turned = jnp.pad(router.T, ((0, 128 - experts), (0, 0)))
    token_grad = token_rows(summed, weighted, state, turned, experts)
    router_part, token_grad = lax.optimization_barrier((router_part, token_grad))
    router_part = jnp.sum(router_part, axis=0)
    router_part = spread(router_part, ("c", "expert"), CORES * experts)
    held = lax.dynamic_slice_in_dim(gathered[:, 2 * group : 2 * group + 3], mine * capacity, capacity, axis=2)
    held = jnp.pad(jnp.transpose(held, (0, 2, 1)), ((0, 0), (0, 0), (0, 5)))
    parts = [(0,) + TURNS[0] + TURNS[1], TURNS[2]]
    places = [
        jnp.stack([shifted(mine, (HALVES - r // RING) % HALVES, (RING - r % RING) % RING) for r in turns])
        for turns in parts
    ]
    expert_grad = expert_rows(places[0], grads, gain, held, [backs[r] for r in parts[0]])
    router_part, expert_grad = lax.optimization_barrier((router_part, expert_grad))
    router_part = jnp.sum(router_part, axis=0)
    router_all = spread(router_part, "u", outer)
    expert_grad = expert_rows(places[1], grads, gain, held, [backs[r] for r in parts[1]], expert_grad)
    router_all, expert_grad = lax.optimization_barrier((router_all, expert_grad))
    router_grad = router_all.reshape(-1, experts, 128).transpose(1, 0, 2).reshape(experts, width).T
    return token_grad, expert_grad.reshape(1, 1, experts, capacity, width), router_grad, loss[0, 0] / pairs


def solution(mesh):
    outer = mesh.shape["dp"] // CORES
    fine = Mesh(mesh.devices.reshape(outer, CORES, mesh.shape["expert"]), ("u", "c", "expert"))
    everywhere = ("u", "c", "expert")
    return jax.shard_map(
        shards,
        mesh=fine,
        in_specs=(
            P(everywhere, None),
            P(everywhere, None),
            P(everywhere),
            P(("u", "c"), "expert", None, None, None),
            P(),
            P(),
            P(),
        ),
        out_specs=(P(everywhere, None), P(("u", "c"), "expert", None, None, None), P(), P()),
        check_vma=False,
    )
```
